32 devices in a mesh: dp: 4 (over y, x), ctx: 2 (over core), tp: 4 (over z).
Axes of the slice: x: 2, y: 2, z: 4, core: 2. Of those that a mesh axis runs over, the one named last changes fastest.
Arguments:
- tokens: bfloat16 [16, 2048, 1024], P('dp', 'ctx', 'tp'), may hold values from -6 to 6
- cotangent: bfloat16 [16, 2048, 1024], P('dp', 'ctx'), may hold values from -6 to 6
- prefix: int32 [16], P('dp'), may hold values from 204 to 1024, as said below
- w_query: bfloat16 [1024, 1024], P(('dp', 'ctx'), 'tp'), may hold values from -0.1875 to 0.1875
- w_key: bfloat16 [1024, 1024], P(('dp', 'ctx'), 'tp'), may hold values from -0.1875 to 0.1875
- w_value: bfloat16 [1024, 1024], P(('dp', 'ctx'), 'tp'), may hold values from -0.1875 to 0.1875
- w_out: bfloat16 [1024, 1024], P('tp', ('dp', 'ctx')), may hold values from -1.5 to 1.5
- w_up: bfloat16 [1024, 4096], P(('dp', 'ctx'), 'tp'), may hold values from -0.1875 to 0.1875
- w_down: bfloat16 [4096, 1024], P('tp', ('dp', 'ctx')), may hold values from -0.09375 to 0.09375
- state_query: bfloat16 [512, 1024], P(('dp', 'ctx'), 'tp'), may hold values from -6 to 6
- state_init: bfloat16 [512, 1024], P(('dp', 'ctx'), 'tp'), may hold values from -6 to 6
- gain_attn: bfloat16 [8, 128], P('tp', ('dp', 'ctx')), may hold values from 0.5 to 1.5
- gain_mlp: bfloat16 [8, 128], P('tp', ('dp', 'ctx')), may hold values from 0.5 to 1.5
- bias_table: bfloat16 [8, 32], P('tp', ('dp', 'ctx')), may hold values from -3 to 3
- gate_bias: bfloat16 [8, 128], P('tp', ('dp', 'ctx')), may hold values from -2 to 4
- state_key: bfloat16 [8, 128, 128], P('tp', ('dp', 'ctx')), may hold values from -0.5 to 0.5
- state_value: bfloat16 [8, 128, 128], P('tp', ('dp', 'ctx')), may hold values from -0.5 to 0.5
Outputs:
- output: bfloat16 [16, 2048, 1024], P('dp', 'ctx', 'tp')
- grad_tokens: bfloat16 [16, 2048, 1024], P('dp', 'ctx', 'tp')
- grad_w_query: float32 [1024, 1024], P(('dp', 'ctx'), 'tp')
- grad_w_key: float32 [1024, 1024], P(('dp', 'ctx'), 'tp')
- grad_w_value: float32 [1024, 1024], P(('dp', 'ctx'), 'tp')
- grad_w_out: float32 [1024, 1024], P('tp', ('dp', 'ctx'))
- grad_w_up: float32 [1024, 4096], P(('dp', 'ctx'), 'tp')
- grad_w_down: float32 [4096, 1024], P('tp', ('dp', 'ctx'))
- grad_state_query: float32 [512, 1024], P(('dp', 'ctx'), 'tp')
- grad_state_init: float32 [512, 1024], P(('dp', 'ctx'), 'tp')
- grad_gain_attn: float32 [8, 128], P('tp', ('dp', 'ctx'))
- grad_gain_mlp: float32 [8, 128], P('tp', ('dp', 'ctx'))
- grad_bias_table: float32 [8, 32], P('tp', ('dp', 'ctx'))
- grad_gate_bias: float32 [8, 128], P('tp', ('dp', 'ctx'))
- grad_state_key: float32 [8, 128, 128], P('tp', ('dp', 'ctx'))
- grad_state_value: float32 [8, 128, 128], P('tp', ('dp', 'ctx'))
The draws below stay inside these ranges and needn't reach their ends.
Inputs may be any that keep to these rules, and one draw needn't show every extreme that they name: `prefix`: tokens of each sequence that attend both ways within the window; some sequence has exactly the least and some exactly the most in every draw.
All inputs are finite; a program needn't handle non-finite values.
Results may differ from the reference program's by a relative error of at most 0.029.
Values may be sent and summed in bfloat16 or wider, within the bound.
No kernel may reach another device: no remote copies, remote signals or barrier semaphores. Data moves between devices by JAX's collectives and lax.ppermute only.
A program may use at most 448 MiB of HBM per device.

```python
import jax
import jax.numpy as jnp
import numpy as np
from jax import lax

D = 1024
HEADS = 8
HEAD_SIZE = 128
FF = 4096
STATES = 512
BLOCK = 512
NBUCKET = 32
SEQS = 16
LEN = 2048


def draw_prefix(key, part):
    low_end = LEN // 10
    high_end = LEN // 2
    drawn = jax.random.randint(jax.random.fold_in(key, 11), (SEQS,), low_end, high_end + 1)
    spots = jax.random.permutation(jax.random.fold_in(key, 12), SEQS)
    drawn = drawn.at[spots[0]].set(high_end)
    drawn = drawn.at[spots[1]].set(low_end)
    return drawn.astype(jnp.int32)


def steps_of(own_key, dims, pieces, least, largest):
    def one(axis_at, shards_of):
        steps = jax.random.uniform(jax.random.fold_in(jax.random.fold_in(own_key, 6), axis_at), (shards_of,), jnp.float32, least / len(pieces), largest / len(pieces))
        return jnp.repeat(jnp.exp(steps), dims[axis_at] // shards_of).reshape((-1,) + (1,) * (len(dims) - axis_at - 1))

    level = one(*pieces[0])
    for cut in pieces[1:]:
        level = level * one(*cut)
    return level


def noise(stream_key, shape, scale, bound, split=(), kind=jnp.bfloat16):
    entries = jax.random.normal(stream_key, shape, jnp.float32) * scale
    if len(split) > 0:
        entries = steps_of(stream_key, shape, split, -0.22, 0.18) * entries
    return jnp.clip(entries, min=-bound, max=bound).astype(kind)


def setup_inputs(seed: int = 0) -> dict:
    key_list = jax.random.split(jax.random.key(seed), 18)
    return {
        "tokens": noise(key_list[0], (SEQS, LEN, D), 1.0, 6.0, ((0, 4), (1, 2), (2, 4))),
        "cotangent": noise(key_list[1], (SEQS, LEN, D), 1.0, 6.0, ((0, 4), (1, 2))),
        "prefix": draw_prefix(jax.random.fold_in(key_list[17], 71), 0),
        "w_query": noise(key_list[3], (D, D), D ** -0.5, 0.1875, ((0, 8), (1, 4))),
        "w_key": noise(key_list[4], (D, D), D ** -0.5, 0.1875, ((0, 8), (1, 4))),
        "w_value": noise(key_list[5], (D, D), D ** -0.5, 0.1875, ((0, 8), (1, 4))),
        "w_out": noise(key_list[6], (D, D), (D // 64) ** -0.5, 1.5, ((0, 4), (1, 8))),
        "w_up": noise(key_list[7], (D, FF), D ** -0.5, 0.1875, ((0, 8), (1, 4))),
        "w_down": noise(key_list[8], (FF, D), FF ** -0.5, 0.09375, ((0, 4), (1, 8))),
        "state_query": noise(key_list[9], (STATES, D), 1.0, 6.0, ((0, 8), (1, 4))),
        "state_init": noise(key_list[10], (STATES, D), 1.0, 6.0, ((0, 8), (1, 4))),
        "gain_attn": jnp.clip(1.0 + 0.1 * jax.random.normal(key_list[11], (HEADS, HEAD_SIZE), jnp.float32), 0.5, 1.5).astype(jnp.bfloat16),
        "gain_mlp": jnp.clip(1.0 + 0.1 * jax.random.normal(key_list[12], (HEADS, HEAD_SIZE), jnp.float32), 0.5, 1.5).astype(jnp.bfloat16),
        "bias_table": noise(key_list[13], (HEADS, NBUCKET), 0.5, 3.0, ((0, 4), (1, 8))),
        "gate_bias": jnp.clip(-2.0 + 6.0 * jax.random.uniform(key_list[14], (HEADS, HEAD_SIZE), jnp.float32) ** steps_of(key_list[14], (HEADS, HEAD_SIZE), ((0, 4), (1, 8)), -0.2, 0.2), -2.0, 4.0).astype(jnp.bfloat16),
        "state_key": noise(key_list[15], (HEADS, HEAD_SIZE, HEAD_SIZE), HEAD_SIZE ** -0.5, 0.5, ((0, 4), (1, 8))),
        "state_value": noise(key_list[16], (HEADS, HEAD_SIZE, HEAD_SIZE), HEAD_SIZE ** -0.5, 0.5, ((0, 4), (1, 8))),
    }


FULL_PRECISION = lax.Precision.HIGHEST
MASKED = -1e+30

@jax.custom_vjp
def low(v):
    return lax.optimization_barrier(v.astype(jnp.bfloat16)).astype(jnp.float32)

@jax.custom_vjp
def low_back(v):
    return v

def low_keep(v):
    return (low(v), None)

def low_pass(kept, grad):
    return (grad,)

def back_keep(v):
    return (v, None)

def back_low(kept, grad):
    return (low(grad),)
low.defvjp(low_keep, low_pass)
low_back.defvjp(back_keep, back_low)

def rounded_both(value):
    return low(low_back(value))

def bucket_index(block_size):
    query_pos = np.arange(block_size)[:, None] + block_size
    key_pos = np.arange(2 * block_size)[None, :]
    distance = query_pos - key_pos
    upper_part = (distance < 0).astype(np.int32) * 16
    magnitude = np.abs(distance)
    scaled = np.log(np.maximum(magnitude, 1) / 8.0) / np.log(16.0) * 8.0
    far_bucket = np.minimum(8 + np.floor(np.maximum(scaled, 0.0)).astype(np.int32), 15)
    return (upper_part + np.where(magnitude < 8, magnitude, far_bucket)).astype(np.int32)

def matmul(left, right):
    return jnp.dot(left, right, precision=FULL_PRECISION, preferred_element_type=jnp.float32)

def rms_norm(features, gain_vector):
    return features * lax.rsqrt(lax.optimization_barrier(jnp.mean(features * features, axis=-1, keepdims=True)) + 1e-06) * gain_vector

def softmax_rows(scores):
    row_peak = lax.optimization_barrier(jnp.max(scores, axis=-1, keepdims=True))
    raised = jnp.exp(scores - row_peak)
    return raised / lax.optimization_barrier(jnp.sum(raised, axis=-1, keepdims=True))

def sequence_forward(token_rows, prefix_length, weights):
    w_query, w_key, w_value, w_out, w_up, w_down, state_query, state_init, gain_attn, gain_mlp, bias_rows, gate_rows, state_key, state_value = weights
    block_count = LEN // BLOCK
    scores_scale = HEAD_SIZE ** (-0.5)
    attn_in = low(rms_norm(token_rows, gain_attn.reshape(D)))
    queries = rounded_both(matmul(attn_in, w_query)).reshape(block_count, BLOCK, HEADS, HEAD_SIZE)
    key_rows = rounded_both(matmul(attn_in, w_key)).reshape(block_count, BLOCK, HEADS, HEAD_SIZE)
    value_rows = rounded_both(matmul(attn_in, w_value)).reshape(block_count, BLOCK, HEADS, HEAD_SIZE)
    query_heads = state_query.reshape(STATES, HEADS, HEAD_SIZE)

    def state_read(pair):
        keys_of_block, values_of_block = pair
        scores = low_back(jnp.einsum('mhe,the->hmt', query_heads, keys_of_block, precision=FULL_PRECISION) * scores_scale)
        probs = softmax_rows(scores)
        return low_back(jnp.einsum('hmt,the->mhe', low(probs), values_of_block, precision=FULL_PRECISION))
    contrib = lax.map(jax.checkpoint(state_read), (key_rows, value_rows))
    gate_value = jax.nn.sigmoid(gate_rows)

    def advance(state, element_entry):
        return (gate_value * state + (1.0 - gate_value) * element_entry, state)
    final_state, state_seq = lax.scan(advance, state_init.reshape(STATES, HEADS, HEAD_SIZE), contrib)
    state_reduced = low(state_seq)
    state_key_rows = rounded_both(jnp.einsum('bmhe,hef->bmhf', state_reduced, state_key, precision=FULL_PRECISION))
    state_values = rounded_both(jnp.einsum('bmhe,hef->bmhf', state_reduced, state_value, precision=FULL_PRECISION))
    zero_block = jnp.zeros((1, BLOCK, HEADS, HEAD_SIZE), jnp.float32)
    window_keys = jnp.concatenate([jnp.concatenate([zero_block, key_rows[:-1]], 0), key_rows], 1)
    window_values = jnp.concatenate([jnp.concatenate([zero_block, value_rows[:-1]], 0), value_rows], 1)
    bias_full = bias_rows[:, jnp.asarray(bucket_index(BLOCK))]

    def token_read(element_entry):
        block_ordinal, queries_of_block, keys_of_block, values_of_block, block_state_keys, block_state_values = element_entry
        window_scores = jnp.einsum('ihe,jhe->hij', queries_of_block, keys_of_block, precision=FULL_PRECISION) * scores_scale + bias_full
        scores_of_state = jnp.einsum('ogl,sgl->gos', queries_of_block, block_state_keys, precision=FULL_PRECISION) * scores_scale
        scores = low_back(jnp.concatenate([window_scores, scores_of_state], -1))
        query_pos = block_ordinal * BLOCK + jnp.arange(BLOCK, dtype=jnp.int32)
        key_pos = (block_ordinal - 1) * BLOCK + jnp.arange(2 * BLOCK, dtype=jnp.int32)
        permitted_mask = (key_pos[None, :] >= 0) & ((key_pos[None, :] <= query_pos[:, None]) | (key_pos[None, :] < prefix_length))
        permitted_mask = jnp.concatenate([permitted_mask, jnp.ones((BLOCK, STATES), jnp.bool_)], 1)
        masked = jnp.where(permitted_mask[None], scores, MASKED)
        probs = low(softmax_rows(masked))
        from_window = jnp.einsum('hij,jhe->ihe', probs[:, :, :2 * BLOCK], values_of_block, precision=FULL_PRECISION)
        from_state = jnp.einsum('wyd,dwg->ywg', probs[:, :, 2 * BLOCK:], block_state_values, precision=FULL_PRECISION)
        return from_window + from_state
    block_numbers = jnp.arange(block_count, dtype=jnp.int32)
    heads_out = lax.map(jax.checkpoint(token_read), (block_numbers, queries, window_keys, window_values, state_key_rows, state_values))
    attended = rounded_both(heads_out.reshape(LEN, D))
    attn_branch = low_back(matmul(attended, w_out))
    middle = token_rows + attn_branch
    mlp_in = low(rms_norm(low(middle), gain_mlp.reshape(D)))
    hidden_pre = low_back(matmul(mlp_in, w_up))
    hidden = low(jax.nn.gelu(hidden_pre, approximate=False))
    return middle + matmul(hidden, w_down)

def reference(tokens, cotangent, prefix, w_query, w_key, w_value, w_out, w_up, w_down, state_query, state_init, gain_attn, gain_mlp, bias_table, gate_bias, state_key, state_value):
    weights = tuple((weight.astype(jnp.float32) for weight in (w_query, w_key, w_value, w_out, w_up, w_down, state_query, state_init, gain_attn, gain_mlp, bias_table, gate_bias, state_key, state_value)))
    one_sequence = jax.checkpoint(sequence_forward)

    def forward(token_values, weight_values):

        def per_item(element_entry):
            return one_sequence(element_entry[0], element_entry[1], weight_values)
        return lax.map(per_item, (token_values, prefix))
    output, pullback = jax.vjp(forward, tokens.astype(jnp.float32), weights)
    grad_tokens, grads = pullback(cotangent.astype(jnp.float32))
    return (output.astype(jnp.bfloat16), grad_tokens.astype(jnp.bfloat16), grads[0], grads[1], grads[2], grads[3], grads[4], grads[5], grads[6], grads[7], grads[8], grads[9], grads[10], grads[11], grads[12], grads[13])
```

```python
import functools

import jax
import jax.numpy as jnp
import numpy as np
from jax import lax
from jax.experimental import pallas as pl
from jax.experimental.pallas import tpu as pltpu
from jax.sharding import PartitionSpec as P

HEAD_SIZE = 128
BLOCK = 512


EPSILON = 1e-06
MASKED = -1e30
ROWS_FORWARD = 128
KEYS_BACKWARD = 256


def from_behind(value, axis, steps):
    count = lax.axis_size(axis)
    first, last = (max(0, -steps), min(count, count - steps))
    return lax.ppermute(value, axis, [(source, source + steps) for source in range(first, last)])


def prefix_2(array, axis, join, neutral, backward):
    count = lax.axis_size(axis)
    place = lax.axis_index(axis)
    ahead = count - 1 - place if backward else place
    gathered = jax.tree.map(
        lambda a, kind: lax.all_gather(a.astype(kind), axis), array, (jnp.bfloat16, jnp.bfloat16)
    )
    state = jax.tree.map(lambda a, e: jnp.zeros_like(a) + jnp.asarray(e, a.dtype), array, neutral)

    def one(hop, state):
        source = count - 1 - hop if backward else hop
        return join(
            state,
            jax.tree.map(
                lambda a, own: lax.dynamic_index_in_dim(a, source, 0, False).astype(own.dtype),
                gathered,
                array,
            ),
        )

    return lax.fori_loop(0, ahead, one, state)


def bucket_index(block_size):
    query_pos = np.arange(block_size)[:, None] + block_size
    key_pos = np.arange(2 * block_size)[None, :]
    distance = query_pos - key_pos
    upper_part = (distance < 0).astype(np.int32) * 16
    magnitude = np.abs(distance)
    scaled = np.log(np.maximum(magnitude, 1) / 8.0) / np.log(16.0) * 8.0
    far_bucket = np.minimum(8 + np.floor(np.maximum(scaled, 0.0)).astype(np.int32), 15)
    return (upper_part + np.where(magnitude < 8, magnitude, far_bucket)).astype(np.int32)


def norm_forward(features, gain_vector):
    inverse = lax.rsqrt(jnp.mean(features * features, axis=-1, keepdims=True) + EPSILON)
    normed = features * inverse
    return (normed, inverse, (normed * gain_vector).astype(jnp.bfloat16))


def norm_backward(grad_normed, normed, inverse, gain_vector):
    scaled = grad_normed * gain_vector
    grad_in = inverse * (scaled - normed * jnp.mean(scaled * normed, axis=-1, keepdims=True))
    return (grad_in, jnp.sum(grad_normed * normed, axis=0))


def compose(earlier, later_pair):
    return (earlier[0] * later_pair[0], later_pair[0] * earlier[1] + later_pair[1])


def bias_matrix(bias_rows, bucket):
    summed = jnp.zeros((bias_rows.shape[0],) + bucket.shape, jnp.float32)
    for number in range(bias_rows.shape[1]):
        summed = (
            summed
            + bias_rows[:, number][:, None, None] * (bucket == number).astype(jnp.float32)[None]
        )
    return summed


def bias_gradient(grad_matrix, bucket, bucket_count):
    columns = [
        jnp.sum(grad_matrix * (bucket == number).astype(jnp.float32)[None], axis=(1, 2))
        for number in range(bucket_count)
    ]
    return jnp.stack(columns, axis=1)


def body(
    tokens,
    cotangent,
    prefix,
    w_query,
    w_key,
    w_value,
    w_out,
    w_up,
    w_down,
    state_query,
    state_init,
    gain_attn,
    gain_mlp,
    bias_table,
    gate_bias,
    state_key,
    state_value,
):
    (
        query_full,
        key_full,
        value_full,
        out_full,
        up_full,
        down_full,
        squery_full,
        sinit_full,
        gain_one,
        gain_two,
        bias_rows,
        gate_rows,
        state_key_complete,
        svalue_full,
    ) = (
        lax.all_gather(w_query, ("dp", "ctx"), axis=0, tiled=True),
        lax.all_gather(w_key, ("dp", "ctx"), axis=0, tiled=True),
        lax.all_gather(w_value, ("dp", "ctx"), axis=0, tiled=True),
        lax.all_gather(w_out, ("dp", "ctx"), axis=1, tiled=True),
        lax.all_gather(w_up, ("dp", "ctx"), axis=0, tiled=True),
        lax.all_gather(w_down, ("dp", "ctx"), axis=1, tiled=True),
        lax.all_gather(state_query, ("dp", "ctx"), axis=0, tiled=True),
        lax.all_gather(state_init, ("dp", "ctx"), axis=0, tiled=True),
        lax.all_gather(gain_attn, ("dp", "ctx"), axis=1, tiled=True),
        lax.all_gather(gain_mlp, ("dp", "ctx"), axis=1, tiled=True),
        lax.all_gather(bias_table, ("dp", "ctx"), axis=1, tiled=True),
        lax.all_gather(gate_bias, ("dp", "ctx"), axis=1, tiled=True),
        lax.all_gather(state_key, ("dp", "ctx"), axis=1, tiled=True),
        lax.all_gather(state_value, ("dp", "ctx"), axis=1, tiled=True),
    )
    seq_count = tokens.shape[0]
    length = tokens.shape[1]
    shard_width = tokens.shape[2]
    full_width = cotangent.shape[2]
    block_count = length // BLOCK
    row_count = seq_count * length
    local_head_count = bias_rows.shape[0]
    local_width = local_head_count * HEAD_SIZE
    state_slot_count = squery_full.shape[0]
    scores_scale = HEAD_SIZE ** (-0.5)
    local_shape = (seq_count, block_count, BLOCK, local_head_count, HEAD_SIZE)
    element_count = seq_count * block_count
    token_full, gain_one_full = (
        lax.all_gather(tokens, "tp", axis=2, tiled=True),
        lax.all_gather(gain_one, "tp", axis=0, tiled=True),
    )
    gain_one_vec = gain_one_full.reshape(full_width).astype(jnp.float32)
    normed_one, inverse_one, attn_in = norm_forward(
        token_full.reshape(row_count, full_width).astype(jnp.float32), gain_one_vec
    )
    queries = (
        jnp.dot(attn_in, query_full, preferred_element_type=jnp.float32)
        .astype(jnp.bfloat16)
        .reshape(local_shape)
    )
    key_rows = (
        jnp.dot(attn_in, key_full, preferred_element_type=jnp.float32)
        .astype(jnp.bfloat16)
        .reshape(local_shape)
    )
    value_rows = (
        jnp.dot(attn_in, value_full, preferred_element_type=jnp.float32)
        .astype(jnp.bfloat16)
        .reshape(local_shape)
    )
    last_keys, last_values = from_behind((key_rows[:, -1], value_rows[:, -1]), "ctx", 1)
    window_keys = jnp.concatenate(
        [jnp.concatenate([last_keys[:, None], key_rows[:, :-1]], 1), key_rows], 2
    )
    window_values = jnp.concatenate(
        [jnp.concatenate([last_values[:, None], value_rows[:, :-1]], 1), value_rows], 2
    )
    query_heads = squery_full.reshape(state_slot_count, local_head_count, HEAD_SIZE)
    read_scores = (
        jnp.einsum("mhe,sbthe->sbhmt", query_heads, key_rows, preferred_element_type=jnp.float32)
        * scores_scale
    )
    read_peak = jnp.max(read_scores, axis=-1, keepdims=True)
    read_raised = jnp.exp(read_scores - read_peak)
    read_probs = read_raised / jnp.sum(read_raised, axis=-1, keepdims=True)
    read_low = read_probs.astype(jnp.bfloat16)
    contrib = jnp.einsum(
        "sbhmt,sbthe->sbmhe", read_low, value_rows, preferred_element_type=jnp.float32
    )
    contrib = contrib.reshape(seq_count, block_count, state_slot_count, local_width)
    gate_value = jax.nn.sigmoid(gate_rows.reshape(local_width).astype(jnp.float32))
    gate_power = jnp.ones((local_width,), jnp.float32)
    accumulated = jnp.zeros((seq_count, state_slot_count, local_width), jnp.float32)
    for block_index in range(block_count):
        accumulated = gate_value * accumulated + (1.0 - gate_value) * contrib[:, block_index]
        gate_power = gate_power * gate_value
    identity = (jnp.ones((local_width,), jnp.float32), jnp.zeros_like(accumulated))
    lead_power, lead_state = prefix_2((gate_power, accumulated), "ctx", compose, identity, False)
    entry_state = lead_power * sinit_full.astype(jnp.float32) + lead_state
    state_list = [entry_state]
    block_index = 0
    state_list.append(gate_value * state_list[-1] + (1.0 - gate_value) * contrib[:, block_index])
    stacked = jnp.stack(state_list, axis=1)
    state_reduced = stacked.astype(jnp.bfloat16).reshape(
        seq_count, block_count, state_slot_count, local_head_count, HEAD_SIZE
    )
    state_key_rows = jnp.einsum(
        "cazqr,qrx->cazqx", state_reduced, state_key_complete, preferred_element_type=jnp.float32
    ).astype(jnp.bfloat16)
    state_values = jnp.einsum(
        "cazqr,qrx->cazqx", state_reduced, svalue_full, preferred_element_type=jnp.float32
    ).astype(jnp.bfloat16)
    bucket = jnp.asarray(bucket_index(BLOCK))
    bias_full = bias_matrix(bias_rows.astype(jnp.float32), bucket)
    block_ids = lax.axis_index("ctx") * block_count + jnp.arange(block_count, dtype=jnp.int32)
    query_pos = block_ids[:, None] * BLOCK + jnp.arange(BLOCK, dtype=jnp.int32)[None, :]
    key_pos = (block_ids[:, None] - 1) * BLOCK + jnp.arange(2 * BLOCK, dtype=jnp.int32)[None, :]
    causal = (key_pos[:, None, :] >= 0) & (key_pos[:, None, :] <= query_pos[:, :, None])
    in_prefix = (key_pos[None, :, None, :] >= 0) & (
        key_pos[None, :, None, :] < prefix[:, None, None, None]
    )
    permitted_mask = (causal[None] | in_prefix).reshape(element_count, 1, BLOCK, 2 * BLOCK)
    flattened_queries = queries.reshape(element_count, BLOCK, local_head_count, HEAD_SIZE)
    flattened_window_keys = window_keys.reshape(
        element_count, 2 * BLOCK, local_head_count, HEAD_SIZE
    )
    flattened_window_values = window_values.reshape(
        element_count, 2 * BLOCK, local_head_count, HEAD_SIZE
    )
    flattened_state_keys = state_key_rows.reshape(
        element_count, state_slot_count, local_head_count, HEAD_SIZE
    )
    flattened_state_values = state_values.reshape(
        element_count, state_slot_count, local_head_count, HEAD_SIZE
    )

    def block_score_rows(
        block_query_rows, block_window_key_rows, block_state_key_rows, block_permitted_mask
    ):
        window_part = (
            jnp.einsum(
                "ihe,jhe->hij",
                block_query_rows,
                block_window_key_rows,
                preferred_element_type=jnp.float32,
            )
            * scores_scale
            + bias_full
        )
        state_part = (
            jnp.einsum(
                "yat,zat->ayz",
                block_query_rows,
                block_state_key_rows,
                preferred_element_type=jnp.float32,
            )
            * scores_scale
        )
        return (jnp.where(block_permitted_mask, window_part, MASKED), state_part)

    def attend_one_block(element_entry):
        (
            block_query_rows,
            block_window_key_rows,
            block_window_value_rows,
            block_state_key_rows,
            block_state_value_rows,
            block_permitted_mask,
        ) = element_entry
        window_scores, scores_of_state = block_score_rows(
            block_query_rows, block_window_key_rows, block_state_key_rows, block_permitted_mask
        )
        row_peak = jnp.maximum(jnp.max(window_scores, axis=-1), jnp.max(scores_of_state, axis=-1))
        window_raised = jnp.exp(window_scores - row_peak[..., None])
        state_raised = jnp.exp(scores_of_state - row_peak[..., None])
        denominator = jnp.sum(window_raised, axis=-1) + jnp.sum(state_raised, axis=-1)
        log_total = row_peak + jnp.log(denominator)
        window_probs = (window_raised / denominator[..., None]).astype(jnp.bfloat16)
        state_probs = (state_raised / denominator[..., None]).astype(jnp.bfloat16)
        block_out = jnp.einsum(
            "hij,jhe->ihe",
            window_probs,
            block_window_value_rows,
            preferred_element_type=jnp.float32,
        ) + jnp.einsum(
            "wyd,dwg->ywg", state_probs, block_state_value_rows, preferred_element_type=jnp.float32
        )
        return (block_out.astype(jnp.bfloat16), log_total)

    attended_blocks, log_totals = lax.map(
        attend_one_block,
        (
            flattened_queries,
            flattened_window_keys,
            flattened_window_values,
            flattened_state_keys,
            flattened_state_values,
            permitted_mask,
        ),
    )
    attended = attended_blocks.reshape(row_count, local_width)
    attn_part = jnp.dot(attended, out_full, preferred_element_type=jnp.float32).reshape(
        seq_count, length, full_width
    )
    attn_share = lax.psum_scatter(
        attn_part.astype(jnp.bfloat16), "tp", scatter_dimension=2, tiled=True
    ).astype(jnp.float32)
    middle = tokens.astype(jnp.float32) + attn_share
    middle_full, gain_two_full = (
        lax.all_gather(middle.astype(jnp.bfloat16), "tp", axis=2, tiled=True),
        lax.all_gather(gain_two, "tp", axis=0, tiled=True),
    )
    gain_two_vec = gain_two_full.reshape(full_width).astype(jnp.float32)
    normed_two, inverse_two, mlp_in = norm_forward(
        middle_full.reshape(row_count, full_width).astype(jnp.float32), gain_two_vec
    )
    hidden_pre = jnp.dot(mlp_in, up_full, preferred_element_type=jnp.float32)
    hidden = jax.nn.gelu(hidden_pre, approximate=False).astype(jnp.bfloat16)
    mlp_part = jnp.dot(hidden, down_full, preferred_element_type=jnp.float32).reshape(
        seq_count, length, full_width
    )
    mlp_share = lax.psum_scatter(
        mlp_part.astype(jnp.bfloat16), "tp", scatter_dimension=2, tiled=True
    ).astype(jnp.float32)
    output = (middle + mlp_share).astype(jnp.bfloat16)
    grad_out = cotangent.reshape(row_count, full_width)
    grad_hidden = jnp.dot(grad_out, down_full.T, preferred_element_type=jnp.float32)
    grad_down = jnp.dot(hidden.T, grad_out, preferred_element_type=jnp.float32)

    def gelu_exact(pre_values):
        return jax.nn.gelu(pre_values, approximate=False)

    gelu_value, gelu_back = jax.vjp(gelu_exact, hidden_pre)
    grad_pre = gelu_back(grad_hidden)[0].astype(jnp.bfloat16)
    grad_up = jnp.dot(mlp_in.T, grad_pre, preferred_element_type=jnp.float32)
    grad_mlp_in = jnp.dot(grad_pre, up_full.T, preferred_element_type=jnp.float32)
    part_middle, part_gain_two = norm_backward(grad_mlp_in, normed_two, inverse_two, gain_two_vec)
    tp_index = lax.axis_index("tp")
    head_total = full_width // HEAD_SIZE
    summed, gain_two_sum = (
        lax.psum(
            part_middle.reshape(seq_count, length, full_width).astype(jnp.bfloat16), "tp"
        ).astype(jnp.float32),
        lax.psum(part_gain_two.reshape(head_total, HEAD_SIZE).astype(jnp.bfloat16), "tp").astype(
            jnp.float32
        ),
    )
    middle_grad_full = cotangent.astype(jnp.float32) + summed
    middle_grad = lax.dynamic_slice_in_dim(middle_grad_full, tp_index * shard_width, shard_width, 2)
    grad_gain_two = lax.dynamic_slice_in_dim(
        gain_two_sum, tp_index * local_head_count, local_head_count, 0
    )
    middle_grad_low = middle_grad_full.astype(jnp.bfloat16)
    middle_grad_rows = middle_grad_low.reshape(row_count, full_width)
    grad_attended = jnp.dot(
        middle_grad_rows, out_full.T, preferred_element_type=jnp.float32
    ).astype(jnp.bfloat16)
    grad_attended = grad_attended.reshape(element_count, BLOCK, local_head_count, HEAD_SIZE)
    grad_wout = jnp.dot(attended.T, middle_grad_rows, preferred_element_type=jnp.float32)

    def attend_back(bias_sum, element_entry):
        (
            block_query_rows,
            block_window_key_rows,
            block_window_value_rows,
            block_state_key_rows,
            block_state_value_rows,
            block_permitted_mask,
            block_lse,
            block_grad,
        ) = element_entry
        window_again, state_again = block_score_rows(
            block_query_rows, block_window_key_rows, block_state_key_rows, block_permitted_mask
        )
        window_exact = jnp.exp(window_again - block_lse[..., None])
        state_exact = jnp.exp(state_again - block_lse[..., None])
        grad_wprob = jnp.einsum(
            "ihe,jhe->hij", block_grad, block_window_value_rows, preferred_element_type=jnp.float32
        )
        grad_sprob = jnp.einsum(
            "yat,zat->ayz", block_grad, block_state_value_rows, preferred_element_type=jnp.float32
        )
        row_delta = jnp.sum(window_exact * grad_wprob, axis=-1) + jnp.sum(
            state_exact * grad_sprob, axis=-1
        )
        grad_wscore = (window_exact * (grad_wprob - row_delta[..., None])).astype(jnp.bfloat16)
        state_score_gradient = (state_exact * (grad_sprob - row_delta[..., None])).astype(
            jnp.bfloat16
        )
        block_grad_q = scores_scale * (
            jnp.einsum(
                "hij,jhe->ihe",
                grad_wscore,
                block_window_key_rows,
                preferred_element_type=jnp.float32,
            )
            + jnp.einsum(
                "wyd,dwg->ywg",
                state_score_gradient,
                block_state_key_rows,
                preferred_element_type=jnp.float32,
            )
        )
        block_grad_wk = scores_scale * jnp.einsum(
            "hij,ihe->jhe", grad_wscore, block_query_rows, preferred_element_type=jnp.float32
        )
        block_grad_wv = jnp.einsum(
            "hij,ihe->jhe",
            window_exact.astype(jnp.bfloat16),
            block_grad,
            preferred_element_type=jnp.float32,
        )
        block_grad_sk = (
            scores_scale
            * jnp.einsum(
                "him,ihe->mhe",
                state_score_gradient,
                block_query_rows,
                preferred_element_type=jnp.float32,
            )
        ).astype(jnp.bfloat16)
        block_grad_sv = jnp.einsum(
            "him,ihe->mhe",
            state_exact.astype(jnp.bfloat16),
            block_grad,
            preferred_element_type=jnp.float32,
        ).astype(jnp.bfloat16)
        return (
            bias_sum + grad_wscore.astype(jnp.float32),
            (block_grad_q, block_grad_wk, block_grad_wv, block_grad_sk, block_grad_sv),
        )

    bias_start = jnp.zeros((local_head_count, BLOCK, 2 * BLOCK), jnp.float32)
    bias_sum, back_items = lax.scan(
        attend_back,
        bias_start,
        (
            flattened_queries,
            flattened_window_keys,
            flattened_window_values,
            flattened_state_keys,
            flattened_state_values,
            permitted_mask,
            log_totals,
            grad_attended,
        ),
    )
    grad_bias = bias_gradient(bias_sum, bucket, bias_rows.shape[1])
    grad_queries = back_items[0].reshape(local_shape)
    grad_window_keys = back_items[1].reshape(
        seq_count, block_count, 2 * BLOCK, local_head_count, HEAD_SIZE
    )
    grad_window_values = back_items[2].reshape(
        seq_count, block_count, 2 * BLOCK, local_head_count, HEAD_SIZE
    )
    state_keys_gradient = back_items[3].reshape(
        seq_count, block_count, state_slot_count, local_head_count, HEAD_SIZE
    )
    grad_state_values = back_items[4].reshape(
        seq_count, block_count, state_slot_count, local_head_count, HEAD_SIZE
    )
    back_keys, back_values = (
        from_behind(grad_window_keys[:, 0, :BLOCK].astype(jnp.bfloat16), "ctx", -1).astype(
            jnp.float32
        ),
        from_behind(grad_window_values[:, 0, :BLOCK].astype(jnp.bfloat16), "ctx", -1).astype(
            jnp.float32
        ),
    )
    key_grad = grad_window_keys[:, :, BLOCK:] + jnp.concatenate(
        [grad_window_keys[:, 1:, :BLOCK], back_keys[:, None]], 1
    )
    value_grad = grad_window_values[:, :, BLOCK:] + jnp.concatenate(
        [grad_window_values[:, 1:, :BLOCK], back_values[:, None]], 1
    )
    state_key_gradient = jnp.einsum(
        "sbmhe,sbmhf->hef", state_reduced, state_keys_gradient, preferred_element_type=jnp.float32
    )
    grad_svalue = jnp.einsum(
        "sbmhe,sbmhf->hef", state_reduced, grad_state_values, preferred_element_type=jnp.float32
    )
    direct = jnp.einsum(
        "palcq,crq->palcr",
        state_keys_gradient,
        state_key_complete,
        preferred_element_type=jnp.float32,
    ) + jnp.einsum(
        "palcq,crq->palcr", grad_state_values, svalue_full, preferred_element_type=jnp.float32
    )
    direct = direct.reshape(seq_count, block_count, state_slot_count, local_width)
    back_accum = jnp.zeros((seq_count, state_slot_count, local_width), jnp.float32)
    for block_index in reversed(range(block_count)):
        back_accum = direct[:, block_index] + gate_value * back_accum
    back_identity = (jnp.ones((local_width,), jnp.float32), jnp.zeros_like(back_accum))
    unused_power, incoming = prefix_2((gate_power, back_accum), "ctx", compose, back_identity, True)
    carried = incoming
    contrib_grads = [None] * block_count
    gate_grad = jnp.zeros((local_width,), jnp.float32)
    for block_index in reversed(range(block_count)):
        contrib_grads[block_index] = ((1.0 - gate_value) * carried).astype(jnp.bfloat16)
        gate_grad = gate_grad + jnp.sum(
            carried * (stacked[:, block_index] - contrib[:, block_index]), axis=(0, 1)
        )
        carried = direct[:, block_index] + gate_value * carried
    first_device = (lax.axis_index("ctx") == 0).astype(jnp.float32)
    grad_sinit = first_device * jnp.sum(carried, axis=0)
    grad_gate = (gate_grad * gate_value * (1.0 - gate_value)).reshape(local_head_count, HEAD_SIZE)
    grad_contrib = jnp.stack(contrib_grads, axis=1).reshape(
        seq_count, block_count, state_slot_count, local_head_count, HEAD_SIZE
    )
    grad_read = jnp.einsum(
        "sbmhe,sbthe->sbhmt", grad_contrib, value_rows, preferred_element_type=jnp.float32
    )
    extra_values = jnp.einsum(
        "sbhmt,sbmhe->sbthe", read_low, grad_contrib, preferred_element_type=jnp.float32
    )
    read_delta = jnp.sum(read_probs * grad_read, axis=-1, keepdims=True)
    grad_read_score = (read_probs * (grad_read - read_delta)).astype(jnp.bfloat16)
    grad_squery = (
        scores_scale
        * jnp.einsum(
            "sbhmt,sbthe->mhe", grad_read_score, key_rows, preferred_element_type=jnp.float32
        )
    ).reshape(state_slot_count, local_width)
    extra_keys = scores_scale * jnp.einsum(
        "sbhmt,mhe->sbthe", grad_read_score, query_heads, preferred_element_type=jnp.float32
    )
    grad_q_rows = grad_queries.astype(jnp.bfloat16).reshape(row_count, local_width)
    grad_k_rows = (key_grad + extra_keys).astype(jnp.bfloat16).reshape(row_count, local_width)
    grad_v_rows = (value_grad + extra_values).astype(jnp.bfloat16).reshape(row_count, local_width)
    grad_wq = jnp.dot(attn_in.T, grad_q_rows, preferred_element_type=jnp.float32)
    grad_wk = jnp.dot(attn_in.T, grad_k_rows, preferred_element_type=jnp.float32)
    grad_wv = jnp.dot(attn_in.T, grad_v_rows, preferred_element_type=jnp.float32)
    grad_attn_in = (
        jnp.dot(grad_q_rows, query_full.T, preferred_element_type=jnp.float32)
        + jnp.dot(grad_k_rows, key_full.T, preferred_element_type=jnp.float32)
        + jnp.dot(grad_v_rows, value_full.T, preferred_element_type=jnp.float32)
    )
    part_tokens, part_gain_one = norm_backward(grad_attn_in, normed_one, inverse_one, gain_one_vec)
    token_share, grad_gain_one = (
        lax.psum_scatter(
            part_tokens.reshape(seq_count, length, full_width).astype(jnp.bfloat16),
            "tp",
            scatter_dimension=2,
            tiled=True,
        ).astype(jnp.float32),
        lax.psum_scatter(
            part_gain_one.reshape(head_total, HEAD_SIZE).astype(jnp.bfloat16),
            "tp",
            scatter_dimension=0,
            tiled=True,
        ).astype(jnp.float32),
    )
    grad_tokens = (middle_grad + token_share).astype(jnp.bfloat16)
    grads = (
        lax.psum_scatter(
            grad_wq.astype(jnp.bfloat16), ("dp", "ctx"), scatter_dimension=0, tiled=True
        ).astype(jnp.float32),
        lax.psum_scatter(
            grad_wk.astype(jnp.bfloat16), ("dp", "ctx"), scatter_dimension=0, tiled=True
        ).astype(jnp.float32),
        lax.psum_scatter(
            grad_wv.astype(jnp.bfloat16), ("dp", "ctx"), scatter_dimension=0, tiled=True
        ).astype(jnp.float32),
        lax.psum_scatter(
            grad_wout.astype(jnp.bfloat16), ("dp", "ctx"), scatter_dimension=1, tiled=True
        ).astype(jnp.float32),
        lax.psum_scatter(
            grad_up.astype(jnp.bfloat16), ("dp", "ctx"), scatter_dimension=0, tiled=True
        ).astype(jnp.float32),
        lax.psum_scatter(
            grad_down.astype(jnp.bfloat16), ("dp", "ctx"), scatter_dimension=1, tiled=True
        ).astype(jnp.float32),
        lax.psum_scatter(
            grad_squery.astype(jnp.bfloat16), ("dp", "ctx"), scatter_dimension=0, tiled=True
        ).astype(jnp.float32),
        lax.psum_scatter(
            grad_sinit.astype(jnp.bfloat16), ("dp", "ctx"), scatter_dimension=0, tiled=True
        ).astype(jnp.float32),
        lax.psum_scatter(
            grad_gain_one.astype(jnp.bfloat16), ("dp", "ctx"), scatter_dimension=1, tiled=True
        ).astype(jnp.float32),
        lax.psum_scatter(
            grad_gain_two.astype(jnp.bfloat16), ("dp", "ctx"), scatter_dimension=1, tiled=True
        ).astype(jnp.float32),
        lax.psum_scatter(
            grad_bias.astype(jnp.bfloat16), ("dp", "ctx"), scatter_dimension=1, tiled=True
        ).astype(jnp.float32),
        lax.psum_scatter(
            grad_gate.astype(jnp.bfloat16), ("dp", "ctx"), scatter_dimension=1, tiled=True
        ).astype(jnp.float32),
        lax.psum_scatter(
            state_key_gradient.astype(jnp.bfloat16), ("dp", "ctx"), scatter_dimension=1, tiled=True
        ).astype(jnp.float32),
        lax.psum_scatter(
            grad_svalue.astype(jnp.bfloat16), ("dp", "ctx"), scatter_dimension=1, tiled=True
        ).astype(jnp.float32),
    )
    return (
        output,
        grad_tokens,
        grads[0],
        grads[1],
        grads[2],
        grads[3],
        grads[4],
        grads[5],
        grads[6],
        grads[7],
        grads[8],
        grads[9],
        grads[10],
        grads[11],
        grads[12],
        grads[13],
    )


LOG2E = 1.4426950408889634
VMEM_BYTES = 58 * 1024 * 1024
BF = jnp.bfloat16
F32 = jnp.float32


def nn(left, right):
    return jnp.dot(left, right, preferred_element_type=F32)


def nt(left, right):
    return lax.dot_general(left, right, (((1,), (1,)), ((), ())), preferred_element_type=F32)


def tn(left, right):
    return lax.dot_general(left, right, (((0,), (0,)), ((), ())), preferred_element_type=F32)


def flat(ref):
    block = ref[0]
    return block.reshape(block.shape[0] * block.shape[1], block.shape[2])


def merged(place_ref, own_ref, other_ref):
    own = own_ref[0, :, 0]
    other = other_ref[0, :, 0]
    is_first = place_ref[0] == 0
    pair = [jnp.where(is_first, own, other), jnp.where(is_first, other, own)]
    block = jnp.stack(pair, axis=1)
    return block.reshape(-1, block.shape[-1])


def inverse_rms(x):
    return lax.rsqrt(jnp.mean(x * x, axis=-1, keepdims=True) + EPSILON)


def params():
    return pltpu.CompilerParams(vmem_limit_bytes=VMEM_BYTES)


def project_kernel(
    place_ref, tok_ref, gain_ref, wq_ref, wqo_ref, wk_ref, wko_ref, wv_ref, wvo_ref,
    q_ref, k_ref, v_ref, ain_ref,
):
    @pl.when(pl.program_id(0) == 0)
    def _():
        x = tok_ref[...].astype(F32)
        ain_ref[...] = (x * inverse_rms(x) * gain_ref[...]).astype(BF)

    a = ain_ref[...]
    for w_ref, w_other, o_ref in (
        (wq_ref, wqo_ref, q_ref), (wk_ref, wko_ref, k_ref), (wv_ref, wvo_ref, v_ref)
    ):
        o_ref[...] = nn(a, merged(place_ref, w_ref, w_other)).astype(BF)


def read_kernel(
    place_ref, sq_ref, sqo_ref, k_ref, v_ref, gate_ref, o_ref, sum_ref, state_ref, *, blocks
):
    n = pl.program_id(1)
    sq = merged(place_ref, sq_ref, sqo_ref)
    k = k_ref[...]
    v = v_ref[...]
    scale = HEAD_SIZE ** (-0.5) * LOG2E
    step = 256
    gate = jnp.where(lax.rem(n, blocks) == 0, 0.0, gate_ref[...])
    fresh = 1.0 - gate_ref[...]

    @pl.when(n == 0)
    def _():
        state_ref[...] = jnp.zeros_like(state_ref)

    for start in range(0, sq.shape[0], step):
        rows = slice(start, start + step)
        s = nt(sq[rows], k) * scale
        p = jnp.exp2(s - jnp.max(s, axis=-1, keepdims=True))
        total = jnp.sum(p, axis=-1, keepdims=True)
        contrib = nn(p.astype(BF), v) / total
        o_ref[rows, :] = contrib
        state = gate * state_ref[rows, :] + fresh * contrib
        state_ref[rows, :] = state
        sum_ref[rows, :] = state.astype(BF)


def attend_kernel(
    place_ref, info_ref, q_ref, k_ref, v_ref, kp_ref, vp_ref, hk_ref, hv_ref,
    wk_ref, wko_ref, wv_ref, wvo_ref, contrib_ref, init_ref, inito_ref, lead_ref, power_ref,
    gate_ref, u_ref, o_ref, lse_ref, low_ref, moved_ref, bias_ref, state_ref, *, blocks,
):
    n = pl.program_id(1)
    first = lax.rem(n, blocks) == 0
    scale = HEAD_SIZE ** (-0.5) * LOG2E

    @pl.when(n == 0)
    def _():
        row = jnp.broadcast_to(u_ref[0], (BLOCK, u_ref.shape[-1]))
        bias_ref[...] = pltpu.roll(row, 0, 1, stride=1, stride_axis=0)[:, : 2 * BLOCK]

    has_previous = info_ref[n, 0] > 0
    reach = info_ref[n, 1]
    k = k_ref[...]
    v = v_ref[...]
    kp = jnp.where(first, hk_ref[...], kp_ref[...])
    vp = jnp.where(first, hv_ref[...], vp_ref[...])

    @pl.when(first)
    def _():
        init = merged(place_ref, init_ref, inito_ref).astype(F32)
        state_ref[...] = power_ref[...] * init + lead_ref[...].astype(F32)

    state = state_ref[...]
    contrib = contrib_ref[...]
    st = state.astype(BF)
    low_ref[...] = st
    moved_ref[...] = (state - contrib).astype(BF)
    state_ref[...] = contrib + gate_ref[...] * (state - contrib)
    sk = nn(st, merged(place_ref, wk_ref, wko_ref)).astype(BF)
    sv = nn(st, merged(place_ref, wv_ref, wvo_ref)).astype(BF)
    step = ROWS_FORWARD

    def run(with_previous):
        for start in range(0, BLOCK, step):
            q = q_ref[start : start + step, :]
            sc = nt(q, k) * scale + bias_ref[start : start + step, BLOCK:]
            row = lax.broadcasted_iota(jnp.int32, (step, 1), 0) + start
            column = lax.broadcasted_iota(jnp.int32, (step, BLOCK), 1)
            sc = jnp.where(column <= jnp.maximum(row, reach - 1), sc, MASKED)
            ss = nt(q, sk) * scale
            peak = jnp.maximum(
                jnp.max(sc, axis=-1, keepdims=True), jnp.max(ss, axis=-1, keepdims=True)
            )
            if with_previous:
                sp = nt(q, kp) * scale + bias_ref[start : start + step, :BLOCK]
                peak = jnp.maximum(peak, jnp.max(sp, axis=-1, keepdims=True))
            pc = jnp.exp2(sc - peak)
            ps = jnp.exp2(ss - peak)
            total = jnp.sum(pc, axis=-1, keepdims=True) + jnp.sum(ps, axis=-1, keepdims=True)
            out = nn(pc.astype(BF), v) + nn(ps.astype(BF), sv)
            if with_previous:
                pp = jnp.exp2(sp - peak)
                total = total + jnp.sum(pp, axis=-1, keepdims=True)
                out = out + nn(pp.astype(BF), vp)
            o_ref[start : start + step, :] = (out / total).astype(BF)
            lse = jnp.broadcast_to(peak + jnp.log2(total), (step, 128))
            lse_ref[0, 0, :, start : start + step] = lse.T[:1]

    @pl.when(has_previous)
    def _():
        run(True)

    @pl.when(jnp.logical_not(has_previous))
    def _():
        run(False)


def attend_back_kernel(
    place_ref, info_ref, q_ref, k_ref, v_ref, kp_ref, vp_ref, hk_ref, hv_ref,
    wk_ref, wko_ref, wv_ref, wvo_ref, st_ref, gate_ref, u_ref, do_ref, o_ref, lse_ref,
    dq_ref, dk_ref, dv_ref, dkp_ref, dvp_ref, direct_ref, gwk_ref, gwv_ref, gb_ref, total_ref,
    bias_ref, sum_ref, dq_acc, state_acc, *, blocks,
):
    step_at = pl.program_id(1)
    n = pl.num_programs(1) - 1 - step_at
    first = lax.rem(n, blocks) == 0
    gate = jnp.where(lax.rem(n, blocks) == blocks - 1, 0.0, gate_ref[...])
    factor = HEAD_SIZE ** (-0.5)
    scale = factor * LOG2E
    window = 2 * BLOCK
    width = BLOCK + window

    @pl.when(step_at == 0)
    def _():
        state_acc[...] = jnp.zeros_like(state_acc)
        row = jnp.broadcast_to(u_ref[0], (window, u_ref.shape[-1]))
        bias_ref[...] = pltpu.roll(row, 0, 1, stride=1, stride_axis=0)[:, :BLOCK]
        sum_ref[...] = jnp.zeros_like(sum_ref)
        gwk_ref[...] = jnp.zeros_like(gwk_ref)
        gwv_ref[...] = jnp.zeros_like(gwv_ref)

    has_previous = info_ref[n, 0] > 0
    reach = info_ref[n, 1]
    q = q_ref[...]
    do = do_ref[...]
    lse = lse_ref[0, 0]
    delta = jnp.sum((do.astype(F32) * o_ref[...].astype(F32)).T, axis=0, keepdims=True)
    step = KEYS_BACKWARD

    def part(key, value, start, bias_start, masked):
        s = nt(key, q) * scale
        if bias_start is not None:
            s = s + bias_ref[bias_start : bias_start + step, :]
        if masked:
            key_at = lax.broadcasted_iota(jnp.int32, (step, BLOCK), 0) + start
            query_at = lax.broadcasted_iota(jnp.int32, (1, BLOCK), 1)
            s = jnp.where(key_at <= jnp.maximum(query_at, reach - 1), s, MASKED)
        p = jnp.exp2(s - lse)
        dp = nt(value, do)
        ds = (p * (dp - delta)).astype(BF)
        if bias_start is not None:
            for block in range(0, step, 128):
                at = window - bias_start - block
                sum_ref[:, at : at + BLOCK] += ds[block : block + 128].astype(F32)
        dq_acc[...] += tn(ds, key)
        return nn(ds, q) * factor, nn(p.astype(BF), do)

    dq_acc[...] = jnp.zeros_like(dq_acc)
    st = st_ref[...]
    key_map = merged(place_ref, wk_ref, wko_ref)
    value_map = merged(place_ref, wv_ref, wvo_ref)
    sk = nn(st, key_map).astype(BF)
    sv = nn(st, value_map).astype(BF)
    for start in range(0, st.shape[0], step):
        rows = slice(start, start + step)
        dk, dv = part(sk[rows], sv[rows], start, None, False)
        dk = dk.astype(BF)
        dv = dv.astype(BF)
        direct = nt(dk, key_map) + nt(dv, value_map)
        direct_ref[rows, :] = direct
        state = direct + gate * state_acc[rows, :]
        state_acc[rows, :] = state
        total_ref[rows, :] = state.astype(BF)
        gwk_ref[0] += tn(st[rows], dk)
        gwv_ref[0] += tn(st[rows], dv)
    for start in range(0, BLOCK, step):
        rows = slice(start, start + step)
        dk, dv = part(k_ref[rows, :], v_ref[rows, :], start, BLOCK + start, True)
        dk_ref[rows, :] = dk
        dv_ref[rows, :] = dv

    @pl.when(has_previous)
    def _():
        for start in range(0, BLOCK, step):
            rows = slice(start, start + step)
            key = jnp.where(first, hk_ref[rows, :], kp_ref[rows, :])
            value = jnp.where(first, hv_ref[rows, :], vp_ref[rows, :])
            dk, dv = part(key, value, start, start, False)
            dkp_ref[rows, :] = dk.astype(BF)
            dvp_ref[rows, :] = dv.astype(BF)

    @pl.when(jnp.logical_not(has_previous))
    def _():
        dkp_ref[...] = jnp.zeros_like(dkp_ref)
        dvp_ref[...] = jnp.zeros_like(dvp_ref)

    dq_ref[...] = (dq_acc[...] * factor).astype(BF)

    @pl.when(n == 0)
    def _():
        folded = sum_ref[...]
        half = 64
        while half >= 8:
            folded = folded[:half] + pltpu.roll(folded[half:], width - half, 1)
            half //= 2
        total = folded[:1]
        for row in range(1, 8):
            total = total + pltpu.roll(folded[row : row + 1], width - row, 1)
        gb_ref[0] = total


def read_back_kernel(
    place_ref, sq_ref, sqo_ref, k_ref, v_ref, direct_ref, moved_ref, later_ref, gate_ref,
    dk_ref, dv_ref, nk_ref, nv_ref, rk_ref, rv_ref,
    gk_ref, gv_ref, gsq_ref, ginit_ref, ggate_ref, carried_ref, *, blocks,
):
    step_at = pl.program_id(1)
    n = pl.num_programs(1) - 1 - step_at
    last = lax.rem(n, blocks) == blocks - 1
    factor = HEAD_SIZE ** (-0.5)

    @pl.when(step_at == 0)
    def _():
        gsq_ref[...] = jnp.zeros_like(gsq_ref)
        ginit_ref[...] = jnp.zeros_like(ginit_ref)
        ggate_ref[...] = jnp.zeros_like(ggate_ref)

    @pl.when(last)
    def _():
        carried_ref[...] = later_ref[...].astype(F32)

    gate = gate_ref[...]
    carried = carried_ref[...]
    gc = ((1.0 - gate) * carried).astype(BF)
    change = jnp.sum(carried * moved_ref[...].astype(F32), axis=0, keepdims=True)
    ggate_ref[0] += change * (gate * (1.0 - gate))
    carried = direct_ref[...] + gate * carried
    carried_ref[...] = carried

    @pl.when((lax.rem(n, blocks) == 0) & (place_ref[0] == 0))
    def _():
        ginit_ref[...] += carried

    sq = merged(place_ref, sq_ref, sqo_ref)
    k = k_ref[...]
    s = nt(k, sq) * (factor * LOG2E)
    p = jnp.exp2(s - jnp.max(s, axis=0, keepdims=True))
    p = p * (1.0 / jnp.sum(p, axis=0, keepdims=True))
    dp = nt(v_ref[...], gc)
    ds = (p * (dp - jnp.sum(p * dp, axis=0, keepdims=True))).astype(BF)
    next_k = jnp.where(last, rk_ref[...], nk_ref[...]).astype(F32)
    next_v = jnp.where(last, rv_ref[...], nv_ref[...]).astype(F32)
    gk_ref[...] = (dk_ref[...] + next_k + nn(ds, sq) * factor).astype(BF)
    gv_ref[...] = (dv_ref[...] + next_v + nn(p.astype(BF), gc)).astype(BF)
    gsq_ref[...] += tn(ds, k) * factor


def pack_kernel(up_ref, down_ref, out_ref, packed_ref):
    hidden = up_ref.shape[1]
    packed_ref[:, :hidden] = up_ref[...]
    packed_ref[:, hidden : 2 * hidden] = down_ref[...].T
    packed_ref[:, 2 * hidden :] = out_ref[...].T


def unpack_kernel(packed_ref, up_ref, down_ref, out_ref):
    hidden = up_ref.shape[1]
    up_ref[...] = packed_ref[:, :hidden].astype(F32)
    down_ref[...] = packed_ref[:, hidden : 2 * hidden].astype(F32).T
    out_ref[...] = packed_ref[:, 2 * hidden :].astype(F32).T


def out_kernel(att_ref, wo_ref, tok_ref, gain_ref, mid_ref, min_ref):
    t = pl.program_id(0)
    part = nt(att_ref[...], flat(wo_ref))

    @pl.when(t == 0)
    def _():
        mid_ref[...] = tok_ref[...].astype(F32) + part

    @pl.when(t > 0)
    def _():
        mid_ref[...] += part

    @pl.when(t == pl.num_programs(0) - 1)
    def _():
        x = mid_ref[...].astype(BF).astype(F32)
        min_ref[...] = (x * inverse_rms(x) * gain_ref[...]).astype(BF)


def mlp_kernel(
    place_ref, min_ref, cot_ref, mid_ref, gain_ref, wu_ref, wd_ref,
    out_ref, gmid_ref, ggain_ref, gw_ref,
    min_t, cot_t, out_acc, gm_acc, hidden_ref,
):
    tile = pl.program_id(0)
    which = pl.program_id(1)

    @pl.when((tile == 0) & (which == 0))
    def _():
        min_t[...] = min_ref[...].T
        cot_t[...] = cot_ref[...].T
        out_acc[...] = jnp.zeros_like(out_acc)
        gm_acc[...] = jnp.zeros_like(gm_acc)

    @pl.when(which == 0)
    def _():
        wu = flat(wu_ref)
        wd = flat(wd_ref)
        pre = nn(min_ref[...], wu)
        cdf = 0.5 + 0.5 * lax.erf(pre * (0.5**0.5))
        density = jnp.exp2(pre * pre * (-0.5 * LOG2E)) * ((2.0 * np.pi) ** -0.5)
        hidden_ref[...] = (pre * cdf).astype(BF)
        grad_pre = (nn(cot_ref[...], wd) * (cdf + pre * density)).astype(BF)
        out_acc[...] += nt(hidden_ref[...], wd)
        gm_acc[...] += nt(grad_pre, wu)
        grad = nn(min_t[...], grad_pre).astype(BF)
        gw_ref[...] = grad.reshape(gw_ref.shape)

    @pl.when(which == 1)
    def _():
        grad = nn(cot_t[...], hidden_ref[...]).astype(BF)
        gw_ref[...] = grad.reshape(gw_ref.shape)

    @pl.when((tile == pl.num_programs(0) - 1) & (which == 1))
    def _():
        mid = mid_ref[...]
        lanes = out_ref.shape[2]
        for part in range(out_ref.shape[0]):
            at = slice(part * lanes, (part + 1) * lanes)
            out_ref[part] = (mid[:, at] + out_acc[:, at]).astype(BF)
        x = mid.astype(BF).astype(F32)
        inverse = inverse_rms(x)
        normed = x * inverse
        gm = gm_acc[...]
        ggain_ref[...] = jnp.sum(gm * normed, axis=0, keepdims=True)
        scaled = gm * gain_ref[...]
        back = inverse * (scaled - normed * jnp.mean(scaled * normed, axis=-1, keepdims=True))
        gmid_ref[...] = (cot_ref[...].astype(F32) + back).astype(BF)


def out_back_kernel(gmid_ref, wo_ref, att_ref, late_ref, gatt_ref, gwo_ref, gmid_t):
    @pl.when(pl.program_id(0) == 0)
    def _():
        gmid_t[...] = gmid_ref[...].T

    gatt_ref[...] = nn(gmid_ref[...], flat(wo_ref)).astype(BF)
    gwo_ref[...] = nn(gmid_t[...], att_ref[...]).astype(BF).reshape(gwo_ref.shape)


def project_back_kernel(
    place_ref, tok_ref, gmid_ref, gain_ref, gq_ref, gk_ref, gv_ref,
    wq_ref, wqo_ref, wk_ref, wko_ref, wv_ref, wvo_ref, gsq_ref, ginit_ref, gmk_ref, gmv_ref,
    gtok_ref, ggain_ref, gown_ref, gother_ref, ain_t, acc_ref, pack_ref,
):
    t = pl.program_id(0)

    @pl.when(t == 0)
    def _():
        x = tok_ref[...].astype(F32)
        ain_t[...] = (x * inverse_rms(x) * gain_ref[...]).astype(BF).T
        acc_ref[...] = jnp.zeros_like(acc_ref)

    groups, _, lanes = pack_ref.shape
    at = 0
    for g_ref, w_ref, w_other in (
        (gq_ref, wq_ref, wqo_ref), (gk_ref, wk_ref, wko_ref), (gv_ref, wv_ref, wvo_ref)
    ):
        g = g_ref[...]
        acc_ref[...] += nt(g, merged(place_ref, w_ref, w_other))
        grad = nn(ain_t[...], g).astype(BF)
        rows = grad.shape[0] // groups
        pack_ref[:, at : at + rows] = grad.reshape(groups, rows, lanes)
        at += rows
    for g_ref in (gsq_ref, ginit_ref):
        rows = g_ref.shape[0] // groups
        pack_ref[:, at : at + rows] = g_ref[...].astype(BF).reshape(groups, rows, lanes)
        at += rows
    for g_ref in (gmk_ref, gmv_ref):
        rows = HEAD_SIZE // groups
        for item in range(g_ref.shape[0]):
            where = slice(item * HEAD_SIZE, (item + 1) * HEAD_SIZE)
            pack_ref[:, at : at + rows, where] = g_ref[item].astype(BF).reshape(groups, rows, -1)
        at += rows
    pack_ref[:, at:] = jnp.zeros_like(pack_ref[:, at:])
    for index in range(groups // 2):
        gown_ref[0, index] = pack_ref[2 * index + place_ref[0]]
        gother_ref[0, index] = pack_ref[2 * index + 1 - place_ref[0]]

    @pl.when(t == pl.num_programs(0) - 1)
    def _():
        x = tok_ref[...].astype(F32)
        inverse = inverse_rms(x)
        normed = x * inverse
        ga = acc_ref[...]
        ggain_ref[...] = jnp.sum(ga * normed, axis=0, keepdims=True)
        scaled = ga * gain_ref[...]
        back = inverse * (scaled - normed * jnp.mean(scaled * normed, axis=-1, keepdims=True))
        grad = (gmid_ref[...].astype(F32) + back).astype(BF)
        for part in range(gtok_ref.shape[0]):
            gtok_ref[part] = grad[:, part * lanes : (part + 1) * lanes]


def distance_bucket(distance):
    magnitude = np.abs(distance)
    scaled = np.log(np.maximum(magnitude, 1) / 8.0) / np.log(16.0) * 8.0
    far = np.minimum(8 + np.floor(np.maximum(scaled, 0.0)).astype(np.int32), 15)
    return (distance < 0).astype(np.int32) * 16 + np.where(magnitude < 8, magnitude, far)


def one_hot(distance, valid, bucket_count):
    hot = distance_bucket(distance)[:, None] == np.arange(bucket_count)[None, :]
    return jnp.asarray((hot & valid[:, None]).astype(np.float32))


def carry(value, power, axis, backward):
    count = lax.axis_size(axis)
    sign = -1 if backward else 1
    total = from_behind(value.astype(BF), axis, sign).astype(F32)
    step = 1
    while step < count - 1:
        moved = from_behind(total.astype(BF), axis, sign * step).astype(F32)
        total = total + power**step * moved
        step *= 2
    return total


def across(value, axis, bit):
    count = lax.axis_size(axis)
    return lax.ppermute(value, axis, [(source, source ^ bit) for source in range(count)])


def take(value, index, dim):
    return lax.dynamic_index_in_dim(value, index, dim, False)


def add_low(left, right):
    return (left.astype(F32) + right.astype(F32)).astype(BF)


def ordered(bit, own, other, dim):
    first = bit == 0
    return jnp.stack([jnp.where(first, own, other), jnp.where(first, other, own)], axis=dim)


def gather_pairs(item):
    shards = lax.axis_size("tp")
    half = shards // 2
    tp = lax.axis_index("tp")
    x_bit = lax.axis_index("dp") % 2
    y_bit = lax.axis_index("dp") // 2
    parts = [item] + [across(item, "tp", k) for k in range(1, shards)]
    bit = 1
    while bit < shards:
        swap = (tp & bit) > 0
        parts = [jnp.where(swap, parts[k ^ bit], parts[k]) for k in range(shards)]
        bit *= 2
    low = jnp.stack(parts[:half])
    high = jnp.stack(parts[half:])
    low_x = across(low, "dp", 1)
    high_y = across(high, "dp", 2)
    low = ordered(x_bit, low, low_x, 0)
    high = ordered(y_bit, high, high_y, 0)
    low_y = across(low, "dp", 2)
    high_x = across(high, "dp", 1)
    low = ordered(y_bit, low, low_y, 0)
    high = ordered(x_bit, high, high_x, 1)
    own = jnp.stack([low, high]).reshape((2, 4, half) + item.shape)
    return own, across(own, "ctx", 1)


def scatter_pairs(own, other):
    shards = own.shape[0]
    half = shards // 2
    tp = lax.axis_index("tp")
    x_bit = lax.axis_index("dp") % 2
    y_bit = lax.axis_index("dp") // 2
    grid = (shards, 2, 2) + own.shape[2:]
    moved = across(other, "ctx", 1).reshape(grid)
    own = own.reshape(grid)

    def both(part, index, dim):
        return add_low(take(own[part], index, dim), take(moved[part], index, dim))

    first, second = slice(0, half), slice(half, shards)
    low_moved = across(both(first, 1 - x_bit, 2), "dp", 1)
    high_moved = across(both(second, 1 - y_bit, 1), "dp", 2)
    low = add_low(both(first, x_bit, 2), low_moved)
    high = add_low(both(second, y_bit, 1), high_moved)
    low_moved = across(take(low, 1 - y_bit, 1), "dp", 2)
    high_moved = across(take(high, 1 - x_bit, 1), "dp", 1)
    low = add_low(take(low, y_bit, 1), low_moved)
    high = add_low(take(high, x_bit, 1), high_moved)
    kept = jnp.concatenate([low, high])
    total = take(kept, tp, 0).astype(F32)
    for k in range(1, shards):
        total = total + across(take(kept, tp ^ k, 0), "tp", k).astype(F32)
    return total


def sequence_body(
    tokens, cotangent, prefix, w_query, w_key, w_value, w_out, w_up, w_down,
    state_query, state_init, gain_attn, gain_mlp, bias_table, gate_bias, state_key, state_value,
):
    shards = lax.axis_size("tp")
    groups = lax.axis_size("dp") * lax.axis_size("ctx")
    pairs = lax.axis_size("dp")
    half = shards // 2
    everywhere = ("tp", "dp", "ctx")
    seq_count, length, shard_width = tokens.shape
    width = cotangent.shape[2]
    seqs = seq_count // shards
    blocks = length // BLOCK
    units = seqs * blocks
    rows = units * BLOCK
    local_heads = bias_table.shape[0]
    heads = local_heads * shards
    buckets = bias_table.shape[1] * groups
    own_rows = w_query.shape[0]
    own_slots = state_query.shape[0]
    slots = own_slots * groups
    hidden = w_up.shape[1]
    tp_index = lax.axis_index("tp")
    ctx_index = lax.axis_index("ctx")
    dp_index = lax.axis_index("dp")
    head = HEAD_SIZE
    map_rows = state_key.shape[1]
    place = jnp.stack([ctx_index, tp_index]).astype(jnp.int32)

    def call(kernel, grid, in_specs, out_specs, out_shape, scratch=(), prefetch=1, **more):
        return pl.pallas_call(
            kernel,
            grid_spec=pltpu.PrefetchScalarGridSpec(
                num_scalar_prefetch=prefetch, grid=grid, in_specs=in_specs, out_specs=out_specs,
                scratch_shapes=list(scratch),
            ),
            out_shape=out_shape,
            compiler_params=params(),
            **more,
        )

    vectors = (gain_attn, gain_mlp, gate_bias, bias_table)
    sizes = [item.size for item in vectors]
    tail = jnp.concatenate([item.reshape(-1) for item in vectors])
    tail = jnp.pad(tail, (0, 16 * shard_width - tail.size)).reshape(16, shard_width)

    def beside(item):
        return jnp.moveaxis(item, 0, 1).reshape(map_rows, shard_width)

    first_own, first_other = gather_pairs(jnp.concatenate([w_query, w_key, w_value, tail], axis=0))
    x = lax.all_to_all(tokens, "tp", 0, 2, tiled=True).reshape(rows, width)
    second_own, second_other = gather_pairs(
        jnp.concatenate(
            [state_query, state_init, beside(state_key), beside(state_value)], axis=0
        )
    )
    late_width = 2 * hidden + shard_width
    late = pl.pallas_call(
        pack_kernel, out_shape=jax.ShapeDtypeStruct((own_rows, late_width), BF)
    )(w_up, w_down, w_out)
    late = lax.all_gather(late, everywhere, axis=0, tiled=True)
    late = late.reshape(shards, groups, own_rows, late_width)

    at_tail = 3 * own_rows
    small = ordered(
        ctx_index, first_own[:, :, :, at_tail], first_other[:, :, :, at_tail], 2
    )
    small = jnp.moveaxis(small, 3, 1).reshape(shards, groups, shard_width)
    ends = np.cumsum([0] + sizes)

    def spread(index):
        item = small[:, :, ends[index] : ends[index + 1]]
        item = item.reshape(shards, groups, local_heads, -1)
        return jnp.moveaxis(item, 1, 2).reshape(heads, -1).astype(F32)

    gain_one = spread(0).reshape(1, width)
    gain_two = spread(1).reshape(1, width)
    gate = jax.nn.sigmoid(spread(2)).reshape(1, width)
    bias_rows = spread(3)

    def whole(shape):
        return pl.BlockSpec(shape, lambda *_: (0,) * len(shape))

    def weight(index):
        spec = pl.BlockSpec(
            (1, pairs, 1, own_rows, shard_width), lambda t, *_: (t // half, 0, t % half, index, 0)
        )
        return [spec, spec]

    def of_head(count, index):
        def at(h, *_):
            t = h // local_heads
            return (t // half, 0, t % half, index, h % local_heads)

        spec = pl.BlockSpec((1, pairs, 1, count, head), at)
        return [spec, spec]

    column = pl.BlockSpec((rows, shard_width), lambda t, *_: (0, t))
    wide = jax.ShapeDtypeStruct((rows, width), BF)
    wide32 = jax.ShapeDtypeStruct((rows, width), F32)
    split = jax.ShapeDtypeStruct((shards, rows, shard_width), BF)
    queries, keys, values, _ = call(
        project_kernel,
        (shards,),
        [whole((rows, width)), whole((1, width))] + weight(0) + weight(1) + weight(2),
        [column, column, column, whole((rows, width))],
        [wide] * 4,
    )(place, x, gain_one, *([first_own, first_other] * 3))

    key_blocks = keys.reshape(seqs, blocks, BLOCK, width)
    value_blocks = values.reshape(seqs, blocks, BLOCK, width)
    halo_keys = from_behind(key_blocks[:, -1], "ctx", 1).reshape(seqs * BLOCK, width)
    halo_values = from_behind(value_blocks[:, -1], "ctx", 1).reshape(seqs * BLOCK, width)

    def along(rows_of, index):
        return pl.BlockSpec((rows_of, head), lambda h, n, *_: (index(n), h))

    def turned(n):
        return units - 1 - n

    query_slots = of_head(own_slots, 0)
    init_slots = of_head(own_slots, 1)
    key_maps = of_head(map_rows, 2 * own_slots // map_rows)
    value_maps = of_head(map_rows, 2 * own_slots // map_rows + 1)
    channel = pl.BlockSpec((1, head), lambda h, n, *_: (0, h))
    slot_rows = units * slots
    slot_f32 = jax.ShapeDtypeStruct((slot_rows, width), F32)
    slot_low = jax.ShapeDtypeStruct((slot_rows, width), BF)
    message = jax.ShapeDtypeStruct((seqs * slots, width), BF)
    slot_scratch = pltpu.VMEM((slots, head), F32)
    own = along(BLOCK, lambda n: n)
    slot = along(slots, lambda n: n)
    slot_of_seq = along(slots, lambda n: n // blocks)
    contrib, accumulated = call(
        functools.partial(read_kernel, blocks=blocks),
        (heads, units),
        query_slots + [own, own, channel],
        [slot, slot_of_seq],
        [slot_f32, message],
        [slot_scratch],
    )(place, second_own, second_other, keys, values, gate)
    power = gate**blocks
    lead = carry(accumulated, power, "ctx", False)
    lead_power = jnp.ones_like(gate)
    for step in range(lax.axis_size("ctx") - 1):
        lead_power = jnp.where(ctx_index > step, lead_power * power, lead_power)

    block_at = ctx_index * blocks + jnp.arange(blocks, dtype=jnp.int32)
    own_prefix = lax.dynamic_slice_in_dim(prefix, tp_index * seqs, seqs, 0)
    info = jnp.stack(
        [
            jnp.broadcast_to(block_at[None], (seqs, blocks)),
            own_prefix[:, None] - block_at[None] * BLOCK,
        ],
        axis=-1,
    ).reshape(units, 2)
    span = 4 * BLOCK
    offset = np.arange(span)
    offset = np.where(offset < 2 * BLOCK, offset, offset - span)
    forward_hot = one_hot(BLOCK - offset, offset > -BLOCK, buckets)
    back_span = 3 * BLOCK
    back_offset = np.arange(back_span)
    back_offset = np.where(back_offset < BLOCK, back_offset, back_offset - back_span)
    backward_hot = one_hot(BLOCK + back_offset, back_offset > -2 * BLOCK, buckets)
    exact = lax.Precision.HIGHEST
    scaled_bias = bias_rows * LOG2E
    forward_bias = jnp.dot(scaled_bias, forward_hot.T, precision=exact)[:, None]
    backward_bias = jnp.dot(scaled_bias, backward_hot.T, precision=exact)[:, None]

    def attend_specs(index):
        before = along(BLOCK, lambda n: jnp.maximum(index(n) - 1, 0))
        by_seq = along(BLOCK, lambda n: index(n) // blocks)
        here = along(BLOCK, index)
        return [here, here, here, before, before, by_seq, by_seq] + key_maps + value_maps

    def lse_spec(index):
        return pl.BlockSpec((1, 1, 1, BLOCK), lambda h, n, *_: (index(n), h, 0, 0))

    def vector(size):
        return pl.BlockSpec((1, 1, size), lambda h, *_: (h, 0, 0))

    attend_args = (
        place, info, queries, keys, values, keys, values, halo_keys, halo_values,
        second_own, second_other, second_own, second_other,
    )
    attended, lse, states, moved = call(
        functools.partial(attend_kernel, blocks=blocks),
        (heads, units),
        attend_specs(lambda n: n)
        + [slot] + init_slots + [slot_of_seq, channel, channel, vector(span)],
        [own, lse_spec(lambda n: n), slot, slot],
        [wide, jax.ShapeDtypeStruct((units, heads, 1, BLOCK), F32), slot_low, slot_low],
        [pltpu.VMEM((BLOCK, 2 * BLOCK), F32), slot_scratch],
        2,
    )(*attend_args, contrib, second_own, second_other, lead, lead_power, gate, forward_bias)

    out_weight = pl.BlockSpec(
        (1, groups, own_rows, shard_width), lambda t, *_: (t, 0, 0, 2 * hidden // shard_width)
    )
    middle, mlp_in = pl.pallas_call(
        out_kernel,
        grid=(shards,),
        in_specs=[column, out_weight, whole((rows, width)), whole((1, width))],
        out_specs=[whole((rows, width)), whole((rows, width))],
        out_shape=[wide32, wide],
        compiler_params=params(),
    )(attended, late, x, gain_two)

    tile = 512
    per_shard = hidden // tile
    tile_block = (1, groups, own_rows, tile)
    output, middle_grad, gain_two_grad, late_grad = call(
        mlp_kernel,
        (shards * per_shard, 2),
        [
            whole((rows, width)),
            pl.BlockSpec((rows, width), lambda i, j, place_ref: (place_ref[1], 0)),
            whole((rows, width)), whole((1, width)),
            pl.BlockSpec(tile_block, lambda i, j, *_: (i // per_shard, 0, 0, i % per_shard)),
            pl.BlockSpec(
                tile_block, lambda i, j, *_: (i // per_shard, 0, 0, per_shard + i % per_shard)
            ),
        ],
        [
            whole((shards, rows, shard_width)), whole((rows, width)), whole((1, width)),
            pl.BlockSpec(
                tile_block, lambda i, j, *_: (i // per_shard, 0, 0, j * per_shard + i % per_shard)
            ),
        ],
        [
            split, wide, jax.ShapeDtypeStruct((1, width), F32),
            jax.ShapeDtypeStruct((shards, groups, own_rows, late_width), BF),
        ],
        [
            pltpu.VMEM((width, rows), BF), pltpu.VMEM((width, rows), BF),
            pltpu.VMEM((rows, width), F32), pltpu.VMEM((rows, width), F32),
            pltpu.VMEM((rows, tile), BF),
        ],
    )(
        place, mlp_in, cotangent.reshape(seq_count * length, width), middle, gain_two, late, late
    )
    output = lax.all_to_all(output, "tp", 0, 0, tiled=True)

    grad_attended, late_grad = pl.pallas_call(
        out_back_kernel,
        grid=(shards,),
        in_specs=[
            whole((rows, width)), out_weight, column, pl.BlockSpec(memory_space=pl.ANY)
        ],
        out_specs=[column, out_weight],
        out_shape=[wide, jax.ShapeDtypeStruct(late_grad.shape, BF)],
        scratch_shapes=[pltpu.VMEM((width, rows), BF)],
        compiler_params=params(),
        input_output_aliases={3: 1},
    )(middle_grad, late, attended, late_grad)
    late_grad = lax.psum_scatter(
        late_grad.reshape(shards * groups * own_rows, late_width), everywhere,
        scatter_dimension=0, tiled=True,
    )
    up_grad, down_grad, out_grad = pl.pallas_call(
        unpack_kernel,
        out_shape=[
            jax.ShapeDtypeStruct(w_up.shape, F32), jax.ShapeDtypeStruct(w_down.shape, F32),
            jax.ShapeDtypeStruct(w_out.shape, F32),
        ],
    )(late_grad)

    head_sum = jax.ShapeDtypeStruct((heads, head, head), F32)
    head_map = pl.BlockSpec((1, head, head), lambda h, n, *_: (h, 0, 0))
    back_own = along(BLOCK, turned)
    back_slot = along(slots, turned)
    back_of_seq = along(slots, lambda n: turned(n) // blocks)
    (
        grad_queries, dk, dv, dk_before, dv_before, direct, key_map_grad, value_map_grad,
        bias_sum, gathered,
    ) = call(
        functools.partial(attend_back_kernel, blocks=blocks),
        (heads, units),
        attend_specs(turned)
        + [back_slot, channel, vector(back_span), back_own, back_own, lse_spec(turned)],
        [back_own] * 5 + [back_slot, head_map, head_map, vector(back_span), back_of_seq],
        [
            wide, wide32, wide32, wide, wide, slot_f32, head_sum, head_sum,
            jax.ShapeDtypeStruct((heads, 1, back_span), F32), message,
        ],
        [
            pltpu.VMEM((2 * BLOCK, BLOCK), F32), pltpu.VMEM((128, back_span), F32),
            pltpu.VMEM((BLOCK, head), F32), slot_scratch,
        ],
        2,
    )(*attend_args, states, gate, backward_bias, grad_attended, attended, lse)
    sum_at = np.arange(back_span) - BLOCK
    sum_hot = one_hot(sum_at, sum_at > -BLOCK, buckets)
    bias_grad = jnp.dot(bias_sum[:, 0], sum_hot, precision=exact)

    later = carry(gathered, power, "ctx", True)
    first_keys = dk_before.reshape(seqs, blocks, BLOCK, width)[:, 0]
    first_values = dv_before.reshape(seqs, blocks, BLOCK, width)[:, 0]
    back_keys = from_behind(first_keys, "ctx", -1).reshape(seqs * BLOCK, width)
    back_values = from_behind(first_values, "ctx", -1).reshape(seqs * BLOCK, width)
    following = along(BLOCK, lambda n: jnp.minimum(turned(n) + 1, units - 1))
    key_of_seq = along(BLOCK, lambda n: turned(n) // blocks)
    kept_slot = pl.BlockSpec((slots, head), lambda h, n, *_: (0, h))
    slot_sum = jax.ShapeDtypeStruct((slots, width), F32)
    grad_keys, grad_values, slot_query_grad, init_grad, gate_grad = call(
        functools.partial(read_back_kernel, blocks=blocks),
        (heads, units),
        query_slots
        + [back_own, back_own, back_slot, back_slot, back_of_seq, channel]
        + [back_own, back_own, following, following, key_of_seq, key_of_seq],
        [back_own, back_own, kept_slot, kept_slot, vector(head)],
        [wide, wide, slot_sum, slot_sum, jax.ShapeDtypeStruct((heads, 1, head), F32)],
        [slot_scratch],
    )(
        place, second_own, second_other, keys, values, direct, moved, later, gate,
        dk, dv, dk_before, dv_before, back_keys, back_values,
    )

    at_slots = 3 * own_rows
    at_init = at_slots + own_slots
    at_maps = at_init + own_slots
    at_vectors = at_maps + 2 * map_rows
    full_rows = at_vectors + 16
    maps_of = pl.BlockSpec((local_heads, head, head), lambda t, *_: (t, 0, 0))
    slots_of = pl.BlockSpec((slots, shard_width), lambda t, *_: (0, t))
    piece = pl.BlockSpec((1, pairs, full_rows, shard_width), lambda t, *_: (t, 0, 0, 0))
    pieces = jax.ShapeDtypeStruct((shards, pairs, full_rows, shard_width), BF)
    token_grad, gain_one_grad, grad_own, grad_other = call(
        project_back_kernel,
        (shards,),
        [whole((rows, width)), whole((rows, width)), whole((1, width)), column, column, column]
        + weight(0) + weight(1) + weight(2) + [slots_of, slots_of, maps_of, maps_of],
        [whole((shards, rows, shard_width)), whole((1, width)), piece, piece],
        [split, jax.ShapeDtypeStruct((1, width), F32), pieces, pieces],
        [
            pltpu.VMEM((width, rows), BF), pltpu.VMEM((rows, width), F32),
            pltpu.VMEM((groups, full_rows, shard_width), BF),
        ],
    )(
        place, x, middle_grad, gain_one, grad_queries, grad_keys, grad_values,
        *([first_own, first_other] * 3), slot_query_grad, init_grad, key_map_grad, value_map_grad,
    )
    token_grad = lax.all_to_all(token_grad, "tp", 0, 0, tiled=True)

    vector_sums = [gain_one_grad, gain_two_grad, gate_grad.reshape(1, width), bias_grad]
    vector_rows = jnp.concatenate([item.reshape(-1) for item in vector_sums])
    vector_rows = jnp.pad(vector_rows, (0, 16 * shard_width - vector_rows.size)).astype(BF)
    vector_rows = jnp.broadcast_to(
        vector_rows.reshape(1, 1, 16, shard_width), (shards, pairs, 16, shard_width)
    )
    grad_own = lax.dynamic_update_slice(grad_own, vector_rows, (0, 0, at_vectors, 0))
    grad_other = lax.dynamic_update_slice(grad_other, vector_rows, (0, 0, at_vectors, 0))
    grads = scatter_pairs(grad_own, grad_other)
    vector_grads = grads[at_vectors:].reshape(-1)
    group = dp_index * lax.axis_size("ctx") + ctx_index

    def own_part(index, like):
        begin = sum(item.size for item in vector_sums[:index])
        item = vector_grads[begin : begin + vector_sums[index].size].reshape(heads, -1)
        return lax.dynamic_slice(
            item, (tp_index * local_heads, group * like.shape[1]), like.shape
        )

    def apart(item):
        return jnp.moveaxis(item.reshape(map_rows, local_heads, head), 1, 0)

    return (
        output.reshape(seq_count, length, shard_width),
        token_grad.reshape(seq_count, length, shard_width),
        grads[:own_rows],
        grads[own_rows : 2 * own_rows],
        grads[2 * own_rows : at_slots],
        out_grad,
        up_grad,
        down_grad,
        grads[at_slots:at_init],
        grads[at_init:at_maps],
        own_part(0, gain_attn),
        own_part(1, gain_mlp),
        own_part(3, bias_table),
        own_part(2, gate_bias),
        apart(grads[at_maps : at_maps + map_rows]),
        apart(grads[at_maps + map_rows : at_vectors]),
    )


def choose(tokens, *others):
    shards = lax.axis_size("tp")
    even = tokens.shape[0] % shards == 0 and shards % 2 == 0 and shards & (shards - 1) == 0
    even = even and lax.axis_size("dp") == 4 and lax.axis_size("ctx") == 2
    return (sequence_body if even else body)(tokens, *others)


def solution(mesh):
    in_specs = (
        P("dp", "ctx", "tp"),
        P("dp", "ctx", None),
        P("dp"),
        P(("dp", "ctx"), "tp"),
        P(("dp", "ctx"), "tp"),
        P(("dp", "ctx"), "tp"),
        P("tp", ("dp", "ctx")),
        P(("dp", "ctx"), "tp"),
        P("tp", ("dp", "ctx")),
        P(("dp", "ctx"), "tp"),
        P(("dp", "ctx"), "tp"),
        P("tp", ("dp", "ctx")),
        P("tp", ("dp", "ctx")),
        P("tp", ("dp", "ctx")),
        P("tp", ("dp", "ctx")),
        P("tp", ("dp", "ctx"), None),
        P("tp", ("dp", "ctx"), None),
    )
    out_specs = (
        P("dp", "ctx", "tp"),
        P("dp", "ctx", "tp"),
        P(("dp", "ctx"), "tp"),
        P(("dp", "ctx"), "tp"),
        P(("dp", "ctx"), "tp"),
        P("tp", ("dp", "ctx")),
        P(("dp", "ctx"), "tp"),
        P("tp", ("dp", "ctx")),
        P(("dp", "ctx"), "tp"),
        P(("dp", "ctx"), "tp"),
        P("tp", ("dp", "ctx")),
        P("tp", ("dp", "ctx")),
        P("tp", ("dp", "ctx")),
        P("tp", ("dp", "ctx")),
        P("tp", ("dp", "ctx"), None),
        P("tp", ("dp", "ctx"), None),
    )
    return jax.shard_map(choose, mesh=mesh, in_specs=in_specs, out_specs=out_specs, check_vma=False)
```

```python
import functools

import jax
import jax.numpy as jnp
import numpy as np
from jax import lax
from jax.experimental import pallas as pl
from jax.experimental.pallas import tpu as pltpu
from jax.sharding import PartitionSpec as P

HEAD_SIZE = 128
BLOCK = 512


EPSILON = 1e-06
MASKED = -1e30
ROWS_FORWARD = 128
KEYS_BACKWARD = 256


def from_behind(value, axis, steps):
    count = lax.axis_size(axis)
    first, last = (max(0, -steps), min(count, count - steps))
    return lax.ppermute(value, axis, [(source, source + steps) for source in range(first, last)])


def prefix_2(array, axis, join, neutral, backward):
    count = lax.axis_size(axis)
    place = lax.axis_index(axis)
    ahead = count - 1 - place if backward else place
    gathered = jax.tree.map(
        lambda a, kind: lax.all_gather(a.astype(kind), axis), array, (jnp.bfloat16, jnp.bfloat16)
    )
    state = jax.tree.map(lambda a, e: jnp.zeros_like(a) + jnp.asarray(e, a.dtype), array, neutral)

    def one(hop, state):
        source = count - 1 - hop if backward else hop
        return join(
            state,
            jax.tree.map(
                lambda a, own: lax.dynamic_index_in_dim(a, source, 0, False).astype(own.dtype),
                gathered,
                array,
            ),
        )

    return lax.fori_loop(0, ahead, one, state)


def bucket_index(block_size):
    query_pos = np.arange(block_size)[:, None] + block_size
    key_pos = np.arange(2 * block_size)[None, :]
    distance = query_pos - key_pos
    upper_part = (distance < 0).astype(np.int32) * 16
    magnitude = np.abs(distance)
    scaled = np.log(np.maximum(magnitude, 1) / 8.0) / np.log(16.0) * 8.0
    far_bucket = np.minimum(8 + np.floor(np.maximum(scaled, 0.0)).astype(np.int32), 15)
    return (upper_part + np.where(magnitude < 8, magnitude, far_bucket)).astype(np.int32)


def norm_forward(features, gain_vector):
    inverse = lax.rsqrt(jnp.mean(features * features, axis=-1, keepdims=True) + EPSILON)
    normed = features * inverse
    return (normed, inverse, (normed * gain_vector).astype(jnp.bfloat16))


def norm_backward(grad_normed, normed, inverse, gain_vector):
    scaled = grad_normed * gain_vector
    grad_in = inverse * (scaled - normed * jnp.mean(scaled * normed, axis=-1, keepdims=True))
    return (grad_in, jnp.sum(grad_normed * normed, axis=0))


def compose(earlier, later_pair):
    return (earlier[0] * later_pair[0], later_pair[0] * earlier[1] + later_pair[1])


def bias_matrix(bias_rows, bucket):
    summed = jnp.zeros((bias_rows.shape[0],) + bucket.shape, jnp.float32)
    for number in range(bias_rows.shape[1]):
        summed = (
            summed
            + bias_rows[:, number][:, None, None] * (bucket == number).astype(jnp.float32)[None]
        )
    return summed


def bias_gradient(grad_matrix, bucket, bucket_count):
    columns = [
        jnp.sum(grad_matrix * (bucket == number).astype(jnp.float32)[None], axis=(1, 2))
        for number in range(bucket_count)
    ]
    return jnp.stack(columns, axis=1)


def body(
    tokens,
    cotangent,
    prefix,
    w_query,
    w_key,
    w_value,
    w_out,
    w_up,
    w_down,
    state_query,
    state_init,
    gain_attn,
    gain_mlp,
    bias_table,
    gate_bias,
    state_key,
    state_value,
):
    (
        query_full,
        key_full,
        value_full,
        out_full,
        up_full,
        down_full,
        squery_full,
        sinit_full,
        gain_one,
        gain_two,
        bias_rows,
        gate_rows,
        state_key_complete,
        svalue_full,
    ) = (
        lax.all_gather(w_query, ("dp", "ctx"), axis=0, tiled=True),
        lax.all_gather(w_key, ("dp", "ctx"), axis=0, tiled=True),
        lax.all_gather(w_value, ("dp", "ctx"), axis=0, tiled=True),
        lax.all_gather(w_out, ("dp", "ctx"), axis=1, tiled=True),
        lax.all_gather(w_up, ("dp", "ctx"), axis=0, tiled=True),
        lax.all_gather(w_down, ("dp", "ctx"), axis=1, tiled=True),
        lax.all_gather(state_query, ("dp", "ctx"), axis=0, tiled=True),
        lax.all_gather(state_init, ("dp", "ctx"), axis=0, tiled=True),
        lax.all_gather(gain_attn, ("dp", "ctx"), axis=1, tiled=True),
        lax.all_gather(gain_mlp, ("dp", "ctx"), axis=1, tiled=True),
        lax.all_gather(bias_table, ("dp", "ctx"), axis=1, tiled=True),
        lax.all_gather(gate_bias, ("dp", "ctx"), axis=1, tiled=True),
        lax.all_gather(state_key, ("dp", "ctx"), axis=1, tiled=True),
        lax.all_gather(state_value, ("dp", "ctx"), axis=1, tiled=True),
    )
    seq_count = tokens.shape[0]
    length = tokens.shape[1]
    shard_width = tokens.shape[2]
    full_width = cotangent.shape[2]
    block_count = length // BLOCK
    row_count = seq_count * length
    local_head_count = bias_rows.shape[0]
    local_width = local_head_count * HEAD_SIZE
    state_slot_count = squery_full.shape[0]
    scores_scale = HEAD_SIZE ** (-0.5)
    local_shape = (seq_count, block_count, BLOCK, local_head_count, HEAD_SIZE)
    element_count = seq_count * block_count
    token_full, gain_one_full = (
        lax.all_gather(tokens, "tp", axis=2, tiled=True),
        lax.all_gather(gain_one, "tp", axis=0, tiled=True),
    )
    gain_one_vec = gain_one_full.reshape(full_width).astype(jnp.float32)
    normed_one, inverse_one, attn_in = norm_forward(
        token_full.reshape(row_count, full_width).astype(jnp.float32), gain_one_vec
    )
    queries = (
        jnp.dot(attn_in, query_full, preferred_element_type=jnp.float32)
        .astype(jnp.bfloat16)
        .reshape(local_shape)
    )
    key_rows = (
        jnp.dot(attn_in, key_full, preferred_element_type=jnp.float32)
        .astype(jnp.bfloat16)
        .reshape(local_shape)
    )
    value_rows = (
        jnp.dot(attn_in, value_full, preferred_element_type=jnp.float32)
        .astype(jnp.bfloat16)
        .reshape(local_shape)
    )
    last_keys, last_values = from_behind((key_rows[:, -1], value_rows[:, -1]), "ctx", 1)
    window_keys = jnp.concatenate(
        [jnp.concatenate([last_keys[:, None], key_rows[:, :-1]], 1), key_rows], 2
    )
    window_values = jnp.concatenate(
        [jnp.concatenate([last_values[:, None], value_rows[:, :-1]], 1), value_rows], 2
    )
    query_heads = squery_full.reshape(state_slot_count, local_head_count, HEAD_SIZE)
    read_scores = (
        jnp.einsum("mhe,sbthe->sbhmt", query_heads, key_rows, preferred_element_type=jnp.float32)
        * scores_scale
    )
    read_peak = jnp.max(read_scores, axis=-1, keepdims=True)
    read_raised = jnp.exp(read_scores - read_peak)
    read_probs = read_raised / jnp.sum(read_raised, axis=-1, keepdims=True)
    read_low = read_probs.astype(jnp.bfloat16)
    contrib = jnp.einsum(
        "sbhmt,sbthe->sbmhe", read_low, value_rows, preferred_element_type=jnp.float32
    )
    contrib = contrib.reshape(seq_count, block_count, state_slot_count, local_width)
    gate_value = jax.nn.sigmoid(gate_rows.reshape(local_width).astype(jnp.float32))
    gate_power = jnp.ones((local_width,), jnp.float32)
    accumulated = jnp.zeros((seq_count, state_slot_count, local_width), jnp.float32)
    for block_index in range(block_count):
        accumulated = gate_value * accumulated + (1.0 - gate_value) * contrib[:, block_index]
        gate_power = gate_power * gate_value
    identity = (jnp.ones((local_width,), jnp.float32), jnp.zeros_like(accumulated))
    lead_power, lead_state = prefix_2((gate_power, accumulated), "ctx", compose, identity, False)
    entry_state = lead_power * sinit_full.astype(jnp.float32) + lead_state
    state_list = [entry_state]
    block_index = 0
    state_list.append(gate_value * state_list[-1] + (1.0 - gate_value) * contrib[:, block_index])
    stacked = jnp.stack(state_list, axis=1)
    state_reduced = stacked.astype(jnp.bfloat16).reshape(
        seq_count, block_count, state_slot_count, local_head_count, HEAD_SIZE
    )
    state_key_rows = jnp.einsum(
        "cazqr,qrx->cazqx", state_reduced, state_key_complete, preferred_element_type=jnp.float32
    ).astype(jnp.bfloat16)
    state_values = jnp.einsum(
        "cazqr,qrx->cazqx", state_reduced, svalue_full, preferred_element_type=jnp.float32
    ).astype(jnp.bfloat16)
    bucket = jnp.asarray(bucket_index(BLOCK))
    bias_full = bias_matrix(bias_rows.astype(jnp.float32), bucket)
    block_ids = lax.axis_index("ctx") * block_count + jnp.arange(block_count, dtype=jnp.int32)
    query_pos = block_ids[:, None] * BLOCK + jnp.arange(BLOCK, dtype=jnp.int32)[None, :]
    key_pos = (block_ids[:, None] - 1) * BLOCK + jnp.arange(2 * BLOCK, dtype=jnp.int32)[None, :]
    causal = (key_pos[:, None, :] >= 0) & (key_pos[:, None, :] <= query_pos[:, :, None])
    in_prefix = (key_pos[None, :, None, :] >= 0) & (
        key_pos[None, :, None, :] < prefix[:, None, None, None]
    )
    permitted_mask = (causal[None] | in_prefix).reshape(element_count, 1, BLOCK, 2 * BLOCK)
    flattened_queries = queries.reshape(element_count, BLOCK, local_head_count, HEAD_SIZE)
    flattened_window_keys = window_keys.reshape(
        element_count, 2 * BLOCK, local_head_count, HEAD_SIZE
    )
    flattened_window_values = window_values.reshape(
        element_count, 2 * BLOCK, local_head_count, HEAD_SIZE
    )
    flattened_state_keys = state_key_rows.reshape(
        element_count, state_slot_count, local_head_count, HEAD_SIZE
    )
    flattened_state_values = state_values.reshape(
        element_count, state_slot_count, local_head_count, HEAD_SIZE
    )

    def block_score_rows(
        block_query_rows, block_window_key_rows, block_state_key_rows, block_permitted_mask
    ):
        window_part = (
            jnp.einsum(
                "ihe,jhe->hij",
                block_query_rows,
                block_window_key_rows,
                preferred_element_type=jnp.float32,
            )
            * scores_scale
            + bias_full
        )
        state_part = (
            jnp.einsum(
                "yat,zat->ayz",
                block_query_rows,
                block_state_key_rows,
                preferred_element_type=jnp.float32,
            )
            * scores_scale
        )
        return (jnp.where(block_permitted_mask, window_part, MASKED), state_part)

    def attend_one_block(element_entry):
        (
            block_query_rows,
            block_window_key_rows,
            block_window_value_rows,
            block_state_key_rows,
            block_state_value_rows,
            block_permitted_mask,
        ) = element_entry
        window_scores, scores_of_state = block_score_rows(
            block_query_rows, block_window_key_rows, block_state_key_rows, block_permitted_mask
        )
        row_peak = jnp.maximum(jnp.max(window_scores, axis=-1), jnp.max(scores_of_state, axis=-1))
        window_raised = jnp.exp(window_scores - row_peak[..., None])
        state_raised = jnp.exp(scores_of_state - row_peak[..., None])
        denominator = jnp.sum(window_raised, axis=-1) + jnp.sum(state_raised, axis=-1)
        log_total = row_peak + jnp.log(denominator)
        window_probs = (window_raised / denominator[..., None]).astype(jnp.bfloat16)
        state_probs = (state_raised / denominator[..., None]).astype(jnp.bfloat16)
        block_out = jnp.einsum(
            "hij,jhe->ihe",
            window_probs,
            block_window_value_rows,
            preferred_element_type=jnp.float32,
        ) + jnp.einsum(
            "wyd,dwg->ywg", state_probs, block_state_value_rows, preferred_element_type=jnp.float32
        )
        return (block_out.astype(jnp.bfloat16), log_total)

    attended_blocks, log_totals = lax.map(
        attend_one_block,
        (
            flattened_queries,
            flattened_window_keys,
            flattened_window_values,
            flattened_state_keys,
            flattened_state_values,
            permitted_mask,
        ),
    )
    attended = attended_blocks.reshape(row_count, local_width)
    attn_part = jnp.dot(attended, out_full, preferred_element_type=jnp.float32).reshape(
        seq_count, length, full_width
    )
    attn_share = lax.psum_scatter(
        attn_part.astype(jnp.bfloat16), "tp", scatter_dimension=2, tiled=True
    ).astype(jnp.float32)
    middle = tokens.astype(jnp.float32) + attn_share
    middle_full, gain_two_full = (
        lax.all_gather(middle.astype(jnp.bfloat16), "tp", axis=2, tiled=True),
        lax.all_gather(gain_two, "tp", axis=0, tiled=True),
    )
    gain_two_vec = gain_two_full.reshape(full_width).astype(jnp.float32)
    normed_two, inverse_two, mlp_in = norm_forward(
        middle_full.reshape(row_count, full_width).astype(jnp.float32), gain_two_vec
    )
    hidden_pre = jnp.dot(mlp_in, up_full, preferred_element_type=jnp.float32)
    hidden = jax.nn.gelu(hidden_pre, approximate=False).astype(jnp.bfloat16)
    mlp_part = jnp.dot(hidden, down_full, preferred_element_type=jnp.float32).reshape(
        seq_count, length, full_width
    )
    mlp_share = lax.psum_scatter(
        mlp_part.astype(jnp.bfloat16), "tp", scatter_dimension=2, tiled=True
    ).astype(jnp.float32)
    output = (middle + mlp_share).astype(jnp.bfloat16)
    grad_out = cotangent.reshape(row_count, full_width)
    grad_hidden = jnp.dot(grad_out, down_full.T, preferred_element_type=jnp.float32)
    grad_down = jnp.dot(hidden.T, grad_out, preferred_element_type=jnp.float32)

    def gelu_exact(pre_values):
        return jax.nn.gelu(pre_values, approximate=False)

    gelu_value, gelu_back = jax.vjp(gelu_exact, hidden_pre)
    grad_pre = gelu_back(grad_hidden)[0].astype(jnp.bfloat16)
    grad_up = jnp.dot(mlp_in.T, grad_pre, preferred_element_type=jnp.float32)
    grad_mlp_in = jnp.dot(grad_pre, up_full.T, preferred_element_type=jnp.float32)
    part_middle, part_gain_two = norm_backward(grad_mlp_in, normed_two, inverse_two, gain_two_vec)
    tp_index = lax.axis_index("tp")
    head_total = full_width // HEAD_SIZE
    summed, gain_two_sum = (
        lax.psum(
            part_middle.reshape(seq_count, length, full_width).astype(jnp.bfloat16), "tp"
        ).astype(jnp.float32),
        lax.psum(part_gain_two.reshape(head_total, HEAD_SIZE).astype(jnp.bfloat16), "tp").astype(
            jnp.float32
        ),
    )
    middle_grad_full = cotangent.astype(jnp.float32) + summed
    middle_grad = lax.dynamic_slice_in_dim(middle_grad_full, tp_index * shard_width, shard_width, 2)
    grad_gain_two = lax.dynamic_slice_in_dim(
        gain_two_sum, tp_index * local_head_count, local_head_count, 0
    )
    middle_grad_low = middle_grad_full.astype(jnp.bfloat16)
    middle_grad_rows = middle_grad_low.reshape(row_count, full_width)
    grad_attended = jnp.dot(
        middle_grad_rows, out_full.T, preferred_element_type=jnp.float32
    ).astype(jnp.bfloat16)
    grad_attended = grad_attended.reshape(element_count, BLOCK, local_head_count, HEAD_SIZE)
    grad_wout = jnp.dot(attended.T, middle_grad_rows, preferred_element_type=jnp.float32)

    def attend_back(bias_sum, element_entry):
        (
            block_query_rows,
            block_window_key_rows,
            block_window_value_rows,
            block_state_key_rows,
            block_state_value_rows,
            block_permitted_mask,
            block_lse,
            block_grad,
        ) = element_entry
        window_again, state_again = block_score_rows(
            block_query_rows, block_window_key_rows, block_state_key_rows, block_permitted_mask
        )
        window_exact = jnp.exp(window_again - block_lse[..., None])
        state_exact = jnp.exp(state_again - block_lse[..., None])
        grad_wprob = jnp.einsum(
            "ihe,jhe->hij", block_grad, block_window_value_rows, preferred_element_type=jnp.float32
        )
        grad_sprob = jnp.einsum(
            "yat,zat->ayz", block_grad, block_state_value_rows, preferred_element_type=jnp.float32
        )
        row_delta = jnp.sum(window_exact * grad_wprob, axis=-1) + jnp.sum(
            state_exact * grad_sprob, axis=-1
        )
        grad_wscore = (window_exact * (grad_wprob - row_delta[..., None])).astype(jnp.bfloat16)
        state_score_gradient = (state_exact * (grad_sprob - row_delta[..., None])).astype(
            jnp.bfloat16
        )
        block_grad_q = scores_scale * (
            jnp.einsum(
                "hij,jhe->ihe",
                grad_wscore,
                block_window_key_rows,
                preferred_element_type=jnp.float32,
            )
            + jnp.einsum(
                "wyd,dwg->ywg",
                state_score_gradient,
                block_state_key_rows,
                preferred_element_type=jnp.float32,
            )
        )
        block_grad_wk = scores_scale * jnp.einsum(
            "hij,ihe->jhe", grad_wscore, block_query_rows, preferred_element_type=jnp.float32
        )
        block_grad_wv = jnp.einsum(
            "hij,ihe->jhe",
            window_exact.astype(jnp.bfloat16),
            block_grad,
            preferred_element_type=jnp.float32,
        )
        block_grad_sk = (
            scores_scale
            * jnp.einsum(
                "him,ihe->mhe",
                state_score_gradient,
                block_query_rows,
                preferred_element_type=jnp.float32,
            )
        ).astype(jnp.bfloat16)
        block_grad_sv = jnp.einsum(
            "him,ihe->mhe",
            state_exact.astype(jnp.bfloat16),
            block_grad,
            preferred_element_type=jnp.float32,
        ).astype(jnp.bfloat16)
        return (
            bias_sum + grad_wscore.astype(jnp.float32),
            (block_grad_q, block_grad_wk, block_grad_wv, block_grad_sk, block_grad_sv),
        )

    bias_start = jnp.zeros((local_head_count, BLOCK, 2 * BLOCK), jnp.float32)
    bias_sum, back_items = lax.scan(
        attend_back,
        bias_start,
        (
            flattened_queries,
            flattened_window_keys,
            flattened_window_values,
            flattened_state_keys,
            flattened_state_values,
            permitted_mask,
            log_totals,
            grad_attended,
        ),
    )
    grad_bias = bias_gradient(bias_sum, bucket, bias_rows.shape[1])
    grad_queries = back_items[0].reshape(local_shape)
    grad_window_keys = back_items[1].reshape(
        seq_count, block_count, 2 * BLOCK, local_head_count, HEAD_SIZE
    )
    grad_window_values = back_items[2].reshape(
        seq_count, block_count, 2 * BLOCK, local_head_count, HEAD_SIZE
    )
    state_keys_gradient = back_items[3].reshape(
        seq_count, block_count, state_slot_count, local_head_count, HEAD_SIZE
    )
    grad_state_values = back_items[4].reshape(
        seq_count, block_count, state_slot_count, local_head_count, HEAD_SIZE
    )
    back_keys, back_values = (
        from_behind(grad_window_keys[:, 0, :BLOCK].astype(jnp.bfloat16), "ctx", -1).astype(
            jnp.float32
        ),
        from_behind(grad_window_values[:, 0, :BLOCK].astype(jnp.bfloat16), "ctx", -1).astype(
            jnp.float32
        ),
    )
    key_grad = grad_window_keys[:, :, BLOCK:] + jnp.concatenate(
        [grad_window_keys[:, 1:, :BLOCK], back_keys[:, None]], 1
    )
    value_grad = grad_window_values[:, :, BLOCK:] + jnp.concatenate(
        [grad_window_values[:, 1:, :BLOCK], back_values[:, None]], 1
    )
    state_key_gradient = jnp.einsum(
        "sbmhe,sbmhf->hef", state_reduced, state_keys_gradient, preferred_element_type=jnp.float32
    )
    grad_svalue = jnp.einsum(
        "sbmhe,sbmhf->hef", state_reduced, grad_state_values, preferred_element_type=jnp.float32
    )
    direct = jnp.einsum(
        "palcq,crq->palcr",
        state_keys_gradient,
        state_key_complete,
        preferred_element_type=jnp.float32,
    ) + jnp.einsum(
        "palcq,crq->palcr", grad_state_values, svalue_full, preferred_element_type=jnp.float32
    )
    direct = direct.reshape(seq_count, block_count, state_slot_count, local_width)
    back_accum = jnp.zeros((seq_count, state_slot_count, local_width), jnp.float32)
    for block_index in reversed(range(block_count)):
        back_accum = direct[:, block_index] + gate_value * back_accum
    back_identity = (jnp.ones((local_width,), jnp.float32), jnp.zeros_like(back_accum))
    unused_power, incoming = prefix_2((gate_power, back_accum), "ctx", compose, back_identity, True)
    carried = incoming
    contrib_grads = [None] * block_count
    gate_grad = jnp.zeros((local_width,), jnp.float32)
    for block_index in reversed(range(block_count)):
        contrib_grads[block_index] = ((1.0 - gate_value) * carried).astype(jnp.bfloat16)
        gate_grad = gate_grad + jnp.sum(
            carried * (stacked[:, block_index] - contrib[:, block_index]), axis=(0, 1)
        )
        carried = direct[:, block_index] + gate_value * carried
    first_device = (lax.axis_index("ctx") == 0).astype(jnp.float32)
    grad_sinit = first_device * jnp.sum(carried, axis=0)
    grad_gate = (gate_grad * gate_value * (1.0 - gate_value)).reshape(local_head_count, HEAD_SIZE)
    grad_contrib = jnp.stack(contrib_grads, axis=1).reshape(
        seq_count, block_count, state_slot_count, local_head_count, HEAD_SIZE
    )
    grad_read = jnp.einsum(
        "sbmhe,sbthe->sbhmt", grad_contrib, value_rows, preferred_element_type=jnp.float32
    )
    extra_values = jnp.einsum(
        "sbhmt,sbmhe->sbthe", read_low, grad_contrib, preferred_element_type=jnp.float32
    )
    read_delta = jnp.sum(read_probs * grad_read, axis=-1, keepdims=True)
    grad_read_score = (read_probs * (grad_read - read_delta)).astype(jnp.bfloat16)
    grad_squery = (
        scores_scale
        * jnp.einsum(
            "sbhmt,sbthe->mhe", grad_read_score, key_rows, preferred_element_type=jnp.float32
        )
    ).reshape(state_slot_count, local_width)
    extra_keys = scores_scale * jnp.einsum(
        "sbhmt,mhe->sbthe", grad_read_score, query_heads, preferred_element_type=jnp.float32
    )
    grad_q_rows = grad_queries.astype(jnp.bfloat16).reshape(row_count, local_width)
    grad_k_rows = (key_grad + extra_keys).astype(jnp.bfloat16).reshape(row_count, local_width)
    grad_v_rows = (value_grad + extra_values).astype(jnp.bfloat16).reshape(row_count, local_width)
    grad_wq = jnp.dot(attn_in.T, grad_q_rows, preferred_element_type=jnp.float32)
    grad_wk = jnp.dot(attn_in.T, grad_k_rows, preferred_element_type=jnp.float32)
    grad_wv = jnp.dot(attn_in.T, grad_v_rows, preferred_element_type=jnp.float32)
    grad_attn_in = (
        jnp.dot(grad_q_rows, query_full.T, preferred_element_type=jnp.float32)
        + jnp.dot(grad_k_rows, key_full.T, preferred_element_type=jnp.float32)
        + jnp.dot(grad_v_rows, value_full.T, preferred_element_type=jnp.float32)
    )
    part_tokens, part_gain_one = norm_backward(grad_attn_in, normed_one, inverse_one, gain_one_vec)
    token_share, grad_gain_one = (
        lax.psum_scatter(
            part_tokens.reshape(seq_count, length, full_width).astype(jnp.bfloat16),
            "tp",
            scatter_dimension=2,
            tiled=True,
        ).astype(jnp.float32),
        lax.psum_scatter(
            part_gain_one.reshape(head_total, HEAD_SIZE).astype(jnp.bfloat16),
            "tp",
            scatter_dimension=0,
            tiled=True,
        ).astype(jnp.float32),
    )
    grad_tokens = (middle_grad + token_share).astype(jnp.bfloat16)
    grads = (
        lax.psum_scatter(
            grad_wq.astype(jnp.bfloat16), ("dp", "ctx"), scatter_dimension=0, tiled=True
        ).astype(jnp.float32),
        lax.psum_scatter(
            grad_wk.astype(jnp.bfloat16), ("dp", "ctx"), scatter_dimension=0, tiled=True
        ).astype(jnp.float32),
        lax.psum_scatter(
            grad_wv.astype(jnp.bfloat16), ("dp", "ctx"), scatter_dimension=0, tiled=True
        ).astype(jnp.float32),
        lax.psum_scatter(
            grad_wout.astype(jnp.bfloat16), ("dp", "ctx"), scatter_dimension=1, tiled=True
        ).astype(jnp.float32),
        lax.psum_scatter(
            grad_up.astype(jnp.bfloat16), ("dp", "ctx"), scatter_dimension=0, tiled=True
        ).astype(jnp.float32),
        lax.psum_scatter(
            grad_down.astype(jnp.bfloat16), ("dp", "ctx"), scatter_dimension=1, tiled=True
        ).astype(jnp.float32),
        lax.psum_scatter(
            grad_squery.astype(jnp.bfloat16), ("dp", "ctx"), scatter_dimension=0, tiled=True
        ).astype(jnp.float32),
        lax.psum_scatter(
            grad_sinit.astype(jnp.bfloat16), ("dp", "ctx"), scatter_dimension=0, tiled=True
        ).astype(jnp.float32),
        lax.psum_scatter(
            grad_gain_one.astype(jnp.bfloat16), ("dp", "ctx"), scatter_dimension=1, tiled=True
        ).astype(jnp.float32),
        lax.psum_scatter(
            grad_gain_two.astype(jnp.bfloat16), ("dp", "ctx"), scatter_dimension=1, tiled=True
        ).astype(jnp.float32),
        lax.psum_scatter(
            grad_bias.astype(jnp.bfloat16), ("dp", "ctx"), scatter_dimension=1, tiled=True
        ).astype(jnp.float32),
        lax.psum_scatter(
            grad_gate.astype(jnp.bfloat16), ("dp", "ctx"), scatter_dimension=1, tiled=True
        ).astype(jnp.float32),
        lax.psum_scatter(
            state_key_gradient.astype(jnp.bfloat16), ("dp", "ctx"), scatter_dimension=1, tiled=True
        ).astype(jnp.float32),
        lax.psum_scatter(
            grad_svalue.astype(jnp.bfloat16), ("dp", "ctx"), scatter_dimension=1, tiled=True
        ).astype(jnp.float32),
    )
    return (
        output,
        grad_tokens,
        grads[0],
        grads[1],
        grads[2],
        grads[3],
        grads[4],
        grads[5],
        grads[6],
        grads[7],
        grads[8],
        grads[9],
        grads[10],
        grads[11],
        grads[12],
        grads[13],
    )


LOG2E = 1.4426950408889634
VMEM_BYTES = 58 * 1024 * 1024
BF = jnp.bfloat16
F32 = jnp.float32


def nn(left, right):
    return jnp.dot(left, right, preferred_element_type=F32)


def nt(left, right):
    return lax.dot_general(left, right, (((1,), (1,)), ((), ())), preferred_element_type=F32)


def tn(left, right):
    return lax.dot_general(left, right, (((0,), (0,)), ((), ())), preferred_element_type=F32)


def flat(ref):
    block = ref[0]
    return block.reshape(block.shape[0] * block.shape[1], block.shape[2])


def merged(place_ref, own_ref, other_ref):
    own = own_ref[0, :, 0]
    other = other_ref[0, :, 0]
    is_first = place_ref[0] == 0
    pair = [jnp.where(is_first, own, other), jnp.where(is_first, other, own)]
    block = jnp.stack(pair, axis=1)
    return block.reshape(-1, block.shape[-1])


def joined(tok_ref):
    return jnp.concatenate([tok_ref[part] for part in range(tok_ref.shape[0])], axis=1).astype(F32)


def inverse_rms(x):
    return lax.rsqrt(jnp.mean(x * x, axis=-1, keepdims=True) + EPSILON)


def params():
    return pltpu.CompilerParams(vmem_limit_bytes=VMEM_BYTES)


def project_kernel(
    place_ref, tok_ref, gain_ref, wq_ref, wqo_ref, wk_ref, wko_ref, wv_ref, wvo_ref,
    q_ref, k_ref, v_ref, ain_ref,
):
    @pl.when(pl.program_id(0) == 0)
    def _():
        x = joined(tok_ref)
        ain_ref[...] = (x * inverse_rms(x) * gain_ref[...]).astype(BF)

    a = ain_ref[...]
    for w_ref, w_other, o_ref in (
        (wq_ref, wqo_ref, q_ref), (wk_ref, wko_ref, k_ref), (wv_ref, wvo_ref, v_ref)
    ):
        o_ref[...] = nn(a, merged(place_ref, w_ref, w_other)).astype(BF)


def read_kernel(
    place_ref, sq_ref, sqo_ref, k_ref, v_ref, gate_ref, o_ref, sum_ref, state_ref, *, blocks
):
    n = pl.program_id(1)
    sq = merged(place_ref, sq_ref, sqo_ref)
    k = k_ref[...]
    v = v_ref[...]
    scale = HEAD_SIZE ** (-0.5) * LOG2E
    step = 256
    gate = jnp.where(lax.rem(n, blocks) == 0, 0.0, gate_ref[...])
    fresh = 1.0 - gate_ref[...]

    @pl.when(n == 0)
    def _():
        state_ref[...] = jnp.zeros_like(state_ref)

    for start in range(0, sq.shape[0], step):
        rows = slice(start, start + step)
        s = nt(sq[rows], k) * scale
        p = jnp.exp2(s - jnp.max(s, axis=-1, keepdims=True))
        total = jnp.sum(p, axis=-1, keepdims=True)
        contrib = nn(p.astype(BF), v) / total
        o_ref[rows, :] = contrib
        state = gate * state_ref[rows, :] + fresh * contrib
        state_ref[rows, :] = state
        sum_ref[rows, :] = state.astype(BF)


def attend_kernel(
    place_ref, info_ref, q_ref, k_ref, v_ref, kp_ref, vp_ref, hk_ref, hv_ref,
    wk_ref, wko_ref, wv_ref, wvo_ref, contrib_ref, init_ref, inito_ref, lead_ref, power_ref,
    gate_ref, u_ref, o_ref, lse_ref, low_ref, moved_ref, bias_ref, state_ref, *, blocks,
):
    n = pl.program_id(1)
    first = lax.rem(n, blocks) == 0
    scale = HEAD_SIZE ** (-0.5) * LOG2E

    @pl.when(n == 0)
    def _():
        row = jnp.broadcast_to(u_ref[0], (BLOCK, u_ref.shape[-1]))
        bias_ref[...] = pltpu.roll(row, 0, 1, stride=1, stride_axis=0)[:, : 2 * BLOCK]

    has_previous = info_ref[n, 0] > 0
    reach = info_ref[n, 1]
    k = k_ref[...]
    v = v_ref[...]
    kp = jnp.where(first, hk_ref[...], kp_ref[...])
    vp = jnp.where(first, hv_ref[...], vp_ref[...])

    @pl.when(first)
    def _():
        init = merged(place_ref, init_ref, inito_ref).astype(F32)
        state_ref[...] = power_ref[...] * init + lead_ref[...].astype(F32)

    state = state_ref[...]
    contrib = contrib_ref[...]
    st = state.astype(BF)
    low_ref[...] = st
    moved_ref[...] = (state - contrib).astype(BF)
    state_ref[...] = contrib + gate_ref[...] * (state - contrib)
    sk = nn(st, merged(place_ref, wk_ref, wko_ref)).astype(BF)
    sv = nn(st, merged(place_ref, wv_ref, wvo_ref)).astype(BF)
    step = ROWS_FORWARD

    def run(with_previous):
        for start in range(0, BLOCK, step):
            q = q_ref[start : start + step, :]
            sc = nt(q, k) * scale + bias_ref[start : start + step, BLOCK:]
            row = lax.broadcasted_iota(jnp.int32, (step, 1), 0) + start
            column = lax.broadcasted_iota(jnp.int32, (step, BLOCK), 1)
            sc = jnp.where(column <= jnp.maximum(row, reach - 1), sc, MASKED)
            ss = nt(q, sk) * scale
            peak = jnp.maximum(
                jnp.max(sc, axis=-1, keepdims=True), jnp.max(ss, axis=-1, keepdims=True)
            )
            if with_previous:
                sp = nt(q, kp) * scale + bias_ref[start : start + step, :BLOCK]
                peak = jnp.maximum(peak, jnp.max(sp, axis=-1, keepdims=True))
            pc = jnp.exp2(sc - peak)
            ps = jnp.exp2(ss - peak)
            total = jnp.sum(pc, axis=-1, keepdims=True) + jnp.sum(ps, axis=-1, keepdims=True)
            out = nn(pc.astype(BF), v) + nn(ps.astype(BF), sv)
            if with_previous:
                pp = jnp.exp2(sp - peak)
                total = total + jnp.sum(pp, axis=-1, keepdims=True)
                out = out + nn(pp.astype(BF), vp)
            o_ref[start : start + step, :] = (out / total).astype(BF)
            lse = jnp.broadcast_to(peak + jnp.log2(total), (step, 128))
            lse_ref[0, 0, :, start : start + step] = lse.T[:1]

    @pl.when(has_previous)
    def _():
        run(True)

    @pl.when(jnp.logical_not(has_previous))
    def _():
        run(False)


def attend_back_kernel(
    place_ref, info_ref, q_ref, k_ref, v_ref, kp_ref, vp_ref, hk_ref, hv_ref,
    wk_ref, wko_ref, wv_ref, wvo_ref, st_ref, gate_ref, u_ref, do_ref, o_ref, lse_ref,
    dq_ref, dk_ref, dv_ref, dkp_ref, dvp_ref, direct_ref, gwk_ref, gwv_ref, gb_ref, total_ref,
    bias_ref, sum_ref, dq_acc, state_acc, *, blocks,
):
    step_at = pl.program_id(1)
    n = pl.num_programs(1) - 1 - step_at
    first = lax.rem(n, blocks) == 0
    gate = jnp.where(lax.rem(n, blocks) == blocks - 1, 0.0, gate_ref[...])
    factor = HEAD_SIZE ** (-0.5)
    scale = factor * LOG2E
    window = 2 * BLOCK
    width = BLOCK + window

    @pl.when(step_at == 0)
    def _():
        state_acc[...] = jnp.zeros_like(state_acc)
        row = jnp.broadcast_to(u_ref[0], (window, u_ref.shape[-1]))
        bias_ref[...] = pltpu.roll(row, 0, 1, stride=1, stride_axis=0)[:, :BLOCK]
        sum_ref[...] = jnp.zeros_like(sum_ref)
        gwk_ref[...] = jnp.zeros_like(gwk_ref)
        gwv_ref[...] = jnp.zeros_like(gwv_ref)

    has_previous = info_ref[n, 0] > 0
    reach = info_ref[n, 1]
    q = q_ref[...]
    do = do_ref[...]
    lse = lse_ref[0, 0]
    delta = jnp.sum((do.astype(F32) * o_ref[...].astype(F32)).T, axis=0, keepdims=True)
    step = KEYS_BACKWARD

    def part(key, value, start, bias_start, masked):
        s = nt(key, q) * scale
        if bias_start is not None:
            s = s + bias_ref[bias_start : bias_start + step, :]
        if masked:
            key_at = lax.broadcasted_iota(jnp.int32, (step, BLOCK), 0) + start
            query_at = lax.broadcasted_iota(jnp.int32, (1, BLOCK), 1)
            s = jnp.where(key_at <= jnp.maximum(query_at, reach - 1), s, MASKED)
        p = jnp.exp2(s - lse)
        dp = nt(value, do)
        ds = (p * (dp - delta)).astype(BF)
        if bias_start is not None:
            for block in range(0, step, 128):
                at = window - bias_start - block
                sum_ref[:, at : at + BLOCK] += ds[block : block + 128].astype(F32)
        dq_acc[...] += tn(ds, key)
        return nn(ds, q) * factor, nn(p.astype(BF), do)

    dq_acc[...] = jnp.zeros_like(dq_acc)
    st = st_ref[...]
    key_map = merged(place_ref, wk_ref, wko_ref)
    value_map = merged(place_ref, wv_ref, wvo_ref)
    sk = nn(st, key_map).astype(BF)
    sv = nn(st, value_map).astype(BF)
    for start in range(0, st.shape[0], step):
        rows = slice(start, start + step)
        dk, dv = part(sk[rows], sv[rows], start, None, False)
        dk = dk.astype(BF)
        dv = dv.astype(BF)
        direct = nt(dk, key_map) + nt(dv, value_map)
        direct_ref[rows, :] = direct
        state = direct + gate * state_acc[rows, :]
        state_acc[rows, :] = state
        total_ref[rows, :] = state.astype(BF)
        gwk_ref[0] += tn(st[rows], dk)
        gwv_ref[0] += tn(st[rows], dv)
    for start in range(0, BLOCK, step):
        rows = slice(start, start + step)
        dk, dv = part(k_ref[rows, :], v_ref[rows, :], start, BLOCK + start, True)
        dk_ref[rows, :] = dk
        dv_ref[rows, :] = dv

    @pl.when(has_previous)
    def _():
        for start in range(0, BLOCK, step):
            rows = slice(start, start + step)
            key = jnp.where(first, hk_ref[rows, :], kp_ref[rows, :])
            value = jnp.where(first, hv_ref[rows, :], vp_ref[rows, :])
            dk, dv = part(key, value, start, start, False)
            dkp_ref[rows, :] = dk.astype(BF)
            dvp_ref[rows, :] = dv.astype(BF)

    @pl.when(jnp.logical_not(has_previous))
    def _():
        dkp_ref[...] = jnp.zeros_like(dkp_ref)
        dvp_ref[...] = jnp.zeros_like(dvp_ref)

    dq_ref[...] = (dq_acc[...] * factor).astype(BF)

    @pl.when(n == 0)
    def _():
        folded = sum_ref[...]
        half = 64
        while half >= 8:
            folded = folded[:half] + pltpu.roll(folded[half:], width - half, 1)
            half //= 2
        total = folded[:1]
        for row in range(1, 8):
            total = total + pltpu.roll(folded[row : row + 1], width - row, 1)
        gb_ref[0] = total


def read_back_kernel(
    place_ref, sq_ref, sqo_ref, k_ref, v_ref, direct_ref, moved_ref, later_ref, gate_ref,
    dk_ref, dv_ref, nk_ref, nv_ref, rk_ref, rv_ref,
    gk_ref, gv_ref, gsq_ref, ginit_ref, ggate_ref, carried_ref, *, blocks,
):
    step_at = pl.program_id(1)
    n = pl.num_programs(1) - 1 - step_at
    last = lax.rem(n, blocks) == blocks - 1
    factor = HEAD_SIZE ** (-0.5)

    @pl.when(step_at == 0)
    def _():
        gsq_ref[...] = jnp.zeros_like(gsq_ref)
        ginit_ref[...] = jnp.zeros_like(ginit_ref)
        ggate_ref[...] = jnp.zeros_like(ggate_ref)

    @pl.when(last)
    def _():
        carried_ref[...] = later_ref[...].astype(F32)

    gate = gate_ref[...]
    carried = carried_ref[...]
    gc = ((1.0 - gate) * carried).astype(BF)
    change = jnp.sum(carried * moved_ref[...].astype(F32), axis=0, keepdims=True)
    ggate_ref[0] += change * (gate * (1.0 - gate))
    carried = direct_ref[...] + gate * carried
    carried_ref[...] = carried

    @pl.when((lax.rem(n, blocks) == 0) & (place_ref[0] == 0))
    def _():
        ginit_ref[...] += carried

    sq = merged(place_ref, sq_ref, sqo_ref)
    k = k_ref[...]
    s = nt(k, sq) * (factor * LOG2E)
    p = jnp.exp2(s - jnp.max(s, axis=0, keepdims=True))
    p = p * (1.0 / jnp.sum(p, axis=0, keepdims=True))
    dp = nt(v_ref[...], gc)
    ds = (p * (dp - jnp.sum(p * dp, axis=0, keepdims=True))).astype(BF)
    next_k = jnp.where(last, rk_ref[...], nk_ref[...]).astype(F32)
    next_v = jnp.where(last, rv_ref[...], nv_ref[...]).astype(F32)
    gk_ref[...] = (dk_ref[...] + next_k + nn(ds, sq) * factor).astype(BF)
    gv_ref[...] = (dv_ref[...] + next_v + nn(p.astype(BF), gc)).astype(BF)
    gsq_ref[...] += tn(ds, k) * factor


def pack_kernel(up_ref, down_ref, out_ref, packed_ref):
    hidden = up_ref.shape[1]
    packed_ref[:, :hidden] = up_ref[...]
    packed_ref[:, hidden : 2 * hidden] = down_ref[...].T
    packed_ref[:, 2 * hidden :] = out_ref[...].T


def unpack_kernel(packed_ref, up_ref, down_ref, out_ref):
    hidden = up_ref.shape[1]
    up_ref[...] = packed_ref[:, :hidden].astype(F32)
    down_ref[...] = packed_ref[:, hidden : 2 * hidden].astype(F32).T
    out_ref[...] = packed_ref[:, 2 * hidden :].astype(F32).T


def out_kernel(att_ref, wo_ref, tok_ref, gain_ref, mid_ref, min_ref):
    t = pl.program_id(0)
    part = nt(att_ref[...], flat(wo_ref))

    @pl.when(t == 0)
    def _():
        mid_ref[...] = joined(tok_ref) + part

    @pl.when(t > 0)
    def _():
        mid_ref[...] += part

    @pl.when(t == pl.num_programs(0) - 1)
    def _():
        x = mid_ref[...].astype(BF).astype(F32)
        min_ref[...] = (x * inverse_rms(x) * gain_ref[...]).astype(BF)


def mlp_kernel(
    place_ref, min_ref, cot_ref, mid_ref, gain_ref, wu_ref, wd_ref,
    out_ref, gmid_ref, ggain_ref, gw_ref,
    min_t, cot_t, out_acc, gm_acc, hidden_ref,
):
    tile = pl.program_id(0)
    which = pl.program_id(1)

    @pl.when((tile == 0) & (which == 0))
    def _():
        min_t[...] = min_ref[...].T
        cot_t[...] = cot_ref[...].T
        out_acc[...] = jnp.zeros_like(out_acc)
        gm_acc[...] = jnp.zeros_like(gm_acc)

    @pl.when(which == 0)
    def _():
        wu = flat(wu_ref)
        wd = flat(wd_ref)
        pre = nn(min_ref[...], wu)
        cdf = 0.5 + 0.5 * lax.erf(pre * (0.5**0.5))
        density = jnp.exp2(pre * pre * (-0.5 * LOG2E)) * ((2.0 * np.pi) ** -0.5)
        hidden_ref[...] = (pre * cdf).astype(BF)
        grad_pre = (nn(cot_ref[...], wd) * (cdf + pre * density)).astype(BF)
        out_acc[...] += nt(hidden_ref[...], wd)
        gm_acc[...] += nt(grad_pre, wu)
        grad = nn(min_t[...], grad_pre).astype(BF)
        gw_ref[...] = grad.reshape(gw_ref.shape)

    @pl.when(which == 1)
    def _():
        grad = nn(cot_t[...], hidden_ref[...]).astype(BF)
        gw_ref[...] = grad.reshape(gw_ref.shape)

    @pl.when((tile == pl.num_programs(0) - 1) & (which == 1))
    def _():
        mid = mid_ref[...]
        lanes = out_ref.shape[2]
        for part in range(out_ref.shape[0]):
            at = slice(part * lanes, (part + 1) * lanes)
            out_ref[part] = (mid[:, at] + out_acc[:, at]).astype(BF)
        x = mid.astype(BF).astype(F32)
        inverse = inverse_rms(x)
        normed = x * inverse
        gm = gm_acc[...]
        ggain_ref[...] = jnp.sum(gm * normed, axis=0, keepdims=True)
        scaled = gm * gain_ref[...]
        back = inverse * (scaled - normed * jnp.mean(scaled * normed, axis=-1, keepdims=True))
        gmid_ref[...] = (cot_ref[...].astype(F32) + back).astype(BF)


def out_back_kernel(gmid_ref, wo_ref, att_ref, late_ref, gatt_ref, gwo_ref, gmid_t):
    @pl.when(pl.program_id(0) == 0)
    def _():
        gmid_t[...] = gmid_ref[...].T

    gatt_ref[...] = nn(gmid_ref[...], flat(wo_ref)).astype(BF)
    gwo_ref[...] = nn(gmid_t[...], att_ref[...]).astype(BF).reshape(gwo_ref.shape)


def project_back_kernel(
    place_ref, tok_ref, gmid_ref, gain_ref, gq_ref, gk_ref, gv_ref,
    wq_ref, wqo_ref, wk_ref, wko_ref, wv_ref, wvo_ref, gsq_ref, ginit_ref, gmk_ref, gmv_ref,
    gtok_ref, ggain_ref, gown_ref, gother_ref, ain_t, acc_ref, pack_ref,
):
    t = pl.program_id(0)

    @pl.when(t == 0)
    def _():
        x = joined(tok_ref)
        ain_t[...] = (x * inverse_rms(x) * gain_ref[...]).astype(BF).T
        acc_ref[...] = jnp.zeros_like(acc_ref)

    groups, _, lanes = pack_ref.shape
    at = 0
    for g_ref, w_ref, w_other in (
        (gq_ref, wq_ref, wqo_ref), (gk_ref, wk_ref, wko_ref), (gv_ref, wv_ref, wvo_ref)
    ):
        g = g_ref[...]
        acc_ref[...] += nt(g, merged(place_ref, w_ref, w_other))
        grad = nn(ain_t[...], g).astype(BF)
        rows = grad.shape[0] // groups
        pack_ref[:, at : at + rows] = grad.reshape(groups, rows, lanes)
        at += rows
    for g_ref in (gsq_ref, ginit_ref):
        rows = g_ref.shape[0] // groups
        pack_ref[:, at : at + rows] = g_ref[...].astype(BF).reshape(groups, rows, lanes)
        at += rows
    for g_ref in (gmk_ref, gmv_ref):
        rows = HEAD_SIZE // groups
        for item in range(g_ref.shape[0]):
            where = slice(item * HEAD_SIZE, (item + 1) * HEAD_SIZE)
            pack_ref[:, at : at + rows, where] = g_ref[item].astype(BF).reshape(groups, rows, -1)
        at += rows
    pack_ref[:, at:] = jnp.zeros_like(pack_ref[:, at:])
    for index in range(groups // 2):
        gown_ref[0, index] = pack_ref[2 * index + place_ref[0]]
        gother_ref[0, index] = pack_ref[2 * index + 1 - place_ref[0]]

    @pl.when(t == pl.num_programs(0) - 1)
    def _():
        x = joined(tok_ref)
        inverse = inverse_rms(x)
        normed = x * inverse
        ga = acc_ref[...]
        ggain_ref[...] = jnp.sum(ga * normed, axis=0, keepdims=True)
        scaled = ga * gain_ref[...]
        back = inverse * (scaled - normed * jnp.mean(scaled * normed, axis=-1, keepdims=True))
        grad = (gmid_ref[...].astype(F32) + back).astype(BF)
        for part in range(gtok_ref.shape[0]):
            gtok_ref[part] = grad[:, part * lanes : (part + 1) * lanes]


def distance_bucket(distance):
    magnitude = np.abs(distance)
    scaled = np.log(np.maximum(magnitude, 1) / 8.0) / np.log(16.0) * 8.0
    far = np.minimum(8 + np.floor(np.maximum(scaled, 0.0)).astype(np.int32), 15)
    return (distance < 0).astype(np.int32) * 16 + np.where(magnitude < 8, magnitude, far)


def one_hot(distance, valid, bucket_count):
    hot = distance_bucket(distance)[:, None] == np.arange(bucket_count)[None, :]
    return jnp.asarray((hot & valid[:, None]).astype(np.float32))


def carry(value, power, axis, backward):
    count = lax.axis_size(axis)
    sign = -1 if backward else 1
    total = from_behind(value.astype(BF), axis, sign).astype(F32)
    step = 1
    while step < count - 1:
        moved = from_behind(total.astype(BF), axis, sign * step).astype(F32)
        total = total + power**step * moved
        step *= 2
    return total


def across(value, axis, bit):
    count = lax.axis_size(axis)
    return lax.ppermute(value, axis, [(source, source ^ bit) for source in range(count)])


def take(value, index, dim):
    return lax.dynamic_index_in_dim(value, index, dim, False)


def add_low(left, right):
    return (left.astype(F32) + right.astype(F32)).astype(BF)


def ordered(bit, own, other, dim):
    first = bit == 0
    return jnp.stack([jnp.where(first, own, other), jnp.where(first, other, own)], axis=dim)


def gather_pairs(item, beside):
    shards = lax.axis_size("tp")
    half = shards // 2
    tp = lax.axis_index("tp")
    x_bit = lax.axis_index("dp") % 2
    y_bit = lax.axis_index("dp") // 2
    parts = [item] + [across(item, "tp", k) for k in range(1, shards)]
    bit = 1
    while bit < shards:
        swap = (tp & bit) > 0
        parts = [jnp.where(swap, parts[k ^ bit], parts[k]) for k in range(shards)]
        bit *= 2
    low = jnp.stack(parts[:half])
    high = jnp.stack(parts[half:])
    low_x = across(low, "dp", 1)
    high_y = across(high, "dp", 2)
    low = ordered(x_bit, low, low_x, 0)
    high = ordered(y_bit, high, high_y, 0)
    low_y = across(low, "dp", 2)
    high_x = across(high, "dp", 1)
    low = ordered(y_bit, low, low_y, 0)
    high = ordered(x_bit, high, high_x, 1)
    own = jnp.stack([low, high]).reshape((2, 4, half) + item.shape)
    own, beside = lax.optimization_barrier((own, beside))
    return own, across(own, "ctx", 1), beside


def scatter_pairs(own, other):
    shards = own.shape[0]
    half = shards // 2
    tp = lax.axis_index("tp")
    x_bit = lax.axis_index("dp") % 2
    y_bit = lax.axis_index("dp") // 2
    grid = (shards, 2, 2) + own.shape[2:]
    moved = across(other, "ctx", 1).reshape(grid)
    own = own.reshape(grid)

    def both(part, index, dim):
        return add_low(take(own[part], index, dim), take(moved[part], index, dim))

    first, second = slice(0, half), slice(half, shards)
    low_moved = across(both(first, 1 - x_bit, 2), "dp", 1)
    high_moved = across(both(second, 1 - y_bit, 1), "dp", 2)
    low = add_low(both(first, x_bit, 2), low_moved)
    high = add_low(both(second, y_bit, 1), high_moved)
    low_moved = across(take(low, 1 - y_bit, 1), "dp", 2)
    high_moved = across(take(high, 1 - x_bit, 1), "dp", 1)
    low = add_low(take(low, y_bit, 1), low_moved)
    high = add_low(take(high, x_bit, 1), high_moved)
    kept = jnp.concatenate([low, high])
    total = take(kept, tp, 0).astype(F32)
    for k in range(1, shards):
        total = total + across(take(kept, tp ^ k, 0), "tp", k).astype(F32)
    return total


def sequence_body(
    tokens, cotangent, prefix, w_query, w_key, w_value, w_out, w_up, w_down,
    state_query, state_init, gain_attn, gain_mlp, bias_table, gate_bias, state_key, state_value,
):
    shards = lax.axis_size("tp")
    groups = lax.axis_size("dp") * lax.axis_size("ctx")
    pairs = lax.axis_size("dp")
    half = shards // 2
    everywhere = ("tp", "dp", "ctx")
    seq_count, length, shard_width = tokens.shape
    width = cotangent.shape[2]
    seqs = seq_count // shards
    blocks = length // BLOCK
    units = seqs * blocks
    rows = units * BLOCK
    local_heads = bias_table.shape[0]
    heads = local_heads * shards
    buckets = bias_table.shape[1] * groups
    own_rows = w_query.shape[0]
    own_slots = state_query.shape[0]
    slots = own_slots * groups
    hidden = w_up.shape[1]
    tp_index = lax.axis_index("tp")
    ctx_index = lax.axis_index("ctx")
    dp_index = lax.axis_index("dp")
    head = HEAD_SIZE
    map_rows = state_key.shape[1]
    place = jnp.stack([ctx_index, tp_index]).astype(jnp.int32)

    def call(kernel, grid, in_specs, out_specs, out_shape, scratch=(), prefetch=1, **more):
        return pl.pallas_call(
            kernel,
            grid_spec=pltpu.PrefetchScalarGridSpec(
                num_scalar_prefetch=prefetch, grid=grid, in_specs=in_specs, out_specs=out_specs,
                scratch_shapes=list(scratch),
            ),
            out_shape=out_shape,
            compiler_params=params(),
            **more,
        )

    vectors = (gain_attn, gain_mlp, gate_bias, bias_table)
    sizes = [item.size for item in vectors]
    tail = jnp.concatenate([item.reshape(-1) for item in vectors])
    tail = jnp.pad(tail, (0, 16 * shard_width - tail.size)).reshape(16, shard_width)

    def beside(item):
        return jnp.moveaxis(item, 0, 1).reshape(map_rows, shard_width)

    x = lax.all_to_all(tokens, "tp", 0, 0, tiled=True)
    first_own, first_other, x = gather_pairs(
        jnp.concatenate(
            [
                w_query, w_key, w_value, state_query, state_init,
                beside(state_key), beside(state_value), tail,
            ],
            axis=0,
        ),
        x,
    )
    x = x.reshape(shards, rows, shard_width)
    late_width = 2 * hidden + shard_width
    late = pl.pallas_call(
        pack_kernel, out_shape=jax.ShapeDtypeStruct((own_rows, late_width), BF)
    )(w_up, w_down, w_out)
    late, first_own = lax.optimization_barrier((late, first_own))
    late = lax.all_gather(late, everywhere, axis=0, tiled=True)
    late = late.reshape(shards, groups, own_rows, late_width)

    at_slots = 3 * own_rows
    at_init = at_slots + own_slots
    at_maps = at_init + own_slots
    at_vectors = at_maps + 2 * map_rows
    full_rows = at_vectors + 16
    small = ordered(
        ctx_index, first_own[:, :, :, at_vectors], first_other[:, :, :, at_vectors], 2
    )
    small = jnp.moveaxis(small, 3, 1).reshape(shards, groups, shard_width)
    ends = np.cumsum([0] + sizes)

    def spread(index):
        item = small[:, :, ends[index] : ends[index + 1]]
        item = item.reshape(shards, groups, local_heads, -1)
        return jnp.moveaxis(item, 1, 2).reshape(heads, -1).astype(F32)

    gain_one = spread(0).reshape(1, width)
    gain_two = spread(1).reshape(1, width)
    gate = jax.nn.sigmoid(spread(2)).reshape(1, width)
    bias_rows = spread(3)

    def whole(shape):
        return pl.BlockSpec(shape, lambda *_: (0,) * len(shape))

    def weight(index):
        spec = pl.BlockSpec(
            (1, pairs, 1, own_rows, shard_width), lambda t, *_: (t // half, 0, t % half, index, 0)
        )
        return [spec, spec]

    def of_head(count, index):
        def at(h, *_):
            t = h // local_heads
            return (t // half, 0, t % half, index, h % local_heads)

        spec = pl.BlockSpec((1, pairs, 1, count, head), at)
        return [spec, spec]

    column = pl.BlockSpec((rows, shard_width), lambda t, *_: (0, t))
    wide = jax.ShapeDtypeStruct((rows, width), BF)
    wide32 = jax.ShapeDtypeStruct((rows, width), F32)
    split = jax.ShapeDtypeStruct((shards, rows, shard_width), BF)
    queries, keys, values, _ = call(
        project_kernel,
        (shards,),
        [whole((shards, rows, shard_width)), whole((1, width))] + weight(0) + weight(1) + weight(2),
        [column, column, column, whole((rows, width))],
        [wide] * 4,
    )(place, x, gain_one, *([first_own, first_other] * 3))

    key_blocks = keys.reshape(seqs, blocks, BLOCK, width)
    value_blocks = values.reshape(seqs, blocks, BLOCK, width)
    halo_keys = from_behind(key_blocks[:, -1], "ctx", 1).reshape(seqs * BLOCK, width)
    halo_values = from_behind(value_blocks[:, -1], "ctx", 1).reshape(seqs * BLOCK, width)

    def along(rows_of, index):
        return pl.BlockSpec((rows_of, head), lambda h, n, *_: (index(n), h))

    def turned(n):
        return units - 1 - n

    query_slots = of_head(own_slots, at_slots // own_slots)
    init_slots = of_head(own_slots, at_init // own_slots)
    key_maps = of_head(map_rows, at_maps // map_rows)
    value_maps = of_head(map_rows, at_maps // map_rows + 1)
    channel = pl.BlockSpec((1, head), lambda h, n, *_: (0, h))
    slot_rows = units * slots
    slot_f32 = jax.ShapeDtypeStruct((slot_rows, width), F32)
    slot_low = jax.ShapeDtypeStruct((slot_rows, width), BF)
    message = jax.ShapeDtypeStruct((seqs * slots, width), BF)
    slot_scratch = pltpu.VMEM((slots, head), F32)
    own = along(BLOCK, lambda n: n)
    slot = along(slots, lambda n: n)
    slot_of_seq = along(slots, lambda n: n // blocks)
    contrib, accumulated = call(
        functools.partial(read_kernel, blocks=blocks),
        (heads, units),
        query_slots + [own, own, channel],
        [slot, slot_of_seq],
        [slot_f32, message],
        [slot_scratch],
    )(place, first_own, first_other, keys, values, gate)
    power = gate**blocks
    lead = carry(accumulated, power, "ctx", False)
    lead_power = jnp.ones_like(gate)
    for step in range(lax.axis_size("ctx") - 1):
        lead_power = jnp.where(ctx_index > step, lead_power * power, lead_power)

    block_at = ctx_index * blocks + jnp.arange(blocks, dtype=jnp.int32)
    own_prefix = lax.dynamic_slice_in_dim(prefix, tp_index * seqs, seqs, 0)
    info = jnp.stack(
        [
            jnp.broadcast_to(block_at[None], (seqs, blocks)),
            own_prefix[:, None] - block_at[None] * BLOCK,
        ],
        axis=-1,
    ).reshape(units, 2)
    span = 4 * BLOCK
    offset = np.arange(span)
    offset = np.where(offset < 2 * BLOCK, offset, offset - span)
    forward_hot = one_hot(BLOCK - offset, offset > -BLOCK, buckets)
    back_span = 3 * BLOCK
    back_offset = np.arange(back_span)
    back_offset = np.where(back_offset < BLOCK, back_offset, back_offset - back_span)
    backward_hot = one_hot(BLOCK + back_offset, back_offset > -2 * BLOCK, buckets)
    exact = lax.Precision.HIGHEST
    scaled_bias = bias_rows * LOG2E
    forward_bias = jnp.dot(scaled_bias, forward_hot.T, precision=exact)[:, None]
    backward_bias = jnp.dot(scaled_bias, backward_hot.T, precision=exact)[:, None]

    def attend_specs(index):
        before = along(BLOCK, lambda n: jnp.maximum(index(n) - 1, 0))
        by_seq = along(BLOCK, lambda n: index(n) // blocks)
        here = along(BLOCK, index)
        return [here, here, here, before, before, by_seq, by_seq] + key_maps + value_maps

    def lse_spec(index):
        return pl.BlockSpec((1, 1, 1, BLOCK), lambda h, n, *_: (index(n), h, 0, 0))

    def vector(size):
        return pl.BlockSpec((1, 1, size), lambda h, *_: (h, 0, 0))

    attend_args = (
        place, info, queries, keys, values, keys, values, halo_keys, halo_values,
        first_own, first_other, first_own, first_other,
    )
    attended, lse, states, moved = call(
        functools.partial(attend_kernel, blocks=blocks),
        (heads, units),
        attend_specs(lambda n: n)
        + [slot] + init_slots + [slot_of_seq, channel, channel, vector(span)],
        [own, lse_spec(lambda n: n), slot, slot],
        [wide, jax.ShapeDtypeStruct((units, heads, 1, BLOCK), F32), slot_low, slot_low],
        [pltpu.VMEM((BLOCK, 2 * BLOCK), F32), slot_scratch],
        2,
    )(*attend_args, contrib, first_own, first_other, lead, lead_power, gate, forward_bias)

    out_weight = pl.BlockSpec(
        (1, groups, own_rows, shard_width), lambda t, *_: (t, 0, 0, 2 * hidden // shard_width)
    )
    middle, mlp_in = pl.pallas_call(
        out_kernel,
        grid=(shards,),
        in_specs=[column, out_weight, whole((shards, rows, shard_width)), whole((1, width))],
        out_specs=[whole((rows, width)), whole((rows, width))],
        out_shape=[wide32, wide],
        compiler_params=params(),
    )(attended, late, x, gain_two)

    tile = 512
    per_shard = hidden // tile
    tile_block = (1, groups, own_rows, tile)
    output, middle_grad, gain_two_grad, late_grad = call(
        mlp_kernel,
        (shards * per_shard, 2),
        [
            whole((rows, width)),
            pl.BlockSpec((rows, width), lambda i, j, place_ref: (place_ref[1], 0)),
            whole((rows, width)), whole((1, width)),
            pl.BlockSpec(tile_block, lambda i, j, *_: (i // per_shard, 0, 0, i % per_shard)),
            pl.BlockSpec(
                tile_block, lambda i, j, *_: (i // per_shard, 0, 0, per_shard + i % per_shard)
            ),
        ],
        [
            whole((shards, rows, shard_width)), whole((rows, width)), whole((1, width)),
            pl.BlockSpec(
                tile_block, lambda i, j, *_: (i // per_shard, 0, 0, j * per_shard + i % per_shard)
            ),
        ],
        [
            split, wide, jax.ShapeDtypeStruct((1, width), F32),
            jax.ShapeDtypeStruct((shards, groups, own_rows, late_width), BF),
        ],
        [
            pltpu.VMEM((width, rows), BF), pltpu.VMEM((width, rows), BF),
            pltpu.VMEM((rows, width), F32), pltpu.VMEM((rows, width), F32),
            pltpu.VMEM((rows, tile), BF),
        ],
    )(
        place, mlp_in, cotangent.reshape(seq_count * length, width), middle, gain_two, late, late
    )
    output = lax.all_to_all(output, "tp", 0, 0, tiled=True)

    grad_attended, late_grad = pl.pallas_call(
        out_back_kernel,
        grid=(shards,),
        in_specs=[
            whole((rows, width)), out_weight, column, pl.BlockSpec(memory_space=pl.ANY)
        ],
        out_specs=[column, out_weight],
        out_shape=[wide, jax.ShapeDtypeStruct(late_grad.shape, BF)],
        scratch_shapes=[pltpu.VMEM((width, rows), BF)],
        compiler_params=params(),
        input_output_aliases={3: 1},
    )(middle_grad, late, attended, late_grad)
    late_grad = lax.psum_scatter(
        late_grad.reshape(shards * groups * own_rows, late_width), everywhere,
        scatter_dimension=0, tiled=True,
    )
    up_grad, down_grad, out_grad = pl.pallas_call(
        unpack_kernel,
        out_shape=[
            jax.ShapeDtypeStruct(w_up.shape, F32), jax.ShapeDtypeStruct(w_down.shape, F32),
            jax.ShapeDtypeStruct(w_out.shape, F32),
        ],
    )(late_grad)

    head_sum = jax.ShapeDtypeStruct((heads, head, head), F32)
    head_map = pl.BlockSpec((1, head, head), lambda h, n, *_: (h, 0, 0))
    back_own = along(BLOCK, turned)
    back_slot = along(slots, turned)
    back_of_seq = along(slots, lambda n: turned(n) // blocks)
    (
        grad_queries, dk, dv, dk_before, dv_before, direct, key_map_grad, value_map_grad,
        bias_sum, gathered,
    ) = call(
        functools.partial(attend_back_kernel, blocks=blocks),
        (heads, units),
        attend_specs(turned)
        + [back_slot, channel, vector(back_span), back_own, back_own, lse_spec(turned)],
        [back_own] * 5 + [back_slot, head_map, head_map, vector(back_span), back_of_seq],
        [
            wide, wide32, wide32, wide, wide, slot_f32, head_sum, head_sum,
            jax.ShapeDtypeStruct((heads, 1, back_span), F32), message,
        ],
        [
            pltpu.VMEM((2 * BLOCK, BLOCK), F32), pltpu.VMEM((128, back_span), F32),
            pltpu.VMEM((BLOCK, head), F32), slot_scratch,
        ],
        2,
    )(*attend_args, states, gate, backward_bias, grad_attended, attended, lse)
    dk, output = lax.optimization_barrier((dk, output))
    sum_at = np.arange(back_span) - BLOCK
    sum_hot = one_hot(sum_at, sum_at > -BLOCK, buckets)
    bias_grad = jnp.dot(bias_sum[:, 0], sum_hot, precision=exact)

    later = carry(gathered, power, "ctx", True)
    first_keys = dk_before.reshape(seqs, blocks, BLOCK, width)[:, 0]
    first_values = dv_before.reshape(seqs, blocks, BLOCK, width)[:, 0]
    back_keys = from_behind(first_keys, "ctx", -1).reshape(seqs * BLOCK, width)
    back_values = from_behind(first_values, "ctx", -1).reshape(seqs * BLOCK, width)
    following = along(BLOCK, lambda n: jnp.minimum(turned(n) + 1, units - 1))
    key_of_seq = along(BLOCK, lambda n: turned(n) // blocks)
    kept_slot = pl.BlockSpec((slots, head), lambda h, n, *_: (0, h))
    slot_sum = jax.ShapeDtypeStruct((slots, width), F32)
    grad_keys, grad_values, slot_query_grad, init_grad, gate_grad = call(
        functools.partial(read_back_kernel, blocks=blocks),
        (heads, units),
        query_slots
        + [back_own, back_own, back_slot, back_slot, back_of_seq, channel]
        + [back_own, back_own, following, following, key_of_seq, key_of_seq],
        [back_own, back_own, kept_slot, kept_slot, vector(head)],
        [wide, wide, slot_sum, slot_sum, jax.ShapeDtypeStruct((heads, 1, head), F32)],
        [slot_scratch],
    )(
        place, first_own, first_other, keys, values, direct, moved, later, gate,
        dk, dv, dk_before, dv_before, back_keys, back_values,
    )

    maps_of = pl.BlockSpec((local_heads, head, head), lambda t, *_: (t, 0, 0))
    slots_of = pl.BlockSpec((slots, shard_width), lambda t, *_: (0, t))
    piece = pl.BlockSpec((1, pairs, full_rows, shard_width), lambda t, *_: (t, 0, 0, 0))
    pieces = jax.ShapeDtypeStruct((shards, pairs, full_rows, shard_width), BF)
    token_grad, gain_one_grad, grad_own, grad_other = call(
        project_back_kernel,
        (shards,),
        [whole((shards, rows, shard_width)), whole((rows, width)), whole((1, width))]
        + [column, column, column]
        + weight(0) + weight(1) + weight(2) + [slots_of, slots_of, maps_of, maps_of],
        [whole((shards, rows, shard_width)), whole((1, width)), piece, piece],
        [split, jax.ShapeDtypeStruct((1, width), F32), pieces, pieces],
        [
            pltpu.VMEM((width, rows), BF), pltpu.VMEM((rows, width), F32),
            pltpu.VMEM((groups, full_rows, shard_width), BF),
        ],
    )(
        place, x, middle_grad, gain_one, grad_queries, grad_keys, grad_values,
        *([first_own, first_other] * 3), slot_query_grad, init_grad, key_map_grad, value_map_grad,
    )
    token_grad = lax.all_to_all(token_grad, "tp", 0, 0, tiled=True)

    vector_sums = [gain_one_grad, gain_two_grad, gate_grad.reshape(1, width), bias_grad]
    vector_rows = jnp.concatenate([item.reshape(-1) for item in vector_sums])
    vector_rows = jnp.pad(vector_rows, (0, 16 * shard_width - vector_rows.size)).astype(BF)
    vector_rows = jnp.broadcast_to(
        vector_rows.reshape(1, 1, 16, shard_width), (shards, pairs, 16, shard_width)
    )
    grad_own = lax.dynamic_update_slice(grad_own, vector_rows, (0, 0, at_vectors, 0))
    grad_other = lax.dynamic_update_slice(grad_other, vector_rows, (0, 0, at_vectors, 0))
    grads = scatter_pairs(grad_own, grad_other)
    vector_grads = grads[at_vectors:].reshape(-1)
    group = dp_index * lax.axis_size("ctx") + ctx_index

    def own_part(index, like):
        begin = sum(item.size for item in vector_sums[:index])
        item = vector_grads[begin : begin + vector_sums[index].size].reshape(heads, -1)
        return lax.dynamic_slice(
            item, (tp_index * local_heads, group * like.shape[1]), like.shape
        )

    def apart(item):
        return jnp.moveaxis(item.reshape(map_rows, local_heads, head), 1, 0)

    return (
        output.reshape(seq_count, length, shard_width),
        token_grad.reshape(seq_count, length, shard_width),
        grads[:own_rows],
        grads[own_rows : 2 * own_rows],
        grads[2 * own_rows : at_slots],
        out_grad,
        up_grad,
        down_grad,
        grads[at_slots:at_init],
        grads[at_init:at_maps],
        own_part(0, gain_attn),
        own_part(1, gain_mlp),
        own_part(3, bias_table),
        own_part(2, gate_bias),
        apart(grads[at_maps : at_maps + map_rows]),
        apart(grads[at_maps + map_rows : at_vectors]),
    )


def choose(tokens, *others):
    shards = lax.axis_size("tp")
    even = tokens.shape[0] % shards == 0 and shards % 2 == 0 and shards & (shards - 1) == 0
    even = even and lax.axis_size("dp") == 4 and lax.axis_size("ctx") == 2
    return (sequence_body if even else body)(tokens, *others)


def solution(mesh):
    in_specs = (
        P("dp", "ctx", "tp"),
        P("dp", "ctx", None),
        P("dp"),
        P(("dp", "ctx"), "tp"),
        P(("dp", "ctx"), "tp"),
        P(("dp", "ctx"), "tp"),
        P("tp", ("dp", "ctx")),
        P(("dp", "ctx"), "tp"),
        P("tp", ("dp", "ctx")),
        P(("dp", "ctx"), "tp"),
        P(("dp", "ctx"), "tp"),
        P("tp", ("dp", "ctx")),
        P("tp", ("dp", "ctx")),
        P("tp", ("dp", "ctx")),
        P("tp", ("dp", "ctx")),
        P("tp", ("dp", "ctx"), None),
        P("tp", ("dp", "ctx"), None),
    )
    out_specs = (
        P("dp", "ctx", "tp"),
        P("dp", "ctx", "tp"),
        P(("dp", "ctx"), "tp"),
        P(("dp", "ctx"), "tp"),
        P(("dp", "ctx"), "tp"),
        P("tp", ("dp", "ctx")),
        P(("dp", "ctx"), "tp"),
        P("tp", ("dp", "ctx")),
        P(("dp", "ctx"), "tp"),
        P(("dp", "ctx"), "tp"),
        P("tp", ("dp", "ctx")),
        P("tp", ("dp", "ctx")),
        P("tp", ("dp", "ctx")),
        P("tp", ("dp", "ctx")),
        P("tp", ("dp", "ctx"), None),
        P("tp", ("dp", "ctx"), None),
    )
    return jax.shard_map(choose, mesh=mesh, in_specs=in_specs, out_specs=out_specs, check_vma=False)
```

```python
import functools

import jax
import jax.numpy as jnp
import numpy as np
from jax import lax
from jax.experimental import pallas as pl
from jax.experimental.pallas import tpu as pltpu
from jax.sharding import PartitionSpec as P

HEAD_SIZE = 128
BLOCK = 512


EPSILON = 1e-06
MASKED = -1e30
ROWS_FORWARD = 128
KEYS_BACKWARD = 256


def from_behind(value, axis, steps):
    count = lax.axis_size(axis)
    first, last = (max(0, -steps), min(count, count - steps))
    return lax.ppermute(value, axis, [(source, source + steps) for source in range(first, last)])


def prefix_2(array, axis, join, neutral, backward):
    count = lax.axis_size(axis)
    place = lax.axis_index(axis)
    ahead = count - 1 - place if backward else place
    gathered = jax.tree.map(
        lambda a, kind: lax.all_gather(a.astype(kind), axis), array, (jnp.bfloat16, jnp.bfloat16)
    )
    state = jax.tree.map(lambda a, e: jnp.zeros_like(a) + jnp.asarray(e, a.dtype), array, neutral)

    def one(hop, state):
        source = count - 1 - hop if backward else hop
        return join(
            state,
            jax.tree.map(
                lambda a, own: lax.dynamic_index_in_dim(a, source, 0, False).astype(own.dtype),
                gathered,
                array,
            ),
        )

    return lax.fori_loop(0, ahead, one, state)


def bucket_index(block_size):
    query_pos = np.arange(block_size)[:, None] + block_size
    key_pos = np.arange(2 * block_size)[None, :]
    distance = query_pos - key_pos
    upper_part = (distance < 0).astype(np.int32) * 16
    magnitude = np.abs(distance)
    scaled = np.log(np.maximum(magnitude, 1) / 8.0) / np.log(16.0) * 8.0
    far_bucket = np.minimum(8 + np.floor(np.maximum(scaled, 0.0)).astype(np.int32), 15)
    return (upper_part + np.where(magnitude < 8, magnitude, far_bucket)).astype(np.int32)


def norm_forward(features, gain_vector):
    inverse = lax.rsqrt(jnp.mean(features * features, axis=-1, keepdims=True) + EPSILON)
    normed = features * inverse
    return (normed, inverse, (normed * gain_vector).astype(jnp.bfloat16))


def norm_backward(grad_normed, normed, inverse, gain_vector):
    scaled = grad_normed * gain_vector
    grad_in = inverse * (scaled - normed * jnp.mean(scaled * normed, axis=-1, keepdims=True))
    return (grad_in, jnp.sum(grad_normed * normed, axis=0))


def compose(earlier, later_pair):
    return (earlier[0] * later_pair[0], later_pair[0] * earlier[1] + later_pair[1])


def bias_matrix(bias_rows, bucket):
    summed = jnp.zeros((bias_rows.shape[0],) + bucket.shape, jnp.float32)
    for number in range(bias_rows.shape[1]):
        summed = (
            summed
            + bias_rows[:, number][:, None, None] * (bucket == number).astype(jnp.float32)[None]
        )
    return summed


def bias_gradient(grad_matrix, bucket, bucket_count):
    columns = [
        jnp.sum(grad_matrix * (bucket == number).astype(jnp.float32)[None], axis=(1, 2))
        for number in range(bucket_count)
    ]
    return jnp.stack(columns, axis=1)


def body(
    tokens,
    cotangent,
    prefix,
    w_query,
    w_key,
    w_value,
    w_out,
    w_up,
    w_down,
    state_query,
    state_init,
    gain_attn,
    gain_mlp,
    bias_table,
    gate_bias,
    state_key,
    state_value,
):
    (
        query_full,
        key_full,
        value_full,
        out_full,
        up_full,
        down_full,
        squery_full,
        sinit_full,
        gain_one,
        gain_two,
        bias_rows,
        gate_rows,
        state_key_complete,
        svalue_full,
    ) = (
        lax.all_gather(w_query, ("dp", "ctx"), axis=0, tiled=True),
        lax.all_gather(w_key, ("dp", "ctx"), axis=0, tiled=True),
        lax.all_gather(w_value, ("dp", "ctx"), axis=0, tiled=True),
        lax.all_gather(w_out, ("dp", "ctx"), axis=1, tiled=True),
        lax.all_gather(w_up, ("dp", "ctx"), axis=0, tiled=True),
        lax.all_gather(w_down, ("dp", "ctx"), axis=1, tiled=True),
        lax.all_gather(state_query, ("dp", "ctx"), axis=0, tiled=True),
        lax.all_gather(state_init, ("dp", "ctx"), axis=0, tiled=True),
        lax.all_gather(gain_attn, ("dp", "ctx"), axis=1, tiled=True),
        lax.all_gather(gain_mlp, ("dp", "ctx"), axis=1, tiled=True),
        lax.all_gather(bias_table, ("dp", "ctx"), axis=1, tiled=True),
        lax.all_gather(gate_bias, ("dp", "ctx"), axis=1, tiled=True),
        lax.all_gather(state_key, ("dp", "ctx"), axis=1, tiled=True),
        lax.all_gather(state_value, ("dp", "ctx"), axis=1, tiled=True),
    )
    seq_count = tokens.shape[0]
    length = tokens.shape[1]
    shard_width = tokens.shape[2]
    full_width = cotangent.shape[2]
    block_count = length // BLOCK
    row_count = seq_count * length
    local_head_count = bias_rows.shape[0]
    local_width = local_head_count * HEAD_SIZE
    state_slot_count = squery_full.shape[0]
    scores_scale = HEAD_SIZE ** (-0.5)
    local_shape = (seq_count, block_count, BLOCK, local_head_count, HEAD_SIZE)
    element_count = seq_count * block_count
    token_full, gain_one_full = (
        lax.all_gather(tokens, "tp", axis=2, tiled=True),
        lax.all_gather(gain_one, "tp", axis=0, tiled=True),
    )
    gain_one_vec = gain_one_full.reshape(full_width).astype(jnp.float32)
    normed_one, inverse_one, attn_in = norm_forward(
        token_full.reshape(row_count, full_width).astype(jnp.float32), gain_one_vec
    )
    queries = (
        jnp.dot(attn_in, query_full, preferred_element_type=jnp.float32)
        .astype(jnp.bfloat16)
        .reshape(local_shape)
    )
    key_rows = (
        jnp.dot(attn_in, key_full, preferred_element_type=jnp.float32)
        .astype(jnp.bfloat16)
        .reshape(local_shape)
    )
    value_rows = (
        jnp.dot(attn_in, value_full, preferred_element_type=jnp.float32)
        .astype(jnp.bfloat16)
        .reshape(local_shape)
    )
    last_keys, last_values = from_behind((key_rows[:, -1], value_rows[:, -1]), "ctx", 1)
    window_keys = jnp.concatenate(
        [jnp.concatenate([last_keys[:, None], key_rows[:, :-1]], 1), key_rows], 2
    )
    window_values = jnp.concatenate(
        [jnp.concatenate([last_values[:, None], value_rows[:, :-1]], 1), value_rows], 2
    )
    query_heads = squery_full.reshape(state_slot_count, local_head_count, HEAD_SIZE)
    read_scores = (
        jnp.einsum("mhe,sbthe->sbhmt", query_heads, key_rows, preferred_element_type=jnp.float32)
        * scores_scale
    )
    read_peak = jnp.max(read_scores, axis=-1, keepdims=True)
    read_raised = jnp.exp(read_scores - read_peak)
    read_probs = read_raised / jnp.sum(read_raised, axis=-1, keepdims=True)
    read_low = read_probs.astype(jnp.bfloat16)
    contrib = jnp.einsum(
        "sbhmt,sbthe->sbmhe", read_low, value_rows, preferred_element_type=jnp.float32
    )
    contrib = contrib.reshape(seq_count, block_count, state_slot_count, local_width)
    gate_value = jax.nn.sigmoid(gate_rows.reshape(local_width).astype(jnp.float32))
    gate_power = jnp.ones((local_width,), jnp.float32)
    accumulated = jnp.zeros((seq_count, state_slot_count, local_width), jnp.float32)
    for block_index in range(block_count):
        accumulated = gate_value * accumulated + (1.0 - gate_value) * contrib[:, block_index]
        gate_power = gate_power * gate_value
    identity = (jnp.ones((local_width,), jnp.float32), jnp.zeros_like(accumulated))
    lead_power, lead_state = prefix_2((gate_power, accumulated), "ctx", compose, identity, False)
    entry_state = lead_power * sinit_full.astype(jnp.float32) + lead_state
    state_list = [entry_state]
    block_index = 0
    state_list.append(gate_value * state_list[-1] + (1.0 - gate_value) * contrib[:, block_index])
    stacked = jnp.stack(state_list, axis=1)
    state_reduced = stacked.astype(jnp.bfloat16).reshape(
        seq_count, block_count, state_slot_count, local_head_count, HEAD_SIZE
    )
    state_key_rows = jnp.einsum(
        "cazqr,qrx->cazqx", state_reduced, state_key_complete, preferred_element_type=jnp.float32
    ).astype(jnp.bfloat16)
    state_values = jnp.einsum(
        "cazqr,qrx->cazqx", state_reduced, svalue_full, preferred_element_type=jnp.float32
    ).astype(jnp.bfloat16)
    bucket = jnp.asarray(bucket_index(BLOCK))
    bias_full = bias_matrix(bias_rows.astype(jnp.float32), bucket)
    block_ids = lax.axis_index("ctx") * block_count + jnp.arange(block_count, dtype=jnp.int32)
    query_pos = block_ids[:, None] * BLOCK + jnp.arange(BLOCK, dtype=jnp.int32)[None, :]
    key_pos = (block_ids[:, None] - 1) * BLOCK + jnp.arange(2 * BLOCK, dtype=jnp.int32)[None, :]
    causal = (key_pos[:, None, :] >= 0) & (key_pos[:, None, :] <= query_pos[:, :, None])
    in_prefix = (key_pos[None, :, None, :] >= 0) & (
        key_pos[None, :, None, :] < prefix[:, None, None, None]
    )
    permitted_mask = (causal[None] | in_prefix).reshape(element_count, 1, BLOCK, 2 * BLOCK)
    flattened_queries = queries.reshape(element_count, BLOCK, local_head_count, HEAD_SIZE)
    flattened_window_keys = window_keys.reshape(
        element_count, 2 * BLOCK, local_head_count, HEAD_SIZE
    )
    flattened_window_values = window_values.reshape(
        element_count, 2 * BLOCK, local_head_count, HEAD_SIZE
    )
    flattened_state_keys = state_key_rows.reshape(
        element_count, state_slot_count, local_head_count, HEAD_SIZE
    )
    flattened_state_values = state_values.reshape(
        element_count, state_slot_count, local_head_count, HEAD_SIZE
    )

    def block_score_rows(
        block_query_rows, block_window_key_rows, block_state_key_rows, block_permitted_mask
    ):
        window_part = (
            jnp.einsum(
                "ihe,jhe->hij",
                block_query_rows,
                block_window_key_rows,
                preferred_element_type=jnp.float32,
            )
            * scores_scale
            + bias_full
        )
        state_part = (
            jnp.einsum(
                "yat,zat->ayz",
                block_query_rows,
                block_state_key_rows,
                preferred_element_type=jnp.float32,
            )
            * scores_scale
        )
        return (jnp.where(block_permitted_mask, window_part, MASKED), state_part)

    def attend_one_block(element_entry):
        (
            block_query_rows,
            block_window_key_rows,
            block_window_value_rows,
            block_state_key_rows,
            block_state_value_rows,
            block_permitted_mask,
        ) = element_entry
        window_scores, scores_of_state = block_score_rows(
            block_query_rows, block_window_key_rows, block_state_key_rows, block_permitted_mask
        )
        row_peak = jnp.maximum(jnp.max(window_scores, axis=-1), jnp.max(scores_of_state, axis=-1))
        window_raised = jnp.exp(window_scores - row_peak[..., None])
        state_raised = jnp.exp(scores_of_state - row_peak[..., None])
        denominator = jnp.sum(window_raised, axis=-1) + jnp.sum(state_raised, axis=-1)
        log_total = row_peak + jnp.log(denominator)
        window_probs = (window_raised / denominator[..., None]).astype(jnp.bfloat16)
        state_probs = (state_raised / denominator[..., None]).astype(jnp.bfloat16)
        block_out = jnp.einsum(
            "hij,jhe->ihe",
            window_probs,
            block_window_value_rows,
            preferred_element_type=jnp.float32,
        ) + jnp.einsum(
            "wyd,dwg->ywg", state_probs, block_state_value_rows, preferred_element_type=jnp.float32
        )
        return (block_out.astype(jnp.bfloat16), log_total)

    attended_blocks, log_totals = lax.map(
        attend_one_block,
        (
            flattened_queries,
            flattened_window_keys,
            flattened_window_values,
            flattened_state_keys,
            flattened_state_values,
            permitted_mask,
        ),
    )
    attended = attended_blocks.reshape(row_count, local_width)
    attn_part = jnp.dot(attended, out_full, preferred_element_type=jnp.float32).reshape(
        seq_count, length, full_width
    )
    attn_share = lax.psum_scatter(
        attn_part.astype(jnp.bfloat16), "tp", scatter_dimension=2, tiled=True
    ).astype(jnp.float32)
    middle = tokens.astype(jnp.float32) + attn_share
    middle_full, gain_two_full = (
        lax.all_gather(middle.astype(jnp.bfloat16), "tp", axis=2, tiled=True),
        lax.all_gather(gain_two, "tp", axis=0, tiled=True),
    )
    gain_two_vec = gain_two_full.reshape(full_width).astype(jnp.float32)
    normed_two, inverse_two, mlp_in = norm_forward(
        middle_full.reshape(row_count, full_width).astype(jnp.float32), gain_two_vec
    )
    hidden_pre = jnp.dot(mlp_in, up_full, preferred_element_type=jnp.float32)
    hidden = jax.nn.gelu(hidden_pre, approximate=False).astype(jnp.bfloat16)
    mlp_part = jnp.dot(hidden, down_full, preferred_element_type=jnp.float32).reshape(
        seq_count, length, full_width
    )
    mlp_share = lax.psum_scatter(
        mlp_part.astype(jnp.bfloat16), "tp", scatter_dimension=2, tiled=True
    ).astype(jnp.float32)
    output = (middle + mlp_share).astype(jnp.bfloat16)
    grad_out = cotangent.reshape(row_count, full_width)
    grad_hidden = jnp.dot(grad_out, down_full.T, preferred_element_type=jnp.float32)
    grad_down = jnp.dot(hidden.T, grad_out, preferred_element_type=jnp.float32)

    def gelu_exact(pre_values):
        return jax.nn.gelu(pre_values, approximate=False)

    gelu_value, gelu_back = jax.vjp(gelu_exact, hidden_pre)
    grad_pre = gelu_back(grad_hidden)[0].astype(jnp.bfloat16)
    grad_up = jnp.dot(mlp_in.T, grad_pre, preferred_element_type=jnp.float32)
    grad_mlp_in = jnp.dot(grad_pre, up_full.T, preferred_element_type=jnp.float32)
    part_middle, part_gain_two = norm_backward(grad_mlp_in, normed_two, inverse_two, gain_two_vec)
    tp_index = lax.axis_index("tp")
    head_total = full_width // HEAD_SIZE
    summed, gain_two_sum = (
        lax.psum(
            part_middle.reshape(seq_count, length, full_width).astype(jnp.bfloat16), "tp"
        ).astype(jnp.float32),
        lax.psum(part_gain_two.reshape(head_total, HEAD_SIZE).astype(jnp.bfloat16), "tp").astype(
            jnp.float32
        ),
    )
    middle_grad_full = cotangent.astype(jnp.float32) + summed
    middle_grad = lax.dynamic_slice_in_dim(middle_grad_full, tp_index * shard_width, shard_width, 2)
    grad_gain_two = lax.dynamic_slice_in_dim(
        gain_two_sum, tp_index * local_head_count, local_head_count, 0
    )
    middle_grad_low = middle_grad_full.astype(jnp.bfloat16)
    middle_grad_rows = middle_grad_low.reshape(row_count, full_width)
    grad_attended = jnp.dot(
        middle_grad_rows, out_full.T, preferred_element_type=jnp.float32
    ).astype(jnp.bfloat16)
    grad_attended = grad_attended.reshape(element_count, BLOCK, local_head_count, HEAD_SIZE)
    grad_wout = jnp.dot(attended.T, middle_grad_rows, preferred_element_type=jnp.float32)

    def attend_back(bias_sum, element_entry):
        (
            block_query_rows,
            block_window_key_rows,
            block_window_value_rows,
            block_state_key_rows,
            block_state_value_rows,
            block_permitted_mask,
            block_lse,
            block_grad,
        ) = element_entry
        window_again, state_again = block_score_rows(
            block_query_rows, block_window_key_rows, block_state_key_rows, block_permitted_mask
        )
        window_exact = jnp.exp(window_again - block_lse[..., None])
        state_exact = jnp.exp(state_again - block_lse[..., None])
        grad_wprob = jnp.einsum(
            "ihe,jhe->hij", block_grad, block_window_value_rows, preferred_element_type=jnp.float32
        )
        grad_sprob = jnp.einsum(
            "yat,zat->ayz", block_grad, block_state_value_rows, preferred_element_type=jnp.float32
        )
        row_delta = jnp.sum(window_exact * grad_wprob, axis=-1) + jnp.sum(
            state_exact * grad_sprob, axis=-1
        )
        grad_wscore = (window_exact * (grad_wprob - row_delta[..., None])).astype(jnp.bfloat16)
        state_score_gradient = (state_exact * (grad_sprob - row_delta[..., None])).astype(
            jnp.bfloat16
        )
        block_grad_q = scores_scale * (
            jnp.einsum(
                "hij,jhe->ihe",
                grad_wscore,
                block_window_key_rows,
                preferred_element_type=jnp.float32,
            )
            + jnp.einsum(
                "wyd,dwg->ywg",
                state_score_gradient,
                block_state_key_rows,
                preferred_element_type=jnp.float32,
            )
        )
        block_grad_wk = scores_scale * jnp.einsum(
            "hij,ihe->jhe", grad_wscore, block_query_rows, preferred_element_type=jnp.float32
        )
        block_grad_wv = jnp.einsum(
            "hij,ihe->jhe",
            window_exact.astype(jnp.bfloat16),
            block_grad,
            preferred_element_type=jnp.float32,
        )
        block_grad_sk = (
            scores_scale
            * jnp.einsum(
                "him,ihe->mhe",
                state_score_gradient,
                block_query_rows,
                preferred_element_type=jnp.float32,
            )
        ).astype(jnp.bfloat16)
        block_grad_sv = jnp.einsum(
            "him,ihe->mhe",
            state_exact.astype(jnp.bfloat16),
            block_grad,
            preferred_element_type=jnp.float32,
        ).astype(jnp.bfloat16)
        return (
            bias_sum + grad_wscore.astype(jnp.float32),
            (block_grad_q, block_grad_wk, block_grad_wv, block_grad_sk, block_grad_sv),
        )

    bias_start = jnp.zeros((local_head_count, BLOCK, 2 * BLOCK), jnp.float32)
    bias_sum, back_items = lax.scan(
        attend_back,
        bias_start,
        (
            flattened_queries,
            flattened_window_keys,
            flattened_window_values,
            flattened_state_keys,
            flattened_state_values,
            permitted_mask,
            log_totals,
            grad_attended,
        ),
    )
    grad_bias = bias_gradient(bias_sum, bucket, bias_rows.shape[1])
    grad_queries = back_items[0].reshape(local_shape)
    grad_window_keys = back_items[1].reshape(
        seq_count, block_count, 2 * BLOCK, local_head_count, HEAD_SIZE
    )
    grad_window_values = back_items[2].reshape(
        seq_count, block_count, 2 * BLOCK, local_head_count, HEAD_SIZE
    )
    state_keys_gradient = back_items[3].reshape(
        seq_count, block_count, state_slot_count, local_head_count, HEAD_SIZE
    )
    grad_state_values = back_items[4].reshape(
        seq_count, block_count, state_slot_count, local_head_count, HEAD_SIZE
    )
    back_keys, back_values = (
        from_behind(grad_window_keys[:, 0, :BLOCK].astype(jnp.bfloat16), "ctx", -1).astype(
            jnp.float32
        ),
        from_behind(grad_window_values[:, 0, :BLOCK].astype(jnp.bfloat16), "ctx", -1).astype(
            jnp.float32
        ),
    )
    key_grad = grad_window_keys[:, :, BLOCK:] + jnp.concatenate(
        [grad_window_keys[:, 1:, :BLOCK], back_keys[:, None]], 1
    )
    value_grad = grad_window_values[:, :, BLOCK:] + jnp.concatenate(
        [grad_window_values[:, 1:, :BLOCK], back_values[:, None]], 1
    )
    state_key_gradient = jnp.einsum(
        "sbmhe,sbmhf->hef", state_reduced, state_keys_gradient, preferred_element_type=jnp.float32
    )
    grad_svalue = jnp.einsum(
        "sbmhe,sbmhf->hef", state_reduced, grad_state_values, preferred_element_type=jnp.float32
    )
    direct = jnp.einsum(
        "palcq,crq->palcr",
        state_keys_gradient,
        state_key_complete,
        preferred_element_type=jnp.float32,
    ) + jnp.einsum(
        "palcq,crq->palcr", grad_state_values, svalue_full, preferred_element_type=jnp.float32
    )
    direct = direct.reshape(seq_count, block_count, state_slot_count, local_width)
    back_accum = jnp.zeros((seq_count, state_slot_count, local_width), jnp.float32)
    for block_index in reversed(range(block_count)):
        back_accum = direct[:, block_index] + gate_value * back_accum
    back_identity = (jnp.ones((local_width,), jnp.float32), jnp.zeros_like(back_accum))
    unused_power, incoming = prefix_2((gate_power, back_accum), "ctx", compose, back_identity, True)
    carried = incoming
    contrib_grads = [None] * block_count
    gate_grad = jnp.zeros((local_width,), jnp.float32)
    for block_index in reversed(range(block_count)):
        contrib_grads[block_index] = ((1.0 - gate_value) * carried).astype(jnp.bfloat16)
        gate_grad = gate_grad + jnp.sum(
            carried * (stacked[:, block_index] - contrib[:, block_index]), axis=(0, 1)
        )
        carried = direct[:, block_index] + gate_value * carried
    first_device = (lax.axis_index("ctx") == 0).astype(jnp.float32)
    grad_sinit = first_device * jnp.sum(carried, axis=0)
    grad_gate = (gate_grad * gate_value * (1.0 - gate_value)).reshape(local_head_count, HEAD_SIZE)
    grad_contrib = jnp.stack(contrib_grads, axis=1).reshape(
        seq_count, block_count, state_slot_count, local_head_count, HEAD_SIZE
    )
    grad_read = jnp.einsum(
        "sbmhe,sbthe->sbhmt", grad_contrib, value_rows, preferred_element_type=jnp.float32
    )
    extra_values = jnp.einsum(
        "sbhmt,sbmhe->sbthe", read_low, grad_contrib, preferred_element_type=jnp.float32
    )
    read_delta = jnp.sum(read_probs * grad_read, axis=-1, keepdims=True)
    grad_read_score = (read_probs * (grad_read - read_delta)).astype(jnp.bfloat16)
    grad_squery = (
        scores_scale
        * jnp.einsum(
            "sbhmt,sbthe->mhe", grad_read_score, key_rows, preferred_element_type=jnp.float32
        )
    ).reshape(state_slot_count, local_width)
    extra_keys = scores_scale * jnp.einsum(
        "sbhmt,mhe->sbthe", grad_read_score, query_heads, preferred_element_type=jnp.float32
    )
    grad_q_rows = grad_queries.astype(jnp.bfloat16).reshape(row_count, local_width)
    grad_k_rows = (key_grad + extra_keys).astype(jnp.bfloat16).reshape(row_count, local_width)
    grad_v_rows = (value_grad + extra_values).astype(jnp.bfloat16).reshape(row_count, local_width)
    grad_wq = jnp.dot(attn_in.T, grad_q_rows, preferred_element_type=jnp.float32)
    grad_wk = jnp.dot(attn_in.T, grad_k_rows, preferred_element_type=jnp.float32)
    grad_wv = jnp.dot(attn_in.T, grad_v_rows, preferred_element_type=jnp.float32)
    grad_attn_in = (
        jnp.dot(grad_q_rows, query_full.T, preferred_element_type=jnp.float32)
        + jnp.dot(grad_k_rows, key_full.T, preferred_element_type=jnp.float32)
        + jnp.dot(grad_v_rows, value_full.T, preferred_element_type=jnp.float32)
    )
    part_tokens, part_gain_one = norm_backward(grad_attn_in, normed_one, inverse_one, gain_one_vec)
    token_share, grad_gain_one = (
        lax.psum_scatter(
            part_tokens.reshape(seq_count, length, full_width).astype(jnp.bfloat16),
            "tp",
            scatter_dimension=2,
            tiled=True,
        ).astype(jnp.float32),
        lax.psum_scatter(
            part_gain_one.reshape(head_total, HEAD_SIZE).astype(jnp.bfloat16),
            "tp",
            scatter_dimension=0,
            tiled=True,
        ).astype(jnp.float32),
    )
    grad_tokens = (middle_grad + token_share).astype(jnp.bfloat16)
    grads = (
        lax.psum_scatter(
            grad_wq.astype(jnp.bfloat16), ("dp", "ctx"), scatter_dimension=0, tiled=True
        ).astype(jnp.float32),
        lax.psum_scatter(
            grad_wk.astype(jnp.bfloat16), ("dp", "ctx"), scatter_dimension=0, tiled=True
        ).astype(jnp.float32),
        lax.psum_scatter(
            grad_wv.astype(jnp.bfloat16), ("dp", "ctx"), scatter_dimension=0, tiled=True
        ).astype(jnp.float32),
        lax.psum_scatter(
            grad_wout.astype(jnp.bfloat16), ("dp", "ctx"), scatter_dimension=1, tiled=True
        ).astype(jnp.float32),
        lax.psum_scatter(
            grad_up.astype(jnp.bfloat16), ("dp", "ctx"), scatter_dimension=0, tiled=True
        ).astype(jnp.float32),
        lax.psum_scatter(
            grad_down.astype(jnp.bfloat16), ("dp", "ctx"), scatter_dimension=1, tiled=True
        ).astype(jnp.float32),
        lax.psum_scatter(
            grad_squery.astype(jnp.bfloat16), ("dp", "ctx"), scatter_dimension=0, tiled=True
        ).astype(jnp.float32),
        lax.psum_scatter(
            grad_sinit.astype(jnp.bfloat16), ("dp", "ctx"), scatter_dimension=0, tiled=True
        ).astype(jnp.float32),
        lax.psum_scatter(
            grad_gain_one.astype(jnp.bfloat16), ("dp", "ctx"), scatter_dimension=1, tiled=True
        ).astype(jnp.float32),
        lax.psum_scatter(
            grad_gain_two.astype(jnp.bfloat16), ("dp", "ctx"), scatter_dimension=1, tiled=True
        ).astype(jnp.float32),
        lax.psum_scatter(
            grad_bias.astype(jnp.bfloat16), ("dp", "ctx"), scatter_dimension=1, tiled=True
        ).astype(jnp.float32),
        lax.psum_scatter(
            grad_gate.astype(jnp.bfloat16), ("dp", "ctx"), scatter_dimension=1, tiled=True
        ).astype(jnp.float32),
        lax.psum_scatter(
            state_key_gradient.astype(jnp.bfloat16), ("dp", "ctx"), scatter_dimension=1, tiled=True
        ).astype(jnp.float32),
        lax.psum_scatter(
            grad_svalue.astype(jnp.bfloat16), ("dp", "ctx"), scatter_dimension=1, tiled=True
        ).astype(jnp.float32),
    )
    return (
        output,
        grad_tokens,
        grads[0],
        grads[1],
        grads[2],
        grads[3],
        grads[4],
        grads[5],
        grads[6],
        grads[7],
        grads[8],
        grads[9],
        grads[10],
        grads[11],
        grads[12],
        grads[13],
    )


LOG2E = 1.4426950408889634
VMEM_BYTES = 58 * 1024 * 1024
BF = jnp.bfloat16
F32 = jnp.float32


def nn(left, right):
    return jnp.dot(left, right, preferred_element_type=F32)


def nt(left, right):
    return lax.dot_general(left, right, (((1,), (1,)), ((), ())), preferred_element_type=F32)


def tn(left, right):
    return lax.dot_general(left, right, (((0,), (0,)), ((), ())), preferred_element_type=F32)


def flat(ref):
    block = ref[0]
    return block.reshape(block.shape[0] * block.shape[1], block.shape[2])


def merged(place_ref, own_ref, other_ref):
    own = own_ref[0, :, 0]
    other = other_ref[0, :, 0]
    is_first = place_ref[0] == 0
    pair = [jnp.where(is_first, own, other), jnp.where(is_first, other, own)]
    block = jnp.stack(pair, axis=1)
    return block.reshape(-1, block.shape[-1])


def joined(tok_ref):
    return jnp.concatenate([tok_ref[part] for part in range(tok_ref.shape[0])], axis=1).astype(F32)


def inverse_rms(x):
    return lax.rsqrt(jnp.mean(x * x, axis=-1, keepdims=True) + EPSILON)


def params():
    return pltpu.CompilerParams(vmem_limit_bytes=VMEM_BYTES)


def project_kernel(
    place_ref, tok_ref, gain_ref, wq_ref, wqo_ref, wk_ref, wko_ref, wv_ref, wvo_ref,
    q_ref, k_ref, v_ref, ain_ref, lastk_ref, lastv_ref,
):
    @pl.when(pl.program_id(0) == 0)
    def _():
        x = joined(tok_ref)
        ain_ref[...] = (x * inverse_rms(x) * gain_ref[...]).astype(BF)

    a = ain_ref[...]
    for w_ref, w_other, o_ref in (
        (wq_ref, wqo_ref, q_ref), (wk_ref, wko_ref, k_ref), (wv_ref, wvo_ref, v_ref)
    ):
        o_ref[...] = nn(a, merged(place_ref, w_ref, w_other)).astype(BF)
    length = k_ref.shape[0] * BLOCK // lastk_ref.shape[0]
    for item in range(lastk_ref.shape[0] // BLOCK):
        last = slice((item + 1) * length - BLOCK, (item + 1) * length)
        lastk_ref[item * BLOCK : (item + 1) * BLOCK] = k_ref[last]
        lastv_ref[item * BLOCK : (item + 1) * BLOCK] = v_ref[last]


def read_kernel(
    place_ref, sq_ref, sqo_ref, k_ref, v_ref, gate_ref, o_ref, sum_ref, state_ref, *, blocks
):
    n = pl.program_id(1)
    sq = merged(place_ref, sq_ref, sqo_ref)
    k = k_ref[...]
    v = v_ref[...]
    scale = HEAD_SIZE ** (-0.5) * LOG2E
    step = 256
    gate = jnp.where(lax.rem(n, blocks) == 0, 0.0, gate_ref[...])
    fresh = 1.0 - gate_ref[...]

    @pl.when(n == 0)
    def _():
        state_ref[...] = jnp.zeros_like(state_ref)

    for start in range(0, sq.shape[0], step):
        rows = slice(start, start + step)
        s = nt(sq[rows], k) * scale
        p = jnp.exp2(s - jnp.max(s, axis=-1, keepdims=True))
        total = jnp.sum(p, axis=-1, keepdims=True)
        contrib = nn(p.astype(BF), v) / total
        o_ref[rows, :] = contrib
        state = gate * state_ref[rows, :] + fresh * contrib
        state_ref[rows, :] = state
        sum_ref[rows, :] = state.astype(BF)


def attend_kernel(
    place_ref, info_ref, q_ref, k_ref, v_ref, kp_ref, vp_ref, hk_ref, hv_ref,
    wk_ref, wko_ref, wv_ref, wvo_ref, contrib_ref, init_ref, inito_ref, lead_ref, power_ref,
    gate_ref, u_ref, o_ref, lse_ref, low_ref, moved_ref, bias_ref, state_ref, *, blocks,
):
    n = pl.program_id(1)
    first = lax.rem(n, blocks) == 0
    scale = HEAD_SIZE ** (-0.5) * LOG2E

    @pl.when(n == 0)
    def _():
        row = jnp.broadcast_to(u_ref[0], (BLOCK, u_ref.shape[-1]))
        bias_ref[...] = pltpu.roll(row, 0, 1, stride=1, stride_axis=0)[:, : 2 * BLOCK]

    has_previous = info_ref[n, 0] > 0
    reach = info_ref[n, 1]
    k = k_ref[...]
    v = v_ref[...]
    kp = jnp.where(first, hk_ref[...], kp_ref[...])
    vp = jnp.where(first, hv_ref[...], vp_ref[...])

    @pl.when(first)
    def _():
        init = merged(place_ref, init_ref, inito_ref).astype(F32)
        state_ref[...] = power_ref[...] * init + lead_ref[...].astype(F32)

    state = state_ref[...]
    contrib = contrib_ref[...]
    st = state.astype(BF)
    low_ref[...] = st
    moved_ref[...] = (state - contrib).astype(BF)
    state_ref[...] = contrib + gate_ref[...] * (state - contrib)
    sk = nn(st, merged(place_ref, wk_ref, wko_ref)).astype(BF)
    sv = nn(st, merged(place_ref, wv_ref, wvo_ref)).astype(BF)
    step = ROWS_FORWARD

    def run(with_previous):
        for start in range(0, BLOCK, step):
            q = q_ref[start : start + step, :]
            sc = nt(q, k) * scale + bias_ref[start : start + step, BLOCK:]
            row = lax.broadcasted_iota(jnp.int32, (step, 1), 0) + start
            column = lax.broadcasted_iota(jnp.int32, (step, BLOCK), 1)
            sc = jnp.where(column <= jnp.maximum(row, reach - 1), sc, MASKED)
            ss = nt(q, sk) * scale
            peak = jnp.maximum(
                jnp.max(sc, axis=-1, keepdims=True), jnp.max(ss, axis=-1, keepdims=True)
            )
            if with_previous:
                sp = nt(q, kp) * scale + bias_ref[start : start + step, :BLOCK]
                peak = jnp.maximum(peak, jnp.max(sp, axis=-1, keepdims=True))
            pc = jnp.exp2(sc - peak)
            ps = jnp.exp2(ss - peak)
            total = jnp.sum(pc, axis=-1, keepdims=True) + jnp.sum(ps, axis=-1, keepdims=True)
            out = nn(pc.astype(BF), v) + nn(ps.astype(BF), sv)
            if with_previous:
                pp = jnp.exp2(sp - peak)
                total = total + jnp.sum(pp, axis=-1, keepdims=True)
                out = out + nn(pp.astype(BF), vp)
            o_ref[start : start + step, :] = (out / total).astype(BF)
            lse = jnp.broadcast_to(peak + jnp.log2(total), (step, 128))
            lse_ref[0, 0, :, start : start + step] = lse.T[:1]

    @pl.when(has_previous)
    def _():
        run(True)

    @pl.when(jnp.logical_not(has_previous))
    def _():
        run(False)


def attend_back_kernel(
    place_ref, info_ref, q_ref, k_ref, v_ref, kp_ref, vp_ref, hk_ref, hv_ref,
    wk_ref, wko_ref, wv_ref, wvo_ref, st_ref, gate_ref, u_ref, do_ref, o_ref, lse_ref,
    dq_ref, dk_ref, dv_ref, dkp_ref, dvp_ref, direct_ref, gwk_ref, gwv_ref, gb_ref, total_ref,
    firstk_ref, firstv_ref, bias_ref, sum_ref, dq_acc, state_acc, *, blocks,
):
    step_at = pl.program_id(1)
    n = pl.num_programs(1) - 1 - step_at
    first = lax.rem(n, blocks) == 0
    gate = jnp.where(lax.rem(n, blocks) == blocks - 1, 0.0, gate_ref[...])
    factor = HEAD_SIZE ** (-0.5)
    scale = factor * LOG2E
    window = 2 * BLOCK
    width = BLOCK + window

    @pl.when(step_at == 0)
    def _():
        state_acc[...] = jnp.zeros_like(state_acc)
        row = jnp.broadcast_to(u_ref[0], (window, u_ref.shape[-1]))
        bias_ref[...] = pltpu.roll(row, 0, 1, stride=1, stride_axis=0)[:, :BLOCK]
        sum_ref[...] = jnp.zeros_like(sum_ref)
        gwk_ref[...] = jnp.zeros_like(gwk_ref)
        gwv_ref[...] = jnp.zeros_like(gwv_ref)

    has_previous = info_ref[n, 0] > 0
    reach = info_ref[n, 1]
    q = q_ref[...]
    do = do_ref[...]
    lse = lse_ref[0, 0]
    delta = jnp.sum((do.astype(F32) * o_ref[...].astype(F32)).T, axis=0, keepdims=True)
    step = KEYS_BACKWARD

    def part(key, value, start, bias_start, masked):
        s = nt(key, q) * scale
        if bias_start is not None:
            s = s + bias_ref[bias_start : bias_start + step, :]
        if masked:
            key_at = lax.broadcasted_iota(jnp.int32, (step, BLOCK), 0) + start
            query_at = lax.broadcasted_iota(jnp.int32, (1, BLOCK), 1)
            s = jnp.where(key_at <= jnp.maximum(query_at, reach - 1), s, MASKED)
        p = jnp.exp2(s - lse)
        dp = nt(value, do)
        ds = (p * (dp - delta)).astype(BF)
        if bias_start is not None:
            for block in range(0, step, 128):
                at = window - bias_start - block
                sum_ref[:, at : at + BLOCK] += ds[block : block + 128].astype(F32)
        dq_acc[...] += tn(ds, key)
        return nn(ds, q) * factor, nn(p.astype(BF), do)

    dq_acc[...] = jnp.zeros_like(dq_acc)
    st = st_ref[...]
    key_map = merged(place_ref, wk_ref, wko_ref)
    value_map = merged(place_ref, wv_ref, wvo_ref)
    sk = nn(st, key_map).astype(BF)
    sv = nn(st, value_map).astype(BF)
    for start in range(0, st.shape[0], step):
        rows = slice(start, start + step)
        dk, dv = part(sk[rows], sv[rows], start, None, False)
        dk = dk.astype(BF)
        dv = dv.astype(BF)
        direct = nt(dk, key_map) + nt(dv, value_map)
        direct_ref[rows, :] = direct
        state = direct + gate * state_acc[rows, :]
        state_acc[rows, :] = state
        total_ref[rows, :] = state.astype(BF)
        gwk_ref[0] += tn(st[rows], dk)
        gwv_ref[0] += tn(st[rows], dv)
    for start in range(0, BLOCK, step):
        rows = slice(start, start + step)
        dk, dv = part(k_ref[rows, :], v_ref[rows, :], start, BLOCK + start, True)
        dk_ref[rows, :] = dk
        dv_ref[rows, :] = dv

    @pl.when(has_previous)
    def _():
        for start in range(0, BLOCK, step):
            rows = slice(start, start + step)
            key = jnp.where(first, hk_ref[rows, :], kp_ref[rows, :])
            value = jnp.where(first, hv_ref[rows, :], vp_ref[rows, :])
            dk, dv = part(key, value, start, start, False)
            dkp_ref[rows, :] = dk.astype(BF)
            dvp_ref[rows, :] = dv.astype(BF)

    @pl.when(jnp.logical_not(has_previous))
    def _():
        dkp_ref[...] = jnp.zeros_like(dkp_ref)
        dvp_ref[...] = jnp.zeros_like(dvp_ref)

    @pl.when(first)
    def _():
        firstk_ref[...] = dkp_ref[...]
        firstv_ref[...] = dvp_ref[...]

    dq_ref[...] = (dq_acc[...] * factor).astype(BF)

    @pl.when(n == 0)
    def _():
        folded = sum_ref[...]
        half = 64
        while half >= 8:
            folded = folded[:half] + pltpu.roll(folded[half:], width - half, 1)
            half //= 2
        total = folded[:1]
        for row in range(1, 8):
            total = total + pltpu.roll(folded[row : row + 1], width - row, 1)
        gb_ref[0] = total


def read_back_kernel(
    place_ref, sq_ref, sqo_ref, k_ref, v_ref, direct_ref, moved_ref, later_ref, gate_ref,
    dk_ref, dv_ref, nk_ref, nv_ref, rk_ref, rv_ref,
    gk_ref, gv_ref, gsq_ref, ginit_ref, ggate_ref, carried_ref, *, blocks,
):
    step_at = pl.program_id(1)
    n = pl.num_programs(1) - 1 - step_at
    last = lax.rem(n, blocks) == blocks - 1
    factor = HEAD_SIZE ** (-0.5)

    @pl.when(step_at == 0)
    def _():
        gsq_ref[...] = jnp.zeros_like(gsq_ref)
        ginit_ref[...] = jnp.zeros_like(ginit_ref)
        ggate_ref[...] = jnp.zeros_like(ggate_ref)

    @pl.when(last)
    def _():
        carried_ref[...] = later_ref[...].astype(F32)

    gate = gate_ref[...]
    carried = carried_ref[...]
    gc = ((1.0 - gate) * carried).astype(BF)
    change = jnp.sum(carried * moved_ref[...].astype(F32), axis=0, keepdims=True)
    ggate_ref[0] += change * (gate * (1.0 - gate))
    carried = direct_ref[...] + gate * carried
    carried_ref[...] = carried

    @pl.when((lax.rem(n, blocks) == 0) & (place_ref[0] == 0))
    def _():
        ginit_ref[...] += carried

    sq = merged(place_ref, sq_ref, sqo_ref)
    k = k_ref[...]
    s = nt(k, sq) * (factor * LOG2E)
    p = jnp.exp2(s - jnp.max(s, axis=0, keepdims=True))
    p = p * (1.0 / jnp.sum(p, axis=0, keepdims=True))
    dp = nt(v_ref[...], gc)
    ds = (p * (dp - jnp.sum(p * dp, axis=0, keepdims=True))).astype(BF)
    next_k = jnp.where(last, rk_ref[...], nk_ref[...]).astype(F32)
    next_v = jnp.where(last, rv_ref[...], nv_ref[...]).astype(F32)
    gk_ref[...] = (dk_ref[...] + next_k + nn(ds, sq) * factor).astype(BF)
    gv_ref[...] = (dv_ref[...] + next_v + nn(p.astype(BF), gc)).astype(BF)
    gsq_ref[...] += tn(ds, k) * factor


def item_kernel(wq_ref, wk_ref, wv_ref, sq_ref, init_ref, mk_ref, mv_ref, tail_ref, out_ref):
    at = 0
    for w_ref in (wq_ref, wk_ref, wv_ref, sq_ref, init_ref):
        out_ref[at : at + w_ref.shape[0]] = w_ref[...]
        at += w_ref.shape[0]
    for w_ref in (mk_ref, mv_ref):
        heads, rows, lanes = w_ref.shape
        for item in range(heads):
            out_ref[at : at + rows, item * lanes : (item + 1) * lanes] = w_ref[item]
        at += rows
    out_ref[at:] = tail_ref[...]


def pack_kernel(up_ref, down_ref, out_ref, packed_ref):
    hidden = up_ref.shape[1]
    packed_ref[:, :hidden] = up_ref[...]
    packed_ref[:, hidden : 2 * hidden] = down_ref[...].T
    packed_ref[:, 2 * hidden :] = out_ref[...].T


def unpack_kernel(packed_ref, up_ref, down_ref, out_ref):
    hidden = up_ref.shape[1]
    up_ref[...] = packed_ref[:, :hidden].astype(F32)
    down_ref[...] = packed_ref[:, hidden : 2 * hidden].astype(F32).T
    out_ref[...] = packed_ref[:, 2 * hidden :].astype(F32).T


def finish_kernel(*refs):
    place_ref, refs = refs[0], refs[1:]
    terms, outs = refs[:-12], refs[-12:-1]
    sum_ref = refs[-1]
    total = terms[0][...].astype(F32)
    for term in terms[1:]:
        total = total + term[...].astype(F32)
    at = 0
    for out_ref in outs[:5]:
        out_ref[...] = total[at : at + out_ref.shape[0]]
        at += out_ref.shape[0]
    for out_ref in outs[5:7]:
        heads, rows, lanes = out_ref.shape
        for item in range(heads):
            out_ref[item] = total[at : at + rows, item * lanes : (item + 1) * lanes]
        at += rows
    sum_ref[...] = total[at:]
    shard, group = place_ref[1], place_ref[2]
    lanes = sum_ref.shape[1]
    for index, out_ref in enumerate(outs[7:]):
        heads, columns = out_ref.shape
        if index < 3:
            stride = HEAD_SIZE
            row = sum_ref[pl.ds(index * len(terms) + shard, 1), :]
            shift = group * columns
        else:
            stride = columns * (HEAD_SIZE // outs[7].shape[1])
            row = sum_ref[index * len(terms) : index * len(terms) + 1, :]
            shift = (shard * heads) * stride + group * columns
        row = pltpu.roll(row, lax.rem(lanes - shift, lanes), 1)
        for item in range(heads):
            out_ref[item : item + 1, :] = row[:, item * stride : item * stride + columns]


def out_kernel(att_ref, wo_ref, tok_ref, gain_ref, mid_ref, min_ref):
    t = pl.program_id(0)
    part = nt(att_ref[...], flat(wo_ref))

    @pl.when(t == 0)
    def _():
        mid_ref[...] = joined(tok_ref) + part

    @pl.when(t > 0)
    def _():
        mid_ref[...] += part

    @pl.when(t == pl.num_programs(0) - 1)
    def _():
        x = mid_ref[...].astype(BF).astype(F32)
        min_ref[...] = (x * inverse_rms(x) * gain_ref[...]).astype(BF)


def mlp_kernel(
    place_ref, min_ref, cot_ref, mid_ref, gain_ref, wu_ref, wd_ref,
    out_ref, gmid_ref, ggain_ref, gw_ref,
    min_t, cot_t, out_acc, gm_acc, hidden_ref,
):
    tile = pl.program_id(0)
    which = pl.program_id(1)

    @pl.when((tile == 0) & (which == 0))
    def _():
        min_t[...] = min_ref[...].T
        cot_t[...] = cot_ref[...].T
        out_acc[...] = jnp.zeros_like(out_acc)
        gm_acc[...] = jnp.zeros_like(gm_acc)

    @pl.when(which == 0)
    def _():
        wu = flat(wu_ref)
        wd = flat(wd_ref)
        pre = nn(min_ref[...], wu)
        cdf = 0.5 + 0.5 * lax.erf(pre * (0.5**0.5))
        density = jnp.exp2(pre * pre * (-0.5 * LOG2E)) * ((2.0 * np.pi) ** -0.5)
        hidden_ref[...] = (pre * cdf).astype(BF)
        grad_pre = (nn(cot_ref[...], wd) * (cdf + pre * density)).astype(BF)
        out_acc[...] += nt(hidden_ref[...], wd)
        gm_acc[...] += nt(grad_pre, wu)
        grad = nn(min_t[...], grad_pre).astype(BF)
        gw_ref[...] = grad.reshape(gw_ref.shape)

    @pl.when(which == 1)
    def _():
        grad = nn(cot_t[...], hidden_ref[...]).astype(BF)
        gw_ref[...] = grad.reshape(gw_ref.shape)

    @pl.when((tile == pl.num_programs(0) - 1) & (which == 1))
    def _():
        mid = mid_ref[...]
        lanes = out_ref.shape[2]
        for part in range(out_ref.shape[0]):
            at = slice(part * lanes, (part + 1) * lanes)
            out_ref[part] = (mid[:, at] + out_acc[:, at]).astype(BF)
        x = mid.astype(BF).astype(F32)
        inverse = inverse_rms(x)
        normed = x * inverse
        gm = gm_acc[...]
        ggain_ref[...] = jnp.sum(gm * normed, axis=0, keepdims=True)
        scaled = gm * gain_ref[...]
        back = inverse * (scaled - normed * jnp.mean(scaled * normed, axis=-1, keepdims=True))
        gmid_ref[...] = (cot_ref[...].astype(F32) + back).astype(BF)


def out_back_kernel(gmid_ref, wo_ref, att_ref, late_ref, gatt_ref, gwo_ref, gmid_t):
    @pl.when(pl.program_id(0) == 0)
    def _():
        gmid_t[...] = gmid_ref[...].T

    gatt_ref[...] = nn(gmid_ref[...], flat(wo_ref)).astype(BF)
    gwo_ref[...] = nn(gmid_t[...], att_ref[...]).astype(BF).reshape(gwo_ref.shape)


def project_back_kernel(
    place_ref, tok_ref, gmid_ref, gain_ref, gq_ref, gk_ref, gv_ref,
    wq_ref, wqo_ref, wk_ref, wko_ref, wv_ref, wvo_ref, gsq_ref, ginit_ref, gmk_ref, gmv_ref,
    gtok_ref, ggain_ref, gown_ref, gother_ref, ain_t, acc_ref, pack_ref,
):
    t = pl.program_id(0)

    @pl.when(t == 0)
    def _():
        x = joined(tok_ref)
        ain_t[...] = (x * inverse_rms(x) * gain_ref[...]).astype(BF).T
        acc_ref[...] = jnp.zeros_like(acc_ref)

    groups, _, lanes = pack_ref.shape
    at = 0
    for g_ref, w_ref, w_other in (
        (gq_ref, wq_ref, wqo_ref), (gk_ref, wk_ref, wko_ref), (gv_ref, wv_ref, wvo_ref)
    ):
        g = g_ref[...]
        acc_ref[...] += nt(g, merged(place_ref, w_ref, w_other))
        grad = nn(ain_t[...], g).astype(BF)
        rows = grad.shape[0] // groups
        pack_ref[:, at : at + rows] = grad.reshape(groups, rows, lanes)
        at += rows
    for g_ref in (gsq_ref, ginit_ref):
        rows = g_ref.shape[0] // groups
        pack_ref[:, at : at + rows] = g_ref[...].astype(BF).reshape(groups, rows, lanes)
        at += rows
    for g_ref in (gmk_ref, gmv_ref):
        rows = HEAD_SIZE // groups
        for item in range(g_ref.shape[0]):
            where = slice(item * HEAD_SIZE, (item + 1) * HEAD_SIZE)
            pack_ref[:, at : at + rows, where] = g_ref[item].astype(BF).reshape(groups, rows, -1)
        at += rows
    pack_ref[:, at:] = jnp.zeros_like(pack_ref[:, at:])
    for index in range(groups // 2):
        gown_ref[0, index] = pack_ref[2 * index + place_ref[0]]
        gother_ref[0, index] = pack_ref[2 * index + 1 - place_ref[0]]

    @pl.when(t == pl.num_programs(0) - 1)
    def _():
        x = joined(tok_ref)
        inverse = inverse_rms(x)
        normed = x * inverse
        ga = acc_ref[...]
        ggain_ref[...] = jnp.sum(ga * normed, axis=0, keepdims=True)
        scaled = ga * gain_ref[...]
        back = inverse * (scaled - normed * jnp.mean(scaled * normed, axis=-1, keepdims=True))
        grad = (gmid_ref[...].astype(F32) + back).astype(BF)
        for part in range(gtok_ref.shape[0]):
            gtok_ref[part] = grad[:, part * lanes : (part + 1) * lanes]


def distance_bucket(distance):
    magnitude = np.abs(distance)
    scaled = np.log(np.maximum(magnitude, 1) / 8.0) / np.log(16.0) * 8.0
    far = np.minimum(8 + np.floor(np.maximum(scaled, 0.0)).astype(np.int32), 15)
    return (distance < 0).astype(np.int32) * 16 + np.where(magnitude < 8, magnitude, far)


def one_hot(distance, valid, bucket_count):
    hot = distance_bucket(distance)[:, None] == np.arange(bucket_count)[None, :]
    return jnp.asarray((hot & valid[:, None]).astype(np.float32))


def carry(value, power, axis, backward):
    count = lax.axis_size(axis)
    sign = -1 if backward else 1
    total = from_behind(value.astype(BF), axis, sign)
    if count == 2:
        return total
    total = total.astype(F32)
    step = 1
    while step < count - 1:
        moved = from_behind(total.astype(BF), axis, sign * step).astype(F32)
        total = total + power**step * moved
        step *= 2
    return total


def across(value, axis, bit):
    count = lax.axis_size(axis)
    return lax.ppermute(value, axis, [(source, source ^ bit) for source in range(count)])


def take(value, index, dim):
    return lax.dynamic_index_in_dim(value, index, dim, False)


def add_low(left, right):
    return (left.astype(F32) + right.astype(F32)).astype(BF)


def ordered(bit, own, other, dim):
    first = bit == 0
    return jnp.stack([jnp.where(first, own, other), jnp.where(first, other, own)], axis=dim)


def gather_pairs(item, beside, behind):
    shards = lax.axis_size("tp")
    half = shards // 2
    tp = lax.axis_index("tp")
    x_bit = lax.axis_index("dp") % 2
    y_bit = lax.axis_index("dp") // 2
    parts = [item] + [across(item, "tp", k) for k in range(1, shards)]
    bit = 1
    while bit < shards:
        swap = (tp & bit) > 0
        parts = [jnp.where(swap, parts[k ^ bit], parts[k]) for k in range(shards)]
        bit *= 2
    low = jnp.stack(parts[:half])
    high = jnp.stack(parts[half:])
    low_x = across(low, "dp", 1)
    high_y = across(high, "dp", 2)
    low = ordered(x_bit, low, low_x, 0)
    high = ordered(y_bit, high, high_y, 0)
    low_y = across(low, "dp", 2)
    high_x = across(high, "dp", 1)
    low_y, high_x, beside, behind = lax.optimization_barrier((low_y, high_x, beside, behind))
    low = ordered(y_bit, low, low_y, 0)
    high = ordered(x_bit, high, high_x, 1)
    own = jnp.stack([low, high]).reshape((2, 4, half) + item.shape)
    return own, across(own, "ctx", 1), beside, behind


def scatter_pairs(own, other):
    shards = own.shape[0]
    half = shards // 2
    tp = lax.axis_index("tp")
    x_bit = lax.axis_index("dp") % 2
    y_bit = lax.axis_index("dp") // 2
    grid = (shards, 2, 2) + own.shape[2:]
    moved = across(other, "ctx", 1).reshape(grid)
    own = own.reshape(grid)

    def both(part, index, dim):
        return add_low(take(own[part], index, dim), take(moved[part], index, dim))

    first, second = slice(0, half), slice(half, shards)
    low_moved = across(both(first, 1 - x_bit, 2), "dp", 1)
    high_moved = across(both(second, 1 - y_bit, 1), "dp", 2)
    low = add_low(both(first, x_bit, 2), low_moved)
    high = add_low(both(second, y_bit, 1), high_moved)
    low_moved = across(take(low, 1 - y_bit, 1), "dp", 2)
    high_moved = across(take(high, 1 - x_bit, 1), "dp", 1)
    low = add_low(take(low, y_bit, 1), low_moved)
    high = add_low(take(high, x_bit, 1), high_moved)
    kept = jnp.concatenate([low, high])
    return [take(kept, tp, 0)] + [
        across(take(kept, tp ^ k, 0), "tp", k) for k in range(1, shards)
    ]


def sequence_body(
    tokens, cotangent, prefix, w_query, w_key, w_value, w_out, w_up, w_down,
    state_query, state_init, gain_attn, gain_mlp, bias_table, gate_bias, state_key, state_value,
):
    shards = lax.axis_size("tp")
    groups = lax.axis_size("dp") * lax.axis_size("ctx")
    pairs = lax.axis_size("dp")
    half = shards // 2
    everywhere = ("tp", "dp", "ctx")
    seq_count, length, shard_width = tokens.shape
    width = cotangent.shape[2]
    seqs = seq_count // shards
    blocks = length // BLOCK
    units = seqs * blocks
    rows = units * BLOCK
    local_heads = bias_table.shape[0]
    heads = local_heads * shards
    buckets = bias_table.shape[1] * groups
    own_rows = w_query.shape[0]
    own_slots = state_query.shape[0]
    slots = own_slots * groups
    hidden = w_up.shape[1]
    tp_index = lax.axis_index("tp")
    ctx_index = lax.axis_index("ctx")
    dp_index = lax.axis_index("dp")
    head = HEAD_SIZE
    map_rows = state_key.shape[1]
    group = dp_index * lax.axis_size("ctx") + ctx_index
    place = jnp.stack([ctx_index, tp_index, group]).astype(jnp.int32)

    def call(kernel, grid, in_specs, out_specs, out_shape, scratch=(), prefetch=1, **more):
        return pl.pallas_call(
            kernel,
            grid_spec=pltpu.PrefetchScalarGridSpec(
                num_scalar_prefetch=prefetch, grid=grid, in_specs=in_specs, out_specs=out_specs,
                scratch_shapes=list(scratch),
            ),
            out_shape=out_shape,
            compiler_params=params(),
            **more,
        )

    at_slots = 3 * own_rows
    at_init = at_slots + own_slots
    at_maps = at_init + own_slots
    at_vectors = at_maps + 2 * map_rows
    full_rows = at_vectors + 16
    vectors = (gain_attn, gain_mlp, gate_bias, bias_table)
    ends = np.cumsum([0] + [item.shape[1] for item in vectors])
    tail = jnp.concatenate(vectors, axis=1)
    tail = jnp.pad(tail, ((0, 16 - local_heads), (0, shard_width - tail.shape[1])))
    item = pl.pallas_call(
        item_kernel, out_shape=jax.ShapeDtypeStruct((full_rows, shard_width), BF)
    )(w_query, w_key, w_value, state_query, state_init, state_key, state_value, tail)
    x = lax.all_to_all(tokens, "tp", 0, 0, tiled=True)
    late_width = 2 * hidden + shard_width
    late = pl.pallas_call(
        pack_kernel, out_shape=jax.ShapeDtypeStruct((own_rows, late_width), BF)
    )(w_up, w_down, w_out)
    first_own, first_other, x, late = gather_pairs(item, x, late)
    x = x.reshape(shards, rows, shard_width)
    late = lax.all_gather(late, everywhere, axis=0, tiled=True)
    late = late.reshape(shards, groups, own_rows, late_width)

    at_heads = slice(at_vectors, at_vectors + local_heads)
    small = ordered(
        ctx_index, first_own[:, :, :, at_heads], first_other[:, :, :, at_heads], 2
    )

    def spread(index):
        part = small[..., ends[index] : ends[index + 1]]
        return jnp.transpose(part, (0, 3, 4, 1, 2, 5)).reshape(heads, -1).astype(F32)

    gain_one = spread(0).reshape(1, width)
    gain_two = spread(1).reshape(1, width)
    gate = jax.nn.sigmoid(spread(2)).reshape(1, width)
    bias_rows = spread(3)

    def whole(shape):
        return pl.BlockSpec(shape, lambda *_: (0,) * len(shape))

    def weight(index):
        spec = pl.BlockSpec(
            (1, pairs, 1, own_rows, shard_width), lambda t, *_: (t // half, 0, t % half, index, 0)
        )
        return [spec, spec]

    def of_head(count, index):
        def at(h, *_):
            t = h // local_heads
            return (t // half, 0, t % half, index, h % local_heads)

        spec = pl.BlockSpec((1, pairs, 1, count, head), at)
        return [spec, spec]

    column = pl.BlockSpec((rows, shard_width), lambda t, *_: (0, t))
    wide = jax.ShapeDtypeStruct((rows, width), BF)
    wide32 = jax.ShapeDtypeStruct((rows, width), F32)
    split = jax.ShapeDtypeStruct((shards, rows, shard_width), BF)
    halo = jax.ShapeDtypeStruct((seqs * BLOCK, width), BF)
    halo_column = pl.BlockSpec((seqs * BLOCK, shard_width), lambda t, *_: (0, t))
    queries, keys, values, _, last_keys, last_values = call(
        project_kernel,
        (shards,),
        [whole((shards, rows, shard_width)), whole((1, width))] + weight(0) + weight(1) + weight(2),
        [column, column, column, whole((rows, width)), halo_column, halo_column],
        [wide] * 4 + [halo] * 2,
    )(place, x, gain_one, *([first_own, first_other] * 3))

    halo_keys = from_behind(last_keys, "ctx", 1)
    halo_values = from_behind(last_values, "ctx", 1)

    def along(rows_of, index):
        return pl.BlockSpec((rows_of, head), lambda h, n, *_: (index(n), h))

    def turned(n):
        return units - 1 - n

    query_slots = of_head(own_slots, at_slots // own_slots)
    init_slots = of_head(own_slots, at_init // own_slots)
    key_maps = of_head(map_rows, at_maps // map_rows)
    value_maps = of_head(map_rows, at_maps // map_rows + 1)
    channel = pl.BlockSpec((1, head), lambda h, n, *_: (0, h))
    slot_rows = units * slots
    slot_f32 = jax.ShapeDtypeStruct((slot_rows, width), F32)
    slot_low = jax.ShapeDtypeStruct((slot_rows, width), BF)
    message = jax.ShapeDtypeStruct((seqs * slots, width), BF)
    slot_scratch = pltpu.VMEM((slots, head), F32)
    own = along(BLOCK, lambda n: n)
    slot = along(slots, lambda n: n)
    slot_of_seq = along(slots, lambda n: n // blocks)
    contrib, accumulated = call(
        functools.partial(read_kernel, blocks=blocks),
        (heads, units),
        query_slots + [own, own, channel],
        [slot, slot_of_seq],
        [slot_f32, message],
        [slot_scratch],
    )(place, first_own, first_other, keys, values, gate)
    power = gate**blocks
    lead = carry(accumulated, power, "ctx", False)
    lead_power = jnp.ones_like(gate)
    for step in range(lax.axis_size("ctx") - 1):
        lead_power = jnp.where(ctx_index > step, lead_power * power, lead_power)

    block_at = ctx_index * blocks + jnp.arange(blocks, dtype=jnp.int32)
    own_prefix = lax.dynamic_slice_in_dim(prefix, tp_index * seqs, seqs, 0)
    info = jnp.stack(
        [
            jnp.broadcast_to(block_at[None], (seqs, blocks)),
            own_prefix[:, None] - block_at[None] * BLOCK,
        ],
        axis=-1,
    ).reshape(units, 2)
    span = 4 * BLOCK
    offset = np.arange(span)
    offset = np.where(offset < 2 * BLOCK, offset, offset - span)
    forward_hot = one_hot(BLOCK - offset, offset > -BLOCK, buckets)
    back_span = 3 * BLOCK
    back_offset = np.arange(back_span)
    back_offset = np.where(back_offset < BLOCK, back_offset, back_offset - back_span)
    backward_hot = one_hot(BLOCK + back_offset, back_offset > -2 * BLOCK, buckets)
    exact = lax.Precision.HIGHEST
    scaled_bias = bias_rows * LOG2E
    forward_bias = jnp.dot(scaled_bias, forward_hot.T, precision=exact)[:, None]
    backward_bias = jnp.dot(scaled_bias, backward_hot.T, precision=exact)[:, None]

    def attend_specs(index):
        before = along(BLOCK, lambda n: jnp.maximum(index(n) - 1, 0))
        by_seq = along(BLOCK, lambda n: index(n) // blocks)
        here = along(BLOCK, index)
        return [here, here, here, before, before, by_seq, by_seq] + key_maps + value_maps

    def lse_spec(index):
        return pl.BlockSpec((1, 1, 1, BLOCK), lambda h, n, *_: (index(n), h, 0, 0))

    def vector(size):
        return pl.BlockSpec((1, 1, size), lambda h, *_: (h, 0, 0))

    attend_args = (
        place, info, queries, keys, values, keys, values, halo_keys, halo_values,
        first_own, first_other, first_own, first_other,
    )
    attended, lse, states, moved = call(
        functools.partial(attend_kernel, blocks=blocks),
        (heads, units),
        attend_specs(lambda n: n)
        + [slot] + init_slots + [slot_of_seq, channel, channel, vector(span)],
        [own, lse_spec(lambda n: n), slot, slot],
        [wide, jax.ShapeDtypeStruct((units, heads, 1, BLOCK), F32), slot_low, slot_low],
        [pltpu.VMEM((BLOCK, 2 * BLOCK), F32), slot_scratch],
        2,
    )(*attend_args, contrib, first_own, first_other, lead, lead_power, gate, forward_bias)

    out_weight = pl.BlockSpec(
        (1, groups, own_rows, shard_width), lambda t, *_: (t, 0, 0, 2 * hidden // shard_width)
    )
    middle, mlp_in = pl.pallas_call(
        out_kernel,
        grid=(shards,),
        in_specs=[column, out_weight, whole((shards, rows, shard_width)), whole((1, width))],
        out_specs=[whole((rows, width)), whole((rows, width))],
        out_shape=[wide32, wide],
        compiler_params=params(),
    )(attended, late, x, gain_two)

    tile = min(hidden, 1024)
    per_shard = hidden // tile
    tile_block = (1, groups, own_rows, tile)
    output, middle_grad, gain_two_grad, late_grad = call(
        mlp_kernel,
        (shards * per_shard, 2),
        [
            whole((rows, width)),
            pl.BlockSpec((rows, width), lambda i, j, place_ref: (place_ref[1], 0)),
            whole((rows, width)), whole((1, width)),
            pl.BlockSpec(tile_block, lambda i, j, *_: (i // per_shard, 0, 0, i % per_shard)),
            pl.BlockSpec(
                tile_block, lambda i, j, *_: (i // per_shard, 0, 0, per_shard + i % per_shard)
            ),
        ],
        [
            whole((shards, rows, shard_width)), whole((rows, width)), whole((1, width)),
            pl.BlockSpec(
                tile_block, lambda i, j, *_: (i // per_shard, 0, 0, j * per_shard + i % per_shard)
            ),
        ],
        [
            split, wide, jax.ShapeDtypeStruct((1, width), F32),
            jax.ShapeDtypeStruct((shards, groups, own_rows, late_width), BF),
        ],
        [
            pltpu.VMEM((width, rows), BF), pltpu.VMEM((width, rows), BF),
            pltpu.VMEM((rows, width), F32), pltpu.VMEM((rows, width), F32),
            pltpu.VMEM((rows, tile), BF),
        ],
    )(
        place, mlp_in, cotangent.reshape(seq_count * length, width), middle, gain_two, late, late
    )
    output = lax.all_to_all(output, "tp", 0, 0, tiled=True)

    grad_attended, late_grad = pl.pallas_call(
        out_back_kernel,
        grid=(shards,),
        in_specs=[
            whole((rows, width)), out_weight, column, pl.BlockSpec(memory_space=pl.ANY)
        ],
        out_specs=[column, out_weight],
        out_shape=[wide, jax.ShapeDtypeStruct(late_grad.shape, BF)],
        scratch_shapes=[pltpu.VMEM((width, rows), BF)],
        compiler_params=params(),
        input_output_aliases={3: 1},
    )(middle_grad, late, attended, late_grad)
    late_grad = lax.psum_scatter(
        late_grad.reshape(shards * groups * own_rows, late_width), everywhere,
        scatter_dimension=0, tiled=True,
    )
    up_grad, down_grad, out_grad = pl.pallas_call(
        unpack_kernel,
        out_shape=[
            jax.ShapeDtypeStruct(w_up.shape, F32), jax.ShapeDtypeStruct(w_down.shape, F32),
            jax.ShapeDtypeStruct(w_out.shape, F32),
        ],
    )(late_grad)

    head_sum = jax.ShapeDtypeStruct((heads, head, head), F32)
    head_map = pl.BlockSpec((1, head, head), lambda h, n, *_: (h, 0, 0))
    back_own = along(BLOCK, turned)
    back_slot = along(slots, turned)
    back_of_seq = along(slots, lambda n: turned(n) // blocks)
    key_of_seq = along(BLOCK, lambda n: turned(n) // blocks)
    (
        grad_queries, dk, dv, dk_before, dv_before, direct, key_map_grad, value_map_grad,
        bias_sum, gathered, first_keys, first_values,
    ) = call(
        functools.partial(attend_back_kernel, blocks=blocks),
        (heads, units),
        attend_specs(turned)
        + [back_slot, channel, vector(back_span), back_own, back_own, lse_spec(turned)],
        [back_own] * 5 + [back_slot, head_map, head_map, vector(back_span), back_of_seq]
        + [key_of_seq, key_of_seq],
        [
            wide, wide32, wide32, wide, wide, slot_f32, head_sum, head_sum,
            jax.ShapeDtypeStruct((heads, 1, back_span), F32), message, halo, halo,
        ],
        [
            pltpu.VMEM((2 * BLOCK, BLOCK), F32), pltpu.VMEM((128, back_span), F32),
            pltpu.VMEM((BLOCK, head), F32), slot_scratch,
        ],
        2,
    )(*attend_args, states, gate, backward_bias, grad_attended, attended, lse)
    dk, output = lax.optimization_barrier((dk, output))
    sum_at = np.arange(back_span) - BLOCK
    sum_hot = one_hot(sum_at, sum_at > -BLOCK, buckets)
    bias_grad = jnp.dot(bias_sum[:, 0], sum_hot, precision=exact)

    later = carry(gathered, power, "ctx", True)
    back_keys = from_behind(first_keys, "ctx", -1)
    back_values = from_behind(first_values, "ctx", -1)
    following = along(BLOCK, lambda n: jnp.minimum(turned(n) + 1, units - 1))
    kept_slot = pl.BlockSpec((slots, head), lambda h, n, *_: (0, h))
    slot_sum = jax.ShapeDtypeStruct((slots, width), F32)
    grad_keys, grad_values, slot_query_grad, init_grad, gate_grad = call(
        functools.partial(read_back_kernel, blocks=blocks),
        (heads, units),
        query_slots
        + [back_own, back_own, back_slot, back_slot, back_of_seq, channel]
        + [back_own, back_own, following, following, key_of_seq, key_of_seq],
        [back_own, back_own, kept_slot, kept_slot, vector(head)],
        [wide, wide, slot_sum, slot_sum, jax.ShapeDtypeStruct((heads, 1, head), F32)],
        [slot_scratch],
    )(
        place, first_own, first_other, keys, values, direct, moved, later, gate,
        dk, dv, dk_before, dv_before, back_keys, back_values,
    )

    maps_of = pl.BlockSpec((local_heads, head, head), lambda t, *_: (t, 0, 0))
    slots_of = pl.BlockSpec((slots, shard_width), lambda t, *_: (0, t))
    piece = pl.BlockSpec((1, pairs, full_rows, shard_width), lambda t, *_: (t, 0, 0, 0))
    pieces = jax.ShapeDtypeStruct((shards, pairs, full_rows, shard_width), BF)
    token_grad, gain_one_grad, grad_own, grad_other = call(
        project_back_kernel,
        (shards,),
        [whole((shards, rows, shard_width)), whole((rows, width)), whole((1, width))]
        + [column, column, column]
        + weight(0) + weight(1) + weight(2) + [slots_of, slots_of, maps_of, maps_of],
        [whole((shards, rows, shard_width)), whole((1, width)), piece, piece],
        [split, jax.ShapeDtypeStruct((1, width), F32), pieces, pieces],
        [
            pltpu.VMEM((width, rows), BF), pltpu.VMEM((rows, width), F32),
            pltpu.VMEM((groups, full_rows, shard_width), BF),
        ],
    )(
        place, x, middle_grad, gain_one, grad_queries, grad_keys, grad_values,
        *([first_own, first_other] * 3), slot_query_grad, init_grad, key_map_grad, value_map_grad,
    )
    token_grad = lax.all_to_all(token_grad, "tp", 0, 0, tiled=True)

    vector_sums = [gain_one_grad, gain_two_grad, gate_grad.reshape(1, width), bias_grad]
    vector_rows = jnp.concatenate([item.reshape(-1) for item in vector_sums])
    vector_rows = jnp.pad(vector_rows, (0, 16 * shard_width - vector_rows.size)).astype(BF)
    vector_rows = jnp.broadcast_to(
        vector_rows.reshape(1, 1, 16, shard_width), (shards, pairs, 16, shard_width)
    )
    grad_own = lax.dynamic_update_slice(grad_own, vector_rows, (0, 0, at_vectors, 0))
    grad_other = lax.dynamic_update_slice(grad_other, vector_rows, (0, 0, at_vectors, 0))
    terms = scatter_pairs(grad_own, grad_other)
    terms, up_grad, down_grad, out_grad = lax.optimization_barrier(
        (terms, up_grad, down_grad, out_grad)
    )
    parts = (
        w_query, w_key, w_value, state_query, state_init, state_key, state_value,
        gain_attn, gain_mlp, gate_bias, bias_table,
    )
    sums = call(
        finish_kernel,
        (1,),
        [whole((full_rows, shard_width))] * shards,
        [whole(item.shape) for item in parts],
        [jax.ShapeDtypeStruct(item.shape, F32) for item in parts],
        [pltpu.VMEM((16, shard_width), F32)],
    )(place, *terms)
    return (
        output.reshape(seq_count, length, shard_width),
        token_grad.reshape(seq_count, length, shard_width),
        *sums[:3],
        out_grad,
        up_grad,
        down_grad,
        *sums[3:5],
        sums[7],
        sums[8],
        sums[10],
        sums[9],
        *sums[5:7],
    )


def choose(tokens, *others):
    shards = lax.axis_size("tp")
    even = tokens.shape[0] % shards == 0 and shards % 2 == 0 and shards & (shards - 1) == 0
    even = even and lax.axis_size("dp") == 4 and lax.axis_size("ctx") == 2
    return (sequence_body if even else body)(tokens, *others)


def solution(mesh):
    in_specs = (
        P("dp", "ctx", "tp"),
        P("dp", "ctx", None),
        P("dp"),
        P(("dp", "ctx"), "tp"),
        P(("dp", "ctx"), "tp"),
        P(("dp", "ctx"), "tp"),
        P("tp", ("dp", "ctx")),
        P(("dp", "ctx"), "tp"),
        P("tp", ("dp", "ctx")),
        P(("dp", "ctx"), "tp"),
        P(("dp", "ctx"), "tp"),
        P("tp", ("dp", "ctx")),
        P("tp", ("dp", "ctx")),
        P("tp", ("dp", "ctx")),
        P("tp", ("dp", "ctx")),
        P("tp", ("dp", "ctx"), None),
        P("tp", ("dp", "ctx"), None),
    )
    out_specs = (
        P("dp", "ctx", "tp"),
        P("dp", "ctx", "tp"),
        P(("dp", "ctx"), "tp"),
        P(("dp", "ctx"), "tp"),
        P(("dp", "ctx"), "tp"),
        P("tp", ("dp", "ctx")),
        P(("dp", "ctx"), "tp"),
        P("tp", ("dp", "ctx")),
        P(("dp", "ctx"), "tp"),
        P(("dp", "ctx"), "tp"),
        P("tp", ("dp", "ctx")),
        P("tp", ("dp", "ctx")),
        P("tp", ("dp", "ctx")),
        P("tp", ("dp", "ctx")),
        P("tp", ("dp", "ctx"), None),
        P("tp", ("dp", "ctx"), None),
    )
    return jax.shard_map(choose, mesh=mesh, in_specs=in_specs, out_specs=out_specs, check_vma=False)
```

```python
import functools

import jax
import jax.numpy as jnp
import numpy as np
from jax import lax
from jax.experimental import pallas as pl
from jax.experimental.pallas import tpu as pltpu
from jax.sharding import PartitionSpec as P

HEAD_SIZE = 128
BLOCK = 512


EPSILON = 1e-06
MASKED = -1e30
ROWS_FORWARD = 128
KEYS_BACKWARD = 256


def from_behind(value, axis, steps):
    count = lax.axis_size(axis)
    first, last = (max(0, -steps), min(count, count - steps))
    return lax.ppermute(value, axis, [(source, source + steps) for source in range(first, last)])


def prefix_2(array, axis, join, neutral, backward):
    count = lax.axis_size(axis)
    place = lax.axis_index(axis)
    ahead = count - 1 - place if backward else place
    gathered = jax.tree.map(
        lambda a, kind: lax.all_gather(a.astype(kind), axis), array, (jnp.bfloat16, jnp.bfloat16)
    )
    state = jax.tree.map(lambda a, e: jnp.zeros_like(a) + jnp.asarray(e, a.dtype), array, neutral)

    def one(hop, state):
        source = count - 1 - hop if backward else hop
        return join(
            state,
            jax.tree.map(
                lambda a, own: lax.dynamic_index_in_dim(a, source, 0, False).astype(own.dtype),
                gathered,
                array,
            ),
        )

    return lax.fori_loop(0, ahead, one, state)


def bucket_index(block_size):
    query_pos = np.arange(block_size)[:, None] + block_size
    key_pos = np.arange(2 * block_size)[None, :]
    distance = query_pos - key_pos
    upper_part = (distance < 0).astype(np.int32) * 16
    magnitude = np.abs(distance)
    scaled = np.log(np.maximum(magnitude, 1) / 8.0) / np.log(16.0) * 8.0
    far_bucket = np.minimum(8 + np.floor(np.maximum(scaled, 0.0)).astype(np.int32), 15)
    return (upper_part + np.where(magnitude < 8, magnitude, far_bucket)).astype(np.int32)


def norm_forward(features, gain_vector):
    inverse = lax.rsqrt(jnp.mean(features * features, axis=-1, keepdims=True) + EPSILON)
    normed = features * inverse
    return (normed, inverse, (normed * gain_vector).astype(jnp.bfloat16))


def norm_backward(grad_normed, normed, inverse, gain_vector):
    scaled = grad_normed * gain_vector
    grad_in = inverse * (scaled - normed * jnp.mean(scaled * normed, axis=-1, keepdims=True))
    return (grad_in, jnp.sum(grad_normed * normed, axis=0))


def compose(earlier, later_pair):
    return (earlier[0] * later_pair[0], later_pair[0] * earlier[1] + later_pair[1])


def bias_matrix(bias_rows, bucket):
    summed = jnp.zeros((bias_rows.shape[0],) + bucket.shape, jnp.float32)
    for number in range(bias_rows.shape[1]):
        summed = (
            summed
            + bias_rows[:, number][:, None, None] * (bucket == number).astype(jnp.float32)[None]
        )
    return summed


def bias_gradient(grad_matrix, bucket, bucket_count):
    columns = [
        jnp.sum(grad_matrix * (bucket == number).astype(jnp.float32)[None], axis=(1, 2))
        for number in range(bucket_count)
    ]
    return jnp.stack(columns, axis=1)


def body(
    tokens,
    cotangent,
    prefix,
    w_query,
    w_key,
    w_value,
    w_out,
    w_up,
    w_down,
    state_query,
    state_init,
    gain_attn,
    gain_mlp,
    bias_table,
    gate_bias,
    state_key,
    state_value,
):
    (
        query_full,
        key_full,
        value_full,
        out_full,
        up_full,
        down_full,
        squery_full,
        sinit_full,
        gain_one,
        gain_two,
        bias_rows,
        gate_rows,
        state_key_complete,
        svalue_full,
    ) = (
        lax.all_gather(w_query, ("dp", "ctx"), axis=0, tiled=True),
        lax.all_gather(w_key, ("dp", "ctx"), axis=0, tiled=True),
        lax.all_gather(w_value, ("dp", "ctx"), axis=0, tiled=True),
        lax.all_gather(w_out, ("dp", "ctx"), axis=1, tiled=True),
        lax.all_gather(w_up, ("dp", "ctx"), axis=0, tiled=True),
        lax.all_gather(w_down, ("dp", "ctx"), axis=1, tiled=True),
        lax.all_gather(state_query, ("dp", "ctx"), axis=0, tiled=True),
        lax.all_gather(state_init, ("dp", "ctx"), axis=0, tiled=True),
        lax.all_gather(gain_attn, ("dp", "ctx"), axis=1, tiled=True),
        lax.all_gather(gain_mlp, ("dp", "ctx"), axis=1, tiled=True),
        lax.all_gather(bias_table, ("dp", "ctx"), axis=1, tiled=True),
        lax.all_gather(gate_bias, ("dp", "ctx"), axis=1, tiled=True),
        lax.all_gather(state_key, ("dp", "ctx"), axis=1, tiled=True),
        lax.all_gather(state_value, ("dp", "ctx"), axis=1, tiled=True),
    )
    seq_count = tokens.shape[0]
    length = tokens.shape[1]
    shard_width = tokens.shape[2]
    full_width = cotangent.shape[2]
    block_count = length // BLOCK
    row_count = seq_count * length
    local_head_count = bias_rows.shape[0]
    local_width = local_head_count * HEAD_SIZE
    state_slot_count = squery_full.shape[0]
    scores_scale = HEAD_SIZE ** (-0.5)
    local_shape = (seq_count, block_count, BLOCK, local_head_count, HEAD_SIZE)
    element_count = seq_count * block_count
    token_full, gain_one_full = (
        lax.all_gather(tokens, "tp", axis=2, tiled=True),
        lax.all_gather(gain_one, "tp", axis=0, tiled=True),
    )
    gain_one_vec = gain_one_full.reshape(full_width).astype(jnp.float32)
    normed_one, inverse_one, attn_in = norm_forward(
        token_full.reshape(row_count, full_width).astype(jnp.float32), gain_one_vec
    )
    queries = (
        jnp.dot(attn_in, query_full, preferred_element_type=jnp.float32)
        .astype(jnp.bfloat16)
        .reshape(local_shape)
    )
    key_rows = (
        jnp.dot(attn_in, key_full, preferred_element_type=jnp.float32)
        .astype(jnp.bfloat16)
        .reshape(local_shape)
    )
    value_rows = (
        jnp.dot(attn_in, value_full, preferred_element_type=jnp.float32)
        .astype(jnp.bfloat16)
        .reshape(local_shape)
    )
    last_keys, last_values = from_behind((key_rows[:, -1], value_rows[:, -1]), "ctx", 1)
    window_keys = jnp.concatenate(
        [jnp.concatenate([last_keys[:, None], key_rows[:, :-1]], 1), key_rows], 2
    )
    window_values = jnp.concatenate(
        [jnp.concatenate([last_values[:, None], value_rows[:, :-1]], 1), value_rows], 2
    )
    query_heads = squery_full.reshape(state_slot_count, local_head_count, HEAD_SIZE)
    read_scores = (
        jnp.einsum("mhe,sbthe->sbhmt", query_heads, key_rows, preferred_element_type=jnp.float32)
        * scores_scale
    )
    read_peak = jnp.max(read_scores, axis=-1, keepdims=True)
    read_raised = jnp.exp(read_scores - read_peak)
    read_probs = read_raised / jnp.sum(read_raised, axis=-1, keepdims=True)
    read_low = read_probs.astype(jnp.bfloat16)
    contrib = jnp.einsum(
        "sbhmt,sbthe->sbmhe", read_low, value_rows, preferred_element_type=jnp.float32
    )
    contrib = contrib.reshape(seq_count, block_count, state_slot_count, local_width)
    gate_value = jax.nn.sigmoid(gate_rows.reshape(local_width).astype(jnp.float32))
    gate_power = jnp.ones((local_width,), jnp.float32)
    accumulated = jnp.zeros((seq_count, state_slot_count, local_width), jnp.float32)
    for block_index in range(block_count):
        accumulated = gate_value * accumulated + (1.0 - gate_value) * contrib[:, block_index]
        gate_power = gate_power * gate_value
    identity = (jnp.ones((local_width,), jnp.float32), jnp.zeros_like(accumulated))
    lead_power, lead_state = prefix_2((gate_power, accumulated), "ctx", compose, identity, False)
    entry_state = lead_power * sinit_full.astype(jnp.float32) + lead_state
    state_list = [entry_state]
    block_index = 0
    state_list.append(gate_value * state_list[-1] + (1.0 - gate_value) * contrib[:, block_index])
    stacked = jnp.stack(state_list, axis=1)
    state_reduced = stacked.astype(jnp.bfloat16).reshape(
        seq_count, block_count, state_slot_count, local_head_count, HEAD_SIZE
    )
    state_key_rows = jnp.einsum(
        "cazqr,qrx->cazqx", state_reduced, state_key_complete, preferred_element_type=jnp.float32
    ).astype(jnp.bfloat16)
    state_values = jnp.einsum(
        "cazqr,qrx->cazqx", state_reduced, svalue_full, preferred_element_type=jnp.float32
    ).astype(jnp.bfloat16)
    bucket = jnp.asarray(bucket_index(BLOCK))
    bias_full = bias_matrix(bias_rows.astype(jnp.float32), bucket)
    block_ids = lax.axis_index("ctx") * block_count + jnp.arange(block_count, dtype=jnp.int32)
    query_pos = block_ids[:, None] * BLOCK + jnp.arange(BLOCK, dtype=jnp.int32)[None, :]
    key_pos = (block_ids[:, None] - 1) * BLOCK + jnp.arange(2 * BLOCK, dtype=jnp.int32)[None, :]
    causal = (key_pos[:, None, :] >= 0) & (key_pos[:, None, :] <= query_pos[:, :, None])
    in_prefix = (key_pos[None, :, None, :] >= 0) & (
        key_pos[None, :, None, :] < prefix[:, None, None, None]
    )
    permitted_mask = (causal[None] | in_prefix).reshape(element_count, 1, BLOCK, 2 * BLOCK)
    flattened_queries = queries.reshape(element_count, BLOCK, local_head_count, HEAD_SIZE)
    flattened_window_keys = window_keys.reshape(
        element_count, 2 * BLOCK, local_head_count, HEAD_SIZE
    )
    flattened_window_values = window_values.reshape(
        element_count, 2 * BLOCK, local_head_count, HEAD_SIZE
    )
    flattened_state_keys = state_key_rows.reshape(
        element_count, state_slot_count, local_head_count, HEAD_SIZE
    )
    flattened_state_values = state_values.reshape(
        element_count, state_slot_count, local_head_count, HEAD_SIZE
    )

    def block_score_rows(
        block_query_rows, block_window_key_rows, block_state_key_rows, block_permitted_mask
    ):
        window_part = (
            jnp.einsum(
                "ihe,jhe->hij",
                block_query_rows,
                block_window_key_rows,
                preferred_element_type=jnp.float32,
            )
            * scores_scale
            + bias_full
        )
        state_part = (
            jnp.einsum(
                "yat,zat->ayz",
                block_query_rows,
                block_state_key_rows,
                preferred_element_type=jnp.float32,
            )
            * scores_scale
        )
        return (jnp.where(block_permitted_mask, window_part, MASKED), state_part)

    def attend_one_block(element_entry):
        (
            block_query_rows,
            block_window_key_rows,
            block_window_value_rows,
            block_state_key_rows,
            block_state_value_rows,
            block_permitted_mask,
        ) = element_entry
        window_scores, scores_of_state = block_score_rows(
            block_query_rows, block_window_key_rows, block_state_key_rows, block_permitted_mask
        )
        row_peak = jnp.maximum(jnp.max(window_scores, axis=-1), jnp.max(scores_of_state, axis=-1))
        window_raised = jnp.exp(window_scores - row_peak[..., None])
        state_raised = jnp.exp(scores_of_state - row_peak[..., None])
        denominator = jnp.sum(window_raised, axis=-1) + jnp.sum(state_raised, axis=-1)
        log_total = row_peak + jnp.log(denominator)
        window_probs = (window_raised / denominator[..., None]).astype(jnp.bfloat16)
        state_probs = (state_raised / denominator[..., None]).astype(jnp.bfloat16)
        block_out = jnp.einsum(
            "hij,jhe->ihe",
            window_probs,
            block_window_value_rows,
            preferred_element_type=jnp.float32,
        ) + jnp.einsum(
            "wyd,dwg->ywg", state_probs, block_state_value_rows, preferred_element_type=jnp.float32
        )
        return (block_out.astype(jnp.bfloat16), log_total)

    attended_blocks, log_totals = lax.map(
        attend_one_block,
        (
            flattened_queries,
            flattened_window_keys,
            flattened_window_values,
            flattened_state_keys,
            flattened_state_values,
            permitted_mask,
        ),
    )
    attended = attended_blocks.reshape(row_count, local_width)
    attn_part = jnp.dot(attended, out_full, preferred_element_type=jnp.float32).reshape(
        seq_count, length, full_width
    )
    attn_share = lax.psum_scatter(
        attn_part.astype(jnp.bfloat16), "tp", scatter_dimension=2, tiled=True
    ).astype(jnp.float32)
    middle = tokens.astype(jnp.float32) + attn_share
    middle_full, gain_two_full = (
        lax.all_gather(middle.astype(jnp.bfloat16), "tp", axis=2, tiled=True),
        lax.all_gather(gain_two, "tp", axis=0, tiled=True),
    )
    gain_two_vec = gain_two_full.reshape(full_width).astype(jnp.float32)
    normed_two, inverse_two, mlp_in = norm_forward(
        middle_full.reshape(row_count, full_width).astype(jnp.float32), gain_two_vec
    )
    hidden_pre = jnp.dot(mlp_in, up_full, preferred_element_type=jnp.float32)
    hidden = jax.nn.gelu(hidden_pre, approximate=False).astype(jnp.bfloat16)
    mlp_part = jnp.dot(hidden, down_full, preferred_element_type=jnp.float32).reshape(
        seq_count, length, full_width
    )
    mlp_share = lax.psum_scatter(
        mlp_part.astype(jnp.bfloat16), "tp", scatter_dimension=2, tiled=True
    ).astype(jnp.float32)
    output = (middle + mlp_share).astype(jnp.bfloat16)
    grad_out = cotangent.reshape(row_count, full_width)
    grad_hidden = jnp.dot(grad_out, down_full.T, preferred_element_type=jnp.float32)
    grad_down = jnp.dot(hidden.T, grad_out, preferred_element_type=jnp.float32)

    def gelu_exact(pre_values):
        return jax.nn.gelu(pre_values, approximate=False)

    gelu_value, gelu_back = jax.vjp(gelu_exact, hidden_pre)
    grad_pre = gelu_back(grad_hidden)[0].astype(jnp.bfloat16)
    grad_up = jnp.dot(mlp_in.T, grad_pre, preferred_element_type=jnp.float32)
    grad_mlp_in = jnp.dot(grad_pre, up_full.T, preferred_element_type=jnp.float32)
    part_middle, part_gain_two = norm_backward(grad_mlp_in, normed_two, inverse_two, gain_two_vec)
    tp_index = lax.axis_index("tp")
    head_total = full_width // HEAD_SIZE
    summed, gain_two_sum = (
        lax.psum(
            part_middle.reshape(seq_count, length, full_width).astype(jnp.bfloat16), "tp"
        ).astype(jnp.float32),
        lax.psum(part_gain_two.reshape(head_total, HEAD_SIZE).astype(jnp.bfloat16), "tp").astype(
            jnp.float32
        ),
    )
    middle_grad_full = cotangent.astype(jnp.float32) + summed
    middle_grad = lax.dynamic_slice_in_dim(middle_grad_full, tp_index * shard_width, shard_width, 2)
    grad_gain_two = lax.dynamic_slice_in_dim(
        gain_two_sum, tp_index * local_head_count, local_head_count, 0
    )
    middle_grad_low = middle_grad_full.astype(jnp.bfloat16)
    middle_grad_rows = middle_grad_low.reshape(row_count, full_width)
    grad_attended = jnp.dot(
        middle_grad_rows, out_full.T, preferred_element_type=jnp.float32
    ).astype(jnp.bfloat16)
    grad_attended = grad_attended.reshape(element_count, BLOCK, local_head_count, HEAD_SIZE)
    grad_wout = jnp.dot(attended.T, middle_grad_rows, preferred_element_type=jnp.float32)

    def attend_back(bias_sum, element_entry):
        (
            block_query_rows,
            block_window_key_rows,
            block_window_value_rows,
            block_state_key_rows,
            block_state_value_rows,
            block_permitted_mask,
            block_lse,
            block_grad,
        ) = element_entry
        window_again, state_again = block_score_rows(
            block_query_rows, block_window_key_rows, block_state_key_rows, block_permitted_mask
        )
        window_exact = jnp.exp(window_again - block_lse[..., None])
        state_exact = jnp.exp(state_again - block_lse[..., None])
        grad_wprob = jnp.einsum(
            "ihe,jhe->hij", block_grad, block_window_value_rows, preferred_element_type=jnp.float32
        )
        grad_sprob = jnp.einsum(
            "yat,zat->ayz", block_grad, block_state_value_rows, preferred_element_type=jnp.float32
        )
        row_delta = jnp.sum(window_exact * grad_wprob, axis=-1) + jnp.sum(
            state_exact * grad_sprob, axis=-1
        )
        grad_wscore = (window_exact * (grad_wprob - row_delta[..., None])).astype(jnp.bfloat16)
        state_score_gradient = (state_exact * (grad_sprob - row_delta[..., None])).astype(
            jnp.bfloat16
        )
        block_grad_q = scores_scale * (
            jnp.einsum(
                "hij,jhe->ihe",
                grad_wscore,
                block_window_key_rows,
                preferred_element_type=jnp.float32,
            )
            + jnp.einsum(
                "wyd,dwg->ywg",
                state_score_gradient,
                block_state_key_rows,
                preferred_element_type=jnp.float32,
            )
        )
        block_grad_wk = scores_scale * jnp.einsum(
            "hij,ihe->jhe", grad_wscore, block_query_rows, preferred_element_type=jnp.float32
        )
        block_grad_wv = jnp.einsum(
            "hij,ihe->jhe",
            window_exact.astype(jnp.bfloat16),
            block_grad,
            preferred_element_type=jnp.float32,
        )
        block_grad_sk = (
            scores_scale
            * jnp.einsum(
                "him,ihe->mhe",
                state_score_gradient,
                block_query_rows,
                preferred_element_type=jnp.float32,
            )
        ).astype(jnp.bfloat16)
        block_grad_sv = jnp.einsum(
            "him,ihe->mhe",
            state_exact.astype(jnp.bfloat16),
            block_grad,
            preferred_element_type=jnp.float32,
        ).astype(jnp.bfloat16)
        return (
            bias_sum + grad_wscore.astype(jnp.float32),
            (block_grad_q, block_grad_wk, block_grad_wv, block_grad_sk, block_grad_sv),
        )

    bias_start = jnp.zeros((local_head_count, BLOCK, 2 * BLOCK), jnp.float32)
    bias_sum, back_items = lax.scan(
        attend_back,
        bias_start,
        (
            flattened_queries,
            flattened_window_keys,
            flattened_window_values,
            flattened_state_keys,
            flattened_state_values,
            permitted_mask,
            log_totals,
            grad_attended,
        ),
    )
    grad_bias = bias_gradient(bias_sum, bucket, bias_rows.shape[1])
    grad_queries = back_items[0].reshape(local_shape)
    grad_window_keys = back_items[1].reshape(
        seq_count, block_count, 2 * BLOCK, local_head_count, HEAD_SIZE
    )
    grad_window_values = back_items[2].reshape(
        seq_count, block_count, 2 * BLOCK, local_head_count, HEAD_SIZE
    )
    state_keys_gradient = back_items[3].reshape(
        seq_count, block_count, state_slot_count, local_head_count, HEAD_SIZE
    )
    grad_state_values = back_items[4].reshape(
        seq_count, block_count, state_slot_count, local_head_count, HEAD_SIZE
    )
    back_keys, back_values = (
        from_behind(grad_window_keys[:, 0, :BLOCK].astype(jnp.bfloat16), "ctx", -1).astype(
            jnp.float32
        ),
        from_behind(grad_window_values[:, 0, :BLOCK].astype(jnp.bfloat16), "ctx", -1).astype(
            jnp.float32
        ),
    )
    key_grad = grad_window_keys[:, :, BLOCK:] + jnp.concatenate(
        [grad_window_keys[:, 1:, :BLOCK], back_keys[:, None]], 1
    )
    value_grad = grad_window_values[:, :, BLOCK:] + jnp.concatenate(
        [grad_window_values[:, 1:, :BLOCK], back_values[:, None]], 1
    )
    state_key_gradient = jnp.einsum(
        "sbmhe,sbmhf->hef", state_reduced, state_keys_gradient, preferred_element_type=jnp.float32
    )
    grad_svalue = jnp.einsum(
        "sbmhe,sbmhf->hef", state_reduced, grad_state_values, preferred_element_type=jnp.float32
    )
    direct = jnp.einsum(
        "palcq,crq->palcr",
        state_keys_gradient,
        state_key_complete,
        preferred_element_type=jnp.float32,
    ) + jnp.einsum(
        "palcq,crq->palcr", grad_state_values, svalue_full, preferred_element_type=jnp.float32
    )
    direct = direct.reshape(seq_count, block_count, state_slot_count, local_width)
    back_accum = jnp.zeros((seq_count, state_slot_count, local_width), jnp.float32)
    for block_index in reversed(range(block_count)):
        back_accum = direct[:, block_index] + gate_value * back_accum
    back_identity = (jnp.ones((local_width,), jnp.float32), jnp.zeros_like(back_accum))
    unused_power, incoming = prefix_2((gate_power, back_accum), "ctx", compose, back_identity, True)
    carried = incoming
    contrib_grads = [None] * block_count
    gate_grad = jnp.zeros((local_width,), jnp.float32)
    for block_index in reversed(range(block_count)):
        contrib_grads[block_index] = ((1.0 - gate_value) * carried).astype(jnp.bfloat16)
        gate_grad = gate_grad + jnp.sum(
            carried * (stacked[:, block_index] - contrib[:, block_index]), axis=(0, 1)
        )
        carried = direct[:, block_index] + gate_value * carried
    first_device = (lax.axis_index("ctx") == 0).astype(jnp.float32)
    grad_sinit = first_device * jnp.sum(carried, axis=0)
    grad_gate = (gate_grad * gate_value * (1.0 - gate_value)).reshape(local_head_count, HEAD_SIZE)
    grad_contrib = jnp.stack(contrib_grads, axis=1).reshape(
        seq_count, block_count, state_slot_count, local_head_count, HEAD_SIZE
    )
    grad_read = jnp.einsum(
        "sbmhe,sbthe->sbhmt", grad_contrib, value_rows, preferred_element_type=jnp.float32
    )
    extra_values = jnp.einsum(
        "sbhmt,sbmhe->sbthe", read_low, grad_contrib, preferred_element_type=jnp.float32
    )
    read_delta = jnp.sum(read_probs * grad_read, axis=-1, keepdims=True)
    grad_read_score = (read_probs * (grad_read - read_delta)).astype(jnp.bfloat16)
    grad_squery = (
        scores_scale
        * jnp.einsum(
            "sbhmt,sbthe->mhe", grad_read_score, key_rows, preferred_element_type=jnp.float32
        )
    ).reshape(state_slot_count, local_width)
    extra_keys = scores_scale * jnp.einsum(
        "sbhmt,mhe->sbthe", grad_read_score, query_heads, preferred_element_type=jnp.float32
    )
    grad_q_rows = grad_queries.astype(jnp.bfloat16).reshape(row_count, local_width)
    grad_k_rows = (key_grad + extra_keys).astype(jnp.bfloat16).reshape(row_count, local_width)
    grad_v_rows = (value_grad + extra_values).astype(jnp.bfloat16).reshape(row_count, local_width)
    grad_wq = jnp.dot(attn_in.T, grad_q_rows, preferred_element_type=jnp.float32)
    grad_wk = jnp.dot(attn_in.T, grad_k_rows, preferred_element_type=jnp.float32)
    grad_wv = jnp.dot(attn_in.T, grad_v_rows, preferred_element_type=jnp.float32)
    grad_attn_in = (
        jnp.dot(grad_q_rows, query_full.T, preferred_element_type=jnp.float32)
        + jnp.dot(grad_k_rows, key_full.T, preferred_element_type=jnp.float32)
        + jnp.dot(grad_v_rows, value_full.T, preferred_element_type=jnp.float32)
    )
    part_tokens, part_gain_one = norm_backward(grad_attn_in, normed_one, inverse_one, gain_one_vec)
    token_share, grad_gain_one = (
        lax.psum_scatter(
            part_tokens.reshape(seq_count, length, full_width).astype(jnp.bfloat16),
            "tp",
            scatter_dimension=2,
            tiled=True,
        ).astype(jnp.float32),
        lax.psum_scatter(
            part_gain_one.reshape(head_total, HEAD_SIZE).astype(jnp.bfloat16),
            "tp",
            scatter_dimension=0,
            tiled=True,
        ).astype(jnp.float32),
    )
    grad_tokens = (middle_grad + token_share).astype(jnp.bfloat16)
    grads = (
        lax.psum_scatter(
            grad_wq.astype(jnp.bfloat16), ("dp", "ctx"), scatter_dimension=0, tiled=True
        ).astype(jnp.float32),
        lax.psum_scatter(
            grad_wk.astype(jnp.bfloat16), ("dp", "ctx"), scatter_dimension=0, tiled=True
        ).astype(jnp.float32),
        lax.psum_scatter(
            grad_wv.astype(jnp.bfloat16), ("dp", "ctx"), scatter_dimension=0, tiled=True
        ).astype(jnp.float32),
        lax.psum_scatter(
            grad_wout.astype(jnp.bfloat16), ("dp", "ctx"), scatter_dimension=1, tiled=True
        ).astype(jnp.float32),
        lax.psum_scatter(
            grad_up.astype(jnp.bfloat16), ("dp", "ctx"), scatter_dimension=0, tiled=True
        ).astype(jnp.float32),
        lax.psum_scatter(
            grad_down.astype(jnp.bfloat16), ("dp", "ctx"), scatter_dimension=1, tiled=True
        ).astype(jnp.float32),
        lax.psum_scatter(
            grad_squery.astype(jnp.bfloat16), ("dp", "ctx"), scatter_dimension=0, tiled=True
        ).astype(jnp.float32),
        lax.psum_scatter(
            grad_sinit.astype(jnp.bfloat16), ("dp", "ctx"), scatter_dimension=0, tiled=True
        ).astype(jnp.float32),
        lax.psum_scatter(
            grad_gain_one.astype(jnp.bfloat16), ("dp", "ctx"), scatter_dimension=1, tiled=True
        ).astype(jnp.float32),
        lax.psum_scatter(
            grad_gain_two.astype(jnp.bfloat16), ("dp", "ctx"), scatter_dimension=1, tiled=True
        ).astype(jnp.float32),
        lax.psum_scatter(
            grad_bias.astype(jnp.bfloat16), ("dp", "ctx"), scatter_dimension=1, tiled=True
        ).astype(jnp.float32),
        lax.psum_scatter(
            grad_gate.astype(jnp.bfloat16), ("dp", "ctx"), scatter_dimension=1, tiled=True
        ).astype(jnp.float32),
        lax.psum_scatter(
            state_key_gradient.astype(jnp.bfloat16), ("dp", "ctx"), scatter_dimension=1, tiled=True
        ).astype(jnp.float32),
        lax.psum_scatter(
            grad_svalue.astype(jnp.bfloat16), ("dp", "ctx"), scatter_dimension=1, tiled=True
        ).astype(jnp.float32),
    )
    return (
        output,
        grad_tokens,
        grads[0],
        grads[1],
        grads[2],
        grads[3],
        grads[4],
        grads[5],
        grads[6],
        grads[7],
        grads[8],
        grads[9],
        grads[10],
        grads[11],
        grads[12],
        grads[13],
    )


LOG2E = 1.4426950408889634
VMEM_BYTES = 58 * 1024 * 1024
BF = jnp.bfloat16
F32 = jnp.float32


def nn(left, right):
    return jnp.dot(left, right, preferred_element_type=F32)


def nt(left, right):
    return lax.dot_general(left, right, (((1,), (1,)), ((), ())), preferred_element_type=F32)


def tn(left, right):
    return lax.dot_general(left, right, (((0,), (0,)), ((), ())), preferred_element_type=F32)


def flat(ref):
    block = ref[0]
    return block.reshape(block.shape[0] * block.shape[1], block.shape[2])


def merged(place_ref, own_ref, other_ref):
    own = own_ref[0, :, 0]
    other = other_ref[0, :, 0]
    is_first = place_ref[0] == 0
    pair = [jnp.where(is_first, own, other), jnp.where(is_first, other, own)]
    block = jnp.stack(pair, axis=1)
    return block.reshape(-1, block.shape[-1])


def joined(tok_ref):
    return jnp.concatenate([tok_ref[part] for part in range(tok_ref.shape[0])], axis=1).astype(F32)


def inverse_rms(x):
    return lax.rsqrt(jnp.mean(x * x, axis=-1, keepdims=True) + EPSILON)


def params():
    return pltpu.CompilerParams(vmem_limit_bytes=VMEM_BYTES)


def project_kernel(
    place_ref, tok_ref, gain_ref, wq_ref, wqo_ref, wk_ref, wko_ref, wv_ref, wvo_ref,
    q_ref, k_ref, v_ref, ain_ref, last_ref,
):
    @pl.when(pl.program_id(0) == 0)
    def _():
        x = joined(tok_ref)
        ain_ref[...] = (x * inverse_rms(x) * gain_ref[...]).astype(BF)

    a = ain_ref[...]
    for w_ref, w_other, o_ref in (
        (wq_ref, wqo_ref, q_ref), (wk_ref, wko_ref, k_ref), (wv_ref, wvo_ref, v_ref)
    ):
        o_ref[...] = nn(a, merged(place_ref, w_ref, w_other)).astype(BF)
    length = k_ref.shape[0] * BLOCK // last_ref.shape[1]
    for item in range(last_ref.shape[1] // BLOCK):
        last = slice((item + 1) * length - BLOCK, (item + 1) * length)
        last_ref[0, item * BLOCK : (item + 1) * BLOCK] = k_ref[last]
        last_ref[1, item * BLOCK : (item + 1) * BLOCK] = v_ref[last]


def read_kernel(
    place_ref, sq_ref, sqo_ref, k_ref, v_ref, gate_ref, o_ref, sum_ref, state_ref, *, blocks
):
    n = pl.program_id(1)
    sq = merged(place_ref, sq_ref, sqo_ref)
    k = k_ref[...]
    v = v_ref[...]
    scale = HEAD_SIZE ** (-0.5) * LOG2E
    step = 256
    gate = jnp.where(lax.rem(n, blocks) == 0, 0.0, gate_ref[...])
    fresh = 1.0 - gate_ref[...]

    @pl.when(n == 0)
    def _():
        state_ref[...] = jnp.zeros_like(state_ref)

    for start in range(0, sq.shape[0], step):
        rows = slice(start, start + step)
        s = nt(sq[rows], k) * scale
        p = jnp.exp2(s - jnp.max(s, axis=-1, keepdims=True))
        total = jnp.sum(p, axis=-1, keepdims=True)
        contrib = nn(p.astype(BF), v) / total
        o_ref[rows, :] = contrib
        state = gate * state_ref[rows, :] + fresh * contrib
        state_ref[rows, :] = state
        sum_ref[rows, :] = state.astype(BF)


def attend_kernel(
    place_ref, info_ref, q_ref, k_ref, v_ref, kp_ref, vp_ref, hk_ref, hv_ref,
    wk_ref, wko_ref, wv_ref, wvo_ref, contrib_ref, init_ref, inito_ref, lead_ref, power_ref,
    gate_ref, u_ref, o_ref, lse_ref, low_ref, moved_ref, bias_ref, state_ref, *, blocks,
):
    n = pl.program_id(1)
    first = lax.rem(n, blocks) == 0
    scale = HEAD_SIZE ** (-0.5) * LOG2E

    @pl.when(n == 0)
    def _():
        row = jnp.broadcast_to(u_ref[0], (BLOCK, u_ref.shape[-1]))
        bias_ref[...] = pltpu.roll(row, 0, 1, stride=1, stride_axis=0)[:, : 2 * BLOCK]

    has_previous = info_ref[n, 0] > 0
    reach = info_ref[n, 1]
    k = k_ref[...]
    v = v_ref[...]
    kp = jnp.where(first, hk_ref[...], kp_ref[...])
    vp = jnp.where(first, hv_ref[...], vp_ref[...])

    @pl.when(first)
    def _():
        init = merged(place_ref, init_ref, inito_ref).astype(F32)
        state_ref[...] = power_ref[...] * init + lead_ref[...].astype(F32)

    state = state_ref[...]
    contrib = contrib_ref[...]
    st = state.astype(BF)
    low_ref[...] = st
    moved_ref[...] = (state - contrib).astype(BF)
    state_ref[...] = contrib + gate_ref[...] * (state - contrib)
    sk = nn(st, merged(place_ref, wk_ref, wko_ref)).astype(BF)
    sv = nn(st, merged(place_ref, wv_ref, wvo_ref)).astype(BF)
    step = ROWS_FORWARD

    def run(with_previous):
        for start in range(0, BLOCK, step):
            q = q_ref[start : start + step, :]
            sc = nt(q, k) * scale + bias_ref[start : start + step, BLOCK:]
            row = lax.broadcasted_iota(jnp.int32, (step, 1), 0) + start
            column = lax.broadcasted_iota(jnp.int32, (step, BLOCK), 1)
            sc = jnp.where(column <= jnp.maximum(row, reach - 1), sc, MASKED)
            ss = nt(q, sk) * scale
            peak = jnp.maximum(
                jnp.max(sc, axis=-1, keepdims=True), jnp.max(ss, axis=-1, keepdims=True)
            )
            if with_previous:
                sp = nt(q, kp) * scale + bias_ref[start : start + step, :BLOCK]
                peak = jnp.maximum(peak, jnp.max(sp, axis=-1, keepdims=True))
            pc = jnp.exp2(sc - peak)
            ps = jnp.exp2(ss - peak)
            total = jnp.sum(pc, axis=-1, keepdims=True) + jnp.sum(ps, axis=-1, keepdims=True)
            out = nn(pc.astype(BF), v) + nn(ps.astype(BF), sv)
            if with_previous:
                pp = jnp.exp2(sp - peak)
                total = total + jnp.sum(pp, axis=-1, keepdims=True)
                out = out + nn(pp.astype(BF), vp)
            o_ref[start : start + step, :] = (out / total).astype(BF)
            lse = jnp.broadcast_to(peak + jnp.log2(total), (step, 128))
            lse_ref[0, 0, :, start : start + step] = lse.T[:1]

    @pl.when(has_previous)
    def _():
        run(True)

    @pl.when(jnp.logical_not(has_previous))
    def _():
        run(False)


def attend_back_kernel(
    place_ref, info_ref, q_ref, k_ref, v_ref, kp_ref, vp_ref, hk_ref, hv_ref,
    wk_ref, wko_ref, wv_ref, wvo_ref, st_ref, gate_ref, u_ref, do_ref, o_ref, lse_ref,
    dq_ref, dk_ref, dv_ref, dkp_ref, dvp_ref, direct_ref, gwk_ref, gwv_ref, gb_ref, total_ref,
    firstk_ref, firstv_ref, bias_ref, sum_ref, dq_acc, state_acc, *, blocks,
):
    step_at = pl.program_id(1)
    n = pl.num_programs(1) - 1 - step_at
    first = lax.rem(n, blocks) == 0
    gate = jnp.where(lax.rem(n, blocks) == blocks - 1, 0.0, gate_ref[...])
    factor = HEAD_SIZE ** (-0.5)
    scale = factor * LOG2E
    window = 2 * BLOCK
    width = BLOCK + window

    @pl.when(step_at == 0)
    def _():
        state_acc[...] = jnp.zeros_like(state_acc)
        row = jnp.broadcast_to(u_ref[0], (window, u_ref.shape[-1]))
        bias_ref[...] = pltpu.roll(row, 0, 1, stride=1, stride_axis=0)[:, :BLOCK]
        sum_ref[...] = jnp.zeros_like(sum_ref)
        gwk_ref[...] = jnp.zeros_like(gwk_ref)
        gwv_ref[...] = jnp.zeros_like(gwv_ref)

    has_previous = info_ref[n, 0] > 0
    reach = info_ref[n, 1]
    q = q_ref[...]
    do = do_ref[...]
    lse = lse_ref[0, 0]
    delta = jnp.sum((do.astype(F32) * o_ref[...].astype(F32)).T, axis=0, keepdims=True)
    step = KEYS_BACKWARD

    def part(key, value, start, bias_start, masked):
        s = nt(key, q) * scale
        if bias_start is not None:
            s = s + bias_ref[bias_start : bias_start + step, :]
        if masked:
            key_at = lax.broadcasted_iota(jnp.int32, (step, BLOCK), 0) + start
            query_at = lax.broadcasted_iota(jnp.int32, (1, BLOCK), 1)
            s = jnp.where(key_at <= jnp.maximum(query_at, reach - 1), s, MASKED)
        p = jnp.exp2(s - lse)
        dp = nt(value, do)
        ds = (p * (dp - delta)).astype(BF)
        if bias_start is not None:
            for block in range(0, step, 128):
                at = window - bias_start - block
                sum_ref[:, at : at + BLOCK] += ds[block : block + 128].astype(F32)
        dq_acc[...] += tn(ds, key)
        return nn(ds, q) * factor, nn(p.astype(BF), do)

    dq_acc[...] = jnp.zeros_like(dq_acc)
    st = st_ref[...]
    key_map = merged(place_ref, wk_ref, wko_ref)
    value_map = merged(place_ref, wv_ref, wvo_ref)
    sk = nn(st, key_map).astype(BF)
    sv = nn(st, value_map).astype(BF)
    for start in range(0, st.shape[0], step):
        rows = slice(start, start + step)
        dk, dv = part(sk[rows], sv[rows], start, None, False)
        dk = dk.astype(BF)
        dv = dv.astype(BF)
        direct = nt(dk, key_map) + nt(dv, value_map)
        direct_ref[rows, :] = direct
        state = direct + gate * state_acc[rows, :]
        state_acc[rows, :] = state
        total_ref[rows, :] = state.astype(BF)
        gwk_ref[0] += tn(st[rows], dk)
        gwv_ref[0] += tn(st[rows], dv)
    for start in range(0, BLOCK, step):
        rows = slice(start, start + step)
        dk, dv = part(k_ref[rows, :], v_ref[rows, :], start, BLOCK + start, True)
        dk_ref[rows, :] = dk
        dv_ref[rows, :] = dv

    @pl.when(has_previous)
    def _():
        for start in range(0, BLOCK, step):
            rows = slice(start, start + step)
            key = jnp.where(first, hk_ref[rows, :], kp_ref[rows, :])
            value = jnp.where(first, hv_ref[rows, :], vp_ref[rows, :])
            dk, dv = part(key, value, start, start, False)
            dkp_ref[rows, :] = dk.astype(BF)
            dvp_ref[rows, :] = dv.astype(BF)

    @pl.when(jnp.logical_not(has_previous))
    def _():
        dkp_ref[...] = jnp.zeros_like(dkp_ref)
        dvp_ref[...] = jnp.zeros_like(dvp_ref)

    @pl.when(first)
    def _():
        firstk_ref[...] = dkp_ref[...]
        firstv_ref[...] = dvp_ref[...]

    dq_ref[...] = (dq_acc[...] * factor).astype(BF)

    @pl.when(n == 0)
    def _():
        folded = sum_ref[...]
        half = 64
        while half >= 8:
            folded = folded[:half] + pltpu.roll(folded[half:], width - half, 1)
            half //= 2
        total = folded[:1]
        for row in range(1, 8):
            total = total + pltpu.roll(folded[row : row + 1], width - row, 1)
        gb_ref[0] = total


def read_back_kernel(
    place_ref, sq_ref, sqo_ref, k_ref, v_ref, direct_ref, moved_ref, later_ref, gate_ref,
    dk_ref, dv_ref, nk_ref, nv_ref, rk_ref, rv_ref,
    gk_ref, gv_ref, gsq_ref, ginit_ref, ggate_ref, carried_ref, *, blocks,
):
    step_at = pl.program_id(1)
    n = pl.num_programs(1) - 1 - step_at
    last = lax.rem(n, blocks) == blocks - 1
    factor = HEAD_SIZE ** (-0.5)

    @pl.when(step_at == 0)
    def _():
        gsq_ref[...] = jnp.zeros_like(gsq_ref)
        ginit_ref[...] = jnp.zeros_like(ginit_ref)
        ggate_ref[...] = jnp.zeros_like(ggate_ref)

    @pl.when(last)
    def _():
        carried_ref[...] = later_ref[...].astype(F32)

    gate = gate_ref[...]
    carried = carried_ref[...]
    gc = ((1.0 - gate) * carried).astype(BF)
    change = jnp.sum(carried * moved_ref[...].astype(F32), axis=0, keepdims=True)
    ggate_ref[0] += change * (gate * (1.0 - gate))
    carried = direct_ref[...] + gate * carried
    carried_ref[...] = carried

    @pl.when((lax.rem(n, blocks) == 0) & (place_ref[0] == 0))
    def _():
        ginit_ref[...] += carried

    sq = merged(place_ref, sq_ref, sqo_ref)
    k = k_ref[...]
    s = nt(k, sq) * (factor * LOG2E)
    p = jnp.exp2(s - jnp.max(s, axis=0, keepdims=True))
    p = p * (1.0 / jnp.sum(p, axis=0, keepdims=True))
    dp = nt(v_ref[...], gc)
    ds = (p * (dp - jnp.sum(p * dp, axis=0, keepdims=True))).astype(BF)
    next_k = jnp.where(last, rk_ref[...], nk_ref[...]).astype(F32)
    next_v = jnp.where(last, rv_ref[...], nv_ref[...]).astype(F32)
    gk_ref[...] = (dk_ref[...] + next_k + nn(ds, sq) * factor).astype(BF)
    gv_ref[...] = (dv_ref[...] + next_v + nn(p.astype(BF), gc)).astype(BF)
    gsq_ref[...] += tn(ds, k) * factor


def item_kernel(wq_ref, wk_ref, wv_ref, sq_ref, init_ref, mk_ref, mv_ref, tail_ref, out_ref):
    at = 0
    for w_ref in (wq_ref, wk_ref, wv_ref, sq_ref, init_ref):
        out_ref[at : at + w_ref.shape[0]] = w_ref[...]
        at += w_ref.shape[0]
    for w_ref in (mk_ref, mv_ref):
        heads, rows, lanes = w_ref.shape
        for item in range(heads):
            out_ref[at : at + rows, item * lanes : (item + 1) * lanes] = w_ref[item]
        at += rows
    out_ref[at:] = tail_ref[...]


def assemble_kernel(place_ref, low_ref, lowy_ref, high_ref, highx_ref, own_ref):
    x_bit = place_ref[3]
    y_bit = place_ref[4]
    for x in range(2):
        own_ref[0, 2 * y_bit + x] = low_ref[x]
        own_ref[0, 2 * (1 - y_bit) + x] = lowy_ref[x]
    for y in range(2):
        own_ref[1, 2 * y + x_bit] = high_ref[y]
        own_ref[1, 2 * y + 1 - x_bit] = highx_ref[y]


def pack_kernel(up_ref, down_ref, out_ref, packed_ref):
    hidden = up_ref.shape[1]
    packed_ref[:, :hidden] = up_ref[...]
    packed_ref[:, hidden : 2 * hidden] = down_ref[...].T
    packed_ref[:, 2 * hidden :] = out_ref[...].T


def unpack_kernel(packed_ref, up_ref, down_ref, out_ref):
    hidden = up_ref.shape[1]
    up_ref[...] = packed_ref[:, :hidden].astype(F32)
    down_ref[...] = packed_ref[:, hidden : 2 * hidden].astype(F32).T
    out_ref[...] = packed_ref[:, 2 * hidden :].astype(F32).T


def finish_kernel(*refs):
    place_ref, refs = refs[0], refs[1:]
    for from_ref, to_ref in zip(refs[:2], refs[-3:-1]):
        to_ref[...] = from_ref[...]
    terms, outs = refs[2:-14], refs[-14:-3]
    sum_ref = refs[-1]
    total = terms[0][...].astype(F32)
    for term in terms[1:]:
        total = total + term[...].astype(F32)
    at = 0
    for out_ref in outs[:5]:
        out_ref[...] = total[at : at + out_ref.shape[0]]
        at += out_ref.shape[0]
    for out_ref in outs[5:7]:
        heads, rows, lanes = out_ref.shape
        for item in range(heads):
            out_ref[item] = total[at : at + rows, item * lanes : (item + 1) * lanes]
        at += rows
    sum_ref[...] = total[at:]
    shard, group = place_ref[1], place_ref[2]
    lanes = sum_ref.shape[1]
    for index, out_ref in enumerate(outs[7:]):
        heads, columns = out_ref.shape
        if index < 3:
            stride = HEAD_SIZE
            row = sum_ref[pl.ds(index * len(terms) + shard, 1), :]
            shift = group * columns
        else:
            stride = columns * (HEAD_SIZE // outs[7].shape[1])
            row = sum_ref[index * len(terms) : index * len(terms) + 1, :]
            shift = (shard * heads) * stride + group * columns
        row = pltpu.roll(row, lax.rem(lanes - shift, lanes), 1)
        for item in range(heads):
            out_ref[item : item + 1, :] = row[:, item * stride : item * stride + columns]


def out_kernel(att_ref, wo_ref, tok_ref, gain_ref, mid_ref, min_ref):
    t = pl.program_id(0)
    part = nt(att_ref[...], flat(wo_ref))

    @pl.when(t == 0)
    def _():
        mid_ref[...] = joined(tok_ref) + part

    @pl.when(t > 0)
    def _():
        mid_ref[...] += part

    @pl.when(t == pl.num_programs(0) - 1)
    def _():
        x = mid_ref[...].astype(BF).astype(F32)
        min_ref[...] = (x * inverse_rms(x) * gain_ref[...]).astype(BF)


def mlp_kernel(
    place_ref, min_ref, cot_ref, mid_ref, gain_ref, wu_ref, wd_ref,
    out_ref, gmid_ref, ggain_ref, gw_ref,
    min_t, cot_t, out_acc, gm_acc, hidden_ref,
):
    tile = pl.program_id(0)
    which = pl.program_id(1)

    @pl.when((tile == 0) & (which == 0))
    def _():
        min_t[...] = min_ref[...].T
        cot_t[...] = cot_ref[...].T
        out_acc[...] = jnp.zeros_like(out_acc)
        gm_acc[...] = jnp.zeros_like(gm_acc)

    @pl.when(which == 0)
    def _():
        wu = flat(wu_ref)
        wd = flat(wd_ref)
        pre = nn(min_ref[...], wu)
        cdf = 0.5 + 0.5 * lax.erf(pre * (0.5**0.5))
        density = jnp.exp2(pre * pre * (-0.5 * LOG2E)) * ((2.0 * np.pi) ** -0.5)
        hidden_ref[...] = (pre * cdf).astype(BF)
        grad_pre = (nn(cot_ref[...], wd) * (cdf + pre * density)).astype(BF)
        out_acc[...] += nt(hidden_ref[...], wd)
        gm_acc[...] += nt(grad_pre, wu)
        grad = nn(min_t[...], grad_pre).astype(BF)
        gw_ref[...] = grad.reshape(gw_ref.shape)

    @pl.when(which == 1)
    def _():
        grad = nn(cot_t[...], hidden_ref[...]).astype(BF)
        gw_ref[...] = grad.reshape(gw_ref.shape)

    @pl.when((tile == pl.num_programs(0) - 1) & (which == 1))
    def _():
        mid = mid_ref[...]
        lanes = out_ref.shape[2]
        for part in range(out_ref.shape[0]):
            at = slice(part * lanes, (part + 1) * lanes)
            out_ref[part] = (mid[:, at] + out_acc[:, at]).astype(BF)
        x = mid.astype(BF).astype(F32)
        inverse = inverse_rms(x)
        normed = x * inverse
        gm = gm_acc[...]
        ggain_ref[...] = jnp.sum(gm * normed, axis=0, keepdims=True)
        scaled = gm * gain_ref[...]
        back = inverse * (scaled - normed * jnp.mean(scaled * normed, axis=-1, keepdims=True))
        gmid_ref[...] = (cot_ref[...].astype(F32) + back).astype(BF)


def out_back_kernel(gmid_ref, wo_ref, att_ref, late_ref, gatt_ref, gwo_ref, gmid_t):
    @pl.when(pl.program_id(0) == 0)
    def _():
        gmid_t[...] = gmid_ref[...].T

    gatt_ref[...] = nn(gmid_ref[...], flat(wo_ref)).astype(BF)
    gwo_ref[...] = nn(gmid_t[...], att_ref[...]).astype(BF).reshape(gwo_ref.shape)


def project_back_kernel(
    place_ref, tok_ref, gmid_ref, gain_ref, gq_ref, gk_ref, gv_ref,
    wq_ref, wqo_ref, wk_ref, wko_ref, wv_ref, wvo_ref, gsq_ref, ginit_ref, gmk_ref, gmv_ref,
    gtok_ref, ggain_ref, gown_ref, gother_ref, ain_t, acc_ref, pack_ref,
):
    t = pl.program_id(0)

    @pl.when(t == 0)
    def _():
        x = joined(tok_ref)
        ain_t[...] = (x * inverse_rms(x) * gain_ref[...]).astype(BF).T
        acc_ref[...] = jnp.zeros_like(acc_ref)

    groups, _, lanes = pack_ref.shape
    at = 0
    for g_ref, w_ref, w_other in (
        (gq_ref, wq_ref, wqo_ref), (gk_ref, wk_ref, wko_ref), (gv_ref, wv_ref, wvo_ref)
    ):
        g = g_ref[...]
        acc_ref[...] += nt(g, merged(place_ref, w_ref, w_other))
        grad = nn(ain_t[...], g).astype(BF)
        rows = grad.shape[0] // groups
        pack_ref[:, at : at + rows] = grad.reshape(groups, rows, lanes)
        at += rows
    for g_ref in (gsq_ref, ginit_ref):
        rows = g_ref.shape[0] // groups
        pack_ref[:, at : at + rows] = g_ref[...].astype(BF).reshape(groups, rows, lanes)
        at += rows
    for g_ref in (gmk_ref, gmv_ref):
        rows = HEAD_SIZE // groups
        for item in range(g_ref.shape[0]):
            where = slice(item * HEAD_SIZE, (item + 1) * HEAD_SIZE)
            pack_ref[:, at : at + rows, where] = g_ref[item].astype(BF).reshape(groups, rows, -1)
        at += rows
    pack_ref[:, at:] = jnp.zeros_like(pack_ref[:, at:])
    for index in range(groups // 2):
        gown_ref[0, index] = pack_ref[2 * index + place_ref[0]]
        gother_ref[0, index] = pack_ref[2 * index + 1 - place_ref[0]]

    @pl.when(t == pl.num_programs(0) - 1)
    def _():
        x = joined(tok_ref)
        inverse = inverse_rms(x)
        normed = x * inverse
        ga = acc_ref[...]
        ggain_ref[...] = jnp.sum(ga * normed, axis=0, keepdims=True)
        scaled = ga * gain_ref[...]
        back = inverse * (scaled - normed * jnp.mean(scaled * normed, axis=-1, keepdims=True))
        grad = (gmid_ref[...].astype(F32) + back).astype(BF)
        for part in range(gtok_ref.shape[0]):
            gtok_ref[part] = grad[:, part * lanes : (part + 1) * lanes]


def distance_bucket(distance):
    magnitude = np.abs(distance)
    scaled = np.log(np.maximum(magnitude, 1) / 8.0) / np.log(16.0) * 8.0
    far = np.minimum(8 + np.floor(np.maximum(scaled, 0.0)).astype(np.int32), 15)
    return (distance < 0).astype(np.int32) * 16 + np.where(magnitude < 8, magnitude, far)


def one_hot(distance, valid, bucket_count):
    hot = distance_bucket(distance)[:, None] == np.arange(bucket_count)[None, :]
    return jnp.asarray((hot & valid[:, None]).astype(np.float32))


def carry(value, power, axis, backward):
    count = lax.axis_size(axis)
    sign = -1 if backward else 1
    total = from_behind(value.astype(BF), axis, sign)
    if count == 2:
        return total
    total = total.astype(F32)
    step = 1
    while step < count - 1:
        moved = from_behind(total.astype(BF), axis, sign * step).astype(F32)
        total = total + power**step * moved
        step *= 2
    return total


def across(value, axis, bit):
    count = lax.axis_size(axis)
    return lax.ppermute(value, axis, [(source, source ^ bit) for source in range(count)])


def take(value, index, dim):
    return lax.dynamic_index_in_dim(value, index, dim, False)


def add_low(left, right):
    return (left.astype(F32) + right.astype(F32)).astype(BF)


def ordered(bit, own, other, dim):
    first = bit == 0
    return jnp.stack([jnp.where(first, own, other), jnp.where(first, other, own)], axis=dim)


def gather_pairs(item, beside, behind, place):
    shards = lax.axis_size("tp")
    half = shards // 2
    tp = lax.axis_index("tp")
    x_bit = lax.axis_index("dp") % 2
    y_bit = lax.axis_index("dp") // 2
    parts = [item] + [across(item, "tp", k) for k in range(1, shards)]
    bit = 1
    while bit < shards:
        swap = (tp & bit) > 0
        parts = [jnp.where(swap, parts[k ^ bit], parts[k]) for k in range(shards)]
        bit *= 2
    low = jnp.stack(parts[:half])
    high = jnp.stack(parts[half:])
    low, high, behind = lax.optimization_barrier((low, high, behind))
    low_x = across(low, "dp", 1)
    high_y = across(high, "dp", 2)
    low = ordered(x_bit, low, low_x, 0)
    high = ordered(y_bit, high, high_y, 0)
    low_y = across(low, "dp", 2)
    high_x = across(high, "dp", 1)
    piece = pl.BlockSpec((2, 1) + item.shape, lambda i, *_: (0, i, 0, 0))
    own = pl.pallas_call(
        assemble_kernel,
        grid_spec=pltpu.PrefetchScalarGridSpec(
            num_scalar_prefetch=1, grid=(half,), in_specs=[piece] * 4,
            out_specs=pl.BlockSpec((2, 4, 1) + item.shape, lambda i, *_: (0, 0, i, 0, 0)),
        ),
        out_shape=jax.ShapeDtypeStruct((2, 4, half) + item.shape, BF),
        compiler_params=params(),
    )(place, low, low_y, high, high_x)
    own, beside = lax.optimization_barrier((own, beside))
    return own, across(own, "ctx", 1), beside, behind


def scatter_pairs(own, other):
    shards = own.shape[0]
    half = shards // 2
    tp = lax.axis_index("tp")
    x_bit = lax.axis_index("dp") % 2
    y_bit = lax.axis_index("dp") // 2
    grid = (shards, 2, 2) + own.shape[2:]
    moved = across(other, "ctx", 1).reshape(grid)
    own = own.reshape(grid)

    def both(part, index, dim):
        return add_low(take(own[part], index, dim), take(moved[part], index, dim))

    first, second = slice(0, half), slice(half, shards)
    low_moved = across(both(first, 1 - x_bit, 2), "dp", 1)
    high_moved = across(both(second, 1 - y_bit, 1), "dp", 2)
    low = add_low(both(first, x_bit, 2), low_moved)
    high = add_low(both(second, y_bit, 1), high_moved)
    low_moved = across(take(low, 1 - y_bit, 1), "dp", 2)
    high_moved = across(take(high, 1 - x_bit, 1), "dp", 1)
    low = add_low(take(low, y_bit, 1), low_moved)
    high = add_low(take(high, x_bit, 1), high_moved)
    kept = jnp.concatenate([low, high])
    return [take(kept, tp, 0)] + [
        across(take(kept, tp ^ k, 0), "tp", k) for k in range(1, shards)
    ]


def sequence_body(
    tokens, cotangent, prefix, w_query, w_key, w_value, w_out, w_up, w_down,
    state_query, state_init, gain_attn, gain_mlp, bias_table, gate_bias, state_key, state_value,
):
    shards = lax.axis_size("tp")
    groups = lax.axis_size("dp") * lax.axis_size("ctx")
    pairs = lax.axis_size("dp")
    half = shards // 2
    everywhere = ("tp", "dp", "ctx")
    seq_count, length, shard_width = tokens.shape
    width = cotangent.shape[2]
    seqs = seq_count // shards
    blocks = length // BLOCK
    units = seqs * blocks
    rows = units * BLOCK
    local_heads = bias_table.shape[0]
    heads = local_heads * shards
    buckets = bias_table.shape[1] * groups
    own_rows = w_query.shape[0]
    own_slots = state_query.shape[0]
    slots = own_slots * groups
    hidden = w_up.shape[1]
    tp_index = lax.axis_index("tp")
    ctx_index = lax.axis_index("ctx")
    dp_index = lax.axis_index("dp")
    head = HEAD_SIZE
    map_rows = state_key.shape[1]
    group = dp_index * lax.axis_size("ctx") + ctx_index
    place = jnp.stack([ctx_index, tp_index, group, dp_index % 2, dp_index // 2]).astype(jnp.int32)

    def call(kernel, grid, in_specs, out_specs, out_shape, scratch=(), prefetch=1, **more):
        return pl.pallas_call(
            kernel,
            grid_spec=pltpu.PrefetchScalarGridSpec(
                num_scalar_prefetch=prefetch, grid=grid, in_specs=in_specs, out_specs=out_specs,
                scratch_shapes=list(scratch),
            ),
            out_shape=out_shape,
            compiler_params=params(),
            **more,
        )

    at_slots = 3 * own_rows
    at_init = at_slots + own_slots
    at_maps = at_init + own_slots
    at_vectors = at_maps + 2 * map_rows
    full_rows = at_vectors + 16
    vectors = (gain_attn, gain_mlp, gate_bias, bias_table)
    ends = np.cumsum([0] + [item.shape[1] for item in vectors])
    tail = jnp.concatenate(vectors, axis=1)
    tail = jnp.pad(tail, ((0, 16 - local_heads), (0, shard_width - tail.shape[1])))
    item = pl.pallas_call(
        item_kernel, out_shape=jax.ShapeDtypeStruct((full_rows, shard_width), BF)
    )(w_query, w_key, w_value, state_query, state_init, state_key, state_value, tail)
    x = lax.all_to_all(tokens, "tp", 0, 0, tiled=True)
    late_width = 2 * hidden + shard_width
    late = pl.pallas_call(
        pack_kernel, out_shape=jax.ShapeDtypeStruct((own_rows, late_width), BF)
    )(w_up, w_down, w_out)
    first_own, first_other, x, late = gather_pairs(item, x, late, place)
    x = x.reshape(shards, rows, shard_width)
    late = lax.all_gather(late, everywhere, axis=0, tiled=True)
    late = late.reshape(shards, groups, own_rows, late_width)

    at_heads = slice(at_vectors, at_vectors + local_heads)
    small = ordered(
        ctx_index, first_own[:, :, :, at_heads], first_other[:, :, :, at_heads], 2
    )

    def spread(index):
        part = small[..., ends[index] : ends[index + 1]]
        return jnp.transpose(part, (0, 3, 4, 1, 2, 5)).reshape(heads, -1).astype(F32)

    gain_one = spread(0).reshape(1, width)
    gain_two = spread(1).reshape(1, width)
    gate = jax.nn.sigmoid(spread(2)).reshape(1, width)
    bias_rows = spread(3)

    def whole(shape):
        return pl.BlockSpec(shape, lambda *_: (0,) * len(shape))

    def weight(index):
        spec = pl.BlockSpec(
            (1, pairs, 1, own_rows, shard_width), lambda t, *_: (t // half, 0, t % half, index, 0)
        )
        return [spec, spec]

    def of_head(count, index):
        def at(h, *_):
            t = h // local_heads
            return (t // half, 0, t % half, index, h % local_heads)

        spec = pl.BlockSpec((1, pairs, 1, count, head), at)
        return [spec, spec]

    column = pl.BlockSpec((rows, shard_width), lambda t, *_: (0, t))
    wide = jax.ShapeDtypeStruct((rows, width), BF)
    wide32 = jax.ShapeDtypeStruct((rows, width), F32)
    split = jax.ShapeDtypeStruct((shards, rows, shard_width), BF)
    halo = jax.ShapeDtypeStruct((seqs * BLOCK, width), BF)
    halo_column = pl.BlockSpec((2, seqs * BLOCK, shard_width), lambda t, *_: (0, 0, t))
    queries, keys, values, _, last_blocks = call(
        project_kernel,
        (shards,),
        [whole((shards, rows, shard_width)), whole((1, width))] + weight(0) + weight(1) + weight(2),
        [column, column, column, whole((rows, width)), halo_column],
        [wide] * 4 + [jax.ShapeDtypeStruct((2, seqs * BLOCK, width), BF)],
    )(place, x, gain_one, *([first_own, first_other] * 3))

    halos = from_behind(last_blocks, "ctx", 1)

    def along(rows_of, index):
        return pl.BlockSpec((rows_of, head), lambda h, n, *_: (index(n), h))

    def turned(n):
        return units - 1 - n

    query_slots = of_head(own_slots, at_slots // own_slots)
    init_slots = of_head(own_slots, at_init // own_slots)
    key_maps = of_head(map_rows, at_maps // map_rows)
    value_maps = of_head(map_rows, at_maps // map_rows + 1)
    channel = pl.BlockSpec((1, head), lambda h, n, *_: (0, h))
    slot_rows = units * slots
    slot_f32 = jax.ShapeDtypeStruct((slot_rows, width), F32)
    slot_low = jax.ShapeDtypeStruct((slot_rows, width), BF)
    message = jax.ShapeDtypeStruct((seqs * slots, width), BF)
    slot_scratch = pltpu.VMEM((slots, head), F32)
    own = along(BLOCK, lambda n: n)
    slot = along(slots, lambda n: n)
    slot_of_seq = along(slots, lambda n: n // blocks)
    contrib, accumulated = call(
        functools.partial(read_kernel, blocks=blocks),
        (heads, units),
        query_slots + [own, own, channel],
        [slot, slot_of_seq],
        [slot_f32, message],
        [slot_scratch],
    )(place, first_own, first_other, keys, values, gate)
    halos, accumulated = lax.optimization_barrier((halos, accumulated))
    power = gate**blocks
    lead = carry(accumulated, power, "ctx", False)
    lead_power = jnp.ones_like(gate)
    for step in range(lax.axis_size("ctx") - 1):
        lead_power = jnp.where(ctx_index > step, lead_power * power, lead_power)

    block_at = ctx_index * blocks + jnp.arange(blocks, dtype=jnp.int32)
    own_prefix = lax.dynamic_slice_in_dim(prefix, tp_index * seqs, seqs, 0)
    info = jnp.stack(
        [
            jnp.broadcast_to(block_at[None], (seqs, blocks)),
            own_prefix[:, None] - block_at[None] * BLOCK,
        ],
        axis=-1,
    ).reshape(units, 2)
    span = 4 * BLOCK
    offset = np.arange(span)
    offset = np.where(offset < 2 * BLOCK, offset, offset - span)
    forward_hot = one_hot(BLOCK - offset, offset > -BLOCK, buckets)
    back_span = 3 * BLOCK
    back_offset = np.arange(back_span)
    back_offset = np.where(back_offset < BLOCK, back_offset, back_offset - back_span)
    backward_hot = one_hot(BLOCK + back_offset, back_offset > -2 * BLOCK, buckets)
    exact = lax.Precision.HIGHEST
    scaled_bias = bias_rows * LOG2E
    forward_bias = jnp.dot(scaled_bias, forward_hot.T, precision=exact)[:, None]
    backward_bias = jnp.dot(scaled_bias, backward_hot.T, precision=exact)[:, None]

    def attend_specs(index):
        before = along(BLOCK, lambda n: jnp.maximum(index(n) - 1, 0))
        by_seq = [
            pl.BlockSpec((None, BLOCK, head), lambda h, n, *_, part=part: (part, index(n) // blocks, h))
            for part in range(2)
        ]
        here = along(BLOCK, index)
        return [here, here, here, before, before] + by_seq + key_maps + value_maps

    def lse_spec(index):
        return pl.BlockSpec((1, 1, 1, BLOCK), lambda h, n, *_: (index(n), h, 0, 0))

    def vector(size):
        return pl.BlockSpec((1, 1, size), lambda h, *_: (h, 0, 0))

    attend_args = (
        place, info, queries, keys, values, keys, values, halos, halos,
        first_own, first_other, first_own, first_other,
    )
    attended, lse, states, moved = call(
        functools.partial(attend_kernel, blocks=blocks),
        (heads, units),
        attend_specs(lambda n: n)
        + [slot] + init_slots + [slot_of_seq, channel, channel, vector(span)],
        [own, lse_spec(lambda n: n), slot, slot],
        [wide, jax.ShapeDtypeStruct((units, heads, 1, BLOCK), F32), slot_low, slot_low],
        [pltpu.VMEM((BLOCK, 2 * BLOCK), F32), slot_scratch],
        2,
    )(*attend_args, contrib, first_own, first_other, lead, lead_power, gate, forward_bias)

    out_weight = pl.BlockSpec(
        (1, groups, own_rows, shard_width), lambda t, *_: (t, 0, 0, 2 * hidden // shard_width)
    )
    middle, mlp_in = pl.pallas_call(
        out_kernel,
        grid=(shards,),
        in_specs=[column, out_weight, whole((shards, rows, shard_width)), whole((1, width))],
        out_specs=[whole((rows, width)), whole((rows, width))],
        out_shape=[wide32, wide],
        compiler_params=params(),
    )(attended, late, x, gain_two)

    tile = min(hidden, 1024)
    per_shard = hidden // tile
    tile_block = (1, groups, own_rows, tile)
    output, middle_grad, gain_two_grad, late_grad = call(
        mlp_kernel,
        (shards * per_shard, 2),
        [
            whole((rows, width)),
            pl.BlockSpec((rows, width), lambda i, j, place_ref: (place_ref[1], 0)),
            whole((rows, width)), whole((1, width)),
            pl.BlockSpec(tile_block, lambda i, j, *_: (i // per_shard, 0, 0, i % per_shard)),
            pl.BlockSpec(
                tile_block, lambda i, j, *_: (i // per_shard, 0, 0, per_shard + i % per_shard)
            ),
        ],
        [
            whole((shards, rows, shard_width)), whole((rows, width)), whole((1, width)),
            pl.BlockSpec(
                tile_block, lambda i, j, *_: (i // per_shard, 0, 0, j * per_shard + i % per_shard)
            ),
        ],
        [
            split, wide, jax.ShapeDtypeStruct((1, width), F32),
            jax.ShapeDtypeStruct((shards, groups, own_rows, late_width), BF),
        ],
        [
            pltpu.VMEM((width, rows), BF), pltpu.VMEM((width, rows), BF),
            pltpu.VMEM((rows, width), F32), pltpu.VMEM((rows, width), F32),
            pltpu.VMEM((rows, tile), BF),
        ],
    )(
        place, mlp_in, cotangent.reshape(seq_count * length, width), middle, gain_two, late, late
    )
    output = lax.all_to_all(output, "tp", 0, 0, tiled=True)

    grad_attended, late_grad = pl.pallas_call(
        out_back_kernel,
        grid=(shards,),
        in_specs=[
            whole((rows, width)), out_weight, column, pl.BlockSpec(memory_space=pl.ANY)
        ],
        out_specs=[column, out_weight],
        out_shape=[wide, jax.ShapeDtypeStruct(late_grad.shape, BF)],
        scratch_shapes=[pltpu.VMEM((width, rows), BF)],
        compiler_params=params(),
        input_output_aliases={3: 1},
    )(middle_grad, late, attended, late_grad)
    late_grad = lax.psum_scatter(
        late_grad.reshape(shards * groups * own_rows, late_width), everywhere,
        scatter_dimension=0, tiled=True,
    )
    head_sum = jax.ShapeDtypeStruct((heads, head, head), F32)
    head_map = pl.BlockSpec((1, head, head), lambda h, n, *_: (h, 0, 0))
    back_own = along(BLOCK, turned)
    back_slot = along(slots, turned)
    back_of_seq = along(slots, lambda n: turned(n) // blocks)
    key_of_seq = along(BLOCK, lambda n: turned(n) // blocks)
    (
        grad_queries, dk, dv, dk_before, dv_before, direct, key_map_grad, value_map_grad,
        bias_sum, gathered, first_keys, first_values,
    ) = call(
        functools.partial(attend_back_kernel, blocks=blocks),
        (heads, units),
        attend_specs(turned)
        + [back_slot, channel, vector(back_span), back_own, back_own, lse_spec(turned)],
        [back_own] * 5 + [back_slot, head_map, head_map, vector(back_span), back_of_seq]
        + [key_of_seq, key_of_seq],
        [
            wide, wide32, wide32, wide, wide, slot_f32, head_sum, head_sum,
            jax.ShapeDtypeStruct((heads, 1, back_span), F32), message, halo, halo,
        ],
        [
            pltpu.VMEM((2 * BLOCK, BLOCK), F32), pltpu.VMEM((128, back_span), F32),
            pltpu.VMEM((BLOCK, head), F32), slot_scratch,
        ],
        2,
    )(*attend_args, states, gate, backward_bias, grad_attended, attended, lse)
    dk, output = lax.optimization_barrier((dk, output))
    sum_at = np.arange(back_span) - BLOCK
    sum_hot = one_hot(sum_at, sum_at > -BLOCK, buckets)
    bias_grad = jnp.dot(bias_sum[:, 0], sum_hot, precision=exact)

    later = carry(gathered, power, "ctx", True)
    back_keys = from_behind(first_keys, "ctx", -1)
    back_values = from_behind(first_values, "ctx", -1)
    following = along(BLOCK, lambda n: jnp.minimum(turned(n) + 1, units - 1))
    kept_slot = pl.BlockSpec((slots, head), lambda h, n, *_: (0, h))
    slot_sum = jax.ShapeDtypeStruct((slots, width), F32)
    grad_keys, grad_values, slot_query_grad, init_grad, gate_grad = call(
        functools.partial(read_back_kernel, blocks=blocks),
        (heads, units),
        query_slots
        + [back_own, back_own, back_slot, back_slot, back_of_seq, channel]
        + [back_own, back_own, following, following, key_of_seq, key_of_seq],
        [back_own, back_own, kept_slot, kept_slot, vector(head)],
        [wide, wide, slot_sum, slot_sum, jax.ShapeDtypeStruct((heads, 1, head), F32)],
        [slot_scratch],
    )(
        place, first_own, first_other, keys, values, direct, moved, later, gate,
        dk, dv, dk_before, dv_before, back_keys, back_values,
    )

    maps_of = pl.BlockSpec((local_heads, head, head), lambda t, *_: (t, 0, 0))
    slots_of = pl.BlockSpec((slots, shard_width), lambda t, *_: (0, t))
    piece = pl.BlockSpec((1, pairs, full_rows, shard_width), lambda t, *_: (t, 0, 0, 0))
    pieces = jax.ShapeDtypeStruct((shards, pairs, full_rows, shard_width), BF)
    token_grad, gain_one_grad, grad_own, grad_other = call(
        project_back_kernel,
        (shards,),
        [whole((shards, rows, shard_width)), whole((rows, width)), whole((1, width))]
        + [column, column, column]
        + weight(0) + weight(1) + weight(2) + [slots_of, slots_of, maps_of, maps_of],
        [whole((shards, rows, shard_width)), whole((1, width)), piece, piece],
        [split, jax.ShapeDtypeStruct((1, width), F32), pieces, pieces],
        [
            pltpu.VMEM((width, rows), BF), pltpu.VMEM((rows, width), F32),
            pltpu.VMEM((groups, full_rows, shard_width), BF),
        ],
    )(
        place, x, middle_grad, gain_one, grad_queries, grad_keys, grad_values,
        *([first_own, first_other] * 3), slot_query_grad, init_grad, key_map_grad, value_map_grad,
    )
    token_grad = lax.all_to_all(token_grad, "tp", 0, 0, tiled=True)

    vector_sums = [gain_one_grad, gain_two_grad, gate_grad.reshape(1, width), bias_grad]
    vector_rows = jnp.concatenate([item.reshape(-1) for item in vector_sums])
    vector_rows = jnp.pad(vector_rows, (0, 16 * shard_width - vector_rows.size)).astype(BF)
    vector_rows = jnp.broadcast_to(
        vector_rows.reshape(1, 1, 16, shard_width), (shards, pairs, 16, shard_width)
    )
    grad_own = lax.dynamic_update_slice(grad_own, vector_rows, (0, 0, at_vectors, 0))
    grad_other = lax.dynamic_update_slice(grad_other, vector_rows, (0, 0, at_vectors, 0))
    terms = scatter_pairs(grad_own, grad_other)
    parts = (
        w_query, w_key, w_value, state_query, state_init, state_key, state_value,
        gain_attn, gain_mlp, gate_bias, bias_table,
    )
    sums = call(
        finish_kernel,
        (1,),
        [whole(output.shape)] * 2 + [whole((full_rows, shard_width))] * shards,
        [whole(item.shape) for item in parts] + [whole(output.shape)] * 2,
        [jax.ShapeDtypeStruct(item.shape, F32) for item in parts]
        + [jax.ShapeDtypeStruct(output.shape, BF)] * 2,
        [pltpu.VMEM((16, shard_width), F32)],
    )(place, output, token_grad, *terms)
    late_grad, sums = lax.optimization_barrier((late_grad, sums))
    up_grad, down_grad, out_grad = pl.pallas_call(
        unpack_kernel,
        out_shape=[
            jax.ShapeDtypeStruct(w_up.shape, F32), jax.ShapeDtypeStruct(w_down.shape, F32),
            jax.ShapeDtypeStruct(w_out.shape, F32),
        ],
    )(late_grad)
    return (
        sums[11].reshape(seq_count, length, shard_width),
        sums[12].reshape(seq_count, length, shard_width),
        *sums[:3],
        out_grad,
        up_grad,
        down_grad,
        *sums[3:5],
        sums[7],
        sums[8],
        sums[10],
        sums[9],
        *sums[5:7],
    )


def choose(tokens, *others):
    shards = lax.axis_size("tp")
    even = tokens.shape[0] % shards == 0 and shards % 2 == 0 and shards & (shards - 1) == 0
    even = even and lax.axis_size("dp") == 4 and lax.axis_size("ctx") == 2
    return (sequence_body if even else body)(tokens, *others)


def solution(mesh):
    in_specs = (
        P("dp", "ctx", "tp"),
        P("dp", "ctx", None),
        P("dp"),
        P(("dp", "ctx"), "tp"),
        P(("dp", "ctx"), "tp"),
        P(("dp", "ctx"), "tp"),
        P("tp", ("dp", "ctx")),
        P(("dp", "ctx"), "tp"),
        P("tp", ("dp", "ctx")),
        P(("dp", "ctx"), "tp"),
        P(("dp", "ctx"), "tp"),
        P("tp", ("dp", "ctx")),
        P("tp", ("dp", "ctx")),
        P("tp", ("dp", "ctx")),
        P("tp", ("dp", "ctx")),
        P("tp", ("dp", "ctx"), None),
        P("tp", ("dp", "ctx"), None),
    )
    out_specs = (
        P("dp", "ctx", "tp"),
        P("dp", "ctx", "tp"),
        P(("dp", "ctx"), "tp"),
        P(("dp", "ctx"), "tp"),
        P(("dp", "ctx"), "tp"),
        P("tp", ("dp", "ctx")),
        P(("dp", "ctx"), "tp"),
        P("tp", ("dp", "ctx")),
        P(("dp", "ctx"), "tp"),
        P(("dp", "ctx"), "tp"),
        P("tp", ("dp", "ctx")),
        P("tp", ("dp", "ctx")),
        P("tp", ("dp", "ctx")),
        P("tp", ("dp", "ctx")),
        P("tp", ("dp", "ctx"), None),
        P("tp", ("dp", "ctx"), None),
    )
    return jax.shard_map(choose, mesh=mesh, in_specs=in_specs, out_specs=out_specs, check_vma=False)
```

```python
import functools

import jax
import jax.numpy as jnp
import numpy as np
from jax import lax
from jax.experimental import pallas as pl
from jax.experimental.pallas import tpu as pltpu
from jax.sharding import PartitionSpec as P

HEAD_SIZE = 128
BLOCK = 512


EPSILON = 1e-06
MASKED = -1e30
ROWS_FORWARD = 128
KEYS_BACKWARD = 256


def from_behind(value, axis, steps):
    count = lax.axis_size(axis)
    first, last = (max(0, -steps), min(count, count - steps))
    return lax.ppermute(value, axis, [(source, source + steps) for source in range(first, last)])


def prefix_2(array, axis, join, neutral, backward):
    count = lax.axis_size(axis)
    place = lax.axis_index(axis)
    ahead = count - 1 - place if backward else place
    gathered = jax.tree.map(
        lambda a, kind: lax.all_gather(a.astype(kind), axis), array, (jnp.bfloat16, jnp.bfloat16)
    )
    state = jax.tree.map(lambda a, e: jnp.zeros_like(a) + jnp.asarray(e, a.dtype), array, neutral)

    def one(hop, state):
        source = count - 1 - hop if backward else hop
        return join(
            state,
            jax.tree.map(
                lambda a, own: lax.dynamic_index_in_dim(a, source, 0, False).astype(own.dtype),
                gathered,
                array,
            ),
        )

    return lax.fori_loop(0, ahead, one, state)


def bucket_index(block_size):
    query_pos = np.arange(block_size)[:, None] + block_size
    key_pos = np.arange(2 * block_size)[None, :]
    distance = query_pos - key_pos
    upper_part = (distance < 0).astype(np.int32) * 16
    magnitude = np.abs(distance)
    scaled = np.log(np.maximum(magnitude, 1) / 8.0) / np.log(16.0) * 8.0
    far_bucket = np.minimum(8 + np.floor(np.maximum(scaled, 0.0)).astype(np.int32), 15)
    return (upper_part + np.where(magnitude < 8, magnitude, far_bucket)).astype(np.int32)


def norm_forward(features, gain_vector):
    inverse = lax.rsqrt(jnp.mean(features * features, axis=-1, keepdims=True) + EPSILON)
    normed = features * inverse
    return (normed, inverse, (normed * gain_vector).astype(jnp.bfloat16))


def norm_backward(grad_normed, normed, inverse, gain_vector):
    scaled = grad_normed * gain_vector
    grad_in = inverse * (scaled - normed * jnp.mean(scaled * normed, axis=-1, keepdims=True))
    return (grad_in, jnp.sum(grad_normed * normed, axis=0))


def compose(earlier, later_pair):
    return (earlier[0] * later_pair[0], later_pair[0] * earlier[1] + later_pair[1])


def bias_matrix(bias_rows, bucket):
    summed = jnp.zeros((bias_rows.shape[0],) + bucket.shape, jnp.float32)
    for number in range(bias_rows.shape[1]):
        summed = (
            summed
            + bias_rows[:, number][:, None, None] * (bucket == number).astype(jnp.float32)[None]
        )
    return summed


def bias_gradient(grad_matrix, bucket, bucket_count):
    columns = [
        jnp.sum(grad_matrix * (bucket == number).astype(jnp.float32)[None], axis=(1, 2))
        for number in range(bucket_count)
    ]
    return jnp.stack(columns, axis=1)


def body(
    tokens,
    cotangent,
    prefix,
    w_query,
    w_key,
    w_value,
    w_out,
    w_up,
    w_down,
    state_query,
    state_init,
    gain_attn,
    gain_mlp,
    bias_table,
    gate_bias,
    state_key,
    state_value,
):
    (
        query_full,
        key_full,
        value_full,
        out_full,
        up_full,
        down_full,
        squery_full,
        sinit_full,
        gain_one,
        gain_two,
        bias_rows,
        gate_rows,
        state_key_complete,
        svalue_full,
    ) = (
        lax.all_gather(w_query, ("dp", "ctx"), axis=0, tiled=True),
        lax.all_gather(w_key, ("dp", "ctx"), axis=0, tiled=True),
        lax.all_gather(w_value, ("dp", "ctx"), axis=0, tiled=True),
        lax.all_gather(w_out, ("dp", "ctx"), axis=1, tiled=True),
        lax.all_gather(w_up, ("dp", "ctx"), axis=0, tiled=True),
        lax.all_gather(w_down, ("dp", "ctx"), axis=1, tiled=True),
        lax.all_gather(state_query, ("dp", "ctx"), axis=0, tiled=True),
        lax.all_gather(state_init, ("dp", "ctx"), axis=0, tiled=True),
        lax.all_gather(gain_attn, ("dp", "ctx"), axis=1, tiled=True),
        lax.all_gather(gain_mlp, ("dp", "ctx"), axis=1, tiled=True),
        lax.all_gather(bias_table, ("dp", "ctx"), axis=1, tiled=True),
        lax.all_gather(gate_bias, ("dp", "ctx"), axis=1, tiled=True),
        lax.all_gather(state_key, ("dp", "ctx"), axis=1, tiled=True),
        lax.all_gather(state_value, ("dp", "ctx"), axis=1, tiled=True),
    )
    seq_count = tokens.shape[0]
    length = tokens.shape[1]
    shard_width = tokens.shape[2]
    full_width = cotangent.shape[2]
    block_count = length // BLOCK
    row_count = seq_count * length
    local_head_count = bias_rows.shape[0]
    local_width = local_head_count * HEAD_SIZE
    state_slot_count = squery_full.shape[0]
    scores_scale = HEAD_SIZE ** (-0.5)
    local_shape = (seq_count, block_count, BLOCK, local_head_count, HEAD_SIZE)
    element_count = seq_count * block_count
    token_full, gain_one_full = (
        lax.all_gather(tokens, "tp", axis=2, tiled=True),
        lax.all_gather(gain_one, "tp", axis=0, tiled=True),
    )
    gain_one_vec = gain_one_full.reshape(full_width).astype(jnp.float32)
    normed_one, inverse_one, attn_in = norm_forward(
        token_full.reshape(row_count, full_width).astype(jnp.float32), gain_one_vec
    )
    queries = (
        jnp.dot(attn_in, query_full, preferred_element_type=jnp.float32)
        .astype(jnp.bfloat16)
        .reshape(local_shape)
    )
    key_rows = (
        jnp.dot(attn_in, key_full, preferred_element_type=jnp.float32)
        .astype(jnp.bfloat16)
        .reshape(local_shape)
    )
    value_rows = (
        jnp.dot(attn_in, value_full, preferred_element_type=jnp.float32)
        .astype(jnp.bfloat16)
        .reshape(local_shape)
    )
    last_keys, last_values = from_behind((key_rows[:, -1], value_rows[:, -1]), "ctx", 1)
    window_keys = jnp.concatenate(
        [jnp.concatenate([last_keys[:, None], key_rows[:, :-1]], 1), key_rows], 2
    )
    window_values = jnp.concatenate(
        [jnp.concatenate([last_values[:, None], value_rows[:, :-1]], 1), value_rows], 2
    )
    query_heads = squery_full.reshape(state_slot_count, local_head_count, HEAD_SIZE)
    read_scores = (
        jnp.einsum("mhe,sbthe->sbhmt", query_heads, key_rows, preferred_element_type=jnp.float32)
        * scores_scale
    )
    read_peak = jnp.max(read_scores, axis=-1, keepdims=True)
    read_raised = jnp.exp(read_scores - read_peak)
    read_probs = read_raised / jnp.sum(read_raised, axis=-1, keepdims=True)
    read_low = read_probs.astype(jnp.bfloat16)
    contrib = jnp.einsum(
        "sbhmt,sbthe->sbmhe", read_low, value_rows, preferred_element_type=jnp.float32
    )
    contrib = contrib.reshape(seq_count, block_count, state_slot_count, local_width)
    gate_value = jax.nn.sigmoid(gate_rows.reshape(local_width).astype(jnp.float32))
    gate_power = jnp.ones((local_width,), jnp.float32)
    accumulated = jnp.zeros((seq_count, state_slot_count, local_width), jnp.float32)
    for block_index in range(block_count):
        accumulated = gate_value * accumulated + (1.0 - gate_value) * contrib[:, block_index]
        gate_power = gate_power * gate_value
    identity = (jnp.ones((local_width,), jnp.float32), jnp.zeros_like(accumulated))
    lead_power, lead_state = prefix_2((gate_power, accumulated), "ctx", compose, identity, False)
    entry_state = lead_power * sinit_full.astype(jnp.float32) + lead_state
    state_list = [entry_state]
    block_index = 0
    state_list.append(gate_value * state_list[-1] + (1.0 - gate_value) * contrib[:, block_index])
    stacked = jnp.stack(state_list, axis=1)
    state_reduced = stacked.astype(jnp.bfloat16).reshape(
        seq_count, block_count, state_slot_count, local_head_count, HEAD_SIZE
    )
    state_key_rows = jnp.einsum(
        "cazqr,qrx->cazqx", state_reduced, state_key_complete, preferred_element_type=jnp.float32
    ).astype(jnp.bfloat16)
    state_values = jnp.einsum(
        "cazqr,qrx->cazqx", state_reduced, svalue_full, preferred_element_type=jnp.float32
    ).astype(jnp.bfloat16)
    bucket = jnp.asarray(bucket_index(BLOCK))
    bias_full = bias_matrix(bias_rows.astype(jnp.float32), bucket)
    block_ids = lax.axis_index("ctx") * block_count + jnp.arange(block_count, dtype=jnp.int32)
    query_pos = block_ids[:, None] * BLOCK + jnp.arange(BLOCK, dtype=jnp.int32)[None, :]
    key_pos = (block_ids[:, None] - 1) * BLOCK + jnp.arange(2 * BLOCK, dtype=jnp.int32)[None, :]
    causal = (key_pos[:, None, :] >= 0) & (key_pos[:, None, :] <= query_pos[:, :, None])
    in_prefix = (key_pos[None, :, None, :] >= 0) & (
        key_pos[None, :, None, :] < prefix[:, None, None, None]
    )
    permitted_mask = (causal[None] | in_prefix).reshape(element_count, 1, BLOCK, 2 * BLOCK)
    flattened_queries = queries.reshape(element_count, BLOCK, local_head_count, HEAD_SIZE)
    flattened_window_keys = window_keys.reshape(
        element_count, 2 * BLOCK, local_head_count, HEAD_SIZE
    )
    flattened_window_values = window_values.reshape(
        element_count, 2 * BLOCK, local_head_count, HEAD_SIZE
    )
    flattened_state_keys = state_key_rows.reshape(
        element_count, state_slot_count, local_head_count, HEAD_SIZE
    )
    flattened_state_values = state_values.reshape(
        element_count, state_slot_count, local_head_count, HEAD_SIZE
    )

    def block_score_rows(
        block_query_rows, block_window_key_rows, block_state_key_rows, block_permitted_mask
    ):
        window_part = (
            jnp.einsum(
                "ihe,jhe->hij",
                block_query_rows,
                block_window_key_rows,
                preferred_element_type=jnp.float32,
            )
            * scores_scale
            + bias_full
        )
        state_part = (
            jnp.einsum(
                "yat,zat->ayz",
                block_query_rows,
                block_state_key_rows,
                preferred_element_type=jnp.float32,
            )
            * scores_scale
        )
        return (jnp.where(block_permitted_mask, window_part, MASKED), state_part)

    def attend_one_block(element_entry):
        (
            block_query_rows,
            block_window_key_rows,
            block_window_value_rows,
            block_state_key_rows,
            block_state_value_rows,
            block_permitted_mask,
        ) = element_entry
        window_scores, scores_of_state = block_score_rows(
            block_query_rows, block_window_key_rows, block_state_key_rows, block_permitted_mask
        )
        row_peak = jnp.maximum(jnp.max(window_scores, axis=-1), jnp.max(scores_of_state, axis=-1))
        window_raised = jnp.exp(window_scores - row_peak[..., None])
        state_raised = jnp.exp(scores_of_state - row_peak[..., None])
        denominator = jnp.sum(window_raised, axis=-1) + jnp.sum(state_raised, axis=-1)
        log_total = row_peak + jnp.log(denominator)
        window_probs = (window_raised / denominator[..., None]).astype(jnp.bfloat16)
        state_probs = (state_raised / denominator[..., None]).astype(jnp.bfloat16)
        block_out = jnp.einsum(
            "hij,jhe->ihe",
            window_probs,
            block_window_value_rows,
            preferred_element_type=jnp.float32,
        ) + jnp.einsum(
            "wyd,dwg->ywg", state_probs, block_state_value_rows, preferred_element_type=jnp.float32
        )
        return (block_out.astype(jnp.bfloat16), log_total)

    attended_blocks, log_totals = lax.map(
        attend_one_block,
        (
            flattened_queries,
            flattened_window_keys,
            flattened_window_values,
            flattened_state_keys,
            flattened_state_values,
            permitted_mask,
        ),
    )
    attended = attended_blocks.reshape(row_count, local_width)
    attn_part = jnp.dot(attended, out_full, preferred_element_type=jnp.float32).reshape(
        seq_count, length, full_width
    )
    attn_share = lax.psum_scatter(
        attn_part.astype(jnp.bfloat16), "tp", scatter_dimension=2, tiled=True
    ).astype(jnp.float32)
    middle = tokens.astype(jnp.float32) + attn_share
    middle_full, gain_two_full = (
        lax.all_gather(middle.astype(jnp.bfloat16), "tp", axis=2, tiled=True),
        lax.all_gather(gain_two, "tp", axis=0, tiled=True),
    )
    gain_two_vec = gain_two_full.reshape(full_width).astype(jnp.float32)
    normed_two, inverse_two, mlp_in = norm_forward(
        middle_full.reshape(row_count, full_width).astype(jnp.float32), gain_two_vec
    )
    hidden_pre = jnp.dot(mlp_in, up_full, preferred_element_type=jnp.float32)
    hidden = jax.nn.gelu(hidden_pre, approximate=False).astype(jnp.bfloat16)
    mlp_part = jnp.dot(hidden, down_full, preferred_element_type=jnp.float32).reshape(
        seq_count, length, full_width
    )
    mlp_share = lax.psum_scatter(
        mlp_part.astype(jnp.bfloat16), "tp", scatter_dimension=2, tiled=True
    ).astype(jnp.float32)
    output = (middle + mlp_share).astype(jnp.bfloat16)
    grad_out = cotangent.reshape(row_count, full_width)
    grad_hidden = jnp.dot(grad_out, down_full.T, preferred_element_type=jnp.float32)
    grad_down = jnp.dot(hidden.T, grad_out, preferred_element_type=jnp.float32)

    def gelu_exact(pre_values):
        return jax.nn.gelu(pre_values, approximate=False)

    gelu_value, gelu_back = jax.vjp(gelu_exact, hidden_pre)
    grad_pre = gelu_back(grad_hidden)[0].astype(jnp.bfloat16)
    grad_up = jnp.dot(mlp_in.T, grad_pre, preferred_element_type=jnp.float32)
    grad_mlp_in = jnp.dot(grad_pre, up_full.T, preferred_element_type=jnp.float32)
    part_middle, part_gain_two = norm_backward(grad_mlp_in, normed_two, inverse_two, gain_two_vec)
    tp_index = lax.axis_index("tp")
    head_total = full_width // HEAD_SIZE
    summed, gain_two_sum = (
        lax.psum(
            part_middle.reshape(seq_count, length, full_width).astype(jnp.bfloat16), "tp"
        ).astype(jnp.float32),
        lax.psum(part_gain_two.reshape(head_total, HEAD_SIZE).astype(jnp.bfloat16), "tp").astype(
            jnp.float32
        ),
    )
    middle_grad_full = cotangent.astype(jnp.float32) + summed
    middle_grad = lax.dynamic_slice_in_dim(middle_grad_full, tp_index * shard_width, shard_width, 2)
    grad_gain_two = lax.dynamic_slice_in_dim(
        gain_two_sum, tp_index * local_head_count, local_head_count, 0
    )
    middle_grad_low = middle_grad_full.astype(jnp.bfloat16)
    middle_grad_rows = middle_grad_low.reshape(row_count, full_width)
    grad_attended = jnp.dot(
        middle_grad_rows, out_full.T, preferred_element_type=jnp.float32
    ).astype(jnp.bfloat16)
    grad_attended = grad_attended.reshape(element_count, BLOCK, local_head_count, HEAD_SIZE)
    grad_wout = jnp.dot(attended.T, middle_grad_rows, preferred_element_type=jnp.float32)

    def attend_back(bias_sum, element_entry):
        (
            block_query_rows,
            block_window_key_rows,
            block_window_value_rows,
            block_state_key_rows,
            block_state_value_rows,
            block_permitted_mask,
            block_lse,
            block_grad,
        ) = element_entry
        window_again, state_again = block_score_rows(
            block_query_rows, block_window_key_rows, block_state_key_rows, block_permitted_mask
        )
        window_exact = jnp.exp(window_again - block_lse[..., None])
        state_exact = jnp.exp(state_again - block_lse[..., None])
        grad_wprob = jnp.einsum(
            "ihe,jhe->hij", block_grad, block_window_value_rows, preferred_element_type=jnp.float32
        )
        grad_sprob = jnp.einsum(
            "yat,zat->ayz", block_grad, block_state_value_rows, preferred_element_type=jnp.float32
        )
        row_delta = jnp.sum(window_exact * grad_wprob, axis=-1) + jnp.sum(
            state_exact * grad_sprob, axis=-1
        )
        grad_wscore = (window_exact * (grad_wprob - row_delta[..., None])).astype(jnp.bfloat16)
        state_score_gradient = (state_exact * (grad_sprob - row_delta[..., None])).astype(
            jnp.bfloat16
        )
        block_grad_q = scores_scale * (
            jnp.einsum(
                "hij,jhe->ihe",
                grad_wscore,
                block_window_key_rows,
                preferred_element_type=jnp.float32,
            )
            + jnp.einsum(
                "wyd,dwg->ywg",
                state_score_gradient,
                block_state_key_rows,
                preferred_element_type=jnp.float32,
            )
        )
        block_grad_wk = scores_scale * jnp.einsum(
            "hij,ihe->jhe", grad_wscore, block_query_rows, preferred_element_type=jnp.float32
        )
        block_grad_wv = jnp.einsum(
            "hij,ihe->jhe",
            window_exact.astype(jnp.bfloat16),
            block_grad,
            preferred_element_type=jnp.float32,
        )
        block_grad_sk = (
            scores_scale
            * jnp.einsum(
                "him,ihe->mhe",
                state_score_gradient,
                block_query_rows,
                preferred_element_type=jnp.float32,
            )
        ).astype(jnp.bfloat16)
        block_grad_sv = jnp.einsum(
            "him,ihe->mhe",
            state_exact.astype(jnp.bfloat16),
            block_grad,
            preferred_element_type=jnp.float32,
        ).astype(jnp.bfloat16)
        return (
            bias_sum + grad_wscore.astype(jnp.float32),
            (block_grad_q, block_grad_wk, block_grad_wv, block_grad_sk, block_grad_sv),
        )

    bias_start = jnp.zeros((local_head_count, BLOCK, 2 * BLOCK), jnp.float32)
    bias_sum, back_items = lax.scan(
        attend_back,
        bias_start,
        (
            flattened_queries,
            flattened_window_keys,
            flattened_window_values,
            flattened_state_keys,
            flattened_state_values,
            permitted_mask,
            log_totals,
            grad_attended,
        ),
    )
    grad_bias = bias_gradient(bias_sum, bucket, bias_rows.shape[1])
    grad_queries = back_items[0].reshape(local_shape)
    grad_window_keys = back_items[1].reshape(
        seq_count, block_count, 2 * BLOCK, local_head_count, HEAD_SIZE
    )
    grad_window_values = back_items[2].reshape(
        seq_count, block_count, 2 * BLOCK, local_head_count, HEAD_SIZE
    )
    state_keys_gradient = back_items[3].reshape(
        seq_count, block_count, state_slot_count, local_head_count, HEAD_SIZE
    )
    grad_state_values = back_items[4].reshape(
        seq_count, block_count, state_slot_count, local_head_count, HEAD_SIZE
    )
    back_keys, back_values = (
        from_behind(grad_window_keys[:, 0, :BLOCK].astype(jnp.bfloat16), "ctx", -1).astype(
            jnp.float32
        ),
        from_behind(grad_window_values[:, 0, :BLOCK].astype(jnp.bfloat16), "ctx", -1).astype(
            jnp.float32
        ),
    )
    key_grad = grad_window_keys[:, :, BLOCK:] + jnp.concatenate(
        [grad_window_keys[:, 1:, :BLOCK], back_keys[:, None]], 1
    )
    value_grad = grad_window_values[:, :, BLOCK:] + jnp.concatenate(
        [grad_window_values[:, 1:, :BLOCK], back_values[:, None]], 1
    )
    state_key_gradient = jnp.einsum(
        "sbmhe,sbmhf->hef", state_reduced, state_keys_gradient, preferred_element_type=jnp.float32
    )
    grad_svalue = jnp.einsum(
        "sbmhe,sbmhf->hef", state_reduced, grad_state_values, preferred_element_type=jnp.float32
    )
    direct = jnp.einsum(
        "palcq,crq->palcr",
        state_keys_gradient,
        state_key_complete,
        preferred_element_type=jnp.float32,
    ) + jnp.einsum(
        "palcq,crq->palcr", grad_state_values, svalue_full, preferred_element_type=jnp.float32
    )
    direct = direct.reshape(seq_count, block_count, state_slot_count, local_width)
    back_accum = jnp.zeros((seq_count, state_slot_count, local_width), jnp.float32)
    for block_index in reversed(range(block_count)):
        back_accum = direct[:, block_index] + gate_value * back_accum
    back_identity = (jnp.ones((local_width,), jnp.float32), jnp.zeros_like(back_accum))
    unused_power, incoming = prefix_2((gate_power, back_accum), "ctx", compose, back_identity, True)
    carried = incoming
    contrib_grads = [None] * block_count
    gate_grad = jnp.zeros((local_width,), jnp.float32)
    for block_index in reversed(range(block_count)):
        contrib_grads[block_index] = ((1.0 - gate_value) * carried).astype(jnp.bfloat16)
        gate_grad = gate_grad + jnp.sum(
            carried * (stacked[:, block_index] - contrib[:, block_index]), axis=(0, 1)
        )
        carried = direct[:, block_index] + gate_value * carried
    first_device = (lax.axis_index("ctx") == 0).astype(jnp.float32)
    grad_sinit = first_device * jnp.sum(carried, axis=0)
    grad_gate = (gate_grad * gate_value * (1.0 - gate_value)).reshape(local_head_count, HEAD_SIZE)
    grad_contrib = jnp.stack(contrib_grads, axis=1).reshape(
        seq_count, block_count, state_slot_count, local_head_count, HEAD_SIZE
    )
    grad_read = jnp.einsum(
        "sbmhe,sbthe->sbhmt", grad_contrib, value_rows, preferred_element_type=jnp.float32
    )
    extra_values = jnp.einsum(
        "sbhmt,sbmhe->sbthe", read_low, grad_contrib, preferred_element_type=jnp.float32
    )
    read_delta = jnp.sum(read_probs * grad_read, axis=-1, keepdims=True)
    grad_read_score = (read_probs * (grad_read - read_delta)).astype(jnp.bfloat16)
    grad_squery = (
        scores_scale
        * jnp.einsum(
            "sbhmt,sbthe->mhe", grad_read_score, key_rows, preferred_element_type=jnp.float32
        )
    ).reshape(state_slot_count, local_width)
    extra_keys = scores_scale * jnp.einsum(
        "sbhmt,mhe->sbthe", grad_read_score, query_heads, preferred_element_type=jnp.float32
    )
    grad_q_rows = grad_queries.astype(jnp.bfloat16).reshape(row_count, local_width)
    grad_k_rows = (key_grad + extra_keys).astype(jnp.bfloat16).reshape(row_count, local_width)
    grad_v_rows = (value_grad + extra_values).astype(jnp.bfloat16).reshape(row_count, local_width)
    grad_wq = jnp.dot(attn_in.T, grad_q_rows, preferred_element_type=jnp.float32)
    grad_wk = jnp.dot(attn_in.T, grad_k_rows, preferred_element_type=jnp.float32)
    grad_wv = jnp.dot(attn_in.T, grad_v_rows, preferred_element_type=jnp.float32)
    grad_attn_in = (
        jnp.dot(grad_q_rows, query_full.T, preferred_element_type=jnp.float32)
        + jnp.dot(grad_k_rows, key_full.T, preferred_element_type=jnp.float32)
        + jnp.dot(grad_v_rows, value_full.T, preferred_element_type=jnp.float32)
    )
    part_tokens, part_gain_one = norm_backward(grad_attn_in, normed_one, inverse_one, gain_one_vec)
    token_share, grad_gain_one = (
        lax.psum_scatter(
            part_tokens.reshape(seq_count, length, full_width).astype(jnp.bfloat16),
            "tp",
            scatter_dimension=2,
            tiled=True,
        ).astype(jnp.float32),
        lax.psum_scatter(
            part_gain_one.reshape(head_total, HEAD_SIZE).astype(jnp.bfloat16),
            "tp",
            scatter_dimension=0,
            tiled=True,
        ).astype(jnp.float32),
    )
    grad_tokens = (middle_grad + token_share).astype(jnp.bfloat16)
    grads = (
        lax.psum_scatter(
            grad_wq.astype(jnp.bfloat16), ("dp", "ctx"), scatter_dimension=0, tiled=True
        ).astype(jnp.float32),
        lax.psum_scatter(
            grad_wk.astype(jnp.bfloat16), ("dp", "ctx"), scatter_dimension=0, tiled=True
        ).astype(jnp.float32),
        lax.psum_scatter(
            grad_wv.astype(jnp.bfloat16), ("dp", "ctx"), scatter_dimension=0, tiled=True
        ).astype(jnp.float32),
        lax.psum_scatter(
            grad_wout.astype(jnp.bfloat16), ("dp", "ctx"), scatter_dimension=1, tiled=True
        ).astype(jnp.float32),
        lax.psum_scatter(
            grad_up.astype(jnp.bfloat16), ("dp", "ctx"), scatter_dimension=0, tiled=True
        ).astype(jnp.float32),
        lax.psum_scatter(
            grad_down.astype(jnp.bfloat16), ("dp", "ctx"), scatter_dimension=1, tiled=True
        ).astype(jnp.float32),
        lax.psum_scatter(
            grad_squery.astype(jnp.bfloat16), ("dp", "ctx"), scatter_dimension=0, tiled=True
        ).astype(jnp.float32),
        lax.psum_scatter(
            grad_sinit.astype(jnp.bfloat16), ("dp", "ctx"), scatter_dimension=0, tiled=True
        ).astype(jnp.float32),
        lax.psum_scatter(
            grad_gain_one.astype(jnp.bfloat16), ("dp", "ctx"), scatter_dimension=1, tiled=True
        ).astype(jnp.float32),
        lax.psum_scatter(
            grad_gain_two.astype(jnp.bfloat16), ("dp", "ctx"), scatter_dimension=1, tiled=True
        ).astype(jnp.float32),
        lax.psum_scatter(
            grad_bias.astype(jnp.bfloat16), ("dp", "ctx"), scatter_dimension=1, tiled=True
        ).astype(jnp.float32),
        lax.psum_scatter(
            grad_gate.astype(jnp.bfloat16), ("dp", "ctx"), scatter_dimension=1, tiled=True
        ).astype(jnp.float32),
        lax.psum_scatter(
            state_key_gradient.astype(jnp.bfloat16), ("dp", "ctx"), scatter_dimension=1, tiled=True
        ).astype(jnp.float32),
        lax.psum_scatter(
            grad_svalue.astype(jnp.bfloat16), ("dp", "ctx"), scatter_dimension=1, tiled=True
        ).astype(jnp.float32),
    )
    return (
        output,
        grad_tokens,
        grads[0],
        grads[1],
        grads[2],
        grads[3],
        grads[4],
        grads[5],
        grads[6],
        grads[7],
        grads[8],
        grads[9],
        grads[10],
        grads[11],
        grads[12],
        grads[13],
    )


LOG2E = 1.4426950408889634
VMEM_BYTES = 58 * 1024 * 1024
BF = jnp.bfloat16
F32 = jnp.float32


def nn(left, right):
    return jnp.dot(left, right, preferred_element_type=F32)


def nt(left, right):
    return lax.dot_general(left, right, (((1,), (1,)), ((), ())), preferred_element_type=F32)


def tn(left, right):
    return lax.dot_general(left, right, (((0,), (0,)), ((), ())), preferred_element_type=F32)


def flat(ref):
    block = ref[0]
    return block.reshape(block.shape[0] * block.shape[1], block.shape[2])


def merged(place_ref, own_ref, other_ref):
    own = own_ref[0, :, 0]
    other = other_ref[0, :, 0]
    is_first = place_ref[0] == 0
    pair = [jnp.where(is_first, own, other), jnp.where(is_first, other, own)]
    block = jnp.stack(pair, axis=1)
    return block.reshape(-1, block.shape[-1])


def joined(tok_ref):
    return jnp.concatenate([tok_ref[part] for part in range(tok_ref.shape[0])], axis=1).astype(F32)


def inverse_rms(x):
    return lax.rsqrt(jnp.mean(x * x, axis=-1, keepdims=True) + EPSILON)


def params():
    return pltpu.CompilerParams(vmem_limit_bytes=VMEM_BYTES)


def project_kernel(
    place_ref, tok_ref, gain_ref, wq_ref, wqo_ref, wk_ref, wko_ref, wv_ref, wvo_ref,
    q_ref, k_ref, v_ref, ain_ref, last_ref,
):
    @pl.when(pl.program_id(0) == 0)
    def _():
        x = joined(tok_ref)
        ain_ref[...] = (x * inverse_rms(x) * gain_ref[...]).astype(BF)

    a = ain_ref[...]
    for w_ref, w_other, o_ref in (
        (wq_ref, wqo_ref, q_ref), (wk_ref, wko_ref, k_ref), (wv_ref, wvo_ref, v_ref)
    ):
        o_ref[...] = nn(a, merged(place_ref, w_ref, w_other)).astype(BF)
    length = k_ref.shape[0] * BLOCK // last_ref.shape[1]
    for item in range(last_ref.shape[1] // BLOCK):
        last = slice((item + 1) * length - BLOCK, (item + 1) * length)
        last_ref[0, item * BLOCK : (item + 1) * BLOCK] = k_ref[last]
        last_ref[1, item * BLOCK : (item + 1) * BLOCK] = v_ref[last]


def read_kernel(
    place_ref, sq_ref, sqo_ref, k_ref, v_ref, gate_ref, o_ref, sum_ref, state_ref, *, blocks
):
    n = pl.program_id(1)
    sq = merged(place_ref, sq_ref, sqo_ref)
    k = k_ref[...]
    v = v_ref[...]
    scale = HEAD_SIZE ** (-0.5) * LOG2E
    step = 256
    gate = jnp.where(lax.rem(n, blocks) == 0, 0.0, gate_ref[...])
    fresh = 1.0 - gate_ref[...]

    @pl.when(n == 0)
    def _():
        state_ref[...] = jnp.zeros_like(state_ref)

    for start in range(0, sq.shape[0], step):
        rows = slice(start, start + step)
        s = nt(sq[rows], k) * scale
        p = jnp.exp2(s - jnp.max(s, axis=-1, keepdims=True))
        total = jnp.sum(p, axis=-1, keepdims=True)
        contrib = nn(p.astype(BF), v) / total
        o_ref[rows, :] = contrib
        state = gate * state_ref[rows, :] + fresh * contrib
        state_ref[rows, :] = state
        sum_ref[rows, :] = state.astype(BF)


def attend_kernel(
    place_ref, info_ref, q_ref, k_ref, v_ref, kp_ref, vp_ref, hk_ref, hv_ref,
    wk_ref, wko_ref, wv_ref, wvo_ref, contrib_ref, init_ref, inito_ref, lead_ref, power_ref,
    gate_ref, u_ref, o_ref, lse_ref, low_ref, moved_ref, bias_ref, state_ref, *, blocks,
):
    n = pl.program_id(1)
    first = lax.rem(n, blocks) == 0
    scale = HEAD_SIZE ** (-0.5) * LOG2E

    @pl.when(n == 0)
    def _():
        row = jnp.broadcast_to(u_ref[0], (BLOCK, u_ref.shape[-1]))
        bias_ref[...] = pltpu.roll(row, 0, 1, stride=1, stride_axis=0)[:, : 2 * BLOCK]

    has_previous = info_ref[n, 0] > 0
    reach = info_ref[n, 1]
    k = k_ref[...]
    v = v_ref[...]
    kp = jnp.where(first, hk_ref[...], kp_ref[...])
    vp = jnp.where(first, hv_ref[...], vp_ref[...])

    @pl.when(first)
    def _():
        init = merged(place_ref, init_ref, inito_ref).astype(F32)
        state_ref[...] = power_ref[...] * init + lead_ref[...].astype(F32)

    state = state_ref[...]
    contrib = contrib_ref[...]
    st = state.astype(BF)
    low_ref[...] = st
    moved_ref[...] = (state - contrib).astype(BF)
    state_ref[...] = contrib + gate_ref[...] * (state - contrib)
    sk = nn(st, merged(place_ref, wk_ref, wko_ref)).astype(BF)
    sv = nn(st, merged(place_ref, wv_ref, wvo_ref)).astype(BF)
    step = ROWS_FORWARD

    def run(with_previous):
        for start in range(0, BLOCK, step):
            q = q_ref[start : start + step, :]
            sc = nt(q, k) * scale + bias_ref[start : start + step, BLOCK:]
            row = lax.broadcasted_iota(jnp.int32, (step, 1), 0) + start
            column = lax.broadcasted_iota(jnp.int32, (step, BLOCK), 1)
            sc = jnp.where(column <= jnp.maximum(row, reach - 1), sc, MASKED)
            ss = nt(q, sk) * scale
            peak = jnp.maximum(
                jnp.max(sc, axis=-1, keepdims=True), jnp.max(ss, axis=-1, keepdims=True)
            )
            if with_previous:
                sp = nt(q, kp) * scale + bias_ref[start : start + step, :BLOCK]
                peak = jnp.maximum(peak, jnp.max(sp, axis=-1, keepdims=True))
            pc = jnp.exp2(sc - peak)
            ps = jnp.exp2(ss - peak)
            total = jnp.sum(pc, axis=-1, keepdims=True) + jnp.sum(ps, axis=-1, keepdims=True)
            out = nn(pc.astype(BF), v) + nn(ps.astype(BF), sv)
            if with_previous:
                pp = jnp.exp2(sp - peak)
                total = total + jnp.sum(pp, axis=-1, keepdims=True)
                out = out + nn(pp.astype(BF), vp)
            o_ref[start : start + step, :] = (out / total).astype(BF)
            lse = jnp.broadcast_to(peak + jnp.log2(total), (step, 128))
            lse_ref[0, 0, :, start : start + step] = lse.T[:1]

    @pl.when(has_previous)
    def _():
        run(True)

    @pl.when(jnp.logical_not(has_previous))
    def _():
        run(False)


def attend_back_kernel(
    place_ref, info_ref, q_ref, k_ref, v_ref, kp_ref, vp_ref, hk_ref, hv_ref,
    wk_ref, wko_ref, wv_ref, wvo_ref, st_ref, gate_ref, u_ref, do_ref, o_ref, lse_ref,
    dq_ref, dk_ref, dv_ref, dkp_ref, dvp_ref, direct_ref, gwk_ref, gwv_ref, gb_ref, total_ref,
    firstk_ref, firstv_ref, bias_ref, sum_ref, dq_acc, state_acc, *, blocks,
):
    step_at = pl.program_id(1)
    n = pl.num_programs(1) - 1 - step_at
    first = lax.rem(n, blocks) == 0
    gate = jnp.where(lax.rem(n, blocks) == blocks - 1, 0.0, gate_ref[...])
    factor = HEAD_SIZE ** (-0.5)
    scale = factor * LOG2E
    window = 2 * BLOCK
    width = BLOCK + window

    @pl.when(step_at == 0)
    def _():
        state_acc[...] = jnp.zeros_like(state_acc)
        row = jnp.broadcast_to(u_ref[0], (window, u_ref.shape[-1]))
        bias_ref[...] = pltpu.roll(row, 0, 1, stride=1, stride_axis=0)[:, :BLOCK]
        sum_ref[...] = jnp.zeros_like(sum_ref)
        gwk_ref[...] = jnp.zeros_like(gwk_ref)
        gwv_ref[...] = jnp.zeros_like(gwv_ref)

    has_previous = info_ref[n, 0] > 0
    reach = info_ref[n, 1]
    q = q_ref[...]
    do = do_ref[...]
    lse = lse_ref[0, 0]
    delta = jnp.sum((do.astype(F32) * o_ref[...].astype(F32)).T, axis=0, keepdims=True)
    step = KEYS_BACKWARD

    def part(key, value, start, bias_start, masked):
        s = nt(key, q) * scale
        if bias_start is not None:
            s = s + bias_ref[bias_start : bias_start + step, :]
        if masked:
            key_at = lax.broadcasted_iota(jnp.int32, (step, BLOCK), 0) + start
            query_at = lax.broadcasted_iota(jnp.int32, (1, BLOCK), 1)
            s = jnp.where(key_at <= jnp.maximum(query_at, reach - 1), s, MASKED)
        p = jnp.exp2(s - lse)
        dp = nt(value, do)
        ds = (p * (dp - delta)).astype(BF)
        if bias_start is not None:
            for block in range(0, step, 128):
                at = window - bias_start - block
                sum_ref[:, at : at + BLOCK] += ds[block : block + 128].astype(F32)
        dq_acc[...] += tn(ds, key)
        return nn(ds, q) * factor, nn(p.astype(BF), do)

    dq_acc[...] = jnp.zeros_like(dq_acc)
    st = st_ref[...]
    key_map = merged(place_ref, wk_ref, wko_ref)
    value_map = merged(place_ref, wv_ref, wvo_ref)
    sk = nn(st, key_map).astype(BF)
    sv = nn(st, value_map).astype(BF)
    for start in range(0, st.shape[0], step):
        rows = slice(start, start + step)
        dk, dv = part(sk[rows], sv[rows], start, None, False)
        dk = dk.astype(BF)
        dv = dv.astype(BF)
        direct = nt(dk, key_map) + nt(dv, value_map)
        direct_ref[rows, :] = direct
        state = direct + gate * state_acc[rows, :]
        state_acc[rows, :] = state
        total_ref[rows, :] = state.astype(BF)
        gwk_ref[0] += tn(st[rows], dk)
        gwv_ref[0] += tn(st[rows], dv)
    for start in range(0, BLOCK, step):
        rows = slice(start, start + step)
        dk, dv = part(k_ref[rows, :], v_ref[rows, :], start, BLOCK + start, True)
        dk_ref[rows, :] = dk
        dv_ref[rows, :] = dv

    @pl.when(has_previous)
    def _():
        for start in range(0, BLOCK, step):
            rows = slice(start, start + step)
            key = jnp.where(first, hk_ref[rows, :], kp_ref[rows, :])
            value = jnp.where(first, hv_ref[rows, :], vp_ref[rows, :])
            dk, dv = part(key, value, start, start, False)
            dkp_ref[rows, :] = dk.astype(BF)
            dvp_ref[rows, :] = dv.astype(BF)

    @pl.when(jnp.logical_not(has_previous))
    def _():
        dkp_ref[...] = jnp.zeros_like(dkp_ref)
        dvp_ref[...] = jnp.zeros_like(dvp_ref)

    @pl.when(first)
    def _():
        firstk_ref[...] = dkp_ref[...]
        firstv_ref[...] = dvp_ref[...]

    dq_ref[...] = (dq_acc[...] * factor).astype(BF)

    @pl.when(n == 0)
    def _():
        folded = sum_ref[...]
        half = 64
        while half >= 8:
            folded = folded[:half] + pltpu.roll(folded[half:], width - half, 1)
            half //= 2
        total = folded[:1]
        for row in range(1, 8):
            total = total + pltpu.roll(folded[row : row + 1], width - row, 1)
        gb_ref[0] = total


def read_back_kernel(
    place_ref, sq_ref, sqo_ref, k_ref, v_ref, direct_ref, moved_ref, later_ref, gate_ref,
    dk_ref, dv_ref, nk_ref, nv_ref, rk_ref, rv_ref,
    gk_ref, gv_ref, gsq_ref, ginit_ref, ggate_ref, carried_ref, *, blocks,
):
    step_at = pl.program_id(1)
    n = pl.num_programs(1) - 1 - step_at
    last = lax.rem(n, blocks) == blocks - 1
    factor = HEAD_SIZE ** (-0.5)

    @pl.when(step_at == 0)
    def _():
        gsq_ref[...] = jnp.zeros_like(gsq_ref)
        ginit_ref[...] = jnp.zeros_like(ginit_ref)
        ggate_ref[...] = jnp.zeros_like(ggate_ref)

    @pl.when(last)
    def _():
        carried_ref[...] = later_ref[...].astype(F32)

    gate = gate_ref[...]
    carried = carried_ref[...]
    gc = ((1.0 - gate) * carried).astype(BF)
    change = jnp.sum(carried * moved_ref[...].astype(F32), axis=0, keepdims=True)
    ggate_ref[0] += change * (gate * (1.0 - gate))
    carried = direct_ref[...] + gate * carried
    carried_ref[...] = carried

    @pl.when((lax.rem(n, blocks) == 0) & (place_ref[0] == 0))
    def _():
        ginit_ref[...] += carried

    sq = merged(place_ref, sq_ref, sqo_ref)
    k = k_ref[...]
    s = nt(k, sq) * (factor * LOG2E)
    p = jnp.exp2(s - jnp.max(s, axis=0, keepdims=True))
    p = p * (1.0 / jnp.sum(p, axis=0, keepdims=True))
    dp = nt(v_ref[...], gc)
    ds = (p * (dp - jnp.sum(p * dp, axis=0, keepdims=True))).astype(BF)
    next_k = jnp.where(last, rk_ref[...], nk_ref[...]).astype(F32)
    next_v = jnp.where(last, rv_ref[...], nv_ref[...]).astype(F32)
    gk_ref[...] = (dk_ref[...] + next_k + nn(ds, sq) * factor).astype(BF)
    gv_ref[...] = (dv_ref[...] + next_v + nn(p.astype(BF), gc)).astype(BF)
    gsq_ref[...] += tn(ds, k) * factor


def item_kernel(wq_ref, wk_ref, wv_ref, sq_ref, init_ref, mk_ref, mv_ref, tail_ref, out_ref):
    at = 0
    for w_ref in (wq_ref, wk_ref, wv_ref, sq_ref, init_ref):
        out_ref[at : at + w_ref.shape[0]] = w_ref[...]
        at += w_ref.shape[0]
    for w_ref in (mk_ref, mv_ref):
        heads, rows, lanes = w_ref.shape
        for item in range(heads):
            out_ref[at : at + rows, item * lanes : (item + 1) * lanes] = w_ref[item]
        at += rows
    out_ref[at:] = tail_ref[...]


def assemble_kernel(place_ref, low_ref, lowy_ref, high_ref, highx_ref, own_ref):
    x_bit = place_ref[3]
    y_bit = place_ref[4]
    for x in range(2):
        own_ref[0, 2 * y_bit + x] = low_ref[x]
        own_ref[0, 2 * (1 - y_bit) + x] = lowy_ref[x]
    for y in range(2):
        own_ref[1, 2 * y + x_bit] = high_ref[y]
        own_ref[1, 2 * y + 1 - x_bit] = highx_ref[y]


def pack_kernel(up_ref, down_ref, out_ref, packed_ref):
    hidden = up_ref.shape[1]
    packed_ref[:, :hidden] = up_ref[...]
    packed_ref[:, hidden : 2 * hidden] = down_ref[...].T
    packed_ref[:, 2 * hidden :] = out_ref[...].T


def unpack_kernel(packed_ref, up_ref, down_ref, out_ref):
    hidden = up_ref.shape[1]
    up_ref[...] = packed_ref[:, :hidden].astype(F32)
    down_ref[...] = packed_ref[:, hidden : 2 * hidden].astype(F32).T
    out_ref[...] = packed_ref[:, 2 * hidden :].astype(F32).T


def finish_kernel(*refs):
    place_ref, refs = refs[0], refs[1:]
    for from_ref, to_ref in zip(refs[:2], refs[-3:-1]):
        to_ref[...] = from_ref[...]
    terms, outs = refs[2:-14], refs[-14:-3]
    sum_ref = refs[-1]
    total = terms[0][...].astype(F32)
    for term in terms[1:]:
        total = total + term[...].astype(F32)
    at = 0
    for out_ref in outs[:5]:
        out_ref[...] = total[at : at + out_ref.shape[0]]
        at += out_ref.shape[0]
    for out_ref in outs[5:7]:
        heads, rows, lanes = out_ref.shape
        for item in range(heads):
            out_ref[item] = total[at : at + rows, item * lanes : (item + 1) * lanes]
        at += rows
    sum_ref[...] = total[at:]
    shard, group = place_ref[1], place_ref[2]
    lanes = sum_ref.shape[1]
    for index, out_ref in enumerate(outs[7:]):
        heads, columns = out_ref.shape
        if index < 3:
            stride = HEAD_SIZE
            row = sum_ref[pl.ds(index * len(terms) + shard, 1), :]
            shift = group * columns
        else:
            stride = columns * (HEAD_SIZE // outs[7].shape[1])
            row = sum_ref[index * len(terms) : index * len(terms) + 1, :]
            shift = (shard * heads) * stride + group * columns
        row = pltpu.roll(row, lax.rem(lanes - shift, lanes), 1)
        for item in range(heads):
            out_ref[item : item + 1, :] = row[:, item * stride : item * stride + columns]


def out_kernel(att_ref, wo_ref, tok_ref, gain_ref, mid_ref, min_ref):
    t = pl.program_id(0)
    part = nt(att_ref[...], flat(wo_ref))

    @pl.when(t == 0)
    def _():
        mid_ref[...] = joined(tok_ref) + part

    @pl.when(t > 0)
    def _():
        mid_ref[...] += part

    @pl.when(t == pl.num_programs(0) - 1)
    def _():
        x = mid_ref[...].astype(BF).astype(F32)
        min_ref[...] = (x * inverse_rms(x) * gain_ref[...]).astype(BF)


def mlp_kernel(
    place_ref, min_ref, cot_ref, mid_ref, gain_ref, wu_ref, wd_ref,
    out_ref, gmid_ref, ggain_ref, gw_ref,
    min_t, cot_t, out_acc, gm_acc, hidden_ref,
):
    tile = pl.program_id(0)
    which = pl.program_id(1)

    @pl.when((tile == 0) & (which == 0))
    def _():
        min_t[...] = min_ref[...].T
        cot_t[...] = cot_ref[...].T
        out_acc[...] = jnp.zeros_like(out_acc)
        gm_acc[...] = jnp.zeros_like(gm_acc)

    @pl.when(which == 0)
    def _():
        wu = flat(wu_ref)
        wd = flat(wd_ref)
        pre = nn(min_ref[...], wu)
        cdf = 0.5 + 0.5 * lax.erf(pre * (0.5**0.5))
        density = jnp.exp2(pre * pre * (-0.5 * LOG2E)) * ((2.0 * np.pi) ** -0.5)
        hidden_ref[...] = (pre * cdf).astype(BF)
        grad_pre = (nn(cot_ref[...], wd) * (cdf + pre * density)).astype(BF)
        out_acc[...] += nt(hidden_ref[...], wd)
        gm_acc[...] += nt(grad_pre, wu)
        grad = nn(min_t[...], grad_pre).astype(BF)
        gw_ref[...] = grad.reshape(gw_ref.shape)

    @pl.when(which == 1)
    def _():
        grad = nn(cot_t[...], hidden_ref[...]).astype(BF)
        gw_ref[...] = grad.reshape(gw_ref.shape)

    @pl.when((tile == pl.num_programs(0) - 1) & (which == 1))
    def _():
        mid = mid_ref[...]
        lanes = out_ref.shape[2]
        for part in range(out_ref.shape[0]):
            at = slice(part * lanes, (part + 1) * lanes)
            out_ref[part] = (mid[:, at] + out_acc[:, at]).astype(BF)
        x = mid.astype(BF).astype(F32)
        inverse = inverse_rms(x)
        normed = x * inverse
        gm = gm_acc[...]
        ggain_ref[...] = jnp.sum(gm * normed, axis=0, keepdims=True)
        scaled = gm * gain_ref[...]
        back = inverse * (scaled - normed * jnp.mean(scaled * normed, axis=-1, keepdims=True))
        gmid_ref[...] = (cot_ref[...].astype(F32) + back).astype(BF)


def out_gradient_kernel(gmid_ref, att_ref, late_ref, gwo_ref, gmid_t):
    @pl.when(pl.program_id(0) == 0)
    def _():
        gmid_t[...] = gmid_ref[...].T

    gwo_ref[...] = nn(gmid_t[...], att_ref[...]).astype(BF).reshape(gwo_ref.shape)


def out_back_kernel(gmid_ref, wo_ref, gatt_ref):
    gatt_ref[...] = nn(gmid_ref[...], flat(wo_ref)).astype(BF)


def weight_back_kernel(
    place_ref, tok_ref, gain_ref, gq_ref, gk_ref, gv_ref, wq_ref, wqo_ref, wk_ref, wko_ref,
    wv_ref, wvo_ref, gsq_ref, ginit_ref, gmk_ref, gmv_ref,
    gown_ref, gother_ref, ggain_ref, ain_t, pack_ref, product_ref,
):
    t = pl.program_id(0)

    @pl.when(t == 0)
    def _():
        x = joined(tok_ref)
        ain_t[...] = (x * inverse_rms(x) * gain_ref[...]).astype(BF).T
        product_ref[...] = jnp.zeros_like(product_ref)

    groups, _, lanes = pack_ref.shape
    at = 0
    for g_ref, w_ref, w_other in (
        (gq_ref, wq_ref, wqo_ref), (gk_ref, wk_ref, wko_ref), (gv_ref, wv_ref, wvo_ref)
    ):
        grad = nn(ain_t[...], g_ref[...])
        product_ref[...] += grad * merged(place_ref, w_ref, w_other).astype(F32)
        rows = grad.shape[0] // groups
        pack_ref[:, at : at + rows] = grad.astype(BF).reshape(groups, rows, lanes)
        at += rows
    for g_ref in (gsq_ref, ginit_ref):
        rows = g_ref.shape[0] // groups
        pack_ref[:, at : at + rows] = g_ref[...].astype(BF).reshape(groups, rows, lanes)
        at += rows
    for g_ref in (gmk_ref, gmv_ref):
        rows = HEAD_SIZE // groups
        for item in range(g_ref.shape[0]):
            where = slice(item * HEAD_SIZE, (item + 1) * HEAD_SIZE)
            pack_ref[:, at : at + rows, where] = g_ref[item].astype(BF).reshape(groups, rows, -1)
        at += rows
    pack_ref[:, at:] = jnp.zeros_like(pack_ref[:, at:])
    for index in range(groups // 2):
        gown_ref[0, index] = pack_ref[2 * index + place_ref[0]]
        gother_ref[0, index] = pack_ref[2 * index + 1 - place_ref[0]]

    @pl.when(t == pl.num_programs(0) - 1)
    def _():
        ggain_ref[...] = jnp.sum(product_ref[...], axis=1, keepdims=True)


def project_back_kernel(
    place_ref, tok_ref, gmid_ref, gain_ref, gq_ref, gk_ref, gv_ref,
    wq_ref, wqo_ref, wk_ref, wko_ref, wv_ref, wvo_ref, gtok_ref, acc_ref,
):
    t = pl.program_id(0)

    @pl.when(t == 0)
    def _():
        acc_ref[...] = jnp.zeros_like(acc_ref)

    total = nt(gq_ref[...], merged(place_ref, wq_ref, wqo_ref))
    total = total + nt(gk_ref[...], merged(place_ref, wk_ref, wko_ref))
    acc_ref[...] += total + nt(gv_ref[...], merged(place_ref, wv_ref, wvo_ref))

    @pl.when(t == pl.num_programs(0) - 1)
    def _():
        x = joined(tok_ref)
        inverse = inverse_rms(x)
        normed = x * inverse
        scaled = acc_ref[...] * gain_ref[...]
        back = inverse * (scaled - normed * jnp.mean(scaled * normed, axis=-1, keepdims=True))
        grad = (gmid_ref[...].astype(F32) + back).astype(BF)
        lanes = gtok_ref.shape[2]
        for part in range(gtok_ref.shape[0]):
            gtok_ref[part] = grad[:, part * lanes : (part + 1) * lanes]


def distance_bucket(distance):
    magnitude = np.abs(distance)
    scaled = np.log(np.maximum(magnitude, 1) / 8.0) / np.log(16.0) * 8.0
    far = np.minimum(8 + np.floor(np.maximum(scaled, 0.0)).astype(np.int32), 15)
    return (distance < 0).astype(np.int32) * 16 + np.where(magnitude < 8, magnitude, far)


def one_hot(distance, valid, bucket_count):
    hot = distance_bucket(distance)[:, None] == np.arange(bucket_count)[None, :]
    return jnp.asarray((hot & valid[:, None]).astype(np.float32))


def carry(value, power, axis, backward):
    count = lax.axis_size(axis)
    sign = -1 if backward else 1
    total = from_behind(value.astype(BF), axis, sign)
    if count == 2:
        return total
    total = total.astype(F32)
    step = 1
    while step < count - 1:
        moved = from_behind(total.astype(BF), axis, sign * step).astype(F32)
        total = total + power**step * moved
        step *= 2
    return total


def across(value, axis, bit):
    count = lax.axis_size(axis)
    return lax.ppermute(value, axis, [(source, source ^ bit) for source in range(count)])


def take(value, index, dim):
    return lax.dynamic_index_in_dim(value, index, dim, False)


def add_low(left, right):
    return (left.astype(F32) + right.astype(F32)).astype(BF)


def ordered(bit, own, other, dim):
    first = bit == 0
    return jnp.stack([jnp.where(first, own, other), jnp.where(first, other, own)], axis=dim)


def gather_pairs(item, beside, behind, place):
    shards = lax.axis_size("tp")
    half = shards // 2
    tp = lax.axis_index("tp")
    x_bit = lax.axis_index("dp") % 2
    y_bit = lax.axis_index("dp") // 2
    parts = [item] + [across(item, "tp", k) for k in range(1, shards)]
    bit = 1
    while bit < shards:
        swap = (tp & bit) > 0
        parts = [jnp.where(swap, parts[k ^ bit], parts[k]) for k in range(shards)]
        bit *= 2
    low = jnp.stack(parts[:half])
    high = jnp.stack(parts[half:])
    low, high, behind = lax.optimization_barrier((low, high, behind))
    low_x = across(low, "dp", 1)
    high_y = across(high, "dp", 2)
    low = ordered(x_bit, low, low_x, 0)
    high = ordered(y_bit, high, high_y, 0)
    low_y = across(low, "dp", 2)
    high_x = across(high, "dp", 1)
    piece = pl.BlockSpec((2, 1) + item.shape, lambda i, *_: (0, i, 0, 0))
    own = pl.pallas_call(
        assemble_kernel,
        grid_spec=pltpu.PrefetchScalarGridSpec(
            num_scalar_prefetch=1, grid=(half,), in_specs=[piece] * 4,
            out_specs=pl.BlockSpec((2, 4, 1) + item.shape, lambda i, *_: (0, 0, i, 0, 0)),
        ),
        out_shape=jax.ShapeDtypeStruct((2, 4, half) + item.shape, BF),
        compiler_params=params(),
    )(place, low, low_y, high, high_x)
    own, beside = lax.optimization_barrier((own, beside))
    return own, across(own, "ctx", 1), beside, behind


def scatter_pairs(own, other):
    shards = own.shape[0]
    half = shards // 2
    tp = lax.axis_index("tp")
    x_bit = lax.axis_index("dp") % 2
    y_bit = lax.axis_index("dp") // 2
    grid = (shards, 2, 2) + own.shape[2:]
    moved = across(other, "ctx", 1).reshape(grid)
    own = own.reshape(grid)

    def both(part, index, dim):
        return add_low(take(own[part], index, dim), take(moved[part], index, dim))

    first, second = slice(0, half), slice(half, shards)
    low_moved = across(both(first, 1 - x_bit, 2), "dp", 1)
    high_moved = across(both(second, 1 - y_bit, 1), "dp", 2)
    low = add_low(both(first, x_bit, 2), low_moved)
    high = add_low(both(second, y_bit, 1), high_moved)
    low_moved = across(take(low, 1 - y_bit, 1), "dp", 2)
    high_moved = across(take(high, 1 - x_bit, 1), "dp", 1)
    low = add_low(take(low, y_bit, 1), low_moved)
    high = add_low(take(high, x_bit, 1), high_moved)
    kept = jnp.concatenate([low, high])
    return [take(kept, tp, 0)] + [
        across(take(kept, tp ^ k, 0), "tp", k) for k in range(1, shards)
    ]


def sequence_body(
    tokens, cotangent, prefix, w_query, w_key, w_value, w_out, w_up, w_down,
    state_query, state_init, gain_attn, gain_mlp, bias_table, gate_bias, state_key, state_value,
):
    shards = lax.axis_size("tp")
    groups = lax.axis_size("dp") * lax.axis_size("ctx")
    pairs = lax.axis_size("dp")
    half = shards // 2
    everywhere = ("tp", "dp", "ctx")
    seq_count, length, shard_width = tokens.shape
    width = cotangent.shape[2]
    seqs = seq_count // shards
    blocks = length // BLOCK
    units = seqs * blocks
    rows = units * BLOCK
    local_heads = bias_table.shape[0]
    heads = local_heads * shards
    buckets = bias_table.shape[1] * groups
    own_rows = w_query.shape[0]
    own_slots = state_query.shape[0]
    slots = own_slots * groups
    hidden = w_up.shape[1]
    tp_index = lax.axis_index("tp")
    ctx_index = lax.axis_index("ctx")
    dp_index = lax.axis_index("dp")
    head = HEAD_SIZE
    map_rows = state_key.shape[1]
    group = dp_index * lax.axis_size("ctx") + ctx_index
    place = jnp.stack([ctx_index, tp_index, group, dp_index % 2, dp_index // 2]).astype(jnp.int32)

    def call(kernel, grid, in_specs, out_specs, out_shape, scratch=(), prefetch=1, **more):
        return pl.pallas_call(
            kernel,
            grid_spec=pltpu.PrefetchScalarGridSpec(
                num_scalar_prefetch=prefetch, grid=grid, in_specs=in_specs, out_specs=out_specs,
                scratch_shapes=list(scratch),
            ),
            out_shape=out_shape,
            compiler_params=params(),
            **more,
        )

    at_slots = 3 * own_rows
    at_init = at_slots + own_slots
    at_maps = at_init + own_slots
    at_vectors = at_maps + 2 * map_rows
    full_rows = at_vectors + 16
    vectors = (gain_attn, gain_mlp, gate_bias, bias_table)
    ends = np.cumsum([0] + [item.shape[1] for item in vectors])
    tail = jnp.concatenate(vectors, axis=1)
    tail = jnp.pad(tail, ((0, 16 - local_heads), (0, shard_width - tail.shape[1])))
    item = pl.pallas_call(
        item_kernel, out_shape=jax.ShapeDtypeStruct((full_rows, shard_width), BF)
    )(w_query, w_key, w_value, state_query, state_init, state_key, state_value, tail)
    x = lax.all_to_all(tokens, "tp", 0, 0, tiled=True)
    late_width = 2 * hidden + shard_width
    late = pl.pallas_call(
        pack_kernel, out_shape=jax.ShapeDtypeStruct((own_rows, late_width), BF)
    )(w_up, w_down, w_out)
    first_own, first_other, x, late = gather_pairs(item, x, late, place)
    x = x.reshape(shards, rows, shard_width)
    late = lax.all_gather(late, everywhere, axis=0, tiled=True)
    late = late.reshape(shards, groups, own_rows, late_width)

    at_heads = slice(at_vectors, at_vectors + local_heads)
    small = ordered(
        ctx_index, first_own[:, :, :, at_heads], first_other[:, :, :, at_heads], 2
    )

    def spread(index):
        part = small[..., ends[index] : ends[index + 1]]
        return jnp.transpose(part, (0, 3, 4, 1, 2, 5)).reshape(heads, -1).astype(F32)

    gain_one = spread(0).reshape(1, width)
    gain_two = spread(1).reshape(1, width)
    gate = jax.nn.sigmoid(spread(2)).reshape(1, width)
    bias_rows = spread(3)

    def whole(shape):
        return pl.BlockSpec(shape, lambda *_: (0,) * len(shape))

    def weight(index):
        spec = pl.BlockSpec(
            (1, pairs, 1, own_rows, shard_width), lambda t, *_: (t // half, 0, t % half, index, 0)
        )
        return [spec, spec]

    def of_head(count, index):
        def at(h, *_):
            t = h // local_heads
            return (t // half, 0, t % half, index, h % local_heads)

        spec = pl.BlockSpec((1, pairs, 1, count, head), at)
        return [spec, spec]

    column = pl.BlockSpec((rows, shard_width), lambda t, *_: (0, t))
    wide = jax.ShapeDtypeStruct((rows, width), BF)
    wide32 = jax.ShapeDtypeStruct((rows, width), F32)
    split = jax.ShapeDtypeStruct((shards, rows, shard_width), BF)
    halo = jax.ShapeDtypeStruct((seqs * BLOCK, width), BF)
    halo_column = pl.BlockSpec((2, seqs * BLOCK, shard_width), lambda t, *_: (0, 0, t))
    queries, keys, values, _, last_blocks = call(
        project_kernel,
        (shards,),
        [whole((shards, rows, shard_width)), whole((1, width))] + weight(0) + weight(1) + weight(2),
        [column, column, column, whole((rows, width)), halo_column],
        [wide] * 4 + [jax.ShapeDtypeStruct((2, seqs * BLOCK, width), BF)],
    )(place, x, gain_one, *([first_own, first_other] * 3))

    halos = from_behind(last_blocks, "ctx", 1)

    def along(rows_of, index):
        return pl.BlockSpec((rows_of, head), lambda h, n, *_: (index(n), h))

    def turned(n):
        return units - 1 - n

    query_slots = of_head(own_slots, at_slots // own_slots)
    init_slots = of_head(own_slots, at_init // own_slots)
    key_maps = of_head(map_rows, at_maps // map_rows)
    value_maps = of_head(map_rows, at_maps // map_rows + 1)
    channel = pl.BlockSpec((1, head), lambda h, n, *_: (0, h))
    slot_rows = units * slots
    slot_f32 = jax.ShapeDtypeStruct((slot_rows, width), F32)
    slot_low = jax.ShapeDtypeStruct((slot_rows, width), BF)
    message = jax.ShapeDtypeStruct((seqs * slots, width), BF)
    slot_scratch = pltpu.VMEM((slots, head), F32)
    own = along(BLOCK, lambda n: n)
    slot = along(slots, lambda n: n)
    slot_of_seq = along(slots, lambda n: n // blocks)
    contrib, accumulated = call(
        functools.partial(read_kernel, blocks=blocks),
        (heads, units),
        query_slots + [own, own, channel],
        [slot, slot_of_seq],
        [slot_f32, message],
        [slot_scratch],
    )(place, first_own, first_other, keys, values, gate)
    halos, accumulated = lax.optimization_barrier((halos, accumulated))
    power = gate**blocks
    lead = carry(accumulated, power, "ctx", False)
    lead_power = jnp.ones_like(gate)
    for step in range(lax.axis_size("ctx") - 1):
        lead_power = jnp.where(ctx_index > step, lead_power * power, lead_power)

    block_at = ctx_index * blocks + jnp.arange(blocks, dtype=jnp.int32)
    own_prefix = lax.dynamic_slice_in_dim(prefix, tp_index * seqs, seqs, 0)
    info = jnp.stack(
        [
            jnp.broadcast_to(block_at[None], (seqs, blocks)),
            own_prefix[:, None] - block_at[None] * BLOCK,
        ],
        axis=-1,
    ).reshape(units, 2)
    span = 4 * BLOCK
    offset = np.arange(span)
    offset = np.where(offset < 2 * BLOCK, offset, offset - span)
    forward_hot = one_hot(BLOCK - offset, offset > -BLOCK, buckets)
    back_span = 3 * BLOCK
    back_offset = np.arange(back_span)
    back_offset = np.where(back_offset < BLOCK, back_offset, back_offset - back_span)
    backward_hot = one_hot(BLOCK + back_offset, back_offset > -2 * BLOCK, buckets)
    exact = lax.Precision.HIGHEST
    scaled_bias = bias_rows * LOG2E
    forward_bias = jnp.dot(scaled_bias, forward_hot.T, precision=exact)[:, None]
    backward_bias = jnp.dot(scaled_bias, backward_hot.T, precision=exact)[:, None]

    def attend_specs(index):
        before = along(BLOCK, lambda n: jnp.maximum(index(n) - 1, 0))
        by_seq = [
            pl.BlockSpec((None, BLOCK, head), lambda h, n, *_, part=part: (part, index(n) // blocks, h))
            for part in range(2)
        ]
        here = along(BLOCK, index)
        return [here, here, here, before, before] + by_seq + key_maps + value_maps

    def lse_spec(index):
        return pl.BlockSpec((1, 1, 1, BLOCK), lambda h, n, *_: (index(n), h, 0, 0))

    def vector(size):
        return pl.BlockSpec((1, 1, size), lambda h, *_: (h, 0, 0))

    attend_args = (
        place, info, queries, keys, values, keys, values, halos, halos,
        first_own, first_other, first_own, first_other,
    )
    attended, lse, states, moved = call(
        functools.partial(attend_kernel, blocks=blocks),
        (heads, units),
        attend_specs(lambda n: n)
        + [slot] + init_slots + [slot_of_seq, channel, channel, vector(span)],
        [own, lse_spec(lambda n: n), slot, slot],
        [wide, jax.ShapeDtypeStruct((units, heads, 1, BLOCK), F32), slot_low, slot_low],
        [pltpu.VMEM((BLOCK, 2 * BLOCK), F32), slot_scratch],
        2,
    )(*attend_args, contrib, first_own, first_other, lead, lead_power, gate, forward_bias)

    out_weight = pl.BlockSpec(
        (1, groups, own_rows, shard_width), lambda t, *_: (t, 0, 0, 2 * hidden // shard_width)
    )
    middle, mlp_in = pl.pallas_call(
        out_kernel,
        grid=(shards,),
        in_specs=[column, out_weight, whole((shards, rows, shard_width)), whole((1, width))],
        out_specs=[whole((rows, width)), whole((rows, width))],
        out_shape=[wide32, wide],
        compiler_params=params(),
    )(attended, late, x, gain_two)

    tile = min(hidden, 1024)
    per_shard = hidden // tile
    tile_block = (1, groups, own_rows, tile)
    output, middle_grad, gain_two_grad, late_grad = call(
        mlp_kernel,
        (shards * per_shard, 2),
        [
            whole((rows, width)),
            pl.BlockSpec((rows, width), lambda i, j, place_ref: (place_ref[1], 0)),
            whole((rows, width)), whole((1, width)),
            pl.BlockSpec(tile_block, lambda i, j, *_: (i // per_shard, 0, 0, i % per_shard)),
            pl.BlockSpec(
                tile_block, lambda i, j, *_: (i // per_shard, 0, 0, per_shard + i % per_shard)
            ),
        ],
        [
            whole((shards, rows, shard_width)), whole((rows, width)), whole((1, width)),
            pl.BlockSpec(
                tile_block, lambda i, j, *_: (i // per_shard, 0, 0, j * per_shard + i % per_shard)
            ),
        ],
        [
            split, wide, jax.ShapeDtypeStruct((1, width), F32),
            jax.ShapeDtypeStruct((shards, groups, own_rows, late_width), BF),
        ],
        [
            pltpu.VMEM((width, rows), BF), pltpu.VMEM((width, rows), BF),
            pltpu.VMEM((rows, width), F32), pltpu.VMEM((rows, width), F32),
            pltpu.VMEM((rows, tile), BF),
        ],
    )(
        place, mlp_in, cotangent.reshape(seq_count * length, width), middle, gain_two, late, late
    )
    output = lax.all_to_all(output, "tp", 0, 0, tiled=True)

    late_grad = pl.pallas_call(
        out_gradient_kernel,
        grid=(shards,),
        in_specs=[whole((rows, width)), column, pl.BlockSpec(memory_space=pl.ANY)],
        out_specs=out_weight,
        out_shape=jax.ShapeDtypeStruct(late_grad.shape, BF),
        scratch_shapes=[pltpu.VMEM((width, rows), BF)],
        compiler_params=params(),
        input_output_aliases={2: 0},
    )(middle_grad, attended, late_grad)
    grad_attended = pl.pallas_call(
        out_back_kernel,
        grid=(shards,),
        in_specs=[whole((rows, width)), out_weight],
        out_specs=column,
        out_shape=wide,
        compiler_params=params(),
    )(middle_grad, late)
    late_grad = lax.psum_scatter(
        late_grad.reshape(shards * groups * own_rows, late_width), everywhere,
        scatter_dimension=0, tiled=True,
    )
    head_sum = jax.ShapeDtypeStruct((heads, head, head), F32)
    head_map = pl.BlockSpec((1, head, head), lambda h, n, *_: (h, 0, 0))
    back_own = along(BLOCK, turned)
    back_slot = along(slots, turned)
    back_of_seq = along(slots, lambda n: turned(n) // blocks)
    key_of_seq = along(BLOCK, lambda n: turned(n) // blocks)
    (
        grad_queries, dk, dv, dk_before, dv_before, direct, key_map_grad, value_map_grad,
        bias_sum, gathered, first_keys, first_values,
    ) = call(
        functools.partial(attend_back_kernel, blocks=blocks),
        (heads, units),
        attend_specs(turned)
        + [back_slot, channel, vector(back_span), back_own, back_own, lse_spec(turned)],
        [back_own] * 5 + [back_slot, head_map, head_map, vector(back_span), back_of_seq]
        + [key_of_seq, key_of_seq],
        [
            wide, wide32, wide32, wide, wide, slot_f32, head_sum, head_sum,
            jax.ShapeDtypeStruct((heads, 1, back_span), F32), message, halo, halo,
        ],
        [
            pltpu.VMEM((2 * BLOCK, BLOCK), F32), pltpu.VMEM((128, back_span), F32),
            pltpu.VMEM((BLOCK, head), F32), slot_scratch,
        ],
        2,
    )(*attend_args, states, gate, backward_bias, grad_attended, attended, lse)
    dk, output = lax.optimization_barrier((dk, output))
    sum_at = np.arange(back_span) - BLOCK
    sum_hot = one_hot(sum_at, sum_at > -BLOCK, buckets)
    bias_grad = jnp.dot(bias_sum[:, 0], sum_hot, precision=exact)

    later = carry(gathered, power, "ctx", True)
    back_keys = from_behind(first_keys, "ctx", -1)
    back_values = from_behind(first_values, "ctx", -1)
    following = along(BLOCK, lambda n: jnp.minimum(turned(n) + 1, units - 1))
    kept_slot = pl.BlockSpec((slots, head), lambda h, n, *_: (0, h))
    slot_sum = jax.ShapeDtypeStruct((slots, width), F32)
    grad_keys, grad_values, slot_query_grad, init_grad, gate_grad = call(
        functools.partial(read_back_kernel, blocks=blocks),
        (heads, units),
        query_slots
        + [back_own, back_own, back_slot, back_slot, back_of_seq, channel]
        + [back_own, back_own, following, following, key_of_seq, key_of_seq],
        [back_own, back_own, kept_slot, kept_slot, vector(head)],
        [wide, wide, slot_sum, slot_sum, jax.ShapeDtypeStruct((heads, 1, head), F32)],
        [slot_scratch],
    )(
        place, first_own, first_other, keys, values, direct, moved, later, gate,
        dk, dv, dk_before, dv_before, back_keys, back_values,
    )

    maps_of = pl.BlockSpec((local_heads, head, head), lambda t, *_: (t, 0, 0))
    slots_of = pl.BlockSpec((slots, shard_width), lambda t, *_: (0, t))
    piece = pl.BlockSpec((1, pairs, full_rows, shard_width), lambda t, *_: (t, 0, 0, 0))
    pieces = jax.ShapeDtypeStruct((shards, pairs, full_rows, shard_width), BF)
    token_shards = whole((shards, rows, shard_width))
    weights = weight(0) + weight(1) + weight(2)
    weight_args = [first_own, first_other] * 3
    grad_own, grad_other, gain_one_grad = call(
        weight_back_kernel,
        (shards,),
        [token_shards, whole((1, width)), column, column, column]
        + weights + [slots_of, slots_of, maps_of, maps_of],
        [piece, piece, whole((width, 1))],
        [pieces, pieces, jax.ShapeDtypeStruct((width, 1), F32)],
        [
            pltpu.VMEM((width, rows), BF), pltpu.VMEM((groups, full_rows, shard_width), BF),
            pltpu.VMEM((width, shard_width), F32),
        ],
    )(
        place, x, gain_one, grad_queries, grad_keys, grad_values, *weight_args,
        slot_query_grad, init_grad, key_map_grad, value_map_grad,
    )
    gain_one_grad = gain_one_grad.reshape(1, width) / gain_one
    token_grad = call(
        project_back_kernel,
        (shards,),
        [token_shards, whole((rows, width)), whole((1, width)), column, column, column] + weights,
        token_shards,
        split,
        [pltpu.VMEM((rows, width), F32)],
    )(place, x, middle_grad, gain_one, grad_queries, grad_keys, grad_values, *weight_args)
    token_grad = lax.all_to_all(token_grad, "tp", 0, 0, tiled=True)

    vector_sums = [gain_one_grad, gain_two_grad, gate_grad.reshape(1, width), bias_grad]
    vector_rows = jnp.concatenate([item.reshape(-1) for item in vector_sums])
    vector_rows = jnp.pad(vector_rows, (0, 16 * shard_width - vector_rows.size)).astype(BF)
    vector_rows = jnp.broadcast_to(
        vector_rows.reshape(1, 1, 16, shard_width), (shards, pairs, 16, shard_width)
    )
    grad_own = lax.dynamic_update_slice(grad_own, vector_rows, (0, 0, at_vectors, 0))
    grad_other = lax.dynamic_update_slice(grad_other, vector_rows, (0, 0, at_vectors, 0))
    terms = scatter_pairs(grad_own, grad_other)
    parts = (
        w_query, w_key, w_value, state_query, state_init, state_key, state_value,
        gain_attn, gain_mlp, gate_bias, bias_table,
    )
    sums = call(
        finish_kernel,
        (1,),
        [whole(output.shape)] * 2 + [whole((full_rows, shard_width))] * shards,
        [whole(item.shape) for item in parts] + [whole(output.shape)] * 2,
        [jax.ShapeDtypeStruct(item.shape, F32) for item in parts]
        + [jax.ShapeDtypeStruct(output.shape, BF)] * 2,
        [pltpu.VMEM((16, shard_width), F32)],
    )(place, output, token_grad, *terms)
    late_grad, sums = lax.optimization_barrier((late_grad, sums))
    up_grad, down_grad, out_grad = pl.pallas_call(
        unpack_kernel,
        out_shape=[
            jax.ShapeDtypeStruct(w_up.shape, F32), jax.ShapeDtypeStruct(w_down.shape, F32),
            jax.ShapeDtypeStruct(w_out.shape, F32),
        ],
    )(late_grad)
    return (
        sums[11].reshape(seq_count, length, shard_width),
        sums[12].reshape(seq_count, length, shard_width),
        *sums[:3],
        out_grad,
        up_grad,
        down_grad,
        *sums[3:5],
        sums[7],
        sums[8],
        sums[10],
        sums[9],
        *sums[5:7],
    )


def choose(tokens, *others):
    shards = lax.axis_size("tp")
    even = tokens.shape[0] % shards == 0 and shards % 2 == 0 and shards & (shards - 1) == 0
    even = even and lax.axis_size("dp") == 4 and lax.axis_size("ctx") == 2
    return (sequence_body if even else body)(tokens, *others)


def solution(mesh):
    in_specs = (
        P("dp", "ctx", "tp"),
        P("dp", "ctx", None),
        P("dp"),
        P(("dp", "ctx"), "tp"),
        P(("dp", "ctx"), "tp"),
        P(("dp", "ctx"), "tp"),
        P("tp", ("dp", "ctx")),
        P(("dp", "ctx"), "tp"),
        P("tp", ("dp", "ctx")),
        P(("dp", "ctx"), "tp"),
        P(("dp", "ctx"), "tp"),
        P("tp", ("dp", "ctx")),
        P("tp", ("dp", "ctx")),
        P("tp", ("dp", "ctx")),
        P("tp", ("dp", "ctx")),
        P("tp", ("dp", "ctx"), None),
        P("tp", ("dp", "ctx"), None),
    )
    out_specs = (
        P("dp", "ctx", "tp"),
        P("dp", "ctx", "tp"),
        P(("dp", "ctx"), "tp"),
        P(("dp", "ctx"), "tp"),
        P(("dp", "ctx"), "tp"),
        P("tp", ("dp", "ctx")),
        P(("dp", "ctx"), "tp"),
        P("tp", ("dp", "ctx")),
        P(("dp", "ctx"), "tp"),
        P(("dp", "ctx"), "tp"),
        P("tp", ("dp", "ctx")),
        P("tp", ("dp", "ctx")),
        P("tp", ("dp", "ctx")),
        P("tp", ("dp", "ctx")),
        P("tp", ("dp", "ctx"), None),
        P("tp", ("dp", "ctx"), None),
    )
    return jax.shard_map(choose, mesh=mesh, in_specs=in_specs, out_specs=out_specs, check_vma=False)
```

```python
import functools

import jax
import jax.numpy as jnp
import numpy as np
from jax import lax
from jax.experimental import pallas as pl
from jax.experimental.pallas import tpu as pltpu
from jax.sharding import PartitionSpec as P

HEAD_SIZE = 128
BLOCK = 512


EPSILON = 1e-06
MASKED = -1e30
ROWS_FORWARD = 128
KEYS_BACKWARD = 256


def from_behind(value, axis, steps):
    count = lax.axis_size(axis)
    first, last = (max(0, -steps), min(count, count - steps))
    return lax.ppermute(value, axis, [(source, source + steps) for source in range(first, last)])


def prefix_2(array, axis, join, neutral, backward):
    count = lax.axis_size(axis)
    place = lax.axis_index(axis)
    ahead = count - 1 - place if backward else place
    gathered = jax.tree.map(
        lambda a, kind: lax.all_gather(a.astype(kind), axis), array, (jnp.bfloat16, jnp.bfloat16)
    )
    state = jax.tree.map(lambda a, e: jnp.zeros_like(a) + jnp.asarray(e, a.dtype), array, neutral)

    def one(hop, state):
        source = count - 1 - hop if backward else hop
        return join(
            state,
            jax.tree.map(
                lambda a, own: lax.dynamic_index_in_dim(a, source, 0, False).astype(own.dtype),
                gathered,
                array,
            ),
        )

    return lax.fori_loop(0, ahead, one, state)


def bucket_index(block_size):
    query_pos = np.arange(block_size)[:, None] + block_size
    key_pos = np.arange(2 * block_size)[None, :]
    distance = query_pos - key_pos
    upper_part = (distance < 0).astype(np.int32) * 16
    magnitude = np.abs(distance)
    scaled = np.log(np.maximum(magnitude, 1) / 8.0) / np.log(16.0) * 8.0
    far_bucket = np.minimum(8 + np.floor(np.maximum(scaled, 0.0)).astype(np.int32), 15)
    return (upper_part + np.where(magnitude < 8, magnitude, far_bucket)).astype(np.int32)


def norm_forward(features, gain_vector):
    inverse = lax.rsqrt(jnp.mean(features * features, axis=-1, keepdims=True) + EPSILON)
    normed = features * inverse
    return (normed, inverse, (normed * gain_vector).astype(jnp.bfloat16))


def norm_backward(grad_normed, normed, inverse, gain_vector):
    scaled = grad_normed * gain_vector
    grad_in = inverse * (scaled - normed * jnp.mean(scaled * normed, axis=-1, keepdims=True))
    return (grad_in, jnp.sum(grad_normed * normed, axis=0))


def compose(earlier, later_pair):
    return (earlier[0] * later_pair[0], later_pair[0] * earlier[1] + later_pair[1])


def bias_matrix(bias_rows, bucket):
    summed = jnp.zeros((bias_rows.shape[0],) + bucket.shape, jnp.float32)
    for number in range(bias_rows.shape[1]):
        summed = (
            summed
            + bias_rows[:, number][:, None, None] * (bucket == number).astype(jnp.float32)[None]
        )
    return summed


def bias_gradient(grad_matrix, bucket, bucket_count):
    columns = [
        jnp.sum(grad_matrix * (bucket == number).astype(jnp.float32)[None], axis=(1, 2))
        for number in range(bucket_count)
    ]
    return jnp.stack(columns, axis=1)


def body(
    tokens,
    cotangent,
    prefix,
    w_query,
    w_key,
    w_value,
    w_out,
    w_up,
    w_down,
    state_query,
    state_init,
    gain_attn,
    gain_mlp,
    bias_table,
    gate_bias,
    state_key,
    state_value,
):
    (
        query_full,
        key_full,
        value_full,
        out_full,
        up_full,
        down_full,
        squery_full,
        sinit_full,
        gain_one,
        gain_two,
        bias_rows,
        gate_rows,
        state_key_complete,
        svalue_full,
    ) = (
        lax.all_gather(w_query, ("dp", "ctx"), axis=0, tiled=True),
        lax.all_gather(w_key, ("dp", "ctx"), axis=0, tiled=True),
        lax.all_gather(w_value, ("dp", "ctx"), axis=0, tiled=True),
        lax.all_gather(w_out, ("dp", "ctx"), axis=1, tiled=True),
        lax.all_gather(w_up, ("dp", "ctx"), axis=0, tiled=True),
        lax.all_gather(w_down, ("dp", "ctx"), axis=1, tiled=True),
        lax.all_gather(state_query, ("dp", "ctx"), axis=0, tiled=True),
        lax.all_gather(state_init, ("dp", "ctx"), axis=0, tiled=True),
        lax.all_gather(gain_attn, ("dp", "ctx"), axis=1, tiled=True),
        lax.all_gather(gain_mlp, ("dp", "ctx"), axis=1, tiled=True),
        lax.all_gather(bias_table, ("dp", "ctx"), axis=1, tiled=True),
        lax.all_gather(gate_bias, ("dp", "ctx"), axis=1, tiled=True),
        lax.all_gather(state_key, ("dp", "ctx"), axis=1, tiled=True),
        lax.all_gather(state_value, ("dp", "ctx"), axis=1, tiled=True),
    )
    seq_count = tokens.shape[0]
    length = tokens.shape[1]
    shard_width = tokens.shape[2]
    full_width = cotangent.shape[2]
    block_count = length // BLOCK
    row_count = seq_count * length
    local_head_count = bias_rows.shape[0]
    local_width = local_head_count * HEAD_SIZE
    state_slot_count = squery_full.shape[0]
    scores_scale = HEAD_SIZE ** (-0.5)
    local_shape = (seq_count, block_count, BLOCK, local_head_count, HEAD_SIZE)
    element_count = seq_count * block_count
    token_full, gain_one_full = (
        lax.all_gather(tokens, "tp", axis=2, tiled=True),
        lax.all_gather(gain_one, "tp", axis=0, tiled=True),
    )
    gain_one_vec = gain_one_full.reshape(full_width).astype(jnp.float32)
    normed_one, inverse_one, attn_in = norm_forward(
        token_full.reshape(row_count, full_width).astype(jnp.float32), gain_one_vec
    )
    queries = (
        jnp.dot(attn_in, query_full, preferred_element_type=jnp.float32)
        .astype(jnp.bfloat16)
        .reshape(local_shape)
    )
    key_rows = (
        jnp.dot(attn_in, key_full, preferred_element_type=jnp.float32)
        .astype(jnp.bfloat16)
        .reshape(local_shape)
    )
    value_rows = (
        jnp.dot(attn_in, value_full, preferred_element_type=jnp.float32)
        .astype(jnp.bfloat16)
        .reshape(local_shape)
    )
    last_keys, last_values = from_behind((key_rows[:, -1], value_rows[:, -1]), "ctx", 1)
    window_keys = jnp.concatenate(
        [jnp.concatenate([last_keys[:, None], key_rows[:, :-1]], 1), key_rows], 2
    )
    window_values = jnp.concatenate(
        [jnp.concatenate([last_values[:, None], value_rows[:, :-1]], 1), value_rows], 2
    )
    query_heads = squery_full.reshape(state_slot_count, local_head_count, HEAD_SIZE)
    read_scores = (
        jnp.einsum("mhe,sbthe->sbhmt", query_heads, key_rows, preferred_element_type=jnp.float32)
        * scores_scale
    )
    read_peak = jnp.max(read_scores, axis=-1, keepdims=True)
    read_raised = jnp.exp(read_scores - read_peak)
    read_probs = read_raised / jnp.sum(read_raised, axis=-1, keepdims=True)
    read_low = read_probs.astype(jnp.bfloat16)
    contrib = jnp.einsum(
        "sbhmt,sbthe->sbmhe", read_low, value_rows, preferred_element_type=jnp.float32
    )
    contrib = contrib.reshape(seq_count, block_count, state_slot_count, local_width)
    gate_value = jax.nn.sigmoid(gate_rows.reshape(local_width).astype(jnp.float32))
    gate_power = jnp.ones((local_width,), jnp.float32)
    accumulated = jnp.zeros((seq_count, state_slot_count, local_width), jnp.float32)
    for block_index in range(block_count):
        accumulated = gate_value * accumulated + (1.0 - gate_value) * contrib[:, block_index]
        gate_power = gate_power * gate_value
    identity = (jnp.ones((local_width,), jnp.float32), jnp.zeros_like(accumulated))
    lead_power, lead_state = prefix_2((gate_power, accumulated), "ctx", compose, identity, False)
    entry_state = lead_power * sinit_full.astype(jnp.float32) + lead_state
    state_list = [entry_state]
    block_index = 0
    state_list.append(gate_value * state_list[-1] + (1.0 - gate_value) * contrib[:, block_index])
    stacked = jnp.stack(state_list, axis=1)
    state_reduced = stacked.astype(jnp.bfloat16).reshape(
        seq_count, block_count, state_slot_count, local_head_count, HEAD_SIZE
    )
    state_key_rows = jnp.einsum(
        "cazqr,qrx->cazqx", state_reduced, state_key_complete, preferred_element_type=jnp.float32
    ).astype(jnp.bfloat16)
    state_values = jnp.einsum(
        "cazqr,qrx->cazqx", state_reduced, svalue_full, preferred_element_type=jnp.float32
    ).astype(jnp.bfloat16)
    bucket = jnp.asarray(bucket_index(BLOCK))
    bias_full = bias_matrix(bias_rows.astype(jnp.float32), bucket)
    block_ids = lax.axis_index("ctx") * block_count + jnp.arange(block_count, dtype=jnp.int32)
    query_pos = block_ids[:, None] * BLOCK + jnp.arange(BLOCK, dtype=jnp.int32)[None, :]
    key_pos = (block_ids[:, None] - 1) * BLOCK + jnp.arange(2 * BLOCK, dtype=jnp.int32)[None, :]
    causal = (key_pos[:, None, :] >= 0) & (key_pos[:, None, :] <= query_pos[:, :, None])
    in_prefix = (key_pos[None, :, None, :] >= 0) & (
        key_pos[None, :, None, :] < prefix[:, None, None, None]
    )
    permitted_mask = (causal[None] | in_prefix).reshape(element_count, 1, BLOCK, 2 * BLOCK)
    flattened_queries = queries.reshape(element_count, BLOCK, local_head_count, HEAD_SIZE)
    flattened_window_keys = window_keys.reshape(
        element_count, 2 * BLOCK, local_head_count, HEAD_SIZE
    )
    flattened_window_values = window_values.reshape(
        element_count, 2 * BLOCK, local_head_count, HEAD_SIZE
    )
    flattened_state_keys = state_key_rows.reshape(
        element_count, state_slot_count, local_head_count, HEAD_SIZE
    )
    flattened_state_values = state_values.reshape(
        element_count, state_slot_count, local_head_count, HEAD_SIZE
    )

    def block_score_rows(
        block_query_rows, block_window_key_rows, block_state_key_rows, block_permitted_mask
    ):
        window_part = (
            jnp.einsum(
                "ihe,jhe->hij",
                block_query_rows,
                block_window_key_rows,
                preferred_element_type=jnp.float32,
            )
            * scores_scale
            + bias_full
        )
        state_part = (
            jnp.einsum(
                "yat,zat->ayz",
                block_query_rows,
                block_state_key_rows,
                preferred_element_type=jnp.float32,
            )
            * scores_scale
        )
        return (jnp.where(block_permitted_mask, window_part, MASKED), state_part)

    def attend_one_block(element_entry):
        (
            block_query_rows,
            block_window_key_rows,
            block_window_value_rows,
            block_state_key_rows,
            block_state_value_rows,
            block_permitted_mask,
        ) = element_entry
        window_scores, scores_of_state = block_score_rows(
            block_query_rows, block_window_key_rows, block_state_key_rows, block_permitted_mask
        )
        row_peak = jnp.maximum(jnp.max(window_scores, axis=-1), jnp.max(scores_of_state, axis=-1))
        window_raised = jnp.exp(window_scores - row_peak[..., None])
        state_raised = jnp.exp(scores_of_state - row_peak[..., None])
        denominator = jnp.sum(window_raised, axis=-1) + jnp.sum(state_raised, axis=-1)
        log_total = row_peak + jnp.log(denominator)
        window_probs = (window_raised / denominator[..., None]).astype(jnp.bfloat16)
        state_probs = (state_raised / denominator[..., None]).astype(jnp.bfloat16)
        block_out = jnp.einsum(
            "hij,jhe->ihe",
            window_probs,
            block_window_value_rows,
            preferred_element_type=jnp.float32,
        ) + jnp.einsum(
            "wyd,dwg->ywg", state_probs, block_state_value_rows, preferred_element_type=jnp.float32
        )
        return (block_out.astype(jnp.bfloat16), log_total)

    attended_blocks, log_totals = lax.map(
        attend_one_block,
        (
            flattened_queries,
            flattened_window_keys,
            flattened_window_values,
            flattened_state_keys,
            flattened_state_values,
            permitted_mask,
        ),
    )
    attended = attended_blocks.reshape(row_count, local_width)
    attn_part = jnp.dot(attended, out_full, preferred_element_type=jnp.float32).reshape(
        seq_count, length, full_width
    )
    attn_share = lax.psum_scatter(
        attn_part.astype(jnp.bfloat16), "tp", scatter_dimension=2, tiled=True
    ).astype(jnp.float32)
    middle = tokens.astype(jnp.float32) + attn_share
    middle_full, gain_two_full = (
        lax.all_gather(middle.astype(jnp.bfloat16), "tp", axis=2, tiled=True),
        lax.all_gather(gain_two, "tp", axis=0, tiled=True),
    )
    gain_two_vec = gain_two_full.reshape(full_width).astype(jnp.float32)
    normed_two, inverse_two, mlp_in = norm_forward(
        middle_full.reshape(row_count, full_width).astype(jnp.float32), gain_two_vec
    )
    hidden_pre = jnp.dot(mlp_in, up_full, preferred_element_type=jnp.float32)
    hidden = jax.nn.gelu(hidden_pre, approximate=False).astype(jnp.bfloat16)
    mlp_part = jnp.dot(hidden, down_full, preferred_element_type=jnp.float32).reshape(
        seq_count, length, full_width
    )
    mlp_share = lax.psum_scatter(
        mlp_part.astype(jnp.bfloat16), "tp", scatter_dimension=2, tiled=True
    ).astype(jnp.float32)
    output = (middle + mlp_share).astype(jnp.bfloat16)
    grad_out = cotangent.reshape(row_count, full_width)
    grad_hidden = jnp.dot(grad_out, down_full.T, preferred_element_type=jnp.float32)
    grad_down = jnp.dot(hidden.T, grad_out, preferred_element_type=jnp.float32)

    def gelu_exact(pre_values):
        return jax.nn.gelu(pre_values, approximate=False)

    gelu_value, gelu_back = jax.vjp(gelu_exact, hidden_pre)
    grad_pre = gelu_back(grad_hidden)[0].astype(jnp.bfloat16)
    grad_up = jnp.dot(mlp_in.T, grad_pre, preferred_element_type=jnp.float32)
    grad_mlp_in = jnp.dot(grad_pre, up_full.T, preferred_element_type=jnp.float32)
    part_middle, part_gain_two = norm_backward(grad_mlp_in, normed_two, inverse_two, gain_two_vec)
    tp_index = lax.axis_index("tp")
    head_total = full_width // HEAD_SIZE
    summed, gain_two_sum = (
        lax.psum(
            part_middle.reshape(seq_count, length, full_width).astype(jnp.bfloat16), "tp"
        ).astype(jnp.float32),
        lax.psum(part_gain_two.reshape(head_total, HEAD_SIZE).astype(jnp.bfloat16), "tp").astype(
            jnp.float32
        ),
    )
    middle_grad_full = cotangent.astype(jnp.float32) + summed
    middle_grad = lax.dynamic_slice_in_dim(middle_grad_full, tp_index * shard_width, shard_width, 2)
    grad_gain_two = lax.dynamic_slice_in_dim(
        gain_two_sum, tp_index * local_head_count, local_head_count, 0
    )
    middle_grad_low = middle_grad_full.astype(jnp.bfloat16)
    middle_grad_rows = middle_grad_low.reshape(row_count, full_width)
    grad_attended = jnp.dot(
        middle_grad_rows, out_full.T, preferred_element_type=jnp.float32
    ).astype(jnp.bfloat16)
    grad_attended = grad_attended.reshape(element_count, BLOCK, local_head_count, HEAD_SIZE)
    grad_wout = jnp.dot(attended.T, middle_grad_rows, preferred_element_type=jnp.float32)

    def attend_back(bias_sum, element_entry):
        (
            block_query_rows,
            block_window_key_rows,
            block_window_value_rows,
            block_state_key_rows,
            block_state_value_rows,
            block_permitted_mask,
            block_lse,
            block_grad,
        ) = element_entry
        window_again, state_again = block_score_rows(
            block_query_rows, block_window_key_rows, block_state_key_rows, block_permitted_mask
        )
        window_exact = jnp.exp(window_again - block_lse[..., None])
        state_exact = jnp.exp(state_again - block_lse[..., None])
        grad_wprob = jnp.einsum(
            "ihe,jhe->hij", block_grad, block_window_value_rows, preferred_element_type=jnp.float32
        )
        grad_sprob = jnp.einsum(
            "yat,zat->ayz", block_grad, block_state_value_rows, preferred_element_type=jnp.float32
        )
        row_delta = jnp.sum(window_exact * grad_wprob, axis=-1) + jnp.sum(
            state_exact * grad_sprob, axis=-1
        )
        grad_wscore = (window_exact * (grad_wprob - row_delta[..., None])).astype(jnp.bfloat16)
        state_score_gradient = (state_exact * (grad_sprob - row_delta[..., None])).astype(
            jnp.bfloat16
        )
        block_grad_q = scores_scale * (
            jnp.einsum(
                "hij,jhe->ihe",
                grad_wscore,
                block_window_key_rows,
                preferred_element_type=jnp.float32,
            )
            + jnp.einsum(
                "wyd,dwg->ywg",
                state_score_gradient,
                block_state_key_rows,
                preferred_element_type=jnp.float32,
            )
        )
        block_grad_wk = scores_scale * jnp.einsum(
            "hij,ihe->jhe", grad_wscore, block_query_rows, preferred_element_type=jnp.float32
        )
        block_grad_wv = jnp.einsum(
            "hij,ihe->jhe",
            window_exact.astype(jnp.bfloat16),
            block_grad,
            preferred_element_type=jnp.float32,
        )
        block_grad_sk = (
            scores_scale
            * jnp.einsum(
                "him,ihe->mhe",
                state_score_gradient,
                block_query_rows,
                preferred_element_type=jnp.float32,
            )
        ).astype(jnp.bfloat16)
        block_grad_sv = jnp.einsum(
            "him,ihe->mhe",
            state_exact.astype(jnp.bfloat16),
            block_grad,
            preferred_element_type=jnp.float32,
        ).astype(jnp.bfloat16)
        return (
            bias_sum + grad_wscore.astype(jnp.float32),
            (block_grad_q, block_grad_wk, block_grad_wv, block_grad_sk, block_grad_sv),
        )

    bias_start = jnp.zeros((local_head_count, BLOCK, 2 * BLOCK), jnp.float32)
    bias_sum, back_items = lax.scan(
        attend_back,
        bias_start,
        (
            flattened_queries,
            flattened_window_keys,
            flattened_window_values,
            flattened_state_keys,
            flattened_state_values,
            permitted_mask,
            log_totals,
            grad_attended,
        ),
    )
    grad_bias = bias_gradient(bias_sum, bucket, bias_rows.shape[1])
    grad_queries = back_items[0].reshape(local_shape)
    grad_window_keys = back_items[1].reshape(
        seq_count, block_count, 2 * BLOCK, local_head_count, HEAD_SIZE
    )
    grad_window_values = back_items[2].reshape(
        seq_count, block_count, 2 * BLOCK, local_head_count, HEAD_SIZE
    )
    state_keys_gradient = back_items[3].reshape(
        seq_count, block_count, state_slot_count, local_head_count, HEAD_SIZE
    )
    grad_state_values = back_items[4].reshape(
        seq_count, block_count, state_slot_count, local_head_count, HEAD_SIZE
    )
    back_keys, back_values = (
        from_behind(grad_window_keys[:, 0, :BLOCK].astype(jnp.bfloat16), "ctx", -1).astype(
            jnp.float32
        ),
        from_behind(grad_window_values[:, 0, :BLOCK].astype(jnp.bfloat16), "ctx", -1).astype(
            jnp.float32
        ),
    )
    key_grad = grad_window_keys[:, :, BLOCK:] + jnp.concatenate(
        [grad_window_keys[:, 1:, :BLOCK], back_keys[:, None]], 1
    )
    value_grad = grad_window_values[:, :, BLOCK:] + jnp.concatenate(
        [grad_window_values[:, 1:, :BLOCK], back_values[:, None]], 1
    )
    state_key_gradient = jnp.einsum(
        "sbmhe,sbmhf->hef", state_reduced, state_keys_gradient, preferred_element_type=jnp.float32
    )
    grad_svalue = jnp.einsum(
        "sbmhe,sbmhf->hef", state_reduced, grad_state_values, preferred_element_type=jnp.float32
    )
    direct = jnp.einsum(
        "palcq,crq->palcr",
        state_keys_gradient,
        state_key_complete,
        preferred_element_type=jnp.float32,
    ) + jnp.einsum(
        "palcq,crq->palcr", grad_state_values, svalue_full, preferred_element_type=jnp.float32
    )
    direct = direct.reshape(seq_count, block_count, state_slot_count, local_width)
    back_accum = jnp.zeros((seq_count, state_slot_count, local_width), jnp.float32)
    for block_index in reversed(range(block_count)):
        back_accum = direct[:, block_index] + gate_value * back_accum
    back_identity = (jnp.ones((local_width,), jnp.float32), jnp.zeros_like(back_accum))
    unused_power, incoming = prefix_2((gate_power, back_accum), "ctx", compose, back_identity, True)
    carried = incoming
    contrib_grads = [None] * block_count
    gate_grad = jnp.zeros((local_width,), jnp.float32)
    for block_index in reversed(range(block_count)):
        contrib_grads[block_index] = ((1.0 - gate_value) * carried).astype(jnp.bfloat16)
        gate_grad = gate_grad + jnp.sum(
            carried * (stacked[:, block_index] - contrib[:, block_index]), axis=(0, 1)
        )
        carried = direct[:, block_index] + gate_value * carried
    first_device = (lax.axis_index("ctx") == 0).astype(jnp.float32)
    grad_sinit = first_device * jnp.sum(carried, axis=0)
    grad_gate = (gate_grad * gate_value * (1.0 - gate_value)).reshape(local_head_count, HEAD_SIZE)
    grad_contrib = jnp.stack(contrib_grads, axis=1).reshape(
        seq_count, block_count, state_slot_count, local_head_count, HEAD_SIZE
    )
    grad_read = jnp.einsum(
        "sbmhe,sbthe->sbhmt", grad_contrib, value_rows, preferred_element_type=jnp.float32
    )
    extra_values = jnp.einsum(
        "sbhmt,sbmhe->sbthe", read_low, grad_contrib, preferred_element_type=jnp.float32
    )
    read_delta = jnp.sum(read_probs * grad_read, axis=-1, keepdims=True)
    grad_read_score = (read_probs * (grad_read - read_delta)).astype(jnp.bfloat16)
    grad_squery = (
        scores_scale
        * jnp.einsum(
            "sbhmt,sbthe->mhe", grad_read_score, key_rows, preferred_element_type=jnp.float32
        )
    ).reshape(state_slot_count, local_width)
    extra_keys = scores_scale * jnp.einsum(
        "sbhmt,mhe->sbthe", grad_read_score, query_heads, preferred_element_type=jnp.float32
    )
    grad_q_rows = grad_queries.astype(jnp.bfloat16).reshape(row_count, local_width)
    grad_k_rows = (key_grad + extra_keys).astype(jnp.bfloat16).reshape(row_count, local_width)
    grad_v_rows = (value_grad + extra_values).astype(jnp.bfloat16).reshape(row_count, local_width)
    grad_wq = jnp.dot(attn_in.T, grad_q_rows, preferred_element_type=jnp.float32)
    grad_wk = jnp.dot(attn_in.T, grad_k_rows, preferred_element_type=jnp.float32)
    grad_wv = jnp.dot(attn_in.T, grad_v_rows, preferred_element_type=jnp.float32)
    grad_attn_in = (
        jnp.dot(grad_q_rows, query_full.T, preferred_element_type=jnp.float32)
        + jnp.dot(grad_k_rows, key_full.T, preferred_element_type=jnp.float32)
        + jnp.dot(grad_v_rows, value_full.T, preferred_element_type=jnp.float32)
    )
    part_tokens, part_gain_one = norm_backward(grad_attn_in, normed_one, inverse_one, gain_one_vec)
    token_share, grad_gain_one = (
        lax.psum_scatter(
            part_tokens.reshape(seq_count, length, full_width).astype(jnp.bfloat16),
            "tp",
            scatter_dimension=2,
            tiled=True,
        ).astype(jnp.float32),
        lax.psum_scatter(
            part_gain_one.reshape(head_total, HEAD_SIZE).astype(jnp.bfloat16),
            "tp",
            scatter_dimension=0,
            tiled=True,
        ).astype(jnp.float32),
    )
    grad_tokens = (middle_grad + token_share).astype(jnp.bfloat16)
    grads = (
        lax.psum_scatter(
            grad_wq.astype(jnp.bfloat16), ("dp", "ctx"), scatter_dimension=0, tiled=True
        ).astype(jnp.float32),
        lax.psum_scatter(
            grad_wk.astype(jnp.bfloat16), ("dp", "ctx"), scatter_dimension=0, tiled=True
        ).astype(jnp.float32),
        lax.psum_scatter(
            grad_wv.astype(jnp.bfloat16), ("dp", "ctx"), scatter_dimension=0, tiled=True
        ).astype(jnp.float32),
        lax.psum_scatter(
            grad_wout.astype(jnp.bfloat16), ("dp", "ctx"), scatter_dimension=1, tiled=True
        ).astype(jnp.float32),
        lax.psum_scatter(
            grad_up.astype(jnp.bfloat16), ("dp", "ctx"), scatter_dimension=0, tiled=True
        ).astype(jnp.float32),
        lax.psum_scatter(
            grad_down.astype(jnp.bfloat16), ("dp", "ctx"), scatter_dimension=1, tiled=True
        ).astype(jnp.float32),
        lax.psum_scatter(
            grad_squery.astype(jnp.bfloat16), ("dp", "ctx"), scatter_dimension=0, tiled=True
        ).astype(jnp.float32),
        lax.psum_scatter(
            grad_sinit.astype(jnp.bfloat16), ("dp", "ctx"), scatter_dimension=0, tiled=True
        ).astype(jnp.float32),
        lax.psum_scatter(
            grad_gain_one.astype(jnp.bfloat16), ("dp", "ctx"), scatter_dimension=1, tiled=True
        ).astype(jnp.float32),
        lax.psum_scatter(
            grad_gain_two.astype(jnp.bfloat16), ("dp", "ctx"), scatter_dimension=1, tiled=True
        ).astype(jnp.float32),
        lax.psum_scatter(
            grad_bias.astype(jnp.bfloat16), ("dp", "ctx"), scatter_dimension=1, tiled=True
        ).astype(jnp.float32),
        lax.psum_scatter(
            grad_gate.astype(jnp.bfloat16), ("dp", "ctx"), scatter_dimension=1, tiled=True
        ).astype(jnp.float32),
        lax.psum_scatter(
            state_key_gradient.astype(jnp.bfloat16), ("dp", "ctx"), scatter_dimension=1, tiled=True
        ).astype(jnp.float32),
        lax.psum_scatter(
            grad_svalue.astype(jnp.bfloat16), ("dp", "ctx"), scatter_dimension=1, tiled=True
        ).astype(jnp.float32),
    )
    return (
        output,
        grad_tokens,
        grads[0],
        grads[1],
        grads[2],
        grads[3],
        grads[4],
        grads[5],
        grads[6],
        grads[7],
        grads[8],
        grads[9],
        grads[10],
        grads[11],
        grads[12],
        grads[13],
    )


LOG2E = 1.4426950408889634
VMEM_BYTES = 58 * 1024 * 1024
BF = jnp.bfloat16
F32 = jnp.float32


def nn(left, right):
    return jnp.dot(left, right, preferred_element_type=F32)


def nt(left, right):
    return lax.dot_general(left, right, (((1,), (1,)), ((), ())), preferred_element_type=F32)


def tn(left, right):
    return lax.dot_general(left, right, (((0,), (0,)), ((), ())), preferred_element_type=F32)


def flat(ref):
    block = ref[0]
    return block.reshape(block.shape[0] * block.shape[1], block.shape[2])


def merged(place_ref, own_ref, other_ref):
    own = own_ref[0, :, 0]
    other = other_ref[0, :, 0]
    is_first = place_ref[0] == 0
    pair = [jnp.where(is_first, own, other), jnp.where(is_first, other, own)]
    block = jnp.stack(pair, axis=1)
    return block.reshape(-1, block.shape[-1])


def joined(tok_ref):
    return jnp.concatenate([tok_ref[part] for part in range(tok_ref.shape[0])], axis=1).astype(F32)


def inverse_rms(x):
    return lax.rsqrt(jnp.mean(x * x, axis=-1, keepdims=True) + EPSILON)


def params():
    return pltpu.CompilerParams(vmem_limit_bytes=VMEM_BYTES)


def project_kernel(
    place_ref, tok_ref, gain_ref, wq_ref, wqo_ref, wk_ref, wko_ref, wv_ref, wvo_ref,
    q_ref, k_ref, v_ref, ain_ref, last_ref,
):
    @pl.when(pl.program_id(0) == 0)
    def _():
        x = joined(tok_ref)
        ain_ref[...] = (x * inverse_rms(x) * gain_ref[...]).astype(BF)

    a = ain_ref[...]
    for w_ref, w_other, o_ref in (
        (wq_ref, wqo_ref, q_ref), (wk_ref, wko_ref, k_ref), (wv_ref, wvo_ref, v_ref)
    ):
        o_ref[...] = nn(a, merged(place_ref, w_ref, w_other)).astype(BF)
    length = k_ref.shape[0] * BLOCK // last_ref.shape[1]
    for item in range(last_ref.shape[1] // BLOCK):
        last = slice((item + 1) * length - BLOCK, (item + 1) * length)
        last_ref[0, item * BLOCK : (item + 1) * BLOCK] = k_ref[last]
        last_ref[1, item * BLOCK : (item + 1) * BLOCK] = v_ref[last]


def read_kernel(
    place_ref, sq_ref, sqo_ref, k_ref, v_ref, gate_ref, o_ref, sum_ref, state_ref, *, blocks
):
    n = pl.program_id(1)
    sq = merged(place_ref, sq_ref, sqo_ref)
    k = k_ref[...]
    v = v_ref[...]
    scale = HEAD_SIZE ** (-0.5) * LOG2E
    step = 256
    gate = jnp.where(lax.rem(n, blocks) == 0, 0.0, gate_ref[...])
    fresh = 1.0 - gate_ref[...]

    @pl.when(n == 0)
    def _():
        state_ref[...] = jnp.zeros_like(state_ref)

    for start in range(0, sq.shape[0], step):
        rows = slice(start, start + step)
        s = nt(sq[rows], k) * scale
        p = jnp.exp2(s - jnp.max(s, axis=-1, keepdims=True))
        total = jnp.sum(p, axis=-1, keepdims=True)
        contrib = nn(p.astype(BF), v) / total
        o_ref[rows, :] = contrib
        state = gate * state_ref[rows, :] + fresh * contrib
        state_ref[rows, :] = state
        sum_ref[rows, :] = state.astype(BF)


def attend_kernel(
    place_ref, info_ref, q_ref, k_ref, v_ref, kp_ref, vp_ref, hk_ref, hv_ref,
    wk_ref, wko_ref, wv_ref, wvo_ref, contrib_ref, init_ref, inito_ref, lead_ref, power_ref,
    gate_ref, u_ref, o_ref, lse_ref, low_ref, moved_ref, bias_ref, state_ref, *, blocks,
):
    n = pl.program_id(1)
    first = lax.rem(n, blocks) == 0
    scale = HEAD_SIZE ** (-0.5) * LOG2E

    @pl.when(n == 0)
    def _():
        row = jnp.broadcast_to(u_ref[0], (BLOCK, u_ref.shape[-1]))
        bias_ref[...] = pltpu.roll(row, 0, 1, stride=1, stride_axis=0)[:, : 2 * BLOCK]

    has_previous = info_ref[n, 0] > 0
    reach = info_ref[n, 1]
    k = k_ref[...]
    v = v_ref[...]
    kp = jnp.where(first, hk_ref[...], kp_ref[...])
    vp = jnp.where(first, hv_ref[...], vp_ref[...])

    @pl.when(first)
    def _():
        init = merged(place_ref, init_ref, inito_ref).astype(F32)
        state_ref[...] = power_ref[...] * init + lead_ref[...].astype(F32)

    state = state_ref[...]
    contrib = contrib_ref[...]
    st = state.astype(BF)
    low_ref[...] = st
    moved_ref[...] = (state - contrib).astype(BF)
    state_ref[...] = contrib + gate_ref[...] * (state - contrib)
    sk = nn(st, merged(place_ref, wk_ref, wko_ref)).astype(BF)
    sv = nn(st, merged(place_ref, wv_ref, wvo_ref)).astype(BF)
    step = ROWS_FORWARD

    def run(with_previous):
        for start in range(0, BLOCK, step):
            q = q_ref[start : start + step, :]
            sc = nt(q, k) * scale + bias_ref[start : start + step, BLOCK:]
            row = lax.broadcasted_iota(jnp.int32, (step, 1), 0) + start
            column = lax.broadcasted_iota(jnp.int32, (step, BLOCK), 1)
            sc = jnp.where(column <= jnp.maximum(row, reach - 1), sc, MASKED)
            ss = nt(q, sk) * scale
            peak = jnp.maximum(
                jnp.max(sc, axis=-1, keepdims=True), jnp.max(ss, axis=-1, keepdims=True)
            )
            if with_previous:
                sp = nt(q, kp) * scale + bias_ref[start : start + step, :BLOCK]
                peak = jnp.maximum(peak, jnp.max(sp, axis=-1, keepdims=True))
            pc = jnp.exp2(sc - peak)
            ps = jnp.exp2(ss - peak)
            total = jnp.sum(pc, axis=-1, keepdims=True) + jnp.sum(ps, axis=-1, keepdims=True)
            out = nn(pc.astype(BF), v) + nn(ps.astype(BF), sv)
            if with_previous:
                pp = jnp.exp2(sp - peak)
                total = total + jnp.sum(pp, axis=-1, keepdims=True)
                out = out + nn(pp.astype(BF), vp)
            o_ref[start : start + step, :] = (out / total).astype(BF)
            lse = jnp.broadcast_to(peak + jnp.log2(total), (step, 128))
            lse_ref[0, 0, :, start : start + step] = lse.T[:1]

    @pl.when(has_previous)
    def _():
        run(True)

    @pl.when(jnp.logical_not(has_previous))
    def _():
        run(False)


def attend_back_kernel(
    place_ref, info_ref, q_ref, k_ref, v_ref, kp_ref, vp_ref, hk_ref, hv_ref,
    wk_ref, wko_ref, wv_ref, wvo_ref, st_ref, gate_ref, u_ref, do_ref, o_ref, lse_ref,
    dq_ref, dk_ref, dv_ref, dkp_ref, dvp_ref, direct_ref, gwk_ref, gwv_ref, gb_ref, total_ref,
    firstk_ref, firstv_ref, bias_ref, sum_ref, dq_acc, state_acc, *, blocks,
):
    step_at = pl.program_id(1)
    n = pl.num_programs(1) - 1 - step_at
    first = lax.rem(n, blocks) == 0
    gate = jnp.where(lax.rem(n, blocks) == blocks - 1, 0.0, gate_ref[...])
    factor = HEAD_SIZE ** (-0.5)
    scale = factor * LOG2E
    window = 2 * BLOCK
    width = BLOCK + window

    @pl.when(step_at == 0)
    def _():
        state_acc[...] = jnp.zeros_like(state_acc)
        row = jnp.broadcast_to(u_ref[0], (window, u_ref.shape[-1]))
        bias_ref[...] = pltpu.roll(row, 0, 1, stride=1, stride_axis=0)[:, :BLOCK]
        sum_ref[...] = jnp.zeros_like(sum_ref)
        gwk_ref[...] = jnp.zeros_like(gwk_ref)
        gwv_ref[...] = jnp.zeros_like(gwv_ref)

    has_previous = info_ref[n, 0] > 0
    reach = info_ref[n, 1]
    q = q_ref[...]
    do = do_ref[...]
    lse = lse_ref[0, 0]
    delta = jnp.sum((do.astype(F32) * o_ref[...].astype(F32)).T, axis=0, keepdims=True)
    step = KEYS_BACKWARD

    def part(key, value, start, bias_start, masked):
        s = nt(key, q) * scale
        if bias_start is not None:
            s = s + bias_ref[bias_start : bias_start + step, :]
        if masked:
            key_at = lax.broadcasted_iota(jnp.int32, (step, BLOCK), 0) + start
            query_at = lax.broadcasted_iota(jnp.int32, (1, BLOCK), 1)
            s = jnp.where(key_at <= jnp.maximum(query_at, reach - 1), s, MASKED)
        p = jnp.exp2(s - lse)
        dp = nt(value, do)
        ds = (p * (dp - delta)).astype(BF)
        if bias_start is not None:
            for block in range(0, step, 128):
                at = window - bias_start - block
                sum_ref[:, at : at + BLOCK] += ds[block : block + 128].astype(F32)
        dq_acc[...] += tn(ds, key)
        return nn(ds, q) * factor, nn(p.astype(BF), do)

    dq_acc[...] = jnp.zeros_like(dq_acc)
    st = st_ref[...]
    key_map = merged(place_ref, wk_ref, wko_ref)
    value_map = merged(place_ref, wv_ref, wvo_ref)
    sk = nn(st, key_map).astype(BF)
    sv = nn(st, value_map).astype(BF)
    for start in range(0, st.shape[0], step):
        rows = slice(start, start + step)
        dk, dv = part(sk[rows], sv[rows], start, None, False)
        dk = dk.astype(BF)
        dv = dv.astype(BF)
        direct = nt(dk, key_map) + nt(dv, value_map)
        direct_ref[rows, :] = direct
        state = direct + gate * state_acc[rows, :]
        state_acc[rows, :] = state
        total_ref[rows, :] = state.astype(BF)
        gwk_ref[0] += tn(st[rows], dk)
        gwv_ref[0] += tn(st[rows], dv)
    for start in range(0, BLOCK, step):
        rows = slice(start, start + step)
        dk, dv = part(k_ref[rows, :], v_ref[rows, :], start, BLOCK + start, True)
        dk_ref[rows, :] = dk
        dv_ref[rows, :] = dv

    @pl.when(has_previous)
    def _():
        for start in range(0, BLOCK, step):
            rows = slice(start, start + step)
            key = jnp.where(first, hk_ref[rows, :], kp_ref[rows, :])
            value = jnp.where(first, hv_ref[rows, :], vp_ref[rows, :])
            dk, dv = part(key, value, start, start, False)
            dkp_ref[rows, :] = dk.astype(BF)
            dvp_ref[rows, :] = dv.astype(BF)

    @pl.when(jnp.logical_not(has_previous))
    def _():
        dkp_ref[...] = jnp.zeros_like(dkp_ref)
        dvp_ref[...] = jnp.zeros_like(dvp_ref)

    @pl.when(first)
    def _():
        firstk_ref[...] = dkp_ref[...]
        firstv_ref[...] = dvp_ref[...]

    dq_ref[...] = (dq_acc[...] * factor).astype(BF)

    @pl.when(n == 0)
    def _():
        folded = sum_ref[...]
        half = 64
        while half >= 8:
            folded = folded[:half] + pltpu.roll(folded[half:], width - half, 1)
            half //= 2
        total = folded[:1]
        for row in range(1, 8):
            total = total + pltpu.roll(folded[row : row + 1], width - row, 1)
        gb_ref[0] = total


def read_back_kernel(
    place_ref, sq_ref, sqo_ref, k_ref, v_ref, direct_ref, moved_ref, later_ref, gate_ref,
    dk_ref, dv_ref, nk_ref, nv_ref, rk_ref, rv_ref,
    gk_ref, gv_ref, gsq_ref, ginit_ref, ggate_ref, carried_ref, *, blocks,
):
    step_at = pl.program_id(1)
    n = pl.num_programs(1) - 1 - step_at
    last = lax.rem(n, blocks) == blocks - 1
    factor = HEAD_SIZE ** (-0.5)

    @pl.when(step_at == 0)
    def _():
        gsq_ref[...] = jnp.zeros_like(gsq_ref)
        ginit_ref[...] = jnp.zeros_like(ginit_ref)
        ggate_ref[...] = jnp.zeros_like(ggate_ref)

    @pl.when(last)
    def _():
        carried_ref[...] = later_ref[...].astype(F32)

    gate = gate_ref[...]
    carried = carried_ref[...]
    gc = ((1.0 - gate) * carried).astype(BF)
    change = jnp.sum(carried * moved_ref[...].astype(F32), axis=0, keepdims=True)
    ggate_ref[0] += change * (gate * (1.0 - gate))
    carried = direct_ref[...] + gate * carried
    carried_ref[...] = carried

    @pl.when((lax.rem(n, blocks) == 0) & (place_ref[0] == 0))
    def _():
        ginit_ref[...] += carried

    sq = merged(place_ref, sq_ref, sqo_ref)
    k = k_ref[...]
    s = nt(k, sq) * (factor * LOG2E)
    p = jnp.exp2(s - jnp.max(s, axis=0, keepdims=True))
    p = p * (1.0 / jnp.sum(p, axis=0, keepdims=True))
    dp = nt(v_ref[...], gc)
    ds = (p * (dp - jnp.sum(p * dp, axis=0, keepdims=True))).astype(BF)
    next_k = jnp.where(last, rk_ref[...], nk_ref[...]).astype(F32)
    next_v = jnp.where(last, rv_ref[...], nv_ref[...]).astype(F32)
    gk_ref[...] = (dk_ref[...] + next_k + nn(ds, sq) * factor).astype(BF)
    gv_ref[...] = (dv_ref[...] + next_v + nn(p.astype(BF), gc)).astype(BF)
    gsq_ref[...] += tn(ds, k) * factor


def item_kernel(wq_ref, wk_ref, wv_ref, sq_ref, init_ref, mk_ref, mv_ref, tail_ref, out_ref):
    at = 0
    for w_ref in (wq_ref, wk_ref, wv_ref, sq_ref, init_ref):
        out_ref[at : at + w_ref.shape[0]] = w_ref[...]
        at += w_ref.shape[0]
    for w_ref in (mk_ref, mv_ref):
        heads, rows, lanes = w_ref.shape
        for item in range(heads):
            out_ref[at : at + rows, item * lanes : (item + 1) * lanes] = w_ref[item]
        at += rows
    out_ref[at:] = tail_ref[...]


def assemble_kernel(place_ref, low_ref, lowy_ref, high_ref, highx_ref, own_ref):
    x_bit = place_ref[3]
    y_bit = place_ref[4]
    for x in range(2):
        own_ref[0, 2 * y_bit + x] = low_ref[x]
        own_ref[0, 2 * (1 - y_bit) + x] = lowy_ref[x]
    for y in range(2):
        own_ref[1, 2 * y + x_bit] = high_ref[y]
        own_ref[1, 2 * y + 1 - x_bit] = highx_ref[y]


def pack_kernel(up_ref, down_ref, out_ref, packed_ref):
    hidden = up_ref.shape[1]
    packed_ref[:, :hidden] = up_ref[...]
    packed_ref[:, hidden : 2 * hidden] = down_ref[...].T
    packed_ref[:, 2 * hidden :] = out_ref[...].T


def unpack_kernel(packed_ref, from_a, from_b, up_ref, down_ref, out_ref, to_a, to_b):
    to_a[...] = from_a[...]
    to_b[...] = from_b[...]
    hidden = up_ref.shape[1]
    up_ref[...] = packed_ref[:, :hidden].astype(F32)
    down_ref[...] = packed_ref[:, hidden : 2 * hidden].astype(F32).T
    out_ref[...] = packed_ref[:, 2 * hidden :].astype(F32).T


def finish_kernel(*refs):
    place_ref, refs = refs[0], refs[1:]
    terms, outs = refs[:-12], refs[-12:-1]
    sum_ref = refs[-1]
    total = terms[0][...].astype(F32)
    for term in terms[1:]:
        total = total + term[...].astype(F32)
    at = 0
    for out_ref in outs[:5]:
        out_ref[...] = total[at : at + out_ref.shape[0]]
        at += out_ref.shape[0]
    for out_ref in outs[5:7]:
        heads, rows, lanes = out_ref.shape
        for item in range(heads):
            out_ref[item] = total[at : at + rows, item * lanes : (item + 1) * lanes]
        at += rows
    sum_ref[...] = total[at:]
    shard, group = place_ref[1], place_ref[2]
    lanes = sum_ref.shape[1]
    for index, out_ref in enumerate(outs[7:]):
        heads, columns = out_ref.shape
        if index < 3:
            stride = HEAD_SIZE
            row = sum_ref[pl.ds(index * len(terms) + shard, 1), :]
            shift = group * columns
        else:
            stride = columns * (HEAD_SIZE // outs[7].shape[1])
            row = sum_ref[index * len(terms) : index * len(terms) + 1, :]
            shift = (shard * heads) * stride + group * columns
        row = pltpu.roll(row, lax.rem(lanes - shift, lanes), 1)
        for item in range(heads):
            out_ref[item : item + 1, :] = row[:, item * stride : item * stride + columns]


def out_kernel(att_ref, wo_ref, tok_ref, gain_ref, mid_ref, min_ref):
    t = pl.program_id(0)
    part = nt(att_ref[...], flat(wo_ref))

    @pl.when(t == 0)
    def _():
        mid_ref[...] = joined(tok_ref) + part

    @pl.when(t > 0)
    def _():
        mid_ref[...] += part

    @pl.when(t == pl.num_programs(0) - 1)
    def _():
        x = mid_ref[...].astype(BF).astype(F32)
        min_ref[...] = (x * inverse_rms(x) * gain_ref[...]).astype(BF)


def mlp_kernel(
    place_ref, min_ref, cot_ref, mid_ref, gain_ref, wu_ref, wd_ref,
    out_ref, gmid_ref, ggain_ref, gw_ref,
    min_t, cot_t, out_acc, gm_acc, hidden_ref,
):
    tile = pl.program_id(0)
    which = pl.program_id(1)

    @pl.when((tile == 0) & (which == 0))
    def _():
        min_t[...] = min_ref[...].T
        cot_t[...] = cot_ref[...].T
        out_acc[...] = jnp.zeros_like(out_acc)
        gm_acc[...] = jnp.zeros_like(gm_acc)

    @pl.when(which == 0)
    def _():
        wu = flat(wu_ref)
        wd = flat(wd_ref)
        pre = nn(min_ref[...], wu)
        cdf = 0.5 + 0.5 * lax.erf(pre * (0.5**0.5))
        density = jnp.exp2(pre * pre * (-0.5 * LOG2E)) * ((2.0 * np.pi) ** -0.5)
        hidden_ref[...] = (pre * cdf).astype(BF)
        grad_pre = (nn(cot_ref[...], wd) * (cdf + pre * density)).astype(BF)
        out_acc[...] += nt(hidden_ref[...], wd)
        gm_acc[...] += nt(grad_pre, wu)
        grad = nn(min_t[...], grad_pre).astype(BF)
        gw_ref[...] = grad.reshape(gw_ref.shape)

    @pl.when(which == 1)
    def _():
        grad = nn(cot_t[...], hidden_ref[...]).astype(BF)
        gw_ref[...] = grad.reshape(gw_ref.shape)

    @pl.when((tile == pl.num_programs(0) - 1) & (which == 1))
    def _():
        mid = mid_ref[...]
        lanes = out_ref.shape[2]
        for part in range(out_ref.shape[0]):
            at = slice(part * lanes, (part + 1) * lanes)
            out_ref[part] = (mid[:, at] + out_acc[:, at]).astype(BF)
        x = mid.astype(BF).astype(F32)
        inverse = inverse_rms(x)
        normed = x * inverse
        gm = gm_acc[...]
        ggain_ref[...] = jnp.sum(gm * normed, axis=0, keepdims=True)
        scaled = gm * gain_ref[...]
        back = inverse * (scaled - normed * jnp.mean(scaled * normed, axis=-1, keepdims=True))
        gmid_ref[...] = (cot_ref[...].astype(F32) + back).astype(BF)


def out_gradient_kernel(gmid_ref, att_ref, late_ref, gwo_ref, gmid_t):
    @pl.when(pl.program_id(0) == 0)
    def _():
        gmid_t[...] = gmid_ref[...].T

    gwo_ref[...] = nn(gmid_t[...], att_ref[...]).astype(BF).reshape(gwo_ref.shape)


def out_back_kernel(gmid_ref, wo_ref, gatt_ref):
    gatt_ref[...] = nn(gmid_ref[...], flat(wo_ref)).astype(BF)


def weight_back_kernel(
    place_ref, tok_ref, gain_ref, gq_ref, gk_ref, gv_ref, wq_ref, wqo_ref, wk_ref, wko_ref,
    wv_ref, wvo_ref, gsq_ref, ginit_ref, gmk_ref, gmv_ref,
    gown_ref, gother_ref, ggain_ref, ain_t, pack_ref, product_ref,
):
    t = pl.program_id(0)

    @pl.when(t == 0)
    def _():
        x = joined(tok_ref)
        ain_t[...] = (x * inverse_rms(x) * gain_ref[...]).astype(BF).T
        product_ref[...] = jnp.zeros_like(product_ref)

    groups, _, lanes = pack_ref.shape
    at = 0
    for g_ref, w_ref, w_other in (
        (gq_ref, wq_ref, wqo_ref), (gk_ref, wk_ref, wko_ref), (gv_ref, wv_ref, wvo_ref)
    ):
        grad = nn(ain_t[...], g_ref[...])
        product_ref[...] += grad * merged(place_ref, w_ref, w_other).astype(F32)
        rows = grad.shape[0] // groups
        pack_ref[:, at : at + rows] = grad.astype(BF).reshape(groups, rows, lanes)
        at += rows
    for g_ref in (gsq_ref, ginit_ref):
        rows = g_ref.shape[0] // groups
        pack_ref[:, at : at + rows] = g_ref[...].astype(BF).reshape(groups, rows, lanes)
        at += rows
    for g_ref in (gmk_ref, gmv_ref):
        rows = HEAD_SIZE // groups
        for item in range(g_ref.shape[0]):
            where = slice(item * HEAD_SIZE, (item + 1) * HEAD_SIZE)
            pack_ref[:, at : at + rows, where] = g_ref[item].astype(BF).reshape(groups, rows, -1)
        at += rows
    pack_ref[:, at:] = jnp.zeros_like(pack_ref[:, at:])
    for index in range(groups // 2):
        gown_ref[0, index] = pack_ref[2 * index + place_ref[0]]
        gother_ref[0, index] = pack_ref[2 * index + 1 - place_ref[0]]

    @pl.when(t == pl.num_programs(0) - 1)
    def _():
        ggain_ref[...] = jnp.sum(product_ref[...], axis=1, keepdims=True)


def project_back_kernel(
    place_ref, tok_ref, gmid_ref, gain_ref, gq_ref, gk_ref, gv_ref,
    wq_ref, wqo_ref, wk_ref, wko_ref, wv_ref, wvo_ref, gtok_ref, acc_ref,
):
    t = pl.program_id(0)

    @pl.when(t == 0)
    def _():
        acc_ref[...] = jnp.zeros_like(acc_ref)

    total = nt(gq_ref[...], merged(place_ref, wq_ref, wqo_ref))
    total = total + nt(gk_ref[...], merged(place_ref, wk_ref, wko_ref))
    acc_ref[...] += total + nt(gv_ref[...], merged(place_ref, wv_ref, wvo_ref))

    @pl.when(t == pl.num_programs(0) - 1)
    def _():
        x = joined(tok_ref)
        inverse = inverse_rms(x)
        normed = x * inverse
        scaled = acc_ref[...] * gain_ref[...]
        back = inverse * (scaled - normed * jnp.mean(scaled * normed, axis=-1, keepdims=True))
        grad = (gmid_ref[...].astype(F32) + back).astype(BF)
        lanes = gtok_ref.shape[2]
        for part in range(gtok_ref.shape[0]):
            gtok_ref[part] = grad[:, part * lanes : (part + 1) * lanes]


def distance_bucket(distance):
    magnitude = np.abs(distance)
    scaled = np.log(np.maximum(magnitude, 1) / 8.0) / np.log(16.0) * 8.0
    far = np.minimum(8 + np.floor(np.maximum(scaled, 0.0)).astype(np.int32), 15)
    return (distance < 0).astype(np.int32) * 16 + np.where(magnitude < 8, magnitude, far)


def one_hot(distance, valid, bucket_count):
    hot = distance_bucket(distance)[:, None] == np.arange(bucket_count)[None, :]
    return jnp.asarray((hot & valid[:, None]).astype(np.float32))


def carry(value, power, axis, backward):
    count = lax.axis_size(axis)
    sign = -1 if backward else 1
    total = from_behind(value.astype(BF), axis, sign)
    if count == 2:
        return total
    total = total.astype(F32)
    step = 1
    while step < count - 1:
        moved = from_behind(total.astype(BF), axis, sign * step).astype(F32)
        total = total + power**step * moved
        step *= 2
    return total


def across(value, axis, bit):
    count = lax.axis_size(axis)
    return lax.ppermute(value, axis, [(source, source ^ bit) for source in range(count)])


def take(value, index, dim):
    return lax.dynamic_index_in_dim(value, index, dim, False)


def add_low(left, right):
    return (left.astype(F32) + right.astype(F32)).astype(BF)


def ordered(bit, own, other, dim):
    first = bit == 0
    return jnp.stack([jnp.where(first, own, other), jnp.where(first, other, own)], axis=dim)


def gather_pairs(item, beside, behind, place):
    shards = lax.axis_size("tp")
    half = shards // 2
    tp = lax.axis_index("tp")
    x_bit = lax.axis_index("dp") % 2
    y_bit = lax.axis_index("dp") // 2
    parts = [item] + [across(item, "tp", k) for k in range(1, shards)]
    bit = 1
    while bit < shards:
        swap = (tp & bit) > 0
        parts = [jnp.where(swap, parts[k ^ bit], parts[k]) for k in range(shards)]
        bit *= 2
    low = jnp.stack(parts[:half])
    high = jnp.stack(parts[half:])
    low, high, behind = lax.optimization_barrier((low, high, behind))
    low_x = across(low, "dp", 1)
    high_y = across(high, "dp", 2)
    low = ordered(x_bit, low, low_x, 0)
    high = ordered(y_bit, high, high_y, 0)
    low_y = across(low, "dp", 2)
    high_x = across(high, "dp", 1)
    piece = pl.BlockSpec((2, 1) + item.shape, lambda i, *_: (0, i, 0, 0))
    own = pl.pallas_call(
        assemble_kernel,
        grid_spec=pltpu.PrefetchScalarGridSpec(
            num_scalar_prefetch=1, grid=(half,), in_specs=[piece] * 4,
            out_specs=pl.BlockSpec((2, 4, 1) + item.shape, lambda i, *_: (0, 0, i, 0, 0)),
        ),
        out_shape=jax.ShapeDtypeStruct((2, 4, half) + item.shape, BF),
        compiler_params=params(),
    )(place, low, low_y, high, high_x)
    own, beside = lax.optimization_barrier((own, beside))
    return own, across(own, "ctx", 1), beside, behind


def scatter_pairs(own, other):
    shards = own.shape[0]
    half = shards // 2
    tp = lax.axis_index("tp")
    x_bit = lax.axis_index("dp") % 2
    y_bit = lax.axis_index("dp") // 2
    grid = (shards, 2, 2) + own.shape[2:]
    moved = across(other, "ctx", 1).reshape(grid)
    own = own.reshape(grid)

    def both(part, index, dim):
        return add_low(take(own[part], index, dim), take(moved[part], index, dim))

    first, second = slice(0, half), slice(half, shards)
    low_moved = across(both(first, 1 - x_bit, 2), "dp", 1)
    high_moved = across(both(second, 1 - y_bit, 1), "dp", 2)
    low = add_low(both(first, x_bit, 2), low_moved)
    high = add_low(both(second, y_bit, 1), high_moved)
    low_moved = across(take(low, 1 - y_bit, 1), "dp", 2)
    high_moved = across(take(high, 1 - x_bit, 1), "dp", 1)
    low = add_low(take(low, y_bit, 1), low_moved)
    high = add_low(take(high, x_bit, 1), high_moved)
    kept = jnp.concatenate([low, high])
    return [take(kept, tp, 0)] + [
        across(take(kept, tp ^ k, 0), "tp", k) for k in range(1, shards)
    ]


def sequence_body(
    tokens, cotangent, prefix, w_query, w_key, w_value, w_out, w_up, w_down,
    state_query, state_init, gain_attn, gain_mlp, bias_table, gate_bias, state_key, state_value,
):
    shards = lax.axis_size("tp")
    groups = lax.axis_size("dp") * lax.axis_size("ctx")
    pairs = lax.axis_size("dp")
    half = shards // 2
    everywhere = ("tp", "dp", "ctx")
    seq_count, length, shard_width = tokens.shape
    width = cotangent.shape[2]
    seqs = seq_count // shards
    blocks = length // BLOCK
    units = seqs * blocks
    rows = units * BLOCK
    local_heads = bias_table.shape[0]
    heads = local_heads * shards
    buckets = bias_table.shape[1] * groups
    own_rows = w_query.shape[0]
    own_slots = state_query.shape[0]
    slots = own_slots * groups
    hidden = w_up.shape[1]
    tp_index = lax.axis_index("tp")
    ctx_index = lax.axis_index("ctx")
    dp_index = lax.axis_index("dp")
    head = HEAD_SIZE
    map_rows = state_key.shape[1]
    group = dp_index * lax.axis_size("ctx") + ctx_index
    place = jnp.stack([ctx_index, tp_index, group, dp_index % 2, dp_index // 2]).astype(jnp.int32)

    def call(kernel, grid, in_specs, out_specs, out_shape, scratch=(), prefetch=1, **more):
        return pl.pallas_call(
            kernel,
            grid_spec=pltpu.PrefetchScalarGridSpec(
                num_scalar_prefetch=prefetch, grid=grid, in_specs=in_specs, out_specs=out_specs,
                scratch_shapes=list(scratch),
            ),
            out_shape=out_shape,
            compiler_params=params(),
            **more,
        )

    at_slots = 3 * own_rows
    at_init = at_slots + own_slots
    at_maps = at_init + own_slots
    at_vectors = at_maps + 2 * map_rows
    full_rows = at_vectors + 16
    vectors = (gain_attn, gain_mlp, gate_bias, bias_table)
    ends = np.cumsum([0] + [item.shape[1] for item in vectors])
    tail = jnp.concatenate(vectors, axis=1)
    tail = jnp.pad(tail, ((0, 16 - local_heads), (0, shard_width - tail.shape[1])))
    item = pl.pallas_call(
        item_kernel, out_shape=jax.ShapeDtypeStruct((full_rows, shard_width), BF)
    )(w_query, w_key, w_value, state_query, state_init, state_key, state_value, tail)
    x = lax.all_to_all(tokens, "tp", 0, 0, tiled=True)
    late_width = 2 * hidden + shard_width
    late = pl.pallas_call(
        pack_kernel, out_shape=jax.ShapeDtypeStruct((own_rows, late_width), BF)
    )(w_up, w_down, w_out)
    first_own, first_other, x, late = gather_pairs(item, x, late, place)
    x = x.reshape(shards, rows, shard_width)
    late = lax.all_gather(late, everywhere, axis=0, tiled=True)
    late = late.reshape(shards, groups, own_rows, late_width)

    at_heads = slice(at_vectors, at_vectors + local_heads)
    small = ordered(
        ctx_index, first_own[:, :, :, at_heads], first_other[:, :, :, at_heads], 2
    )

    def spread(index):
        part = small[..., ends[index] : ends[index + 1]]
        return jnp.transpose(part, (0, 3, 4, 1, 2, 5)).reshape(heads, -1).astype(F32)

    gain_one = spread(0).reshape(1, width)
    gain_two = spread(1).reshape(1, width)
    gate = jax.nn.sigmoid(spread(2)).reshape(1, width)
    bias_rows = spread(3)

    def whole(shape):
        return pl.BlockSpec(shape, lambda *_: (0,) * len(shape))

    def weight(index):
        spec = pl.BlockSpec(
            (1, pairs, 1, own_rows, shard_width), lambda t, *_: (t // half, 0, t % half, index, 0)
        )
        return [spec, spec]

    def of_head(count, index):
        def at(h, *_):
            t = h // local_heads
            return (t // half, 0, t % half, index, h % local_heads)

        spec = pl.BlockSpec((1, pairs, 1, count, head), at)
        return [spec, spec]

    column = pl.BlockSpec((rows, shard_width), lambda t, *_: (0, t))
    wide = jax.ShapeDtypeStruct((rows, width), BF)
    wide32 = jax.ShapeDtypeStruct((rows, width), F32)
    split = jax.ShapeDtypeStruct((shards, rows, shard_width), BF)
    halo = jax.ShapeDtypeStruct((seqs * BLOCK, width), BF)
    halo_column = pl.BlockSpec((2, seqs * BLOCK, shard_width), lambda t, *_: (0, 0, t))
    queries, keys, values, _, last_blocks = call(
        project_kernel,
        (shards,),
        [whole((shards, rows, shard_width)), whole((1, width))] + weight(0) + weight(1) + weight(2),
        [column, column, column, whole((rows, width)), halo_column],
        [wide] * 4 + [jax.ShapeDtypeStruct((2, seqs * BLOCK, width), BF)],
    )(place, x, gain_one, *([first_own, first_other] * 3))

    halos = from_behind(last_blocks, "ctx", 1)

    def along(rows_of, index):
        return pl.BlockSpec((rows_of, head), lambda h, n, *_: (index(n), h))

    def turned(n):
        return units - 1 - n

    query_slots = of_head(own_slots, at_slots // own_slots)
    init_slots = of_head(own_slots, at_init // own_slots)
    key_maps = of_head(map_rows, at_maps // map_rows)
    value_maps = of_head(map_rows, at_maps // map_rows + 1)
    channel = pl.BlockSpec((1, head), lambda h, n, *_: (0, h))
    slot_rows = units * slots
    slot_f32 = jax.ShapeDtypeStruct((slot_rows, width), F32)
    slot_low = jax.ShapeDtypeStruct((slot_rows, width), BF)
    message = jax.ShapeDtypeStruct((seqs * slots, width), BF)
    slot_scratch = pltpu.VMEM((slots, head), F32)
    own = along(BLOCK, lambda n: n)
    slot = along(slots, lambda n: n)
    slot_of_seq = along(slots, lambda n: n // blocks)
    contrib, accumulated = call(
        functools.partial(read_kernel, blocks=blocks),
        (heads, units),
        query_slots + [own, own, channel],
        [slot, slot_of_seq],
        [slot_f32, message],
        [slot_scratch],
    )(place, first_own, first_other, keys, values, gate)
    halos, accumulated = lax.optimization_barrier((halos, accumulated))
    power = gate**blocks
    lead = carry(accumulated, power, "ctx", False)
    lead_power = jnp.ones_like(gate)
    for step in range(lax.axis_size("ctx") - 1):
        lead_power = jnp.where(ctx_index > step, lead_power * power, lead_power)

    block_at = ctx_index * blocks + jnp.arange(blocks, dtype=jnp.int32)
    own_prefix = lax.dynamic_slice_in_dim(prefix, tp_index * seqs, seqs, 0)
    info = jnp.stack(
        [
            jnp.broadcast_to(block_at[None], (seqs, blocks)),
            own_prefix[:, None] - block_at[None] * BLOCK,
        ],
        axis=-1,
    ).reshape(units, 2)
    span = 4 * BLOCK
    offset = np.arange(span)
    offset = np.where(offset < 2 * BLOCK, offset, offset - span)
    forward_hot = one_hot(BLOCK - offset, offset > -BLOCK, buckets)
    back_span = 3 * BLOCK
    back_offset = np.arange(back_span)
    back_offset = np.where(back_offset < BLOCK, back_offset, back_offset - back_span)
    backward_hot = one_hot(BLOCK + back_offset, back_offset > -2 * BLOCK, buckets)
    exact = lax.Precision.HIGHEST
    scaled_bias = bias_rows * LOG2E
    forward_bias = jnp.dot(scaled_bias, forward_hot.T, precision=exact)[:, None]
    backward_bias = jnp.dot(scaled_bias, backward_hot.T, precision=exact)[:, None]

    def attend_specs(index):
        before = along(BLOCK, lambda n: jnp.maximum(index(n) - 1, 0))
        by_seq = [
            pl.BlockSpec((None, BLOCK, head), lambda h, n, *_, part=part: (part, index(n) // blocks, h))
            for part in range(2)
        ]
        here = along(BLOCK, index)
        return [here, here, here, before, before] + by_seq + key_maps + value_maps

    def lse_spec(index):
        return pl.BlockSpec((1, 1, 1, BLOCK), lambda h, n, *_: (index(n), h, 0, 0))

    def vector(size):
        return pl.BlockSpec((1, 1, size), lambda h, *_: (h, 0, 0))

    attend_args = (
        place, info, queries, keys, values, keys, values, halos, halos,
        first_own, first_other, first_own, first_other,
    )
    attended, lse, states, moved = call(
        functools.partial(attend_kernel, blocks=blocks),
        (heads, units),
        attend_specs(lambda n: n)
        + [slot] + init_slots + [slot_of_seq, channel, channel, vector(span)],
        [own, lse_spec(lambda n: n), slot, slot],
        [wide, jax.ShapeDtypeStruct((units, heads, 1, BLOCK), F32), slot_low, slot_low],
        [pltpu.VMEM((BLOCK, 2 * BLOCK), F32), slot_scratch],
        2,
    )(*attend_args, contrib, first_own, first_other, lead, lead_power, gate, forward_bias)

    out_weight = pl.BlockSpec(
        (1, groups, own_rows, shard_width), lambda t, *_: (t, 0, 0, 2 * hidden // shard_width)
    )
    middle, mlp_in = pl.pallas_call(
        out_kernel,
        grid=(shards,),
        in_specs=[column, out_weight, whole((shards, rows, shard_width)), whole((1, width))],
        out_specs=[whole((rows, width)), whole((rows, width))],
        out_shape=[wide32, wide],
        compiler_params=params(),
    )(attended, late, x, gain_two)

    tile = min(hidden, 1024)
    per_shard = hidden // tile
    tile_block = (1, groups, own_rows, tile)
    output, middle_grad, gain_two_grad, late_grad = call(
        mlp_kernel,
        (shards * per_shard, 2),
        [
            whole((rows, width)),
            pl.BlockSpec((rows, width), lambda i, j, place_ref: (place_ref[1], 0)),
            whole((rows, width)), whole((1, width)),
            pl.BlockSpec(tile_block, lambda i, j, *_: (i // per_shard, 0, 0, i % per_shard)),
            pl.BlockSpec(
                tile_block, lambda i, j, *_: (i // per_shard, 0, 0, per_shard + i % per_shard)
            ),
        ],
        [
            whole((shards, rows, shard_width)), whole((rows, width)), whole((1, width)),
            pl.BlockSpec(
                tile_block, lambda i, j, *_: (i // per_shard, 0, 0, j * per_shard + i % per_shard)
            ),
        ],
        [
            split, wide, jax.ShapeDtypeStruct((1, width), F32),
            jax.ShapeDtypeStruct((shards, groups, own_rows, late_width), BF),
        ],
        [
            pltpu.VMEM((width, rows), BF), pltpu.VMEM((width, rows), BF),
            pltpu.VMEM((rows, width), F32), pltpu.VMEM((rows, width), F32),
            pltpu.VMEM((rows, tile), BF),
        ],
    )(
        place, mlp_in, cotangent.reshape(seq_count * length, width), middle, gain_two, late, late
    )
    output = lax.all_to_all(output, "tp", 0, 0, tiled=True)

    late_grad = pl.pallas_call(
        out_gradient_kernel,
        grid=(shards,),
        in_specs=[whole((rows, width)), column, pl.BlockSpec(memory_space=pl.ANY)],
        out_specs=out_weight,
        out_shape=jax.ShapeDtypeStruct(late_grad.shape, BF),
        scratch_shapes=[pltpu.VMEM((width, rows), BF)],
        compiler_params=params(),
        input_output_aliases={2: 0},
    )(middle_grad, attended, late_grad)
    grad_attended = pl.pallas_call(
        out_back_kernel,
        grid=(shards,),
        in_specs=[whole((rows, width)), out_weight],
        out_specs=column,
        out_shape=wide,
        compiler_params=params(),
    )(middle_grad, late)
    late_grad = lax.psum_scatter(
        late_grad.reshape(shards * groups * own_rows, late_width), everywhere,
        scatter_dimension=0, tiled=True,
    )
    head_sum = jax.ShapeDtypeStruct((heads, head, head), F32)
    head_map = pl.BlockSpec((1, head, head), lambda h, n, *_: (h, 0, 0))
    back_own = along(BLOCK, turned)
    back_slot = along(slots, turned)
    back_of_seq = along(slots, lambda n: turned(n) // blocks)
    key_of_seq = along(BLOCK, lambda n: turned(n) // blocks)
    (
        grad_queries, dk, dv, dk_before, dv_before, direct, key_map_grad, value_map_grad,
        bias_sum, gathered, first_keys, first_values,
    ) = call(
        functools.partial(attend_back_kernel, blocks=blocks),
        (heads, units),
        attend_specs(turned)
        + [back_slot, channel, vector(back_span), back_own, back_own, lse_spec(turned)],
        [back_own] * 5 + [back_slot, head_map, head_map, vector(back_span), back_of_seq]
        + [key_of_seq, key_of_seq],
        [
            wide, wide32, wide32, wide, wide, slot_f32, head_sum, head_sum,
            jax.ShapeDtypeStruct((heads, 1, back_span), F32), message, halo, halo,
        ],
        [
            pltpu.VMEM((2 * BLOCK, BLOCK), F32), pltpu.VMEM((128, back_span), F32),
            pltpu.VMEM((BLOCK, head), F32), slot_scratch,
        ],
        2,
    )(*attend_args, states, gate, backward_bias, grad_attended, attended, lse)
    dk, output = lax.optimization_barrier((dk, output))
    sum_at = np.arange(back_span) - BLOCK
    sum_hot = one_hot(sum_at, sum_at > -BLOCK, buckets)
    bias_grad = jnp.dot(bias_sum[:, 0], sum_hot, precision=exact)

    later = carry(gathered, power, "ctx", True)
    back_keys = from_behind(first_keys, "ctx", -1)
    back_values = from_behind(first_values, "ctx", -1)
    following = along(BLOCK, lambda n: jnp.minimum(turned(n) + 1, units - 1))
    kept_slot = pl.BlockSpec((slots, head), lambda h, n, *_: (0, h))
    slot_sum = jax.ShapeDtypeStruct((slots, width), F32)
    grad_keys, grad_values, slot_query_grad, init_grad, gate_grad = call(
        functools.partial(read_back_kernel, blocks=blocks),
        (heads, units),
        query_slots
        + [back_own, back_own, back_slot, back_slot, back_of_seq, channel]
        + [back_own, back_own, following, following, key_of_seq, key_of_seq],
        [back_own, back_own, kept_slot, kept_slot, vector(head)],
        [wide, wide, slot_sum, slot_sum, jax.ShapeDtypeStruct((heads, 1, head), F32)],
        [slot_scratch],
    )(
        place, first_own, first_other, keys, values, direct, moved, later, gate,
        dk, dv, dk_before, dv_before, back_keys, back_values,
    )

    maps_of = pl.BlockSpec((local_heads, head, head), lambda t, *_: (t, 0, 0))
    slots_of = pl.BlockSpec((slots, shard_width), lambda t, *_: (0, t))
    piece = pl.BlockSpec((1, pairs, full_rows, shard_width), lambda t, *_: (t, 0, 0, 0))
    pieces = jax.ShapeDtypeStruct((shards, pairs, full_rows, shard_width), BF)
    token_shards = whole((shards, rows, shard_width))
    weights = weight(0) + weight(1) + weight(2)
    weight_args = [first_own, first_other] * 3
    grad_own, grad_other, gain_one_grad = call(
        weight_back_kernel,
        (shards,),
        [token_shards, whole((1, width)), column, column, column]
        + weights + [slots_of, slots_of, maps_of, maps_of],
        [piece, piece, whole((width, 1))],
        [pieces, pieces, jax.ShapeDtypeStruct((width, 1), F32)],
        [
            pltpu.VMEM((width, rows), BF), pltpu.VMEM((groups, full_rows, shard_width), BF),
            pltpu.VMEM((width, shard_width), F32),
        ],
    )(
        place, x, gain_one, grad_queries, grad_keys, grad_values, *weight_args,
        slot_query_grad, init_grad, key_map_grad, value_map_grad,
    )
    gain_one_grad = gain_one_grad.reshape(1, width) / gain_one
    token_grad = call(
        project_back_kernel,
        (shards,),
        [token_shards, whole((rows, width)), whole((1, width)), column, column, column] + weights,
        token_shards,
        split,
        [pltpu.VMEM((rows, width), F32)],
    )(place, x, middle_grad, gain_one, grad_queries, grad_keys, grad_values, *weight_args)
    token_grad = lax.all_to_all(token_grad, "tp", 0, 0, tiled=True)

    vector_sums = [gain_one_grad, gain_two_grad, gate_grad.reshape(1, width), bias_grad]
    vector_rows = jnp.concatenate([item.reshape(-1) for item in vector_sums])
    vector_rows = jnp.pad(vector_rows, (0, 16 * shard_width - vector_rows.size)).astype(BF)
    vector_rows = jnp.broadcast_to(
        vector_rows.reshape(1, 1, 16, shard_width), (shards, pairs, 16, shard_width)
    )
    grad_own = lax.dynamic_update_slice(grad_own, vector_rows, (0, 0, at_vectors, 0))
    grad_other = lax.dynamic_update_slice(grad_other, vector_rows, (0, 0, at_vectors, 0))
    terms = scatter_pairs(grad_own, grad_other)
    activation = jax.ShapeDtypeStruct(output.shape, BF)
    late_parts = pl.pallas_call(
        unpack_kernel,
        out_shape=[
            jax.ShapeDtypeStruct(w_up.shape, F32), jax.ShapeDtypeStruct(w_down.shape, F32),
            jax.ShapeDtypeStruct(w_out.shape, F32), activation, activation,
        ],
        compiler_params=params(),
    )(late_grad, output, token_grad)
    terms, late_parts = lax.optimization_barrier((terms, late_parts))
    up_grad, down_grad, out_grad, output, token_grad = late_parts
    parts = (
        w_query, w_key, w_value, state_query, state_init, state_key, state_value,
        gain_attn, gain_mlp, gate_bias, bias_table,
    )
    sums = call(
        finish_kernel,
        (1,),
        [whole((full_rows, shard_width))] * shards,
        [whole(item.shape) for item in parts],
        [jax.ShapeDtypeStruct(item.shape, F32) for item in parts],
        [pltpu.VMEM((16, shard_width), F32)],
    )(place, *terms)
    return (
        output.reshape(seq_count, length, shard_width),
        token_grad.reshape(seq_count, length, shard_width),
        *sums[:3],
        out_grad,
        up_grad,
        down_grad,
        *sums[3:5],
        sums[7],
        sums[8],
        sums[10],
        sums[9],
        *sums[5:7],
    )


def choose(tokens, *others):
    shards = lax.axis_size("tp")
    even = tokens.shape[0] % shards == 0 and shards % 2 == 0 and shards & (shards - 1) == 0
    even = even and lax.axis_size("dp") == 4 and lax.axis_size("ctx") == 2
    return (sequence_body if even else body)(tokens, *others)


def solution(mesh):
    in_specs = (
        P("dp", "ctx", "tp"),
        P("dp", "ctx", None),
        P("dp"),
        P(("dp", "ctx"), "tp"),
        P(("dp", "ctx"), "tp"),
        P(("dp", "ctx"), "tp"),
        P("tp", ("dp", "ctx")),
        P(("dp", "ctx"), "tp"),
        P("tp", ("dp", "ctx")),
        P(("dp", "ctx"), "tp"),
        P(("dp", "ctx"), "tp"),
        P("tp", ("dp", "ctx")),
        P("tp", ("dp", "ctx")),
        P("tp", ("dp", "ctx")),
        P("tp", ("dp", "ctx")),
        P("tp", ("dp", "ctx"), None),
        P("tp", ("dp", "ctx"), None),
    )
    out_specs = (
        P("dp", "ctx", "tp"),
        P("dp", "ctx", "tp"),
        P(("dp", "ctx"), "tp"),
        P(("dp", "ctx"), "tp"),
        P(("dp", "ctx"), "tp"),
        P("tp", ("dp", "ctx")),
        P(("dp", "ctx"), "tp"),
        P("tp", ("dp", "ctx")),
        P(("dp", "ctx"), "tp"),
        P(("dp", "ctx"), "tp"),
        P("tp", ("dp", "ctx")),
        P("tp", ("dp", "ctx")),
        P("tp", ("dp", "ctx")),
        P("tp", ("dp", "ctx")),
        P("tp", ("dp", "ctx"), None),
        P("tp", ("dp", "ctx"), None),
    )
    return jax.shard_map(choose, mesh=mesh, in_specs=in_specs, out_specs=out_specs, check_vma=False)
```
